32 devices in a mesh: dp: 16 (over z, y, x), mp: 2 (over core).
Axes of the slice: x: 2, y: 2, z: 4, core: 2. Of those that a mesh axis runs over, the one named last changes fastest.
Arguments:
- tokens: bfloat16 [32768, 768], P('dp'), may hold values from -6 to 6
- cond: bfloat16 [32768, 128], P('dp'), may hold values from -6 to 6
- segments: int32 [32, 1024], P('dp'), may hold values from 0 to 3, never falling along the last dimension, each value on 1 to 512 neighbouring positions
- out_grad: bfloat16 [32768, 768], P('dp'), may hold values from -6 to 6
- step: int32 [1], replicated, may hold values from 2 to 20
- ada_weight: float32 [128, 4608], P(None, 'dp'), may hold values from -0.5 to 0.5
- ada_first: float32 [128, 4608], P(None, 'dp'), may hold values from -0.00061035156 to 0.00061035156
- ada_second: float32 [128, 4608], P(None, 'dp'), may hold values from 1.3031258e-10 to 5.212503e-10
- norm_params: float32 [8, 768], P(None, 'dp'), may hold values from 0.5 to 1.5
- norm_first: float32 [8, 768], P(None, 'dp'), may hold values from -0.0024414062 to 0.0024414062
- norm_second: float32 [8, 768], P(None, 'dp'), may hold values from 2.6062516e-10 to 1.0425006e-09
- qkv_weight: float32 [3, 768, 768], P(None, 'dp', 'mp'), may hold values from -0.109375 to 0.109375
- qkv_first: float32 [3, 768, 768], P(None, 'dp', 'mp'), may hold values from -0.00061035156 to 0.00061035156
- qkv_second: float32 [3, 768, 768], P(None, 'dp', 'mp'), may hold values from 1.3031258e-10 to 5.212503e-10
- out_weight: float32 [768, 768], P('mp', 'dp'), may hold values from -1.75 to 1.75
- out_first: float32 [768, 768], P('mp', 'dp'), may hold values from -0.00061035156 to 0.00061035156
- out_second: float32 [768, 768], P('mp', 'dp'), may hold values from 1.6289073e-11 to 6.515629e-11
- up_weight: float32 [768, 3072], P('dp', 'mp'), may hold values from -0.21875 to 0.21875
- up_first: float32 [768, 3072], P('dp', 'mp'), may hold values from -0.00061035156 to 0.00061035156
- up_second: float32 [768, 3072], P('dp', 'mp'), may hold values from 1.3031258e-10 to 5.212503e-10
- down_weight: float32 [3072, 768], P('mp', 'dp'), may hold values from -0.109375 to 0.109375
- down_first: float32 [3072, 768], P('mp', 'dp'), may hold values from -0.00061035156 to 0.00061035156
- down_second: float32 [3072, 768], P('mp', 'dp'), may hold values from 1.3031258e-10 to 5.212503e-10
Outputs:
- result: bfloat16 [32768, 768], P('dp')
- input_grad: float32 [32768, 768], P('dp')
- grad_norm: float32 [1], replicated
- ada_weight_next: float32 [128, 4608], P(None, 'dp')
- ada_first_next: float32 [128, 4608], P(None, 'dp')
- ada_second_next: float32 [128, 4608], P(None, 'dp')
- norm_params_next: float32 [8, 768], P(None, 'dp')
- norm_first_next: float32 [8, 768], P(None, 'dp')
- norm_second_next: float32 [8, 768], P(None, 'dp')
- qkv_weight_next: float32 [3, 768, 768], P(None, 'dp', 'mp')
- qkv_first_next: float32 [3, 768, 768], P(None, 'dp', 'mp')
- qkv_second_next: float32 [3, 768, 768], P(None, 'dp', 'mp')
- out_weight_next: float32 [768, 768], P('mp', 'dp')
- out_first_next: float32 [768, 768], P('mp', 'dp')
- out_second_next: float32 [768, 768], P('mp', 'dp')
- up_weight_next: float32 [768, 3072], P('dp', 'mp')
- up_first_next: float32 [768, 3072], P('dp', 'mp')
- up_second_next: float32 [768, 3072], P('dp', 'mp')
- down_weight_next: float32 [3072, 768], P('mp', 'dp')
- down_first_next: float32 [3072, 768], P('mp', 'dp')
- down_second_next: float32 [3072, 768], P('mp', 'dp')
The draws below stay inside these ranges and needn't reach their ends.
Inputs may be any that keep to these rules, and one draw needn't show every extreme that they name: `segments`: along each sequence document ids never fall; each document holds 1 to 512 positions, and one document of a sequence holds exactly 512.
All inputs are finite; a program needn't handle non-finite values.
Results may differ from the reference program's by a relative error of at most 0.012.
The reference program's roundings to bfloat16 on the way count: a program that leaves them out, or rounds other values in their place, can miss the bound.
Values may be sent and summed in bfloat16 or wider, within the bound.
A program may use at most 320 MiB of HBM per device.

```python
import math
import jax
import jax.numpy as jnp
import numpy as np
from jax import lax

D = 768
HEADS = 12
HEAD_DIM = 64
FF = 3072
COND = 128
SEQ_LEN = 1024
DOCS = 4
SEQS = 32
TOKENS = 32768
PARAMS = 7673856


def levels(rng, extent, shards, least, high):
    factor_of, own = 1.0, jax.random.fold_in(rng, 6)
    for position, shards_of in shards:
        draws = jnp.exp(jax.random.uniform(jax.random.fold_in(own, position), (shards_of,), jnp.float32, least / len(shards), high / len(shards)))
        factor_of = factor_of * jnp.repeat(draws, extent[position] // shards_of).reshape([-1 if axis == position else 1 for axis in range(len(extent))])
    return factor_of


def split_up(number_of, total, limit, skew):
    loads = [(1 << 20) // math.isqrt(standing ** skew) + 1 for standing in range(2, number_of + 1)]
    spare, counts = total - limit - (number_of - 1), [1] * (number_of - 1)
    while spare > 0:
        candidates = [i for i in range(number_of - 1) if counts[i] < limit]
        mass, budget = sum([loads[i] for i in candidates]), spare
        for i in candidates:
            addition = min(limit - counts[i], max(1, budget * loads[i] // mass), spare)
            counts[i] = counts[i] + addition
            spare = spare - addition
    return np.array([limit] + counts)


def ragged_sizes(rng, count, total, bound, lean):
    if count == 2:
        one = jax.random.randint(rng, (), max(1, total - bound), min(bound, total - 1) + 1)
        return jnp.stack([one, total - one])
    tallies = jnp.asarray(split_up(count, total, bound, lean), jnp.int32)
    couples = (count - 1) // 2
    source_of, taker = tallies[1:1 + 2 * couples:2], tallies[2:2 + 2 * couples:2]
    margin = jnp.minimum(source_of - 1, bound - taker)
    passed = jax.random.randint(jax.random.fold_in(rng, 1), (couples,), 0, 1 << 20) % (margin + 1)
    tallies = tallies.at[1:1 + 2 * couples:2].set(source_of - passed).at[2:2 + 2 * couples:2].set(taker + passed)
    return tallies[jax.random.permutation(jax.random.fold_in(rng, 2), count)]


def bell_draw(rng, shape, scale, most, shards=(), kind=jnp.bfloat16):
    entries = scale * jax.random.normal(rng, shape, jnp.float32)
    if shards:
        entries = entries * levels(rng, shape, shards, -0.22, 0.18)
    return jnp.clip(entries, -most, most).astype(kind)


def setup_inputs(seed: int = 0) -> dict:
    key_list = jax.random.split(jax.random.key(seed), 24)
    return {
        "tokens": bell_draw(key_list[0], (TOKENS, D), 1.0, 6.0, ((0, 16),)),
        "cond": bell_draw(key_list[1], (TOKENS, COND), 1.0, 6.0, ((0, 16),)),
        "segments": jax.vmap(lambda own: jnp.searchsorted(jnp.cumsum(ragged_sizes(own, DOCS, SEQ_LEN, SEQ_LEN // 2, 1)), jnp.arange(SEQ_LEN), side="right"))(jax.random.split(key_list[2], SEQS)).reshape((SEQS, SEQ_LEN)).astype(jnp.int32),
        "out_grad": bell_draw(key_list[3], (TOKENS, D), 1.0, 6.0, ((0, 16),)),
        "step": jax.random.randint(key_list[4], (1,), 2, 21).astype(jnp.int32),
        "ada_weight": bell_draw(key_list[5], (COND, 6 * D), COND ** -0.5, 0.5, ((1, 16),), jnp.float32),
        "ada_first": bell_draw(key_list[6], (COND, 6 * D), (0.11 / PARAMS ** 0.5), 0.00061035156, ((1, 16),), jnp.float32),
        "ada_second": jnp.clip(jnp.exp(math.log(5.212503206841745e-10) - 1.3862944 * jax.random.uniform(key_list[7], (COND, 6 * D), jnp.float32) ** levels(key_list[7], (COND, 6 * D), ((1, 16),), -0.2, 0.2)), 1.3031258017104363e-10, 5.212503206841745e-10),
        "norm_params": jnp.clip(1.0 + 0.1 * jax.random.normal(key_list[8], (8, D), jnp.float32), 0.5, 1.5),
        "norm_first": bell_draw(key_list[9], (8, D), (0.44 / PARAMS ** 0.5), 0.0024414062, ((1, 16),), jnp.float32),
        "norm_second": jnp.clip(jnp.exp(math.log(1.042500641368349e-09) - 1.3862944 * jax.random.uniform(key_list[10], (8, D), jnp.float32) ** levels(key_list[10], (8, D), ((1, 16),), -0.2, 0.2)), 2.6062516034208727e-10, 1.042500641368349e-09),
        "qkv_weight": bell_draw(key_list[11], (3, D, D), (4 * D) ** -0.5, 0.109375, ((1, 16), (2, 2)), jnp.float32),
        "qkv_first": bell_draw(key_list[12], (3, D, D), (0.11 / PARAMS ** 0.5), 0.00061035156, ((1, 16), (2, 2)), jnp.float32),
        "qkv_second": jnp.clip(jnp.exp(math.log(5.212503206841745e-10) - 1.3862944 * jax.random.uniform(key_list[13], (3, D, D), jnp.float32) ** levels(key_list[13], (3, D, D), ((1, 16), (2, 2)), -0.2, 0.2)), 1.3031258017104363e-10, 5.212503206841745e-10),
        "out_weight": bell_draw(key_list[14], (D, D), (D // 64) ** -0.5, 1.75, ((0, 2), (1, 16)), jnp.float32),
        "out_first": bell_draw(key_list[15], (D, D), (0.11 / PARAMS ** 0.5), 0.00061035156, ((0, 2), (1, 16)), jnp.float32),
        "out_second": jnp.clip(jnp.exp(math.log(6.515629008552182e-11) - 1.3862944 * jax.random.uniform(key_list[16], (D, D), jnp.float32) ** levels(key_list[16], (D, D), ((0, 2), (1, 16)), -0.2, 0.2)), 1.6289072521380454e-11, 6.515629008552182e-11),
        "up_weight": bell_draw(key_list[17], (D, FF), D ** -0.5, 0.21875, ((0, 16), (1, 2)), jnp.float32),
        "up_first": bell_draw(key_list[18], (D, FF), (0.11 / PARAMS ** 0.5), 0.00061035156, ((0, 16), (1, 2)), jnp.float32),
        "up_second": jnp.clip(jnp.exp(math.log(5.212503206841745e-10) - 1.3862944 * jax.random.uniform(key_list[19], (D, FF), jnp.float32) ** levels(key_list[19], (D, FF), ((0, 16), (1, 2)), -0.2, 0.2)), 1.3031258017104363e-10, 5.212503206841745e-10),
        "down_weight": bell_draw(key_list[20], (FF, D), FF ** -0.5, 0.109375, ((0, 2), (1, 16)), jnp.float32),
        "down_first": bell_draw(key_list[21], (FF, D), (0.11 / PARAMS ** 0.5), 0.00061035156, ((0, 2), (1, 16)), jnp.float32),
        "down_second": jnp.clip(jnp.exp(math.log(5.212503206841745e-10) - 1.3862944 * jax.random.uniform(key_list[22], (FF, D), jnp.float32) ** levels(key_list[22], (FF, D), ((0, 2), (1, 16)), -0.2, 0.2)), 1.3031258017104363e-10, 5.212503206841745e-10),
    }


@jax.custom_vjp
def low(v):
    return lax.optimization_barrier(v.astype(jnp.bfloat16)).astype(jnp.float32)

@jax.custom_vjp
def low_back(v):
    return v

def low_keep(v):
    return (low(v), None)

def low_pass(kept, grad):
    return (grad,)

def back_keep(v):
    return (v, None)

def back_low(kept, grad):
    return (low(grad),)
low.defvjp(low_keep, low_pass)
low_back.defvjp(back_keep, back_low)
clip_limit = 1.0
step_rates = (0.075, 0.75, 0.075, 0.25, 0.075, 0.075)
decay_rates = (0.01, 0.0, 0.01, 0.01, 0.01, 0.01)

def precise(left, right):
    return jnp.dot(left, right, precision=lax.Precision.HIGHEST)

def modnorm(inputs, gain_row, shift_row, scale_row):
    centre = inputs - lax.optimization_barrier(jnp.mean(inputs, axis=-1, keepdims=True))
    spread = lax.optimization_barrier(jnp.mean(centre * centre, axis=-1, keepdims=True))
    return centre * lax.rsqrt(spread + 1e-05) * gain_row * (1.0 + scale_row) + shift_row

def rope_tables(length, head_size):
    half_dim = head_size // 2
    inverse = jnp.exp(jnp.arange(half_dim, dtype=jnp.float32) * (-2.0 * math.log(10000.0) / head_size))
    angles = jnp.arange(length, dtype=jnp.float32)[:, None] * inverse[None, :]
    return (jnp.cos(angles), jnp.sin(angles))

def rotate(values, cosines, sines):
    half_dim = values.shape[-1] // 2
    first_half = values[..., :half_dim]
    second_half = values[..., half_dim:]
    cos_row = cosines[:, None, :]
    sin_row = sines[:, None, :]
    return jnp.concatenate([first_half * cos_row - second_half * sin_row, second_half * cos_row + first_half * sin_row], axis=-1)

def adam_update(weight, first_moment, second_moment, grad_mean, clip_factor, step_count, step_rate, decay_rate):
    clipped = grad_mean * clip_factor
    first_new = 0.9 * first_moment + 0.1 * clipped
    second_new = 0.999 * second_moment + 0.001 * clipped * clipped
    fix_one = 1.0 - jnp.exp(step_count * math.log(0.9))
    fix_two = 1.0 - jnp.exp(step_count * math.log(0.999))
    update = first_new / fix_one / (jnp.sqrt(second_new / fix_two) + 1e-08) + decay_rate * weight
    return (weight - step_rate * update, first_new, second_new)

def reference(tokens, cond, segments, out_grad, step, ada_weight, ada_first, ada_second, norm_params, norm_first, norm_second, qkv_weight, qkv_first, qkv_second, out_weight, out_first, out_second, up_weight, up_first, up_second, down_weight, down_first, down_second):
    inputs = tokens.astype(jnp.float32)
    cond_low = low(jax.nn.silu(cond.astype(jnp.float32)))
    cosines, sines = rope_tables(SEQ_LEN, HEAD_DIM)
    score_scale = HEAD_DIM ** (-0.5)

    def attend(packed):
        query_block, key_block, value_block, segment_row = packed
        raw_scores = low_back(jnp.einsum('qhd,khd->hqk', query_block, key_block, precision=lax.Precision.HIGHEST))
        same_doc = segment_row[:, None] == segment_row[None, :]
        scores = jnp.where(same_doc[None], raw_scores * score_scale, -1e+30)
        softmax_w = jax.nn.softmax(scores, axis=-1)
        mixed_out = jnp.einsum('hqk,khd->qhd', low(softmax_w), value_block, precision=lax.Precision.HIGHEST)
        return low(low_back(mixed_out))

    def forward(inputs, ada_master, norm_master, qkv_master, out_master, up_master, down_master):
        ada_low = low(ada_master)
        norm_low = low(norm_master)
        qkv_low = low(qkv_master)
        out_low = low(out_master)
        up_low = low(up_master)
        down_low = low(down_master)
        modulation = low_back(precise(cond_low, ada_low) + norm_low[2:].reshape(-1))
        shift_one = modulation[:, 0:D]
        scale_one = modulation[:, D:2 * D]
        gate_one = modulation[:, 2 * D:3 * D]
        shift_two = modulation[:, 3 * D:4 * D]
        scale_two = modulation[:, 4 * D:5 * D]
        gate_two = modulation[:, 5 * D:6 * D]
        h_one = low(modnorm(inputs, norm_low[0], shift_one, scale_one))
        proj_q = low_back(precise(h_one, qkv_low[0])).reshape(SEQS, SEQ_LEN, HEADS, HEAD_DIM)
        proj_k = low_back(precise(h_one, qkv_low[1])).reshape(SEQS, SEQ_LEN, HEADS, HEAD_DIM)
        proj_v = low_back(precise(h_one, qkv_low[2])).reshape(SEQS, SEQ_LEN, HEADS, HEAD_DIM)
        queries = low(rotate(proj_q, cosines, sines))
        keys = low(rotate(proj_k, cosines, sines))
        values = low(proj_v)
        attended = lax.map(jax.checkpoint(attend), (queries, keys, values, segments))
        branch = low_back(precise(attended.reshape(TOKENS, D), out_low))
        middle = inputs + gate_one * branch
        h_two = low(modnorm(middle, norm_low[1], shift_two, scale_two))
        hidden_pre = low_back(precise(h_two, up_low))
        hidden = low(jax.nn.gelu(hidden_pre, approximate=True))
        mlp_out = low_back(precise(hidden, down_low))
        return middle + gate_two * mlp_out
    result, backward = jax.vjp(forward, inputs, ada_weight, norm_params, qkv_weight, out_weight, up_weight, down_weight)
    grads_all = backward(out_grad.astype(jnp.float32))
    input_grad = grads_all[0]
    grad_means = [grad_w / TOKENS for grad_w in grads_all[1:]]
    total_sq = sum((jnp.sum(grad_w * grad_w) for grad_w in grad_means))
    grad_norm = jnp.sqrt(total_sq)
    clip_factor = jnp.minimum(1.0, clip_limit / (grad_norm + 1e-06))
    step_count = step[0].astype(jnp.float32)
    ada_new = adam_update(ada_weight, ada_first, ada_second, grad_means[0], clip_factor, step_count, step_rates[0], decay_rates[0])
    norm_new = adam_update(norm_params, norm_first, norm_second, grad_means[1], clip_factor, step_count, step_rates[1], decay_rates[1])
    qkv_new = adam_update(qkv_weight, qkv_first, qkv_second, grad_means[2], clip_factor, step_count, step_rates[2], decay_rates[2])
    out_new = adam_update(out_weight, out_first, out_second, grad_means[3], clip_factor, step_count, step_rates[3], decay_rates[3])
    up_new = adam_update(up_weight, up_first, up_second, grad_means[4], clip_factor, step_count, step_rates[4], decay_rates[4])
    down_new = adam_update(down_weight, down_first, down_second, grad_means[5], clip_factor, step_count, step_rates[5], decay_rates[5])
    return (result.astype(jnp.bfloat16), input_grad, grad_norm.reshape(1), ada_new[0], ada_new[1], ada_new[2], norm_new[0], norm_new[1], norm_new[2], qkv_new[0], qkv_new[1], qkv_new[2], out_new[0], out_new[1], out_new[2], up_new[0], up_new[1], up_new[2], down_new[0], down_new[1], down_new[2])
```

```python
import functools
import math

import jax
import jax.numpy as jnp
from jax import lax
from jax.experimental import pallas as pl
from jax.experimental.pallas import tpu as pltpu
from jax.sharding import PartitionSpec as P

HEAD_DIM = 64
LANES = 128
MASKED = -1e30
ROW_BLOCK = 256
VMEM_LIMIT = 64_000_000
clip_limit = 1.0
step_rates = (0.075, 0.75, 0.075, 0.25, 0.075, 0.075)
decay_rates = (0.01, 0.0, 0.01, 0.01, 0.01, 0.01)

F32 = jnp.float32
BF = jnp.bfloat16
NN = (((1,), (0,)), ((), ()))
NT = (((1,), (1,)), ((), ()))


def dot(left, right, dims=NN):
    return lax.dot_general(left, right, dims, preferred_element_type=F32)


def shape_of(shape, dtype):
    return jax.ShapeDtypeStruct(shape, dtype)


def resident(shape, index):
    return pl.BlockSpec(shape, lambda *_: index, pipeline_mode=pl.Buffered(1))


def params():
    return pltpu.CompilerParams(vmem_limit_bytes=VMEM_LIMIT)


def adam_update(weight, first, second, grad, clip_factor, fix_one, fix_two, rate, decay):
    clipped = grad * clip_factor
    first_new = 0.9 * first + 0.1 * clipped
    second_new = 0.999 * second + 0.001 * clipped * clipped
    update = first_new / fix_one / (jnp.sqrt(second_new / fix_two) + 1e-08) + decay * weight
    return (weight - rate * update, first_new, second_new)


def rope_tables(length):
    half = HEAD_DIM // 2
    inverse = jnp.exp(jnp.arange(half, dtype=F32) * (-2.0 * math.log(10000.0) / HEAD_DIM))
    angles = jnp.arange(length, dtype=F32)[:, None] * inverse[None, :]
    cosines, sines = jnp.cos(angles), jnp.sin(angles)
    return (
        jnp.concatenate([cosines] * 4, axis=1),
        jnp.concatenate([-sines, sines, -sines, sines], axis=1),
    )


def swap_halves(values):
    width = values.shape[1]
    lane = lax.broadcasted_iota(jnp.int32, values.shape, 1)
    ahead = pltpu.roll(values, width - HEAD_DIM // 2, 1)
    behind = pltpu.roll(values, HEAD_DIM // 2, 1)
    return jnp.where(lane % HEAD_DIM < HEAD_DIM // 2, ahead, behind)


def silu_low(cond):
    value = cond.astype(F32)
    return (value / (1.0 + jnp.exp(-value))).astype(BF)


def normalize(rows):
    centre = rows - jnp.mean(rows, axis=-1, keepdims=True)
    scale = lax.rsqrt(jnp.mean(centre * centre, axis=-1, keepdims=True) + 1e-05)
    return centre * scale, scale


def norm_backward(grad, normal, scale):
    return scale * (
        grad
        - jnp.mean(grad, axis=-1, keepdims=True)
        - normal * jnp.mean(grad * normal, axis=-1, keepdims=True)
    )


def cond_rows(cond):
    return jnp.concatenate([cond.T, jnp.ones((16, cond.shape[0]), BF)], axis=0)


def first_kernel(half, x_ref, c_ref, wa_ref, p_ref, wqa_ref, wqb_ref, cos_ref, sin_ref,
                 h_ref, q_ref, k_ref, v_ref):
    width = x_ref.shape[1]
    own = width // 2
    cond = silu_low(c_ref[...])
    mod = dot(cond, wa_ref[0 : 2 * width, :], NT)
    shift = mod[:, :width] + p_ref[2:3, :]
    scale = mod[:, width:] + p_ref[3:4, :]
    normal, _ = normalize(x_ref[...].astype(F32))
    h = (normal * p_ref[0:1, :] * (1.0 + scale) + shift).astype(BF)
    h_ref[...] = h
    cos = jnp.concatenate([cos_ref[...]] * (own // LANES), axis=1)
    sin = jnp.concatenate([sin_ref[...]] * (own // LANES), axis=1)
    for start, w_ref in ((0, wqa_ref), (own, wqb_ref)):
        cols = slice(start, start + own)
        query = dot(h, w_ref[:, 0:own])
        query = query * cos + swap_halves(query) * sin
        q_ref[:, cols] = (query * HEAD_DIM**-0.5).astype(BF)
        key = dot(h, w_ref[:, own : 2 * own])
        k_ref[:, cols] = (key * cos + swap_halves(key) * sin).astype(BF)
        v_ref[:, cols] = dot(h, w_ref[:, 2 * own :]).astype(BF)


def first_stage(half, tokens, cond, wa, norms, near, far, tables):
    width = tokens.shape[1]
    rows = tables[0].shape[0]
    blocks = rows // ROW_BLOCK
    mine = lambda i, half: (half[0] * blocks + i, 0)
    plain = lambda i, half: (i, 0)
    row = pl.BlockSpec((ROW_BLOCK, width), plain)
    return pl.pallas_call(
        first_kernel,
        grid_spec=pltpu.PrefetchScalarGridSpec(
            num_scalar_prefetch=1,
            grid=(blocks,),
            in_specs=[
                pl.BlockSpec((ROW_BLOCK, width), mine),
                pl.BlockSpec((ROW_BLOCK, cond.shape[1]), mine),
                resident(wa.shape, (0, 0)),
                resident(norms.shape, (0, 0)),
                resident((width, 3 * width // 2), (0, 0)),
                resident((width, 3 * width // 2), (0, 0)),
                pl.BlockSpec((ROW_BLOCK, LANES), plain),
                pl.BlockSpec((ROW_BLOCK, LANES), plain),
            ],
            out_specs=[row] * 4,
        ),
        out_shape=[shape_of((rows, width), BF)] * 4,
        compiler_params=params(),
        name="first_stage",
    )(half, tokens, cond, wa, norms, near, far, *tables)


def split_heads(pair, other):
    low = lax.broadcasted_iota(jnp.int32, pair.shape, 1) < HEAD_DIM
    return jnp.where(low, pair, other), jnp.where(low, other, pair)


def attend_kernel(lo_ref, hi_ref, q_ref, k_ref, v_ref, fq_ref, fk_ref, o_ref, lse_ref,
                  qz, kz, vt, *, bq, bk):
    length = q_ref.shape[0]
    qz[0], qz[1] = split_heads(q_ref[...], fq_ref[...])
    kz[0], kz[1] = split_heads(k_ref[...], fk_ref[...])
    vt[...] = v_ref[...].T

    def query_block(i, _):
        off = pl.multiple_of(i * bq, bq)
        queries = [qz[h, pl.ds(off, bq), :] for h in range(2)]

        def key_block(j, carry):
            koff = pl.multiple_of(j * bk, bk)
            scores = [dot(kz[h, pl.ds(koff, bk), :], queries[h], NT) for h in range(2)]
            out = []
            for h in range(2):
                top, total, mixed = carry[3 * h : 3 * h + 3]
                new_top = jnp.maximum(top, jnp.max(scores[h], axis=0, keepdims=True))
                weights = jnp.exp(scores[h] - new_top)
                fade = jnp.exp(top - new_top)
                total = total * fade + jnp.sum(weights, axis=0, keepdims=True)
                values = vt[HEAD_DIM * h : HEAD_DIM * (h + 1), pl.ds(koff, bk)]
                mixed = mixed * fade + dot(values, weights.astype(BF))
                out += [new_top, total, mixed]
            return tuple(out)

        start = (
            jnp.full((1, bq), -3e38, F32),
            jnp.zeros((1, bq), F32),
            jnp.zeros((HEAD_DIM, bq), F32),
        )
        done = lax.fori_loop(lo_ref[i], hi_ref[i], key_block, start * 2)
        mixed = jnp.concatenate([done[2] / done[1], done[5] / done[4]], axis=0)
        o_ref[pl.ds(off, bq), :] = mixed.T.astype(BF)
        lse_ref[0, 0:1, pl.ds(off, bq)] = done[0] + jnp.log(done[1])
        lse_ref[0, 1:2, pl.ds(off, bq)] = done[3] + jnp.log(done[4])
        return 0

    lax.fori_loop(0, length // bq, query_block, 0)


def block_ranges(segment, block, other):
    first, last = segment[::block], segment[block - 1 :: block]
    low = jnp.sum(segment[None, :] < first[:, None], axis=1)
    high = jnp.sum(segment[None, :] <= last[:, None], axis=1)
    return (low // other).astype(jnp.int32), ((high + other - 1) // other).astype(jnp.int32)


def document_features(segment):
    lane = lax.broadcasted_iota(jnp.int32, (segment.shape[0], LANES), 1) % HEAD_DIM
    same = lane == segment[:, None]
    query = jnp.where(same, 1.0, 0.0).astype(BF)
    key = jnp.where((lane < 4) & ~same, MASKED, 0.0).astype(BF)
    return query, key


def attend(queries, keys, values, segment, features, bq=1024, bk=512):
    length, width = queries.shape
    bq, bk = min(bq, length), min(bk, length)
    pairs = width // LANES
    low, high = block_ranges(segment, bq, bk)
    pair = pl.BlockSpec((length, LANES), lambda p, *_: (0, p))
    fixed = pl.BlockSpec((length, LANES), lambda p, *_: (0, 0))
    scratch = pltpu.VMEM((2, length, LANES), BF)
    return pl.pallas_call(
        functools.partial(attend_kernel, bq=bq, bk=bk),
        grid_spec=pltpu.PrefetchScalarGridSpec(
            num_scalar_prefetch=2,
            grid=(pairs,),
            in_specs=[pair, pair, pair, fixed, fixed],
            out_specs=[pair, pl.BlockSpec((1, 2, length), lambda p, *_: (p, 0, 0))],
            scratch_shapes=[scratch, scratch, pltpu.VMEM((LANES, length), BF)],
        ),
        out_shape=[shape_of((length, width), BF), shape_of((pairs, 2, length), F32)],
        compiler_params=params(),
        name="attend",
    )(low, high, queries, keys, values, *features)


def attend_back_kernel(lo_ref, hi_ref, q_ref, k_ref, v_ref, do_ref, o_ref, lse_ref, fq_ref,
                       fk_ref, cos_ref, sin_ref, dq_ref, dk_ref, dv_ref,
                       qz, kz, qm, dm, vm, kt, delta, dqt, *, bq, bk):
    length = q_ref.shape[0]
    zero = jnp.zeros((length, LANES), BF)
    qz[0], qz[1] = split_heads(q_ref[...], fq_ref[...])
    kz[0], kz[1] = split_heads(k_ref[...], fk_ref[...])
    qm[0], qm[1] = split_heads(q_ref[...], zero)
    dm[0], dm[1] = split_heads(do_ref[...], zero)
    vm[0], vm[1] = split_heads(v_ref[...], zero)
    kt[...] = k_ref[...].T
    product = (do_ref[...].astype(F32) * o_ref[...].astype(F32)).T
    delta[0:1, :] = jnp.sum(product[:HEAD_DIM], axis=0, keepdims=True)
    delta[1:2, :] = jnp.sum(product[HEAD_DIM:], axis=0, keepdims=True)
    dqt[...] = jnp.zeros_like(dqt)

    def unrotate(grad, off, rows):
        cos, sin = cos_ref[pl.ds(off, rows), :], sin_ref[pl.ds(off, rows), :]
        return (grad * cos - swap_halves(grad) * sin).astype(BF)

    def key_block(j, _):
        koff = pl.multiple_of(j * bk, bk)
        keys = [kz[h, pl.ds(koff, bk), :] for h in range(2)]
        values = [vm[h, pl.ds(koff, bk), :] for h in range(2)]

        def query_block(i, carry):
            dk, dv = carry
            off = pl.multiple_of(i * bq, bq)
            scores = [dot(keys[h], qz[h, pl.ds(off, bq), :], NT) for h in range(2)]
            grads = [dot(values[h], dm[h, pl.ds(off, bq), :], NT) for h in range(2)]
            for h in range(2):
                weights = jnp.exp(scores[h] - lse_ref[0, h : h + 1, pl.ds(off, bq)])
                dv = dv + dot(weights.astype(BF), dm[h, pl.ds(off, bq), :])
                ds = (weights * (grads[h] - delta[h : h + 1, pl.ds(off, bq)])).astype(BF)
                dk = dk + dot(ds, qm[h, pl.ds(off, bq), :])
                head = slice(HEAD_DIM * h, HEAD_DIM * (h + 1))
                dqt[head, pl.ds(off, bq)] += dot(kt[head, pl.ds(koff, bk)], ds)
            return dk, dv

        zeros = jnp.zeros((bk, LANES), F32)
        dk, dv = lax.fori_loop(lo_ref[j], hi_ref[j], query_block, (zeros, zeros))
        dk_ref[pl.ds(koff, bk), :] = unrotate(dk, koff, bk)
        dv_ref[pl.ds(koff, bk), :] = dv.astype(BF)
        return 0

    lax.fori_loop(0, length // bk, key_block, 0)
    dq_ref[...] = unrotate(dqt[...].T * HEAD_DIM**-0.5, 0, length)


def attend_back(queries, keys, values, upstream, mixed, lse, segment, features, tables,
                bq=512, bk=256):
    length, width = queries.shape
    bq, bk = min(bq, length), min(bk, length)
    pairs = width // LANES
    low, high = block_ranges(segment, bk, bq)
    pair = pl.BlockSpec((length, LANES), lambda p, *_: (0, p))
    fixed = pl.BlockSpec((length, LANES), lambda p, *_: (0, 0))
    scratch = pltpu.VMEM((2, length, LANES), BF)
    return pl.pallas_call(
        functools.partial(attend_back_kernel, bq=bq, bk=bk),
        grid_spec=pltpu.PrefetchScalarGridSpec(
            num_scalar_prefetch=2,
            grid=(pairs,),
            in_specs=[pair] * 5
            + [pl.BlockSpec((1, 2, length), lambda p, *_: (p, 0, 0))]
            + [fixed] * 4,
            out_specs=[pair] * 3,
            scratch_shapes=[scratch] * 5
            + [
                pltpu.VMEM((LANES, length), BF),
                pltpu.VMEM((8, length), F32),
                pltpu.VMEM((LANES, length), F32),
            ],
        ),
        out_shape=[shape_of((length, width), BF)] * 3,
        compiler_params=params(),
        name="attend_back",
    )(low, high, queries, keys, values, upstream, mixed, lse, *features, *tables)


def middle_kernel(half, x_ref, g_ref, c_ref, o_ref, wa_ref, p_ref, woa_ref, wob_ref, w1a_ref,
                  w1b_ref, w2a_ref, w2b_ref,
                  res_ref, dx_ref, do_ref, z_ref, gy_ref, h_ref, du_ref, ga_ref, dwa_ref,
                  dp_ref, slope, *, chunk):
    width = x_ref.shape[1]
    own = width // 2
    hidden = w1a_ref.shape[1]
    cond = silu_low(c_ref[...])

    def modulation(block):
        rows = wa_ref[block * width : (block + 1) * width, :]
        return dot(cond, rows, NT) + p_ref[block + 2 : block + 3, :]

    gate_one, shift, scale, gate_two = (modulation(block) for block in (2, 3, 4, 5))
    branch = dot(o_ref[:, :own], woa_ref[...], NT) + dot(o_ref[:, own:], wob_ref[...], NT)
    middle = x_ref[...].astype(F32) + gate_one * branch
    normal, rstd = normalize(middle)
    gain = p_ref[1:2, :]
    spread = 1.0 + scale
    h = (normal * gain * spread + shift).astype(BF)
    h_ref[...] = h

    out = jnp.zeros_like(middle)
    for start, up_ref, down_ref in ((0, w1a_ref, w2a_ref), (hidden, w1b_ref, w2b_ref)):
        for at in range(0, hidden, chunk):
            u = dot(h, up_ref[:, at : at + chunk])
            square = u * u
            flat = jnp.tanh(math.sqrt(2.0 / math.pi) * u * (1.0 + 0.044715 * square))
            half_up = 0.5 * (1.0 + flat)
            z = (u * half_up).astype(BF)
            z_ref[:, start + at : start + at + chunk] = z
            slope[:, start + at : start + at + chunk] = half_up + 0.5 * u * (
                1.0 - flat * flat
            ) * (math.sqrt(2.0 / math.pi) * (1.0 + 3.0 * 0.044715 * square))
            out = out + dot(z, down_ref[:, at : at + chunk], NT)

    g = g_ref[...].astype(F32)
    res_ref[...] = (middle + gate_two * out).astype(BF)
    gy = (gate_two * g).astype(BF)
    gy_ref[...] = gy
    dgate_two = (g * out).astype(BF)

    dh = jnp.zeros_like(middle)
    for start, up_ref, down_ref in ((0, w1a_ref, w2a_ref), (hidden, w1b_ref, w2b_ref)):
        for at in range(0, hidden, chunk):
            dz = dot(gy, down_ref[:, at : at + chunk])
            du = (dz * slope[:, start + at : start + at + chunk]).astype(BF)
            du_ref[:, start + at : start + at + chunk] = du
            dh = dh + dot(du, up_ref[:, at : at + chunk], NT)

    dn = dh * normal
    dx = g + norm_backward(dh * gain * spread, normal, rstd)
    dx_ref[...] = dx
    ga = (gate_one * dx).astype(BF)
    ga_ref[...] = ga
    do_ref[:, :own] = dot(ga, woa_ref[...]).astype(BF)
    do_ref[:, own:] = dot(ga, wob_ref[...]).astype(BF)

    @pl.when(pl.program_id(0) == 0)
    def _():
        dwa_ref[...] = jnp.zeros_like(dwa_ref)
        dp_ref[...] = jnp.zeros_like(dp_ref)

    rows = cond_rows(cond)
    grads = ((dx * branch).astype(BF), dh.astype(BF), (dn * gain).astype(BF), dgate_two)
    for block, grad in enumerate(grads):
        dwa_ref[:, block * width : (block + 1) * width] += dot(rows, grad)
    dp_ref[0:1, :] += jnp.sum(dn * spread, axis=0, keepdims=True)


def middle_stage(half, tokens, out_grad, cond, mixed, wa, norms, near, far, wide_near, wide_far):
    width = tokens.shape[1]
    rows = mixed.shape[0]
    hidden = wide_near.shape[1] // 2
    blocks = rows // ROW_BLOCK
    mine = lambda i, half: (half[0] * blocks + i, 0)
    plain = lambda i, half: (i, 0)
    row = pl.BlockSpec((ROW_BLOCK, width), plain)
    wide = pl.BlockSpec((ROW_BLOCK, 2 * hidden), plain)
    narrow = shape_of((rows, width), BF)
    broad = shape_of((rows, 2 * hidden), BF)
    total = (cond.shape[1] + 16, 4 * width)
    return pl.pallas_call(
        functools.partial(middle_kernel, chunk=768),
        grid_spec=pltpu.PrefetchScalarGridSpec(
            num_scalar_prefetch=1,
            grid=(blocks,),
            in_specs=[
                pl.BlockSpec((ROW_BLOCK, width), mine),
                pl.BlockSpec((ROW_BLOCK, width), mine),
                pl.BlockSpec((ROW_BLOCK, cond.shape[1]), mine),
                row,
                resident(wa.shape, (0, 0)),
                resident(norms.shape, (0, 0)),
                resident((width, width // 2), (0, 3)),
                resident((width, width // 2), (0, 3)),
                resident((width, hidden), (0, 0)),
                resident((width, hidden), (0, 0)),
                resident((width, hidden), (0, 1)),
                resident((width, hidden), (0, 1)),
            ],
            out_specs=[row, row, row, wide, row, row, wide, row,
                       pl.BlockSpec(total, lambda i, half: (0, 0)),
                       pl.BlockSpec((8, width), lambda i, half: (0, 0))],
            scratch_shapes=[pltpu.VMEM((ROW_BLOCK, 2 * hidden), F32)],
        ),
        out_shape=[narrow, shape_of((rows, width), F32), narrow, broad, narrow, narrow, broad,
                   narrow, shape_of(total, F32), shape_of((8, width), F32)],
        compiler_params=params(),
        name="middle_stage",
    )(half, tokens, out_grad, cond, mixed, wa, norms, near, far, wide_near, wide_far,
      wide_near, wide_far)


def last_kernel(half, x_ref, c_ref, dx_ref, dq_ref, dk_ref, dv_ref, wa_ref, p_ref, wqa_ref,
                wqb_ref, out_ref, dwa_ref, dp_ref):
    width = x_ref.shape[1]
    own = width // 2
    cond = silu_low(c_ref[...])
    scale = dot(cond, wa_ref[width : 2 * width, :], NT) + p_ref[3:4, :]
    dh = jnp.zeros(x_ref.shape, F32)
    for start, w_ref in ((0, wqa_ref), (own, wqb_ref)):
        cols = slice(start, start + own)
        for index, grad_ref in enumerate((dq_ref, dk_ref, dv_ref)):
            dh = dh + dot(grad_ref[:, cols], w_ref[:, index * own : (index + 1) * own], NT)
    normal, rstd = normalize(x_ref[...].astype(F32))
    gain = p_ref[0:1, :]
    spread = 1.0 + scale
    dn = dh * normal
    out_ref[...] = dx_ref[...] + norm_backward(dh * gain * spread, normal, rstd)

    @pl.when(pl.program_id(0) == 0)
    def _():
        dwa_ref[...] = jnp.zeros_like(dwa_ref)
        dp_ref[...] = jnp.zeros_like(dp_ref)

    rows = cond_rows(cond)
    dwa_ref[:, :width] += dot(rows, dh.astype(BF))
    dwa_ref[:, width:] += dot(rows, (dn * gain).astype(BF))
    dp_ref[0:1, :] += jnp.sum(dn * spread, axis=0, keepdims=True)


def last_stage(half, tokens, cond, dx, grads, wa, norms, near, far):
    width = tokens.shape[1]
    rows = dx.shape[0]
    blocks = rows // ROW_BLOCK
    mine = lambda i, half: (half[0] * blocks + i, 0)
    row = pl.BlockSpec((ROW_BLOCK, width), lambda i, half: (i, 0))
    total = (cond.shape[1] + 16, 2 * width)
    return pl.pallas_call(
        last_kernel,
        grid_spec=pltpu.PrefetchScalarGridSpec(
            num_scalar_prefetch=1,
            grid=(blocks,),
            in_specs=[
                pl.BlockSpec((ROW_BLOCK, width), mine),
                pl.BlockSpec((ROW_BLOCK, cond.shape[1]), mine),
                row, row, row, row,
                resident(wa.shape, (0, 0)),
                resident(norms.shape, (0, 0)),
                resident((width, 3 * width // 2), (0, 0)),
                resident((width, 3 * width // 2), (0, 0)),
            ],
            out_specs=[row, pl.BlockSpec(total, lambda i, half: (0, 0)),
                       pl.BlockSpec((8, width), lambda i, half: (0, 0))],
        ),
        out_shape=[shape_of((rows, width), F32), shape_of(total, F32), shape_of((8, width), F32)],
        compiler_params=params(),
        name="last_stage",
    )(half, tokens, cond, dx, *grads, wa, norms, near, far)


def weight_grad_kernel(*refs, plan):
    lefts, rights = plan["lefts"], plan["rights"]
    left_refs, right_refs = refs[:lefts], refs[lefts : lefts + rights]
    out_ref, turned = refs[lefts + rights :]
    step = pl.program_id(0)
    for begin, end, left, right in plan["spans"]:

        @pl.when(step == begin)
        def _():
            turned[...] = left_refs[left][...].T

        @pl.when((step >= begin) & (step < end))
        def _():
            out_ref[...] = dot(turned[...], right_refs[right][...]).astype(BF)


def weight_grads(lefts, rights, spans, block, name):
    rows, width = lefts[0].shape
    begin, plan, maps = 0, [], []
    for steps, left, right, first in spans:
        plan.append((begin, begin + steps, left, right))
        maps.append((begin, steps, first))
        begin += steps

    def column_map(begin, steps, first):
        return lambda i: (0, first + jnp.clip(i - begin, 0, steps - 1))

    return pl.pallas_call(
        functools.partial(
            weight_grad_kernel,
            plan={"lefts": len(lefts), "rights": len(rights), "spans": plan},
        ),
        grid=(begin,),
        in_specs=[resident((rows, width), (0, 0))] * len(lefts)
        + [pl.BlockSpec((rows, block), column_map(*entry)) for entry in maps],
        out_specs=pl.BlockSpec((width, block), lambda i: (0, i)),
        out_shape=shape_of((width, begin * block), BF),
        scratch_shapes=[pltpu.VMEM((width, rows), BF)],
        compiler_params=params(),
        name=name,
    )(*lefts, *rights)


def factors(count):
    return (count // 4, 2, 2)


def swap_mp(value):
    return lax.ppermute(value, "mp", [(0, 1), (1, 0)])


def swap_dp(value, distance):
    count = lax.axis_size("dp")
    return lax.ppermute(value, "dp", [(i, i ^ distance) for i in range(count)])


def turn_dp(value, distance):
    count = lax.axis_size("dp")
    return lax.ppermute(value, "dp", [(i, (i + distance) % count) for i in range(count)])


def pick(value, index, axis):
    return lax.dynamic_index_in_dim(value, index, axis, keepdims=False)


def scatter_sum(parts, order):
    count = lax.axis_size("dp")
    outer, mid, inner = factors(count)
    me = lax.axis_index("dp")
    place = {4: me // 4, 2: (me // 2) % 2, 1: me % 2}

    def widen(part):
        return part.reshape((outer, mid, inner) + part.shape[1:]).astype(F32)

    total = widen(parts[0])
    for part in parts[1:]:
        total = total + widen(part)
    for distance in order:
        axis = 1 if (distance == 2 or total.ndim == 4) else 2
        gone = pick(total, 1 - place[distance], axis).astype(BF)
        total = pick(total, place[distance], axis) + swap_dp(gone, distance).astype(F32)
    arrived = [
        turn_dp(pick(total, (place[4] + hop) % outer, 0).astype(BF), 4 * hop)
        for hop in range(1, outer)
    ]
    total = pick(total, place[4], 0)
    for piece in arrived:
        total = total + piece.astype(F32)
    return total


def scatter_halves(near, far_sum):
    count = lax.axis_size("dp")
    width, columns = near.shape
    cut = columns // 2 // LANES * LANES
    shards = lambda value: value.reshape(count, width // count, value.shape[1])
    first = scatter_sum([shards(near[:, :cut]), shards(far_sum[:, :cut])], (2, 1))
    second = scatter_sum([shards(near[:, cut:]), shards(far_sum[:, cut:])], (1, 2))
    return jnp.concatenate([first, second], axis=1)


def sum_everywhere(value):
    value = value + swap_mp(value)
    distance = 1
    while distance < lax.axis_size("dp"):
        value = value + swap_dp(value, distance)
        distance *= 2
    return value


def in_order(half, near, far):
    first = jnp.where(half == 0, near, far)
    second = jnp.where(half == 0, far, near)
    return jnp.concatenate([first, second], axis=0)


def per_device(
    tokens, cond, segments, out_grad, step,
    ada_weight, ada_first, ada_second,
    norm_params, norm_first, norm_second,
    qkv_weight, qkv_first, qkv_second,
    out_weight, out_first, out_second,
    up_weight, up_first, up_second,
    down_weight, down_first, down_second,
):
    count = lax.axis_size("dp")
    width = tokens.shape[1]
    rows = tokens.shape[0] // 2
    conds = cond.shape[1]
    part = width // count
    half = lax.axis_index("mp")
    half_ref = half.reshape(1).astype(jnp.int32)
    token_total = float(tokens.shape[0] * count)

    ada_shard = ada_weight.T.astype(BF)
    qkv_shard = qkv_weight.astype(BF).transpose(1, 0, 2).reshape(part, -1)
    near_shard = jnp.concatenate([qkv_shard, out_weight.astype(BF).T], axis=1)
    wide_shard = jnp.concatenate([up_weight.astype(BF), down_weight.astype(BF).T], axis=1)
    wa = lax.all_gather(ada_shard, "dp", axis=0, tiled=True)
    norms = lax.all_gather(norm_params.astype(BF), "dp", axis=1, tiled=True).astype(F32)
    near = lax.all_gather(near_shard, "dp", axis=0, tiled=True)
    far = swap_mp(near)
    wide_near = lax.all_gather(wide_shard, "dp", axis=0, tiled=True)
    wide_far = swap_mp(wide_near)

    segment = pick(segments, half, 0)
    features = document_features(segment)
    tables = rope_tables(rows)

    h_one, queries, keys, values = first_stage(
        half_ref, tokens, cond, wa, norms, near, far, tables
    )
    mixed, lse = attend(queries, keys, values, segment, features)
    result, dx, upstream, z, gy, h_two, du, ga, dwa_two, dp_two = middle_stage(
        half_ref, tokens, out_grad, cond, mixed, wa, norms, near, far, wide_near, wide_far
    )
    result_far = swap_mp(result)

    block = width // 2
    steps = du.shape[1] // 2 // block

    def middle_grads(which, name):
        return weight_grads(
            [gy, h_two, ga], [du, z, mixed],
            [(steps, 1, 0, which * steps), (steps, 0, 1, which * steps), (1, 2, 2, which)],
            block, name,
        )

    middle_far = swap_mp(middle_grads(1, "middle_grads_far"))
    middle_near = middle_grads(0, "middle_grads_near")
    middle_sum = scatter_halves(middle_near, middle_far)

    grads = attend_back(queries, keys, values, upstream, mixed, lse, segment, features, tables)

    def first_grads(which, name):
        return weight_grads(
            [h_one], list(grads), [(1, 0, index, which) for index in range(3)], block, name
        )

    first_far = swap_mp(first_grads(1, "first_grads_far"))
    first_near = first_grads(0, "first_grads_near")
    first_sum = scatter_halves(first_near, first_far)

    input_grad, dwa_one, dp_one = last_stage(
        half_ref, tokens, cond, dx, grads, wa, norms, near, far
    )
    input_far = swap_mp(input_grad)

    dwa = jnp.concatenate([dwa_one, dwa_two], axis=1)
    ada_cols = dwa.shape[1] // count
    dwa_rows = dwa[:conds].T.astype(BF).reshape(count, 2, ada_cols // 2, conds)
    ada_near, ada_far = pick(dwa_rows, half, 1), swap_mp(pick(dwa_rows, 1 - half, 1))
    ada_half = scatter_sum([ada_near, ada_far], (2, 1))
    norm_rows = jnp.concatenate(
        [dp_one[0:1], dp_two[0:1], dwa[conds].reshape(6, width)], axis=0
    )
    norm_sum = lax.psum_scatter(
        norm_rows + swap_mp(norm_rows), "dp", scatter_dimension=1, tiled=True
    )

    wide_cols = du.shape[1] // 2
    up_mean = middle_sum[:, :wide_cols] / token_total
    down_mean = middle_sum[:, wide_cols : 2 * wide_cols] / token_total
    out_mean = middle_sum[:, 2 * wide_cols :] / token_total
    qkv_mean = first_sum / token_total
    ada_mean = ada_half / token_total
    norm_mean = norm_sum / token_total
    local_sq = (
        jnp.sum(qkv_mean * qkv_mean)
        + jnp.sum(out_mean * out_mean)
        + jnp.sum(up_mean * up_mean)
        + jnp.sum(down_mean * down_mean)
        + jnp.sum(ada_mean * ada_mean)
        + 0.5 * jnp.sum(norm_mean * norm_mean)
    )
    grad_norm = jnp.sqrt(sum_everywhere(jnp.full((8, LANES), local_sq, F32))[0, 0])
    clip_factor = jnp.minimum(1.0, clip_limit / (grad_norm + 1e-06))
    step_count = step[0].astype(F32)
    fix_one = 1.0 - jnp.exp(step_count * math.log(0.9))
    fix_two = 1.0 - jnp.exp(step_count * math.log(0.999))

    ada_grad = in_order(half, ada_mean, swap_mp(ada_mean)).T
    qkv_grad = qkv_mean.reshape(part, 3, -1).transpose(1, 0, 2)
    state = (
        (ada_weight, ada_first, ada_second, ada_grad),
        (norm_params, norm_first, norm_second, norm_mean),
        (qkv_weight, qkv_first, qkv_second, qkv_grad),
        (out_weight, out_first, out_second, out_mean.T),
        (up_weight, up_first, up_second, up_mean),
        (down_weight, down_first, down_second, down_mean.T),
    )
    outputs = [
        in_order(half, result, result_far),
        in_order(half, input_grad, input_far),
        grad_norm.reshape(1),
    ]
    for index, entry in enumerate(state):
        outputs += adam_update(
            *entry, clip_factor, fix_one, fix_two, step_rates[index], decay_rates[index]
        )
    return tuple(outputs)


def solution(mesh):
    column = (P(None, "dp"),) * 3
    weights = (
        column
        + column
        + (P(None, "dp", "mp"),) * 3
        + (P("mp", "dp"),) * 3
        + (P("dp", "mp"),) * 3
        + (P("mp", "dp"),) * 3
    )
    row = P("dp", None)
    return jax.shard_map(
        per_device,
        mesh=mesh,
        in_specs=(row, row, row, row, P()) + weights,
        out_specs=(row, row, P()) + weights,
        check_vma=False,
    )
```

```python
import functools
import math

import jax
import jax.numpy as jnp
from jax import lax
from jax.experimental import pallas as pl
from jax.experimental.pallas import tpu as pltpu
from jax.sharding import PartitionSpec as P

HEAD_DIM = 64
LANES = 128
MASKED = -1e30
ROW_BLOCK = 256
VMEM_LIMIT = 64_000_000
clip_limit = 1.0
step_rates = (0.075, 0.75, 0.075, 0.25, 0.075, 0.075)
decay_rates = (0.01, 0.0, 0.01, 0.01, 0.01, 0.01)

F32 = jnp.float32
BF = jnp.bfloat16
NN = (((1,), (0,)), ((), ()))
NT = (((1,), (1,)), ((), ()))


def dot(left, right, dims=NN):
    return lax.dot_general(left, right, dims, preferred_element_type=F32)


def shape_of(shape, dtype):
    return jax.ShapeDtypeStruct(shape, dtype)


def resident(shape, index):
    return pl.BlockSpec(shape, lambda *_: index, pipeline_mode=pl.Buffered(1))


def params():
    return pltpu.CompilerParams(vmem_limit_bytes=VMEM_LIMIT)


def adam_update(weight, first, second, grad, clip_factor, fix_one, fix_two, rate, decay):
    clipped = grad * clip_factor
    first_new = 0.9 * first + 0.1 * clipped
    second_new = 0.999 * second + 0.001 * clipped * clipped
    update = first_new / fix_one / (jnp.sqrt(second_new / fix_two) + 1e-08) + decay * weight
    return (weight - rate * update, first_new, second_new)


def rope_tables(length):
    half = HEAD_DIM // 2
    inverse = jnp.exp(jnp.arange(half, dtype=F32) * (-2.0 * math.log(10000.0) / HEAD_DIM))
    angles = jnp.arange(length, dtype=F32)[:, None] * inverse[None, :]
    cosines, sines = jnp.cos(angles), jnp.sin(angles)
    return (
        jnp.concatenate([cosines] * 4, axis=1),
        jnp.concatenate([-sines, sines, -sines, sines], axis=1),
    )


def swap_halves(values):
    width = values.shape[1]
    lane = lax.broadcasted_iota(jnp.int32, values.shape, 1)
    ahead = pltpu.roll(values, width - HEAD_DIM // 2, 1)
    behind = pltpu.roll(values, HEAD_DIM // 2, 1)
    return jnp.where(lane % HEAD_DIM < HEAD_DIM // 2, ahead, behind)


def silu_low(cond):
    value = cond.astype(F32)
    return (value / (1.0 + jnp.exp(-value))).astype(BF)


def normalize(rows):
    centre = rows - jnp.mean(rows, axis=-1, keepdims=True)
    scale = lax.rsqrt(jnp.mean(centre * centre, axis=-1, keepdims=True) + 1e-05)
    return centre * scale, scale


def norm_backward(grad, normal, scale):
    return scale * (
        grad
        - jnp.mean(grad, axis=-1, keepdims=True)
        - normal * jnp.mean(grad * normal, axis=-1, keepdims=True)
    )


def cond_rows(cond):
    return jnp.concatenate([cond.T, jnp.ones((16, cond.shape[0]), BF)], axis=0)


def first_kernel(half, x_ref, c_ref, wa_ref, p_ref, wqa_ref, wqb_ref, cos_ref, sin_ref,
                 h_ref, q_ref, k_ref, v_ref):
    width = x_ref.shape[1]
    own = width // 2
    cond = silu_low(c_ref[...])
    mod = dot(cond, wa_ref[0 : 2 * width, :], NT)
    shift = mod[:, :width] + p_ref[2:3, :]
    scale = mod[:, width:] + p_ref[3:4, :]
    normal, _ = normalize(x_ref[...].astype(F32))
    h = (normal * p_ref[0:1, :] * (1.0 + scale) + shift).astype(BF)
    h_ref[...] = h
    cos = jnp.concatenate([cos_ref[...]] * (own // LANES), axis=1)
    sin = jnp.concatenate([sin_ref[...]] * (own // LANES), axis=1)
    for start, w_ref in ((0, wqa_ref), (own, wqb_ref)):
        cols = slice(start, start + own)
        query = dot(h, w_ref[:, 0:own])
        query = query * cos + swap_halves(query) * sin
        q_ref[:, cols] = (query * HEAD_DIM**-0.5).astype(BF)
        key = dot(h, w_ref[:, own : 2 * own])
        k_ref[:, cols] = (key * cos + swap_halves(key) * sin).astype(BF)
        v_ref[:, cols] = dot(h, w_ref[:, 2 * own :]).astype(BF)


def first_stage(half, tokens, cond, wa, norms, near, far, tables):
    width = tokens.shape[1]
    rows = tables[0].shape[0]
    blocks = rows // ROW_BLOCK
    mine = lambda i, half: (half[0] * blocks + i, 0)
    plain = lambda i, half: (i, 0)
    row = pl.BlockSpec((ROW_BLOCK, width), plain)
    return pl.pallas_call(
        first_kernel,
        grid_spec=pltpu.PrefetchScalarGridSpec(
            num_scalar_prefetch=1,
            grid=(blocks,),
            in_specs=[
                pl.BlockSpec((ROW_BLOCK, width), mine),
                pl.BlockSpec((ROW_BLOCK, cond.shape[1]), mine),
                resident(wa.shape, (0, 0)),
                resident(norms.shape, (0, 0)),
                resident((width, 3 * width // 2), (0, 0)),
                resident((width, 3 * width // 2), (0, 0)),
                pl.BlockSpec((ROW_BLOCK, LANES), plain),
                pl.BlockSpec((ROW_BLOCK, LANES), plain),
            ],
            out_specs=[row] * 4,
        ),
        out_shape=[shape_of((rows, width), BF)] * 4,
        compiler_params=params(),
        name="first_stage",
    )(half, tokens, cond, wa, norms, near, far, *tables)


def split_heads(pair, other):
    low = lax.broadcasted_iota(jnp.int32, pair.shape, 1) < HEAD_DIM
    return jnp.where(low, pair, other), jnp.where(low, other, pair)


def attend_kernel(lo_ref, hi_ref, q_ref, k_ref, v_ref, fq_ref, fk_ref, o_ref, lse_ref,
                  qz, kz, vt, *, bq, bk):
    length = q_ref.shape[0]
    qz[0], qz[1] = split_heads(q_ref[...], fq_ref[...])
    kz[0], kz[1] = split_heads(k_ref[...], fk_ref[...])
    vt[...] = v_ref[...].T

    def query_block(i, _):
        off = pl.multiple_of(i * bq, bq)
        queries = [qz[h, pl.ds(off, bq), :] for h in range(2)]

        def key_block(j, carry):
            koff = pl.multiple_of(j * bk, bk)
            scores = [dot(kz[h, pl.ds(koff, bk), :], queries[h], NT) for h in range(2)]
            out = []
            for h in range(2):
                top, total, mixed = carry[3 * h : 3 * h + 3]
                new_top = jnp.maximum(top, jnp.max(scores[h], axis=0, keepdims=True))
                weights = jnp.exp(scores[h] - new_top)
                fade = jnp.exp(top - new_top)
                total = total * fade + jnp.sum(weights, axis=0, keepdims=True)
                values = vt[HEAD_DIM * h : HEAD_DIM * (h + 1), pl.ds(koff, bk)]
                mixed = mixed * fade + dot(values, weights.astype(BF))
                out += [new_top, total, mixed]
            return tuple(out)

        start = (
            jnp.full((1, bq), -3e38, F32),
            jnp.zeros((1, bq), F32),
            jnp.zeros((HEAD_DIM, bq), F32),
        )
        done = lax.fori_loop(lo_ref[i], hi_ref[i], key_block, start * 2)
        mixed = jnp.concatenate([done[2] / done[1], done[5] / done[4]], axis=0)
        o_ref[pl.ds(off, bq), :] = mixed.T.astype(BF)
        lse_ref[0, 0:1, pl.ds(off, bq)] = done[0] + jnp.log(done[1])
        lse_ref[0, 1:2, pl.ds(off, bq)] = done[3] + jnp.log(done[4])
        return 0

    lax.fori_loop(0, length // bq, query_block, 0)


def block_ranges(segment, block, other):
    first, last = segment[::block], segment[block - 1 :: block]
    low = jnp.sum(segment[None, :] < first[:, None], axis=1)
    high = jnp.sum(segment[None, :] <= last[:, None], axis=1)
    return (low // other).astype(jnp.int32), ((high + other - 1) // other).astype(jnp.int32)


def document_features(segment):
    lane = lax.broadcasted_iota(jnp.int32, (segment.shape[0], LANES), 1) % HEAD_DIM
    same = lane == segment[:, None]
    query = jnp.where(same, 1.0, 0.0).astype(BF)
    key = jnp.where((lane < 4) & ~same, MASKED, 0.0).astype(BF)
    return query, key


def attend(queries, keys, values, segment, features, bq=1024, bk=512):
    length, width = queries.shape
    bq, bk = min(bq, length), min(bk, length)
    pairs = width // LANES
    low, high = block_ranges(segment, bq, bk)
    pair = pl.BlockSpec((length, LANES), lambda p, *_: (0, p))
    fixed = pl.BlockSpec((length, LANES), lambda p, *_: (0, 0))
    scratch = pltpu.VMEM((2, length, LANES), BF)
    return pl.pallas_call(
        functools.partial(attend_kernel, bq=bq, bk=bk),
        grid_spec=pltpu.PrefetchScalarGridSpec(
            num_scalar_prefetch=2,
            grid=(pairs,),
            in_specs=[pair, pair, pair, fixed, fixed],
            out_specs=[pair, pl.BlockSpec((1, 2, length), lambda p, *_: (p, 0, 0))],
            scratch_shapes=[scratch, scratch, pltpu.VMEM((LANES, length), BF)],
        ),
        out_shape=[shape_of((length, width), BF), shape_of((pairs, 2, length), F32)],
        compiler_params=params(),
        name="attend",
    )(low, high, queries, keys, values, *features)


def attend_back_kernel(lo_ref, hi_ref, q_ref, k_ref, v_ref, do_ref, o_ref, lse_ref, fq_ref,
                       fk_ref, cos_ref, sin_ref, dq_ref, dk_ref, dv_ref,
                       qz, kz, qm, dm, vm, kt, delta, dqt, *, bq, bk):
    length = q_ref.shape[0]
    zero = jnp.zeros((length, LANES), BF)
    qz[0], qz[1] = split_heads(q_ref[...], fq_ref[...])
    kz[0], kz[1] = split_heads(k_ref[...], fk_ref[...])
    qm[0], qm[1] = split_heads(q_ref[...], zero)
    dm[0], dm[1] = split_heads(do_ref[...], zero)
    vm[0], vm[1] = split_heads(v_ref[...], zero)
    kt[...] = k_ref[...].T
    product = (do_ref[...].astype(F32) * o_ref[...].astype(F32)).T
    delta[0:1, :] = jnp.sum(product[:HEAD_DIM], axis=0, keepdims=True)
    delta[1:2, :] = jnp.sum(product[HEAD_DIM:], axis=0, keepdims=True)
    dqt[...] = jnp.zeros_like(dqt)

    def unrotate(grad, off, rows):
        cos, sin = cos_ref[pl.ds(off, rows), :], sin_ref[pl.ds(off, rows), :]
        return (grad * cos - swap_halves(grad) * sin).astype(BF)

    def key_block(j, _):
        koff = pl.multiple_of(j * bk, bk)
        keys = [kz[h, pl.ds(koff, bk), :] for h in range(2)]
        values = [vm[h, pl.ds(koff, bk), :] for h in range(2)]

        def query_block(i, carry):
            dk, dv = carry
            off = pl.multiple_of(i * bq, bq)
            scores = [dot(keys[h], qz[h, pl.ds(off, bq), :], NT) for h in range(2)]
            grads = [dot(values[h], dm[h, pl.ds(off, bq), :], NT) for h in range(2)]
            for h in range(2):
                weights = jnp.exp(scores[h] - lse_ref[0, h : h + 1, pl.ds(off, bq)])
                dv = dv + dot(weights.astype(BF), dm[h, pl.ds(off, bq), :])
                ds = (weights * (grads[h] - delta[h : h + 1, pl.ds(off, bq)])).astype(BF)
                dk = dk + dot(ds, qm[h, pl.ds(off, bq), :])
                head = slice(HEAD_DIM * h, HEAD_DIM * (h + 1))
                dqt[head, pl.ds(off, bq)] += dot(kt[head, pl.ds(koff, bk)], ds)
            return dk, dv

        zeros = jnp.zeros((bk, LANES), F32)
        dk, dv = lax.fori_loop(lo_ref[j], hi_ref[j], query_block, (zeros, zeros))
        dk_ref[pl.ds(koff, bk), :] = unrotate(dk, koff, bk)
        dv_ref[pl.ds(koff, bk), :] = dv.astype(BF)
        return 0

    lax.fori_loop(0, length // bk, key_block, 0)
    dq_ref[...] = unrotate(dqt[...].T * HEAD_DIM**-0.5, 0, length)


def attend_back(queries, keys, values, upstream, mixed, lse, segment, features, tables,
                bq=512, bk=256):
    length, width = queries.shape
    bq, bk = min(bq, length), min(bk, length)
    pairs = width // LANES
    low, high = block_ranges(segment, bk, bq)
    pair = pl.BlockSpec((length, LANES), lambda p, *_: (0, p))
    fixed = pl.BlockSpec((length, LANES), lambda p, *_: (0, 0))
    scratch = pltpu.VMEM((2, length, LANES), BF)
    return pl.pallas_call(
        functools.partial(attend_back_kernel, bq=bq, bk=bk),
        grid_spec=pltpu.PrefetchScalarGridSpec(
            num_scalar_prefetch=2,
            grid=(pairs,),
            in_specs=[pair] * 5
            + [pl.BlockSpec((1, 2, length), lambda p, *_: (p, 0, 0))]
            + [fixed] * 4,
            out_specs=[pair] * 3,
            scratch_shapes=[scratch] * 5
            + [
                pltpu.VMEM((LANES, length), BF),
                pltpu.VMEM((8, length), F32),
                pltpu.VMEM((LANES, length), F32),
            ],
        ),
        out_shape=[shape_of((length, width), BF)] * 3,
        compiler_params=params(),
        name="attend_back",
    )(low, high, queries, keys, values, upstream, mixed, lse, *features, *tables)


def middle_kernel(half, x_ref, g_ref, c_ref, o_ref, wa_ref, p_ref, woa_ref, wob_ref, w1a_ref,
                  w1b_ref, w2a_ref, w2b_ref,
                  res_ref, dx_ref, do_ref, z_ref, gy_ref, h_ref, du_ref, ga_ref, dwa_ref,
                  dp_ref, slope, *, chunk):
    width = x_ref.shape[1]
    own = width // 2
    hidden = w1a_ref.shape[1]
    cond = silu_low(c_ref[...])

    def modulation(block):
        rows = wa_ref[block * width : (block + 1) * width, :]
        return dot(cond, rows, NT) + p_ref[block + 2 : block + 3, :]

    gate_one, shift, scale, gate_two = (modulation(block) for block in (2, 3, 4, 5))
    branch = dot(o_ref[:, :own], woa_ref[...], NT) + dot(o_ref[:, own:], wob_ref[...], NT)
    middle = x_ref[...].astype(F32) + gate_one * branch
    normal, rstd = normalize(middle)
    gain = p_ref[1:2, :]
    spread = 1.0 + scale
    h = (normal * gain * spread + shift).astype(BF)
    h_ref[...] = h

    out = jnp.zeros_like(middle)
    for start, up_ref, down_ref in ((0, w1a_ref, w2a_ref), (hidden, w1b_ref, w2b_ref)):
        for at in range(0, hidden, chunk):
            u = dot(h, up_ref[:, at : at + chunk])
            square = u * u
            flat = jnp.tanh(math.sqrt(2.0 / math.pi) * u * (1.0 + 0.044715 * square))
            half_up = 0.5 * (1.0 + flat)
            z = (u * half_up).astype(BF)
            z_ref[:, start + at : start + at + chunk] = z
            slope[:, start + at : start + at + chunk] = half_up + 0.5 * u * (
                1.0 - flat * flat
            ) * (math.sqrt(2.0 / math.pi) * (1.0 + 3.0 * 0.044715 * square))
            out = out + dot(z, down_ref[:, at : at + chunk], NT)

    g = g_ref[...].astype(F32)
    res_ref[...] = (middle + gate_two * out).astype(BF)
    gy = (gate_two * g).astype(BF)
    gy_ref[...] = gy
    dgate_two = (g * out).astype(BF)

    dh = jnp.zeros_like(middle)
    for start, up_ref, down_ref in ((0, w1a_ref, w2a_ref), (hidden, w1b_ref, w2b_ref)):
        for at in range(0, hidden, chunk):
            dz = dot(gy, down_ref[:, at : at + chunk])
            du = (dz * slope[:, start + at : start + at + chunk]).astype(BF)
            du_ref[:, start + at : start + at + chunk] = du
            dh = dh + dot(du, up_ref[:, at : at + chunk], NT)

    dn = dh * normal
    dx = g + norm_backward(dh * gain * spread, normal, rstd)
    dx_ref[...] = dx
    ga = (gate_one * dx).astype(BF)
    ga_ref[...] = ga
    do_ref[:, :own] = dot(ga, woa_ref[...]).astype(BF)
    do_ref[:, own:] = dot(ga, wob_ref[...]).astype(BF)

    @pl.when(pl.program_id(0) == 0)
    def _():
        dwa_ref[...] = jnp.zeros_like(dwa_ref)
        dp_ref[...] = jnp.zeros_like(dp_ref)

    rows = cond_rows(cond)
    grads = ((dx * branch).astype(BF), dh.astype(BF), (dn * gain).astype(BF), dgate_two)
    for block, grad in enumerate(grads):
        dwa_ref[:, block * width : (block + 1) * width] += dot(rows, grad)
    dp_ref[0:1, :] += jnp.sum(dn * spread, axis=0, keepdims=True)


def middle_stage(half, tokens, out_grad, cond, mixed, wa, norms, wide_near, wide_far):
    width = tokens.shape[1]
    rows = mixed.shape[0]
    hidden = (wide_near.shape[1] - width // 2) // 2
    blocks = rows // ROW_BLOCK
    mine = lambda i, half: (half[0] * blocks + i, 0)
    plain = lambda i, half: (i, 0)
    row = pl.BlockSpec((ROW_BLOCK, width), plain)
    wide = pl.BlockSpec((ROW_BLOCK, 2 * hidden), plain)
    narrow = shape_of((rows, width), BF)
    broad = shape_of((rows, 2 * hidden), BF)
    total = (cond.shape[1] + 16, 4 * width)
    return pl.pallas_call(
        functools.partial(middle_kernel, chunk=768),
        grid_spec=pltpu.PrefetchScalarGridSpec(
            num_scalar_prefetch=1,
            grid=(blocks,),
            in_specs=[
                pl.BlockSpec((ROW_BLOCK, width), mine),
                pl.BlockSpec((ROW_BLOCK, width), mine),
                pl.BlockSpec((ROW_BLOCK, cond.shape[1]), mine),
                row,
                resident(wa.shape, (0, 0)),
                resident(norms.shape, (0, 0)),
                resident((width, width // 2), (0, 4 * hidden // width)),
                resident((width, width // 2), (0, 4 * hidden // width)),
                resident((width, hidden), (0, 0)),
                resident((width, hidden), (0, 0)),
                resident((width, hidden), (0, 1)),
                resident((width, hidden), (0, 1)),
            ],
            out_specs=[row, row, row, wide, row, row, wide, row,
                       pl.BlockSpec(total, lambda i, half: (0, 0)),
                       pl.BlockSpec((8, width), lambda i, half: (0, 0))],
            scratch_shapes=[pltpu.VMEM((ROW_BLOCK, 2 * hidden), F32)],
        ),
        out_shape=[narrow, shape_of((rows, width), F32), narrow, broad, narrow, narrow, broad,
                   narrow, shape_of(total, F32), shape_of((8, width), F32)],
        compiler_params=params(),
        name="middle_stage",
    )(half, tokens, out_grad, cond, mixed, wa, norms, wide_near, wide_far, wide_near, wide_far,
      wide_near, wide_far)


def last_kernel(half, x_ref, c_ref, dx_ref, dq_ref, dk_ref, dv_ref, wa_ref, p_ref, wqa_ref,
                wqb_ref, out_ref, dwa_ref, dp_ref):
    width = x_ref.shape[1]
    own = width // 2
    cond = silu_low(c_ref[...])
    scale = dot(cond, wa_ref[width : 2 * width, :], NT) + p_ref[3:4, :]
    dh = jnp.zeros(x_ref.shape, F32)
    for start, w_ref in ((0, wqa_ref), (own, wqb_ref)):
        cols = slice(start, start + own)
        for index, grad_ref in enumerate((dq_ref, dk_ref, dv_ref)):
            dh = dh + dot(grad_ref[:, cols], w_ref[:, index * own : (index + 1) * own], NT)
    normal, rstd = normalize(x_ref[...].astype(F32))
    gain = p_ref[0:1, :]
    spread = 1.0 + scale
    dn = dh * normal
    out_ref[...] = dx_ref[...] + norm_backward(dh * gain * spread, normal, rstd)

    @pl.when(pl.program_id(0) == 0)
    def _():
        dwa_ref[...] = jnp.zeros_like(dwa_ref)
        dp_ref[...] = jnp.zeros_like(dp_ref)

    rows = cond_rows(cond)
    dwa_ref[:, :width] += dot(rows, dh.astype(BF))
    dwa_ref[:, width:] += dot(rows, (dn * gain).astype(BF))
    dp_ref[0:1, :] += jnp.sum(dn * spread, axis=0, keepdims=True)


def last_stage(half, tokens, cond, dx, grads, wa, norms, near, far):
    width = tokens.shape[1]
    rows = dx.shape[0]
    blocks = rows // ROW_BLOCK
    mine = lambda i, half: (half[0] * blocks + i, 0)
    row = pl.BlockSpec((ROW_BLOCK, width), lambda i, half: (i, 0))
    total = (cond.shape[1] + 16, 2 * width)
    return pl.pallas_call(
        last_kernel,
        grid_spec=pltpu.PrefetchScalarGridSpec(
            num_scalar_prefetch=1,
            grid=(blocks,),
            in_specs=[
                pl.BlockSpec((ROW_BLOCK, width), mine),
                pl.BlockSpec((ROW_BLOCK, cond.shape[1]), mine),
                row, row, row, row,
                resident(wa.shape, (0, 0)),
                resident(norms.shape, (0, 0)),
                resident((width, 3 * width // 2), (0, 0)),
                resident((width, 3 * width // 2), (0, 0)),
            ],
            out_specs=[row, pl.BlockSpec(total, lambda i, half: (0, 0)),
                       pl.BlockSpec((8, width), lambda i, half: (0, 0))],
        ),
        out_shape=[shape_of((rows, width), F32), shape_of(total, F32), shape_of((8, width), F32)],
        compiler_params=params(),
        name="last_stage",
    )(half, tokens, cond, dx, *grads, wa, norms, near, far)


def weight_grad_kernel(*refs, plan):
    lefts, rights = plan["lefts"], plan["rights"]
    left_refs, right_refs = refs[:lefts], refs[lefts : lefts + rights]
    out_ref, turned = refs[lefts + rights :]
    step = pl.program_id(0)
    for begin, end, left, right in plan["spans"]:

        @pl.when(step == begin)
        def _():
            turned[...] = left_refs[left][...].T

        @pl.when((step >= begin) & (step < end))
        def _():
            out_ref[...] = dot(turned[...], right_refs[right][...]).astype(BF)


def weight_grads(lefts, rights, spans, block, name):
    rows, width = lefts[0].shape
    begin, plan, maps = 0, [], []
    for steps, left, right, first in spans:
        plan.append((begin, begin + steps, left, right))
        maps.append((begin, steps, first))
        begin += steps

    def column_map(begin, steps, first):
        return lambda i: (0, first + jnp.clip(i - begin, 0, steps - 1))

    return pl.pallas_call(
        functools.partial(
            weight_grad_kernel,
            plan={"lefts": len(lefts), "rights": len(rights), "spans": plan},
        ),
        grid=(begin,),
        in_specs=[resident((rows, width), (0, 0))] * len(lefts)
        + [pl.BlockSpec((rows, block), column_map(*entry)) for entry in maps],
        out_specs=pl.BlockSpec((width, block), lambda i: (0, i)),
        out_shape=shape_of((width, begin * block), BF),
        scratch_shapes=[pltpu.VMEM((width, rows), BF)],
        compiler_params=params(),
        name=name,
    )(*lefts, *rights)


class Gather:
    def __init__(self, shard, near, far, cut, sems, place):
        outer, inner, mid, core = place["outer"], place["x"], place["y"], place["core"]
        z = place["z"]
        columns = near.shape[-1]
        split = near.shape[0] != place["outer"] * 4
        rows = near.shape[0] // (4 * outer)

        def slots(ref, first, number, cols):
            if split:
                at = pl.multiple_of(first * rows, 16)
                return ref.at[pl.ds(at, number * rows), cols]
            return ref.at[pl.ds(first, number), core, :, cols]

        def copy(src, dst, name, index, device):
            return pltpu.make_async_remote_copy(
                src_ref=src,
                dst_ref=dst,
                send_sem=sems[name].at[0, index],
                recv_sem=sems[name].at[1, index],
                device_id=device,
                device_id_type=pl.DeviceIdType.MESH,
            )

        def peer(zz, yy, xx):
            return (4 * zz + 2 * yy + xx, core)

        whole = slice(None)
        parts = [("a", slice(0, cut))] + ([("b", slice(cut, columns))] if cut < columns else [])
        mine = 4 * z + 2 * mid + inner
        self.outer = outer
        self.parts = [name for name, _ in parts]
        self.local = (shard, slots(near, mine, 1, whole))
        source = shard if split else shard
        self.hops = {
            hop: copy(source, slots(near, mine, 1, whole), "hop", hop - 1,
                      peer(lax.rem(z + hop, outer), mid, inner))
            for hop in range(1, outer)
        }
        self.one, self.two, self.swap = {}, {}, {}
        for step in range(outer):
            zz = lax.rem(z + outer - step, outer)
            base = 4 * zz
            for index, (name, cols) in enumerate(parts):
                own = base + 2 * mid + inner
                device = peer(z, mid, 1 - inner) if name == "a" else peer(z, 1 - mid, inner)
                if step == 0:
                    src = shard.at[:, cols] if split else shard.at[:, :, cols]
                else:
                    src = slots(near, own, 1, cols)
                self.one[name, step] = copy(
                    src, slots(near, own, 1, cols), "one", index * outer + step, device
                )
            if True:
                self.two["a", step] = [
                    copy(slots(near, base + 2 * mid, 2, parts[0][1]),
                         slots(near, base + 2 * mid, 2, parts[0][1]),
                         "two", step, peer(z, 1 - mid, inner))
                ]
            if len(parts) > 1:
                self.two["b", step] = [
                    copy(slots(near, base + 2 * yy + inner, 1, parts[1][1]),
                         slots(near, base + 2 * yy + inner, 1, parts[1][1]),
                         "two", outer + 2 * step + yy, peer(z, mid, 1 - inner))
                    for yy in range(2)
                ]
            target = far if split else near
            self.swap[step] = copy(
                slots(near, base, 4, whole), slots(target, base, 4, whole),
                "swap", step, (4 * z + 2 * mid + inner, 1 - core)
            )

    @staticmethod
    def semaphores(outer):
        kind = pltpu.SemaphoreType.DMA
        return [kind((2, outer)), kind((2, 2 * outer)), kind((2, 3 * outer)), kind((2, outer))]

    @staticmethod
    def named(refs):
        return dict(zip(("hop", "one", "two", "swap"), refs))

    def start_hops(self):
        for hop in self.hops.values():
            hop.start()

    def phase_one(self, step):
        if step:
            self.hops[step].wait_recv()
        for name in self.parts:
            self.one[name, step].start()

    def phase_two(self, step):
        for name in self.parts:
            self.one[name, step].wait_recv()
        for name in self.parts:
            for entry in self.two[name, step]:
                entry.start()

    def phase_swap(self, step):
        for name in self.parts:
            for entry in self.two[name, step]:
                entry.wait_recv()
        self.swap[step].start()

    def finish(self, step):
        self.swap[step].wait_recv()

    def drain(self):
        for hop in self.hops.values():
            hop.wait_send()
        for step in range(self.outer):
            for name in self.parts:
                self.one[name, step].wait_send()
                for entry in self.two[name, step]:
                    entry.wait_send()
            self.swap[step].wait_send()


def my_place(count):
    me, core = lax.axis_index("dp"), lax.axis_index("mp")
    return {"outer": count // 4, "z": me // 4, "y": lax.rem(me // 2, 2), "x": lax.rem(me, 2),
            "core": core, "me": me}


def meet(place):
    z, y, x, core, outer = (place[name] for name in ("z", "y", "x", "core", "outer"))
    here = 2 * y + x
    others = [(4 * lax.rem(z + hop, outer) + here, core) for hop in range(1, outer)]
    others += [(4 * z + 2 * y + 1 - x, core), (4 * z + 2 * (1 - y) + x, core),
               (4 * z + here, 1 - core)]
    barrier = pltpu.get_barrier_semaphore()
    for other in others:
        pl.semaphore_signal(barrier, inc=1, device_id=other, device_id_type=pl.DeviceIdType.MESH)
    pl.semaphore_wait(barrier, len(others))


def opening_kernel(tok_ref, cond_ref, g1_ref, ada_ref, g2_ref, cos_ref, sin_ref, fq_ref, fk_ref,
                   h_ref, q_ref, k_ref, v_ref, o_ref, lse_ref, near_ref, far_ref, wa_ref,
                   norm_ref, wide_near, wide_far,
                   x_vm, c_vm, qz, kz, vt, local, *sems, count, cuts, bk):
    place = my_place(count)
    outer, core = place["outer"], place["core"]
    rows, width = x_vm.shape
    own = width // 2
    groups = [Gather.named(sems[4 * i : 4 * i + 4]) for i in range(3)]
    small = Gather(g1_ref, near_ref, far_ref, cuts[0], groups[0], place)
    ada = Gather(ada_ref, wa_ref, None, ada_ref.shape[-1], groups[1], place)
    wide = Gather(g2_ref, wide_near, wide_far, cuts[1], groups[2], place)

    start = pl.multiple_of(core * rows, rows)
    loads = [
        pltpu.make_async_copy(tok_ref.at[pl.ds(start, rows)], x_vm, local.at[0]),
        pltpu.make_async_copy(cond_ref.at[pl.ds(start, rows)], c_vm, local.at[1]),
        pltpu.make_async_copy(*wide.local, local.at[2]),
        pltpu.make_async_copy(*small.local, local.at[3]),
        pltpu.make_async_copy(*ada.local, local.at[4]),
    ]
    for load in loads:
        load.start()
    meet(place)
    ada.start_hops()
    small.start_hops()
    for load in loads:
        load.wait()
    for step in range(outer):
        ada.phase_one(step)
        small.phase_one(step)
    wide.start_hops()
    for step in range(outer):
        ada.phase_two(step)
        small.phase_two(step)
    for step in range(outer):
        ada.phase_swap(step)
        small.phase_swap(step)
    wide.phase_one(0)
    for step in range(outer):
        ada.finish(step)
        small.finish(step)

    table = near_ref[:, 3 * own :].astype(F32).T
    norm_ref[...] = table[0:8, :]
    wa = wa_ref[...].reshape(6 * width, c_vm.shape[1])

    def row_block(i, _):
        at = pl.ds(pl.multiple_of(i * ROW_BLOCK, ROW_BLOCK), ROW_BLOCK)
        cond = silu_low(c_vm[at, :])
        shift = dot(cond, wa[:width], NT) + norm_ref[2:3, :]
        scale = dot(cond, wa[width : 2 * width], NT) + norm_ref[3:4, :]
        normal, _ = normalize(x_vm[at, :].astype(F32))
        h = (normal * norm_ref[0:1, :] * (1.0 + scale) + shift).astype(BF)
        h_ref[at, :] = h
        cos = jnp.concatenate([cos_ref[at, :]] * (own // LANES), axis=1)
        sin = jnp.concatenate([sin_ref[at, :]] * (own // LANES), axis=1)
        for first, w_ref in ((0, near_ref), (own, far_ref)):
            cols = slice(first, first + own)
            query = dot(h, w_ref[:, 0:own])
            query = query * cos + swap_halves(query) * sin
            q_ref[at, cols] = (query * HEAD_DIM**-0.5).astype(BF)
            key = dot(h, w_ref[:, own : 2 * own])
            k_ref[at, cols] = (key * cos + swap_halves(key) * sin).astype(BF)
            v_ref[at, cols] = dot(h, w_ref[:, 2 * own : 3 * own]).astype(BF)
        for step in range(1, outer):

            @pl.when(i == step - 1)
            def _():
                wide.phase_one(step)

        return 0

    lax.fori_loop(0, rows // ROW_BLOCK, row_block, 0)

    def head_pair(p, _):
        lanes = pl.ds(pl.multiple_of(p * LANES, LANES), LANES)
        qz[0], qz[1] = split_heads(q_ref[:, lanes], fq_ref[...])
        kz[0], kz[1] = split_heads(k_ref[:, lanes], fk_ref[...])
        vt[...] = v_ref[:, lanes].T
        state = [None, None]
        for j in range(rows // bk):
            block = slice(j * bk, (j + 1) * bk)
            scores = [dot(kz[h, block, :], qz[h], NT) for h in range(2)]
            for h in range(2):
                values = vt[HEAD_DIM * h : HEAD_DIM * (h + 1), block]
                top = jnp.max(scores[h], axis=0, keepdims=True)
                if j:
                    top = jnp.maximum(state[h][0], top)
                weights = jnp.exp(scores[h] - top)
                total = jnp.sum(weights, axis=0, keepdims=True)
                result = dot(values, weights.astype(BF))
                if j:
                    fade = jnp.exp(state[h][0] - top)
                    total = state[h][1] * fade + total
                    result = state[h][2] * fade + result
                state[h] = (top, total, result)
        done = jnp.concatenate([entry[2] / entry[1] for entry in state], axis=0)
        o_ref[:, lanes] = done.T.astype(BF)
        for h in range(2):
            lse_ref[p, h : h + 1, :] = state[h][0] + jnp.log(state[h][1])

        for step in range(outer):

            @pl.when(p == step // 2)
            def _():
                wide.phase_two(step)

            @pl.when(p == 3 + step // 2)
            def _():
                wide.phase_swap(step)

        return 0

    lax.fori_loop(0, width // LANES, head_pair, 0)
    for step in range(outer):
        wide.finish(step)
    for group in (ada, small, wide):
        group.drain()


def opening(count, tokens, cond, small_shard, ada_shard, wide_shard, tables, features):
    rows, width = tokens.shape[0] // 2, tokens.shape[1]
    conds = cond.shape[1]
    vm = pl.BlockSpec(memory_space=pltpu.VMEM)
    hbm = pl.BlockSpec(memory_space=pl.ANY)
    small = shape_of((width, small_shard.shape[1]), BF)
    wide = shape_of((width, wide_shard.shape[1]), BF)
    act = shape_of((rows, width), BF)
    pairs = width // LANES
    scratch = pltpu.VMEM((2, rows, LANES), BF)
    cuts = (512, wide_shard.shape[1] // 2 // LANES * LANES)
    return pl.pallas_call(
        functools.partial(opening_kernel, count=count, cuts=cuts, bk=512),
        in_specs=[hbm, hbm] + [vm] * 7,
        out_specs=[vm] * 10 + [hbm, hbm],
        out_shape=[act, act, act, act, act, shape_of((pairs, 2, rows), F32), small, small,
                   shape_of((count, 2, ada_shard.shape[1], conds), BF),
                   shape_of((8, width), F32), wide, wide],
        scratch_shapes=[
            pltpu.VMEM((rows, width), BF), pltpu.VMEM((rows, conds), BF),
            scratch, scratch, pltpu.VMEM((LANES, rows), BF),
            pltpu.SemaphoreType.DMA((5,)),
        ] + Gather.semaphores(count // 4) * 3,
        compiler_params=pltpu.CompilerParams(
            vmem_limit_bytes=VMEM_LIMIT, collective_id=0, has_side_effects=True
        ),
        name="opening",
    )(tokens, cond, small_shard, ada_shard, wide_shard, *tables, *features)


def factors(count):
    return (count // 4, 2, 2)


def swap_mp(value):
    return lax.ppermute(value, "mp", [(0, 1), (1, 0)])


def swap_dp(value, distance):
    count = lax.axis_size("dp")
    return lax.ppermute(value, "dp", [(i, i ^ distance) for i in range(count)])


def turn_dp(value, distance):
    count = lax.axis_size("dp")
    return lax.ppermute(value, "dp", [(i, (i + distance) % count) for i in range(count)])


def pick(value, index, axis):
    return lax.dynamic_index_in_dim(value, index, axis, keepdims=False)


def scatter_sum(parts, order):
    count = lax.axis_size("dp")
    outer, mid, inner = factors(count)
    me = lax.axis_index("dp")
    place = {4: me // 4, 2: (me // 2) % 2, 1: me % 2}

    def widen(part):
        return part.reshape((outer, mid, inner) + part.shape[1:]).astype(F32)

    total = widen(parts[0])
    for part in parts[1:]:
        total = total + widen(part)
    for distance in order:
        axis = 1 if (distance == 2 or total.ndim == 4) else 2
        gone = pick(total, 1 - place[distance], axis).astype(BF)
        total = pick(total, place[distance], axis) + swap_dp(gone, distance).astype(F32)
    arrived = [
        turn_dp(pick(total, (place[4] + hop) % outer, 0).astype(BF), 4 * hop)
        for hop in range(1, outer)
    ]
    total = pick(total, place[4], 0)
    for piece in arrived:
        total = total + piece.astype(F32)
    return total


def scatter_halves(near, far_sum):
    count = lax.axis_size("dp")
    width, columns = near.shape
    cut = columns // 2 // LANES * LANES
    shards = lambda value: value.reshape(count, width // count, value.shape[1])
    first = scatter_sum([shards(near[:, :cut]), shards(far_sum[:, :cut])], (2, 1))
    second = scatter_sum([shards(near[:, cut:]), shards(far_sum[:, cut:])], (1, 2))
    return jnp.concatenate([first, second], axis=1)


def sum_everywhere(value):
    value = value + swap_mp(value)
    distance = 1
    while distance < lax.axis_size("dp"):
        value = value + swap_dp(value, distance)
        distance *= 2
    return value


def in_order(half, near, far):
    first = jnp.where(half == 0, near, far)
    second = jnp.where(half == 0, far, near)
    return jnp.concatenate([first, second], axis=0)


def per_device(
    tokens, cond, segments, out_grad, step,
    ada_weight, ada_first, ada_second,
    norm_params, norm_first, norm_second,
    qkv_weight, qkv_first, qkv_second,
    out_weight, out_first, out_second,
    up_weight, up_first, up_second,
    down_weight, down_first, down_second,
):
    count = lax.axis_size("dp")
    width = tokens.shape[1]
    rows = tokens.shape[0] // 2
    conds = cond.shape[1]
    part = width // count
    half = lax.axis_index("mp")
    half_ref = half.reshape(1).astype(jnp.int32)
    token_total = float(tokens.shape[0] * count)

    ada_shard = ada_weight.T.astype(BF).reshape(2, -1, cond.shape[1])
    small_shard = jnp.concatenate(
        [
            qkv_weight.astype(BF).transpose(1, 0, 2).reshape(part, -1),
            jnp.pad(norm_params.astype(BF).T, ((0, 0), (0, LANES - 8))),
        ],
        axis=1,
    )
    wide_shard = jnp.concatenate(
        [up_weight.astype(BF), down_weight.astype(BF).T, out_weight.astype(BF).T], axis=1
    )
    segment = pick(segments, half, 0)
    features = document_features(segment)
    tables = rope_tables(rows)
    if part % 16 == 0 and ada_shard.shape[1] % 16 == 0:
        (h_one, queries, keys, values, mixed, lse, near, far, wa, norms, wide_near,
         wide_far) = opening(
            count, tokens, cond, small_shard, pick(ada_shard, half, 0)[None], wide_shard, tables,
            features,
        )
        wa = wa.reshape(-1, conds)
    else:
        wa = lax.all_gather(ada_shard.reshape(-1, conds), "dp", axis=0, tiled=True)
        near = lax.all_gather(small_shard, "dp", axis=0, tiled=True)
        far = swap_mp(near)
        norms = near[:, -LANES:].T[:8].astype(F32)
        wide_near = lax.all_gather(wide_shard, "dp", axis=0, tiled=True)
        wide_far = swap_mp(wide_near)
        h_one, queries, keys, values = first_stage(
            half_ref, tokens, cond, wa, norms, near, far, tables
        )
        mixed, lse = attend(queries, keys, values, segment, features)
    result, dx, upstream, z, gy, h_two, du, ga, dwa_two, dp_two = middle_stage(
        half_ref, tokens, out_grad, cond, mixed, wa, norms, wide_near, wide_far
    )
    result_far = swap_mp(result)

    block = width // 2
    steps = du.shape[1] // 2 // block

    def middle_grads(which, name):
        return weight_grads(
            [gy, h_two, ga], [du, z, mixed],
            [(steps, 1, 0, which * steps), (steps, 0, 1, which * steps), (1, 2, 2, which)],
            block, name,
        )

    middle_far = swap_mp(middle_grads(1, "middle_grads_far"))
    middle_near = middle_grads(0, "middle_grads_near")
    middle_sum = scatter_halves(middle_near, middle_far)

    grads = attend_back(queries, keys, values, upstream, mixed, lse, segment, features, tables)

    def first_grads(which, name):
        return weight_grads(
            [h_one], list(grads), [(1, 0, index, which) for index in range(3)], block, name
        )

    first_far = swap_mp(first_grads(1, "first_grads_far"))
    first_near = first_grads(0, "first_grads_near")
    first_sum = scatter_halves(first_near, first_far)

    input_grad, dwa_one, dp_one = last_stage(
        half_ref, tokens, cond, dx, grads, wa, norms, near, far
    )
    input_far = swap_mp(input_grad)

    dwa = jnp.concatenate([dwa_one, dwa_two], axis=1)
    ada_cols = dwa.shape[1] // count
    dwa_rows = dwa[:conds].T.astype(BF).reshape(count, 2, ada_cols // 2, conds)
    norm_rows = jnp.concatenate(
        [dp_one[0:1], dp_two[0:1], dwa[conds].reshape(6, width)], axis=0
    ).astype(BF)
    norm_rows = norm_rows.reshape(8, count, part).transpose(1, 0, 2)
    norm_rows = jnp.pad(norm_rows, ((0, 0), (0, 0), (0, conds - part)))
    ada_near = jnp.concatenate([pick(dwa_rows, half, 1), norm_rows], axis=1)
    ada_far = swap_mp(jnp.concatenate([pick(dwa_rows, 1 - half, 1), norm_rows], axis=1))
    ada_sum = scatter_sum([ada_near, ada_far], (2, 1))
    ada_half, norm_sum = ada_sum[: ada_cols // 2], ada_sum[ada_cols // 2 :, :part]

    wide_cols = du.shape[1] // 2
    up_mean = middle_sum[:, :wide_cols] / token_total
    down_mean = middle_sum[:, wide_cols : 2 * wide_cols] / token_total
    out_mean = middle_sum[:, 2 * wide_cols :] / token_total
    qkv_mean = first_sum / token_total
    ada_mean = ada_half / token_total
    norm_mean = norm_sum / token_total
    local_sq = (
        jnp.sum(qkv_mean * qkv_mean)
        + jnp.sum(out_mean * out_mean)
        + jnp.sum(up_mean * up_mean)
        + jnp.sum(down_mean * down_mean)
        + jnp.sum(ada_mean * ada_mean)
        + 0.5 * jnp.sum(norm_mean * norm_mean)
    )
    grad_norm = jnp.sqrt(sum_everywhere(jnp.full((8, LANES), local_sq, F32))[0, 0])
    clip_factor = jnp.minimum(1.0, clip_limit / (grad_norm + 1e-06))
    step_count = step[0].astype(F32)
    fix_one = 1.0 - jnp.exp(step_count * math.log(0.9))
    fix_two = 1.0 - jnp.exp(step_count * math.log(0.999))

    ada_grad = in_order(half, ada_mean, swap_mp(ada_mean)).T
    qkv_grad = qkv_mean.reshape(part, 3, -1).transpose(1, 0, 2)
    state = (
        (ada_weight, ada_first, ada_second, ada_grad),
        (norm_params, norm_first, norm_second, norm_mean),
        (qkv_weight, qkv_first, qkv_second, qkv_grad),
        (out_weight, out_first, out_second, out_mean.T),
        (up_weight, up_first, up_second, up_mean),
        (down_weight, down_first, down_second, down_mean.T),
    )
    outputs = [
        in_order(half, result, result_far),
        in_order(half, input_grad, input_far),
        grad_norm.reshape(1),
    ]
    for index, entry in enumerate(state):
        outputs += adam_update(
            *entry, clip_factor, fix_one, fix_two, step_rates[index], decay_rates[index]
        )
    return tuple(outputs)


def solution(mesh):
    column = (P(None, "dp"),) * 3
    weights = (
        column
        + column
        + (P(None, "dp", "mp"),) * 3
        + (P("mp", "dp"),) * 3
        + (P("dp", "mp"),) * 3
        + (P("mp", "dp"),) * 3
    )
    row = P("dp", None)
    return jax.shard_map(
        per_device,
        mesh=mesh,
        in_specs=(row, row, row, row, P()) + weights,
        out_specs=(row, row, P()) + weights,
        check_vma=False,
    )
```

```python
import functools
import math

import jax
import jax.numpy as jnp
from jax import lax
from jax.experimental import pallas as pl
from jax.experimental.pallas import tpu as pltpu
from jax.sharding import PartitionSpec as P

HEAD_DIM = 64
LANES = 128
MASKED = -1e30
ROW_BLOCK = 256
VMEM_LIMIT = 64_000_000
clip_limit = 1.0
step_rates = (0.075, 0.75, 0.075, 0.25, 0.075, 0.075)
decay_rates = (0.01, 0.0, 0.01, 0.01, 0.01, 0.01)

F32 = jnp.float32
BF = jnp.bfloat16
NN = (((1,), (0,)), ((), ()))
NT = (((1,), (1,)), ((), ()))


def dot(left, right, dims=NN):
    return lax.dot_general(left, right, dims, preferred_element_type=F32)


def shape_of(shape, dtype):
    return jax.ShapeDtypeStruct(shape, dtype)


def resident(shape, index):
    return pl.BlockSpec(shape, lambda *_: index, pipeline_mode=pl.Buffered(1))


def params():
    return pltpu.CompilerParams(vmem_limit_bytes=VMEM_LIMIT)


def adam_update(weight, first, second, grad, clip_factor, fix_one, fix_two, rate, decay):
    clipped = grad * clip_factor
    first_new = 0.9 * first + 0.1 * clipped
    second_new = 0.999 * second + 0.001 * clipped * clipped
    update = first_new / fix_one / (jnp.sqrt(second_new / fix_two) + 1e-08) + decay * weight
    return (weight - rate * update, first_new, second_new)


def rope_tables(length):
    half = HEAD_DIM // 2
    inverse = jnp.exp(jnp.arange(half, dtype=F32) * (-2.0 * math.log(10000.0) / HEAD_DIM))
    angles = jnp.arange(length, dtype=F32)[:, None] * inverse[None, :]
    cosines, sines = jnp.cos(angles), jnp.sin(angles)
    return (
        jnp.concatenate([cosines] * 4, axis=1),
        jnp.concatenate([-sines, sines, -sines, sines], axis=1),
    )


def swap_halves(values):
    width = values.shape[1]
    lane = lax.broadcasted_iota(jnp.int32, values.shape, 1)
    ahead = pltpu.roll(values, width - HEAD_DIM // 2, 1)
    behind = pltpu.roll(values, HEAD_DIM // 2, 1)
    return jnp.where(lane % HEAD_DIM < HEAD_DIM // 2, ahead, behind)


def silu_low(cond):
    value = cond.astype(F32)
    return (value / (1.0 + jnp.exp(-value))).astype(BF)


def normalize(rows):
    centre = rows - jnp.mean(rows, axis=-1, keepdims=True)
    scale = lax.rsqrt(jnp.mean(centre * centre, axis=-1, keepdims=True) + 1e-05)
    return centre * scale, scale


def norm_backward(grad, normal, scale):
    return scale * (
        grad
        - jnp.mean(grad, axis=-1, keepdims=True)
        - normal * jnp.mean(grad * normal, axis=-1, keepdims=True)
    )


def cond_rows(cond):
    return jnp.concatenate([cond.T, jnp.ones((16, cond.shape[0]), BF)], axis=0)


def first_kernel(half, x_ref, c_ref, wa_ref, p_ref, wqa_ref, wqb_ref, cos_ref, sin_ref,
                 h_ref, q_ref, k_ref, v_ref):
    width = x_ref.shape[1]
    own = width // 2
    cond = silu_low(c_ref[...])
    mod = dot(cond, wa_ref[0 : 2 * width, :], NT)
    shift = mod[:, :width] + p_ref[2:3, :]
    scale = mod[:, width:] + p_ref[3:4, :]
    normal, _ = normalize(x_ref[...].astype(F32))
    h = (normal * p_ref[0:1, :] * (1.0 + scale) + shift).astype(BF)
    h_ref[...] = h
    cos = jnp.concatenate([cos_ref[...]] * (own // LANES), axis=1)
    sin = jnp.concatenate([sin_ref[...]] * (own // LANES), axis=1)
    for start, w_ref in ((0, wqa_ref), (own, wqb_ref)):
        cols = slice(start, start + own)
        query = dot(h, w_ref[:, 0:own])
        query = query * cos + swap_halves(query) * sin
        q_ref[:, cols] = (query * HEAD_DIM**-0.5).astype(BF)
        key = dot(h, w_ref[:, own : 2 * own])
        k_ref[:, cols] = (key * cos + swap_halves(key) * sin).astype(BF)
        v_ref[:, cols] = dot(h, w_ref[:, 2 * own :]).astype(BF)


def first_stage(half, tokens, cond, wa, norms, near, far, tables):
    width = tokens.shape[1]
    rows = tables[0].shape[0]
    blocks = rows // ROW_BLOCK
    mine = lambda i, half: (half[0] * blocks + i, 0)
    plain = lambda i, half: (i, 0)
    row = pl.BlockSpec((ROW_BLOCK, width), plain)
    return pl.pallas_call(
        first_kernel,
        grid_spec=pltpu.PrefetchScalarGridSpec(
            num_scalar_prefetch=1,
            grid=(blocks,),
            in_specs=[
                pl.BlockSpec((ROW_BLOCK, width), mine),
                pl.BlockSpec((ROW_BLOCK, cond.shape[1]), mine),
                resident(wa.shape, (0, 0)),
                resident(norms.shape, (0, 0)),
                resident((width, 3 * width // 2), (0, 0)),
                resident((width, 3 * width // 2), (0, 0)),
                pl.BlockSpec((ROW_BLOCK, LANES), plain),
                pl.BlockSpec((ROW_BLOCK, LANES), plain),
            ],
            out_specs=[row] * 4,
        ),
        out_shape=[shape_of((rows, width), BF)] * 4,
        compiler_params=params(),
        name="first_stage",
    )(half, tokens, cond, wa, norms, near, far, *tables)


def split_heads(pair, other):
    low = lax.broadcasted_iota(jnp.int32, pair.shape, 1) < HEAD_DIM
    return jnp.where(low, pair, other), jnp.where(low, other, pair)


def attend_kernel(lo_ref, hi_ref, q_ref, k_ref, v_ref, fq_ref, fk_ref, o_ref, lse_ref,
                  qz, kz, vt, *, bq, bk):
    length = q_ref.shape[0]
    qz[0], qz[1] = split_heads(q_ref[...], fq_ref[...])
    kz[0], kz[1] = split_heads(k_ref[...], fk_ref[...])
    vt[...] = v_ref[...].T

    def query_block(i, _):
        off = pl.multiple_of(i * bq, bq)
        queries = [qz[h, pl.ds(off, bq), :] for h in range(2)]

        def key_block(j, carry):
            koff = pl.multiple_of(j * bk, bk)
            scores = [dot(kz[h, pl.ds(koff, bk), :], queries[h], NT) for h in range(2)]
            out = []
            for h in range(2):
                top, total, mixed = carry[3 * h : 3 * h + 3]
                new_top = jnp.maximum(top, jnp.max(scores[h], axis=0, keepdims=True))
                weights = jnp.exp(scores[h] - new_top)
                fade = jnp.exp(top - new_top)
                total = total * fade + jnp.sum(weights, axis=0, keepdims=True)
                values = vt[HEAD_DIM * h : HEAD_DIM * (h + 1), pl.ds(koff, bk)]
                mixed = mixed * fade + dot(values, weights.astype(BF))
                out += [new_top, total, mixed]
            return tuple(out)

        start = (
            jnp.full((1, bq), -3e38, F32),
            jnp.zeros((1, bq), F32),
            jnp.zeros((HEAD_DIM, bq), F32),
        )
        done = lax.fori_loop(lo_ref[i], hi_ref[i], key_block, start * 2)
        mixed = jnp.concatenate([done[2] / done[1], done[5] / done[4]], axis=0)
        o_ref[pl.ds(off, bq), :] = mixed.T.astype(BF)
        lse_ref[0, 0:1, pl.ds(off, bq)] = done[0] + jnp.log(done[1])
        lse_ref[0, 1:2, pl.ds(off, bq)] = done[3] + jnp.log(done[4])
        return 0

    lax.fori_loop(0, length // bq, query_block, 0)


def block_ranges(segment, block, other):
    first, last = segment[::block], segment[block - 1 :: block]
    low = jnp.sum(segment[None, :] < first[:, None], axis=1)
    high = jnp.sum(segment[None, :] <= last[:, None], axis=1)
    return (low // other).astype(jnp.int32), ((high + other - 1) // other).astype(jnp.int32)


def document_features(segment):
    lane = lax.broadcasted_iota(jnp.int32, (segment.shape[0], LANES), 1) % HEAD_DIM
    same = lane == segment[:, None]
    query = jnp.where(same, 1.0, 0.0).astype(BF)
    key = jnp.where((lane < 4) & ~same, MASKED, 0.0).astype(BF)
    return query, key


def attend(queries, keys, values, segment, features, bq=1024, bk=512):
    length, width = queries.shape
    bq, bk = min(bq, length), min(bk, length)
    pairs = width // LANES
    low, high = block_ranges(segment, bq, bk)
    pair = pl.BlockSpec((length, LANES), lambda p, *_: (0, p))
    fixed = pl.BlockSpec((length, LANES), lambda p, *_: (0, 0))
    scratch = pltpu.VMEM((2, length, LANES), BF)
    return pl.pallas_call(
        functools.partial(attend_kernel, bq=bq, bk=bk),
        grid_spec=pltpu.PrefetchScalarGridSpec(
            num_scalar_prefetch=2,
            grid=(pairs,),
            in_specs=[pair, pair, pair, fixed, fixed],
            out_specs=[pair, pl.BlockSpec((1, 2, length), lambda p, *_: (p, 0, 0))],
            scratch_shapes=[scratch, scratch, pltpu.VMEM((LANES, length), BF)],
        ),
        out_shape=[shape_of((length, width), BF), shape_of((pairs, 2, length), F32)],
        compiler_params=params(),
        name="attend",
    )(low, high, queries, keys, values, *features)


def attend_back_kernel(lo_ref, hi_ref, q_ref, k_ref, v_ref, do_ref, o_ref, lse_ref, fq_ref,
                       fk_ref, cos_ref, sin_ref, dq_ref, dk_ref, dv_ref,
                       qz, kz, qm, dm, vm, kt, delta, dqt, *, bq, bk):
    length = q_ref.shape[0]
    zero = jnp.zeros((length, LANES), BF)
    qz[0], qz[1] = split_heads(q_ref[...], fq_ref[...])
    kz[0], kz[1] = split_heads(k_ref[...], fk_ref[...])
    qm[0], qm[1] = split_heads(q_ref[...], zero)
    dm[0], dm[1] = split_heads(do_ref[...], zero)
    vm[0], vm[1] = split_heads(v_ref[...], zero)
    kt[...] = k_ref[...].T
    product = (do_ref[...].astype(F32) * o_ref[...].astype(F32)).T
    delta[0:1, :] = jnp.sum(product[:HEAD_DIM], axis=0, keepdims=True)
    delta[1:2, :] = jnp.sum(product[HEAD_DIM:], axis=0, keepdims=True)
    dqt[...] = jnp.zeros_like(dqt)

    def unrotate(grad, off, rows):
        cos, sin = cos_ref[pl.ds(off, rows), :], sin_ref[pl.ds(off, rows), :]
        return (grad * cos - swap_halves(grad) * sin).astype(BF)

    def key_block(j, _):
        koff = pl.multiple_of(j * bk, bk)
        keys = [kz[h, pl.ds(koff, bk), :] for h in range(2)]
        values = [vm[h, pl.ds(koff, bk), :] for h in range(2)]

        def query_block(i, carry):
            dk, dv = carry
            off = pl.multiple_of(i * bq, bq)
            scores = [dot(keys[h], qz[h, pl.ds(off, bq), :], NT) for h in range(2)]
            grads = [dot(values[h], dm[h, pl.ds(off, bq), :], NT) for h in range(2)]
            for h in range(2):
                weights = jnp.exp(scores[h] - lse_ref[0, h : h + 1, pl.ds(off, bq)])
                dv = dv + dot(weights.astype(BF), dm[h, pl.ds(off, bq), :])
                ds = (weights * (grads[h] - delta[h : h + 1, pl.ds(off, bq)])).astype(BF)
                dk = dk + dot(ds, qm[h, pl.ds(off, bq), :])
                head = slice(HEAD_DIM * h, HEAD_DIM * (h + 1))
                dqt[head, pl.ds(off, bq)] += dot(kt[head, pl.ds(koff, bk)], ds)
            return dk, dv

        zeros = jnp.zeros((bk, LANES), F32)
        dk, dv = lax.fori_loop(lo_ref[j], hi_ref[j], query_block, (zeros, zeros))
        dk_ref[pl.ds(koff, bk), :] = unrotate(dk, koff, bk)
        dv_ref[pl.ds(koff, bk), :] = dv.astype(BF)
        return 0

    lax.fori_loop(0, length // bk, key_block, 0)
    dq_ref[...] = unrotate(dqt[...].T * HEAD_DIM**-0.5, 0, length)


def attend_back(queries, keys, values, upstream, mixed, lse, segment, features, tables,
                bq=512, bk=256):
    length, width = queries.shape
    bq, bk = min(bq, length), min(bk, length)
    pairs = width // LANES
    low, high = block_ranges(segment, bk, bq)
    pair = pl.BlockSpec((length, LANES), lambda p, *_: (0, p))
    fixed = pl.BlockSpec((length, LANES), lambda p, *_: (0, 0))
    scratch = pltpu.VMEM((2, length, LANES), BF)
    return pl.pallas_call(
        functools.partial(attend_back_kernel, bq=bq, bk=bk),
        grid_spec=pltpu.PrefetchScalarGridSpec(
            num_scalar_prefetch=2,
            grid=(pairs,),
            in_specs=[pair] * 5
            + [pl.BlockSpec((1, 2, length), lambda p, *_: (p, 0, 0))]
            + [fixed] * 4,
            out_specs=[pair] * 3,
            scratch_shapes=[scratch] * 5
            + [
                pltpu.VMEM((LANES, length), BF),
                pltpu.VMEM((8, length), F32),
                pltpu.VMEM((LANES, length), F32),
            ],
        ),
        out_shape=[shape_of((length, width), BF)] * 3,
        compiler_params=params(),
        name="attend_back",
    )(low, high, queries, keys, values, upstream, mixed, lse, *features, *tables)


def middle_kernel(half, x_ref, g_ref, c_ref, o_ref, wa_ref, p_ref, woa_ref, wob_ref, w1a_ref,
                  w1b_ref, w2a_ref, w2b_ref,
                  res_ref, dx_ref, do_ref, z_ref, gy_ref, h_ref, du_ref, ga_ref, dwa_ref,
                  dp_ref, slope, *, chunk):
    width = x_ref.shape[1]
    own = width // 2
    hidden = w1a_ref.shape[1]
    cond = silu_low(c_ref[...])

    def modulation(block):
        rows = wa_ref[block * width : (block + 1) * width, :]
        return dot(cond, rows, NT) + p_ref[block + 2 : block + 3, :]

    gate_one, shift, scale, gate_two = (modulation(block) for block in (2, 3, 4, 5))
    branch = dot(o_ref[:, :own], woa_ref[...], NT) + dot(o_ref[:, own:], wob_ref[...], NT)
    middle = x_ref[...].astype(F32) + gate_one * branch
    normal, rstd = normalize(middle)
    gain = p_ref[1:2, :]
    spread = 1.0 + scale
    h = (normal * gain * spread + shift).astype(BF)
    h_ref[...] = h

    out = jnp.zeros_like(middle)
    for start, up_ref, down_ref in ((0, w1a_ref, w2a_ref), (hidden, w1b_ref, w2b_ref)):
        for at in range(0, hidden, chunk):
            u = dot(h, up_ref[:, at : at + chunk])
            square = u * u
            flat = jnp.tanh(math.sqrt(2.0 / math.pi) * u * (1.0 + 0.044715 * square))
            half_up = 0.5 * (1.0 + flat)
            z = (u * half_up).astype(BF)
            z_ref[:, start + at : start + at + chunk] = z
            slope[:, start + at : start + at + chunk] = half_up + 0.5 * u * (
                1.0 - flat * flat
            ) * (math.sqrt(2.0 / math.pi) * (1.0 + 3.0 * 0.044715 * square))
            out = out + dot(z, down_ref[:, at : at + chunk], NT)

    g = g_ref[...].astype(F32)
    res_ref[...] = (middle + gate_two * out).astype(BF)
    gy = (gate_two * g).astype(BF)
    gy_ref[...] = gy
    dgate_two = (g * out).astype(BF)

    dh = jnp.zeros_like(middle)
    for start, up_ref, down_ref in ((0, w1a_ref, w2a_ref), (hidden, w1b_ref, w2b_ref)):
        for at in range(0, hidden, chunk):
            dz = dot(gy, down_ref[:, at : at + chunk])
            du = (dz * slope[:, start + at : start + at + chunk]).astype(BF)
            du_ref[:, start + at : start + at + chunk] = du
            dh = dh + dot(du, up_ref[:, at : at + chunk], NT)

    dn = dh * normal
    dx = g + norm_backward(dh * gain * spread, normal, rstd)
    dx_ref[...] = dx
    ga = (gate_one * dx).astype(BF)
    ga_ref[...] = ga
    do_ref[:, :own] = dot(ga, woa_ref[...]).astype(BF)
    do_ref[:, own:] = dot(ga, wob_ref[...]).astype(BF)

    @pl.when(pl.program_id(0) == 0)
    def _():
        dwa_ref[...] = jnp.zeros_like(dwa_ref)
        dp_ref[...] = jnp.zeros_like(dp_ref)

    rows = cond_rows(cond)
    grads = ((dx * branch).astype(BF), dh.astype(BF), (dn * gain).astype(BF), dgate_two)
    for block, grad in enumerate(grads):
        dwa_ref[:, block * width : (block + 1) * width] += dot(rows, grad)
    dp_ref[0:1, :] += jnp.sum(dn * spread, axis=0, keepdims=True)


def middle_stage(half, tokens, out_grad, cond, mixed, wa, norms, wide_near, wide_far):
    width = tokens.shape[1]
    rows = mixed.shape[0]
    hidden = (wide_near.shape[1] - width // 2) // 2
    blocks = rows // ROW_BLOCK
    mine = lambda i, half: (half[0] * blocks + i, 0)
    plain = lambda i, half: (i, 0)
    row = pl.BlockSpec((ROW_BLOCK, width), plain)
    wide = pl.BlockSpec((ROW_BLOCK, 2 * hidden), plain)
    narrow = shape_of((rows, width), BF)
    broad = shape_of((rows, 2 * hidden), BF)
    total = (cond.shape[1] + 16, 4 * width)
    return pl.pallas_call(
        functools.partial(middle_kernel, chunk=768),
        grid_spec=pltpu.PrefetchScalarGridSpec(
            num_scalar_prefetch=1,
            grid=(blocks,),
            in_specs=[
                pl.BlockSpec((ROW_BLOCK, width), mine),
                pl.BlockSpec((ROW_BLOCK, width), mine),
                pl.BlockSpec((ROW_BLOCK, cond.shape[1]), mine),
                row,
                resident(wa.shape, (0, 0)),
                resident(norms.shape, (0, 0)),
                resident((width, width // 2), (0, 4 * hidden // width)),
                resident((width, width // 2), (0, 4 * hidden // width)),
                resident((width, hidden), (0, 0)),
                resident((width, hidden), (0, 0)),
                resident((width, hidden), (0, 1)),
                resident((width, hidden), (0, 1)),
            ],
            out_specs=[row, row, row, wide, row, row, wide, row,
                       pl.BlockSpec(total, lambda i, half: (0, 0)),
                       pl.BlockSpec((8, width), lambda i, half: (0, 0))],
            scratch_shapes=[pltpu.VMEM((ROW_BLOCK, 2 * hidden), F32)],
        ),
        out_shape=[narrow, shape_of((rows, width), F32), narrow, broad, narrow, narrow, broad,
                   narrow, shape_of(total, F32), shape_of((8, width), F32)],
        compiler_params=params(),
        name="middle_stage",
    )(half, tokens, out_grad, cond, mixed, wa, norms, wide_near, wide_far, wide_near, wide_far,
      wide_near, wide_far)


def last_kernel(half, x_ref, c_ref, dx_ref, dq_ref, dk_ref, dv_ref, wa_ref, p_ref, wqa_ref,
                wqb_ref, out_ref, dwa_ref, dp_ref):
    width = x_ref.shape[1]
    own = width // 2
    cond = silu_low(c_ref[...])
    scale = dot(cond, wa_ref[width : 2 * width, :], NT) + p_ref[3:4, :]
    dh = jnp.zeros(x_ref.shape, F32)
    for start, w_ref in ((0, wqa_ref), (own, wqb_ref)):
        cols = slice(start, start + own)
        for index, grad_ref in enumerate((dq_ref, dk_ref, dv_ref)):
            dh = dh + dot(grad_ref[:, cols], w_ref[:, index * own : (index + 1) * own], NT)
    normal, rstd = normalize(x_ref[...].astype(F32))
    gain = p_ref[0:1, :]
    spread = 1.0 + scale
    dn = dh * normal
    out_ref[...] = dx_ref[...] + norm_backward(dh * gain * spread, normal, rstd)

    @pl.when(pl.program_id(0) == 0)
    def _():
        dwa_ref[...] = jnp.zeros_like(dwa_ref)
        dp_ref[...] = jnp.zeros_like(dp_ref)

    rows = cond_rows(cond)
    dwa_ref[:, :width] += dot(rows, dh.astype(BF))
    dwa_ref[:, width:] += dot(rows, (dn * gain).astype(BF))
    dp_ref[0:1, :] += jnp.sum(dn * spread, axis=0, keepdims=True)


def last_stage(half, tokens, cond, dx, grads, wa, norms, near, far):
    width = tokens.shape[1]
    rows = dx.shape[0]
    blocks = rows // ROW_BLOCK
    mine = lambda i, half: (half[0] * blocks + i, 0)
    row = pl.BlockSpec((ROW_BLOCK, width), lambda i, half: (i, 0))
    total = (cond.shape[1] + 16, 2 * width)
    return pl.pallas_call(
        last_kernel,
        grid_spec=pltpu.PrefetchScalarGridSpec(
            num_scalar_prefetch=1,
            grid=(blocks,),
            in_specs=[
                pl.BlockSpec((ROW_BLOCK, width), mine),
                pl.BlockSpec((ROW_BLOCK, cond.shape[1]), mine),
                row, row, row, row,
                resident(wa.shape, (0, 0)),
                resident(norms.shape, (0, 0)),
                resident((width, 3 * width // 2), (0, 0)),
                resident((width, 3 * width // 2), (0, 0)),
            ],
            out_specs=[row, pl.BlockSpec(total, lambda i, half: (0, 0)),
                       pl.BlockSpec((8, width), lambda i, half: (0, 0))],
        ),
        out_shape=[shape_of((rows, width), F32), shape_of(total, F32), shape_of((8, width), F32)],
        compiler_params=params(),
        name="last_stage",
    )(half, tokens, cond, dx, *grads, wa, norms, near, far)


def weight_grad_kernel(*refs, plan):
    lefts, rights = plan["lefts"], plan["rights"]
    left_refs, right_refs = refs[:lefts], refs[lefts : lefts + rights]
    out_ref, turned = refs[lefts + rights :]
    step = pl.program_id(0)
    for begin, end, left, right in plan["spans"]:

        @pl.when(step == begin)
        def _():
            turned[...] = left_refs[left][...].T

        @pl.when((step >= begin) & (step < end))
        def _():
            out_ref[...] = dot(turned[...], right_refs[right][...]).astype(BF)


def weight_grads(lefts, rights, spans, block, name):
    rows, width = lefts[0].shape
    begin, plan, maps = 0, [], []
    for steps, left, right, first in spans:
        plan.append((begin, begin + steps, left, right))
        maps.append((begin, steps, first))
        begin += steps

    def column_map(begin, steps, first):
        return lambda i: (0, first + jnp.clip(i - begin, 0, steps - 1))

    return pl.pallas_call(
        functools.partial(
            weight_grad_kernel,
            plan={"lefts": len(lefts), "rights": len(rights), "spans": plan},
        ),
        grid=(begin,),
        in_specs=[resident((rows, width), (0, 0))] * len(lefts)
        + [pl.BlockSpec((rows, block), column_map(*entry)) for entry in maps],
        out_specs=pl.BlockSpec((width, block), lambda i: (0, i)),
        out_shape=shape_of((width, begin * block), BF),
        scratch_shapes=[pltpu.VMEM((width, rows), BF)],
        compiler_params=params(),
        name=name,
    )(*lefts, *rights)


class Gather:
    def __init__(self, shard, near, far, cut, sems, place):
        outer, inner, mid, core = place["outer"], place["x"], place["y"], place["core"]
        z = place["z"]
        columns = near.shape[-1]
        split = near.shape[0] != place["outer"] * 4
        rows = near.shape[0] // (4 * outer)

        def slots(ref, first, number, cols):
            if split:
                at = pl.multiple_of(first * rows, 16)
                return ref.at[pl.ds(at, number * rows), cols]
            return ref.at[pl.ds(first, number), core, :, cols]

        def copy(src, dst, name, index, device):
            return pltpu.make_async_remote_copy(
                src_ref=src,
                dst_ref=dst,
                send_sem=sems[name].at[0, index],
                recv_sem=sems[name].at[1, index],
                device_id=device,
                device_id_type=pl.DeviceIdType.MESH,
            )

        def peer(zz, yy, xx):
            return (4 * zz + 2 * yy + xx, core)

        whole = slice(None)
        parts = [("a", slice(0, cut))] + ([("b", slice(cut, columns))] if cut < columns else [])
        mine = 4 * z + 2 * mid + inner
        self.outer = outer
        self.parts = [name for name, _ in parts]
        self.local = (shard, slots(near, mine, 1, whole))
        source = shard if split else shard
        self.hops = {
            hop: copy(source, slots(near, mine, 1, whole), "hop", hop - 1,
                      peer(lax.rem(z + hop, outer), mid, inner))
            for hop in range(1, outer)
        }
        self.one, self.two, self.swap = {}, {}, {}
        for step in range(outer):
            zz = lax.rem(z + outer - step, outer)
            base = 4 * zz
            for index, (name, cols) in enumerate(parts):
                own = base + 2 * mid + inner
                device = peer(z, mid, 1 - inner) if name == "a" else peer(z, 1 - mid, inner)
                if step == 0:
                    src = shard.at[:, cols] if split else shard.at[:, :, cols]
                else:
                    src = slots(near, own, 1, cols)
                self.one[name, step] = copy(
                    src, slots(near, own, 1, cols), "one", index * outer + step, device
                )
            if True:
                self.two["a", step] = [
                    copy(slots(near, base + 2 * mid, 2, parts[0][1]),
                         slots(near, base + 2 * mid, 2, parts[0][1]),
                         "two", step, peer(z, 1 - mid, inner))
                ]
            if len(parts) > 1:
                self.two["b", step] = [
                    copy(slots(near, base + 2 * yy + inner, 1, parts[1][1]),
                         slots(near, base + 2 * yy + inner, 1, parts[1][1]),
                         "two", outer + 2 * step + yy, peer(z, mid, 1 - inner))
                    for yy in range(2)
                ]
            target = far if split else near
            self.swap[step] = copy(
                slots(near, base, 4, whole), slots(target, base, 4, whole),
                "swap", step, (4 * z + 2 * mid + inner, 1 - core)
            )

    @staticmethod
    def semaphores(outer):
        kind = pltpu.SemaphoreType.DMA
        return [kind((2, outer)), kind((2, 2 * outer)), kind((2, 3 * outer)), kind((2, outer))]

    @staticmethod
    def named(refs):
        return dict(zip(("hop", "one", "two", "swap"), refs))

    def start_hops(self):
        for hop in self.hops.values():
            hop.start()

    def phase_one(self, step):
        if step:
            self.hops[step].wait_recv()
        for name in self.parts:
            self.one[name, step].start()

    def phase_two(self, step):
        for name in self.parts:
            self.one[name, step].wait_recv()
        for name in self.parts:
            for entry in self.two[name, step]:
                entry.start()

    def phase_swap(self, step):
        for name in self.parts:
            for entry in self.two[name, step]:
                entry.wait_recv()
        self.swap[step].start()

    def finish(self, step):
        self.swap[step].wait_recv()

    def drain(self):
        for hop in self.hops.values():
            hop.wait_send()
        for step in range(self.outer):
            for name in self.parts:
                self.one[name, step].wait_send()
                for entry in self.two[name, step]:
                    entry.wait_send()
            self.swap[step].wait_send()


def my_place(count):
    me, core = lax.axis_index("dp"), lax.axis_index("mp")
    return {"outer": count // 4, "z": me // 4, "y": lax.rem(me // 2, 2), "x": lax.rem(me, 2),
            "core": core, "me": me}


def meet(place):
    z, y, x, core, outer = (place[name] for name in ("z", "y", "x", "core", "outer"))
    here = 2 * y + x
    others = [(4 * lax.rem(z + hop, outer) + here, core) for hop in range(1, outer)]
    others += [(4 * z + 2 * y + 1 - x, core), (4 * z + 2 * (1 - y) + x, core),
               (4 * z + here, 1 - core)]
    barrier = pltpu.get_barrier_semaphore()
    for other in others:
        pl.semaphore_signal(barrier, inc=1, device_id=other, device_id_type=pl.DeviceIdType.MESH)
    pl.semaphore_wait(barrier, len(others))


def opening_kernel(tok_ref, cond_ref, g1_ref, ada_ref, g2_ref, cos_ref, sin_ref, fq_ref, fk_ref,
                   h_ref, q_ref, k_ref, v_ref, o_ref, lse_ref, near_ref, far_ref, wa_ref,
                   norm_ref, wide_near, wide_far,
                   x_vm, c_vm, qz, kz, vt, local, *sems, count, cuts, bk):
    place = my_place(count)
    outer, core = place["outer"], place["core"]
    rows, width = x_vm.shape
    own = width // 2
    groups = [Gather.named(sems[4 * i : 4 * i + 4]) for i in range(3)]
    small = Gather(g1_ref, near_ref, far_ref, cuts[0], groups[0], place)
    ada = Gather(ada_ref, wa_ref, None, ada_ref.shape[-1], groups[1], place)
    wide = Gather(g2_ref, wide_near, wide_far, cuts[1], groups[2], place)

    start = pl.multiple_of(core * rows, rows)
    loads = [
        pltpu.make_async_copy(tok_ref.at[pl.ds(start, rows)], x_vm, local.at[0]),
        pltpu.make_async_copy(cond_ref.at[pl.ds(start, rows)], c_vm, local.at[1]),
        pltpu.make_async_copy(*wide.local, local.at[2]),
        pltpu.make_async_copy(*small.local, local.at[3]),
        pltpu.make_async_copy(*ada.local, local.at[4]),
    ]
    for load in loads:
        load.start()
    meet(place)
    ada.start_hops()
    small.start_hops()
    for load in loads:
        load.wait()
    for step in range(outer):
        ada.phase_one(step)
        small.phase_one(step)
    wide.start_hops()
    for step in range(outer):
        ada.phase_two(step)
        small.phase_two(step)
    for step in range(outer):
        ada.phase_swap(step)
        small.phase_swap(step)
    wide.phase_one(0)
    for step in range(outer):
        ada.finish(step)
        small.finish(step)

    table = near_ref[:, 3 * own :].astype(F32).T
    norm_ref[...] = table[0:8, :]
    wa = wa_ref[...].reshape(6 * width, c_vm.shape[1])

    def row_block(i, _):
        at = pl.ds(pl.multiple_of(i * ROW_BLOCK, ROW_BLOCK), ROW_BLOCK)
        cond = silu_low(c_vm[at, :])
        shift = dot(cond, wa[:width], NT) + norm_ref[2:3, :]
        scale = dot(cond, wa[width : 2 * width], NT) + norm_ref[3:4, :]
        normal, _ = normalize(x_vm[at, :].astype(F32))
        h = (normal * norm_ref[0:1, :] * (1.0 + scale) + shift).astype(BF)
        h_ref[at, :] = h
        cos = jnp.concatenate([cos_ref[at, :]] * (own // LANES), axis=1)
        sin = jnp.concatenate([sin_ref[at, :]] * (own // LANES), axis=1)
        for first, w_ref in ((0, near_ref), (own, far_ref)):
            cols = slice(first, first + own)
            query = dot(h, w_ref[:, 0:own])
            query = query * cos + swap_halves(query) * sin
            q_ref[at, cols] = (query * HEAD_DIM**-0.5).astype(BF)
            key = dot(h, w_ref[:, own : 2 * own])
            k_ref[at, cols] = (key * cos + swap_halves(key) * sin).astype(BF)
            v_ref[at, cols] = dot(h, w_ref[:, 2 * own : 3 * own]).astype(BF)
        for step in range(1, outer):

            @pl.when(i == step - 1)
            def _():
                wide.phase_one(step)

        return 0

    lax.fori_loop(0, rows // ROW_BLOCK, row_block, 0)

    def head_pair(p, _):
        lanes = pl.ds(pl.multiple_of(p * LANES, LANES), LANES)
        qz[0], qz[1] = split_heads(q_ref[:, lanes], fq_ref[...])
        kz[0], kz[1] = split_heads(k_ref[:, lanes], fk_ref[...])
        vt[...] = v_ref[:, lanes].T
        state = [None, None]
        for j in range(rows // bk):
            block = slice(j * bk, (j + 1) * bk)
            scores = [dot(kz[h, block, :], qz[h], NT) for h in range(2)]
            for h in range(2):
                values = vt[HEAD_DIM * h : HEAD_DIM * (h + 1), block]
                top = jnp.max(scores[h], axis=0, keepdims=True)
                if j:
                    top = jnp.maximum(state[h][0], top)
                weights = jnp.exp(scores[h] - top)
                total = jnp.sum(weights, axis=0, keepdims=True)
                result = dot(values, weights.astype(BF))
                if j:
                    fade = jnp.exp(state[h][0] - top)
                    total = state[h][1] * fade + total
                    result = state[h][2] * fade + result
                state[h] = (top, total, result)
        done = jnp.concatenate([entry[2] / entry[1] for entry in state], axis=0)
        o_ref[:, lanes] = done.T.astype(BF)
        for h in range(2):
            lse_ref[p, h : h + 1, :] = state[h][0] + jnp.log(state[h][1])

        for step in range(outer):

            @pl.when(p == step // 2)
            def _():
                wide.phase_two(step)

            @pl.when(p == 3 + step // 2)
            def _():
                wide.phase_swap(step)

        return 0

    lax.fori_loop(0, width // LANES, head_pair, 0)
    for step in range(outer):
        wide.finish(step)
    for group in (ada, small, wide):
        group.drain()


def opening(count, tokens, cond, small_shard, ada_shard, wide_shard, tables, features):
    rows, width = tokens.shape[0] // 2, tokens.shape[1]
    conds = cond.shape[1]
    vm = pl.BlockSpec(memory_space=pltpu.VMEM)
    hbm = pl.BlockSpec(memory_space=pl.ANY)
    small = shape_of((width, small_shard.shape[1]), BF)
    wide = shape_of((width, wide_shard.shape[1]), BF)
    act = shape_of((rows, width), BF)
    pairs = width // LANES
    scratch = pltpu.VMEM((2, rows, LANES), BF)
    cuts = (512, wide_shard.shape[1] // 2 // LANES * LANES)
    return pl.pallas_call(
        functools.partial(opening_kernel, count=count, cuts=cuts, bk=512),
        in_specs=[hbm, hbm] + [vm] * 7,
        out_specs=[vm] * 10 + [hbm, hbm],
        out_shape=[act, act, act, act, act, shape_of((pairs, 2, rows), F32), small, small,
                   shape_of((count, 2, ada_shard.shape[1], conds), BF),
                   shape_of((8, width), F32), wide, wide],
        scratch_shapes=[
            pltpu.VMEM((rows, width), BF), pltpu.VMEM((rows, conds), BF),
            scratch, scratch, pltpu.VMEM((LANES, rows), BF),
            pltpu.SemaphoreType.DMA((5,)),
        ] + Gather.semaphores(count // 4) * 3,
        compiler_params=pltpu.CompilerParams(
            vmem_limit_bytes=VMEM_LIMIT, collective_id=0, has_side_effects=True
        ),
        name="opening",
    )(tokens, cond, small_shard, ada_shard, wide_shard, *tables, *features)


class Scatter:
    def __init__(self, place, first, total, one, two, hops, sems):
        z, y, x, core, outer = (place[name] for name in ("z", "y", "x", "core", "outer"))

        def copy(src, dst, device):
            index = place["next"]
            place["next"] = index + 1
            return pltpu.make_async_remote_copy(
                src_ref=src,
                dst_ref=dst,
                send_sem=sems.at[0, index],
                recv_sem=sems.at[1, index],
                device_id=device,
                device_id_type=pl.DeviceIdType.MESH,
            )

        across_x = (4 * z + 2 * y + 1 - x, core)
        across_y = (4 * z + 2 * (1 - y) + x, core)
        self.one, self.two, self.hops, self.z, self.outer = one, two, hops, z, outer
        if first == "y":
            self.keep_one, self.keep_two = total.at[:, y], one.at[:, x]
            self.copy_one = copy(total.at[:, 1 - y], one, across_y)
            self.copy_two = copy(one.at[:, 1 - x], two, across_x)
        else:
            self.keep_one, self.keep_two = total.at[:, :, x], one.at[:, y]
            self.copy_one = copy(total.at[:, :, 1 - x], one, across_x)
            self.copy_two = copy(one.at[:, 1 - y], two, across_y)
        self.copy_hops = [
            copy(two.at[lax.rem(z + hop, outer)], hops.at[hop - 1],
                 (4 * lax.rem(z + hop, outer) + 2 * y + x, core))
            for hop in range(1, outer)
        ]

    def start(self):
        self.copy_one.start()

    def phase_two(self):
        self.copy_one.wait_recv()
        self.one[...] = (self.one[...].astype(F32) + self.keep_one[...].astype(F32)).astype(BF)
        self.copy_two.start()

    def phase_hops(self):
        self.copy_two.wait_recv()
        self.two[...] = (self.two[...].astype(F32) + self.keep_two[...].astype(F32)).astype(BF)
        for entry in self.copy_hops:
            entry.start()

    def finish(self):
        total = self.two[self.z].astype(F32)
        for hop, entry in enumerate(self.copy_hops):
            entry.wait_recv()
            total = total + self.hops[hop].astype(F32)
        return total

    def drain(self):
        for entry in [self.copy_one, self.copy_two] + self.copy_hops:
            entry.wait_send()


def across_cores(place, src, dst, sems):
    index = place["next"]
    place["next"] = index + 1
    return pltpu.make_async_remote_copy(
        src_ref=src,
        dst_ref=dst,
        send_sem=sems.at[0, index],
        recv_sem=sems.at[1, index],
        device_id=(place["me"], 1 - place["core"]),
        device_id_type=pl.DeviceIdType.MESH,
    )


def scatter_buffers(outer, blocks, rows, columns):
    lead = () if blocks is None else (blocks,)
    return [
        pltpu.VMEM(lead + (outer, 2, 2, rows, columns), BF),
        pltpu.VMEM(lead + (outer, 2, 2, rows, columns), BF),
        pltpu.VMEM(lead + (outer, 2, rows, columns), BF),
        pltpu.VMEM(lead + (outer, rows, columns), BF),
        pltpu.VMEM(lead + (outer - 1, rows, columns), BF),
    ]


def spread_kernel(h_ref, gy_ref, ga_ref, du_ref, z_ref, o_ref, q_ref, k_ref, v_ref, do_ref,
                  lse_ref, fq_ref, fk_ref, cos_ref, sin_ref,
                  dq_ref, dk_ref, dv_ref, sum_ref,
                  h_turn, gy_turn, ga_turn, right, far6, sum6, one6, two6, hop6,
                  far1, sum1, one1, two1, hop1, qz, kz, qm, dm, vm, kt, delta, dqt,
                  load_sems, sems, *, count, bk):
    place = my_place(count)
    place["next"] = 0
    outer = place["outer"]
    rows, width = o_ref.shape
    own = width // 2
    each, block = right.shape[0], right.shape[2]
    span = 2 * each * block
    shards = far6.shape[1:]
    tail = far1.shape

    swaps = [across_cores(place, far6.at[j], sum6.at[j], sems) for j in range(2 * each)]
    swaps.append(across_cores(place, far1, sum1, sems))
    scatters = [
        Scatter(place, "yx"[j % 2], sum6.at[j], one6.at[j], two6.at[j], hop6.at[j], sems)
        for j in range(2 * each)
    ]
    scatters.append(Scatter(place, "y", sum1, one1, two1, hop1, sems))

    lefts, sources = (h_turn, gy_turn), (du_ref, z_ref)
    groups = [(side, index) for side in (1, 0) for index in range(2)]

    def load(group, b):
        side, index = groups[group]
        at = pl.multiple_of(side * (span // 2) + b * block, block)
        return pltpu.make_async_copy(
            sources[index].at[:, pl.ds(at, block)], right.at[b], load_sems.at[b]
        )

    for b in range(each):
        load(0, b).start()
    meet(place)
    h_turn[...] = h_ref[...].T
    gy_turn[...] = gy_ref[...].T
    ga_turn[...] = ga_ref[...].T

    for group, (side, index) in enumerate(groups):

        def grad_block(b, _):
            load(group, b).wait()
            grad = dot(lefts[index][...], right[b])
            if group + 1 < len(groups):
                load(group + 1, b).start()
            j = index * each + b
            if side:
                far6[j] = grad.reshape(shards).astype(BF)
            for b_static in range(each):
                at = index * each + b_static

                @pl.when(b == b_static)
                def _():
                    if side:
                        swaps[at].start()
                    else:
                        swaps[at].wait_recv()

            if not side:
                sum6[j] = (grad.reshape(shards) + sum6[j].astype(F32)).astype(BF)
                for b_static in range(each):
                    at = index * each + b_static
                    if at < 3:

                        @pl.when(b == b_static)
                        def _():
                            scatters[at].start()

            return 0

        lax.fori_loop(0, each, grad_block, 0)
        if index == 1:
            grad = dot(ga_turn[...], o_ref[:, side * own : (side + 1) * own])
            if side:
                far1[...] = grad.reshape(tail).astype(BF)
                swaps[-1].start()
            else:
                swaps[-1].wait_recv()
                sum1[...] = (grad.reshape(tail) + sum1[...].astype(F32)).astype(BF)

    def finish(j):
        at = j * block
        sum_ref[:, at : at + scatters[j].hops.shape[-1]] = scatters[j].finish()

    def events(p):
        if p == 0:
            scatters[0].phase_two()
            scatters[1].phase_two()
            scatters[3].start()
            scatters[4].start()
        if p == 1:
            scatters[2].phase_two()
            scatters[0].phase_hops()
            scatters[1].phase_hops()
            scatters[5].start()
        if p == 2:
            scatters[3].phase_two()
            scatters[6].start()
            scatters[2].phase_hops()
        if p == 3:
            scatters[4].phase_two()
            scatters[3].phase_hops()
            finish(0)
            finish(1)
        if p == 4:
            scatters[5].phase_two()
            scatters[6].phase_two()
            scatters[4].phase_hops()
            finish(2)
        if p == 5:
            scatters[5].phase_hops()
            scatters[6].phase_hops()
            for j in (3, 4, 5, 6):
                finish(j)

    zero = jnp.zeros((rows, LANES), BF)

    def unrotate(grad, at):
        return (grad * cos_ref[at, :] - swap_halves(grad) * sin_ref[at, :]).astype(BF)

    def head_pair(p, _):
        lanes = pl.ds(pl.multiple_of(p * LANES, LANES), LANES)
        qz[0], qz[1] = split_heads(q_ref[:, lanes], fq_ref[...])
        kz[0], kz[1] = split_heads(k_ref[:, lanes], fk_ref[...])
        qm[0], qm[1] = split_heads(q_ref[:, lanes], zero)
        dm[0], dm[1] = split_heads(do_ref[:, lanes], zero)
        vm[0], vm[1] = split_heads(v_ref[:, lanes], zero)
        kt[...] = k_ref[:, lanes].T
        product = (do_ref[:, lanes].astype(F32) * o_ref[:, lanes].astype(F32)).T
        delta[0:1, :] = jnp.sum(product[:HEAD_DIM], axis=0, keepdims=True)
        delta[1:2, :] = jnp.sum(product[HEAD_DIM:], axis=0, keepdims=True)
        dqt[...] = jnp.zeros_like(dqt)

        def key_block(j, _):
            off = pl.multiple_of(j * bk, bk)
            at = pl.ds(off, bk)
            dk = jnp.zeros((bk, LANES), F32)
            dv = jnp.zeros((bk, LANES), F32)
            scores = [dot(kz[h, at, :], qz[h], NT) for h in range(2)]
            grads = [dot(vm[h, at, :], dm[h], NT) for h in range(2)]
            for h in range(2):
                weights = jnp.exp(scores[h] - lse_ref[p, h : h + 1, :])
                dv = dv + dot(weights.astype(BF), dm[h])
                ds = (weights * (grads[h] - delta[h : h + 1, :])).astype(BF)
                dk = dk + dot(ds, qm[h])
                head = slice(HEAD_DIM * h, HEAD_DIM * (h + 1))
                dqt[head, :] += dot(kt[head, at], ds)
            dk_ref[at, lanes] = unrotate(dk, at)
            dv_ref[at, lanes] = dv.astype(BF)
            return 0

        lax.fori_loop(0, rows // bk, key_block, 0)
        dq_ref[:, lanes] = unrotate(dqt[...].T * HEAD_DIM**-0.5, pl.ds(0, rows))
        for step in range(6):

            @pl.when(p == step)
            def _():
                events(step)

        return 0

    lax.fori_loop(0, width // LANES, head_pair, 0)
    for entry in swaps:
        entry.wait_send()
    for entry in scatters:
        entry.drain()


def spread(count, h_two, gy, ga, du, z, mixed, queries, keys, values, upstream, lse, features,
           tables):
    rows, width = mixed.shape
    part = width // count
    outer = count // 4
    hidden = du.shape[1] // 2
    each = 3
    block = hidden // each
    vm = pl.BlockSpec(memory_space=pltpu.VMEM)
    hbm = pl.BlockSpec(memory_space=pl.ANY)
    act = shape_of((rows, width), BF)
    turn = pltpu.VMEM((width, rows), BF)
    pair = pltpu.VMEM((2, rows, LANES), BF)
    copies = 7 + 7 * (2 + outer - 1)
    return pl.pallas_call(
        functools.partial(spread_kernel, count=count, bk=256),
        in_specs=[vm, vm, vm, hbm, hbm] + [vm] * 10,
        out_specs=[vm] * 4,
        out_shape=[act, act, act, shape_of((part, 2 * hidden + width // 2), F32)],
        scratch_shapes=[turn, turn, turn, pltpu.VMEM((each, rows, block), BF)]
        + scatter_buffers(outer, 2 * each, part, block)
        + scatter_buffers(outer, None, part, width // 2)
        + [pair] * 5
        + [
            pltpu.VMEM((LANES, rows), BF),
            pltpu.VMEM((8, rows), F32),
            pltpu.VMEM((LANES, rows), F32),
            pltpu.SemaphoreType.DMA((each,)),
            pltpu.SemaphoreType.DMA((2, copies)),
        ],
        compiler_params=pltpu.CompilerParams(
            vmem_limit_bytes=VMEM_LIMIT, collective_id=1, has_side_effects=True
        ),
        name="spread",
    )(h_two, gy, ga, du, z, mixed, queries, keys, values, upstream, lse, *features, *tables)


def closing_kernel(tok_ref, cond_ref, h_ref, dq_ref, dk_ref, dv_ref, dx_ref, wa_ref, p_ref,
                   near_ref, far_ref, dwa_two_ref, dp_two_ref, mid_ref,
                   rows_ref, qkv_ref, ada_ref, norm_ref, square_ref,
                   x_vm, c_vm, turned, mine, dh_vm, dwa_vm, dp_vm, dwt, plane, column,
                   far3, sum3, one3, two3, hop3, far2, sum2, one2, two2, hop2,
                   local, sems, *, count, token_total):
    place = my_place(count)
    place["next"] = 0
    z, y, x, core, outer, me = (place[name] for name in ("z", "y", "x", "core", "outer", "me"))
    rows, width = x_vm.shape
    own = width // 2
    part = width // count
    conds = c_vm.shape[1]
    half_cols = ada_ref.shape[1]
    cut = sum2.shape[4]
    shards = far3.shape[1:]

    start = pl.multiple_of(core * rows, rows)
    loads = [
        pltpu.make_async_copy(tok_ref.at[pl.ds(start, rows)], x_vm, local.at[0]),
        pltpu.make_async_copy(cond_ref.at[pl.ds(start, rows)], c_vm, local.at[1]),
    ]
    for load in loads:
        load.start()

    swaps = [across_cores(place, far3.at[c], sum3.at[c], sems) for c in range(3)]
    scatters = [
        Scatter(place, "yxy"[c], sum3.at[c], one3.at[c], two3.at[c], hop3.at[c], sems)
        for c in range(3)
    ]
    ada_swaps = [across_cores(place, far2.at[c], sum2.at[c], sems) for c in range(2)]
    adas = [
        Scatter(place, "xy"[c], sum2.at[c], one2.at[c], two2.at[c], hop2.at[c], sems)
        for c in range(2)
    ]
    sends = []

    def copy(src, dst, device):
        index = place["next"]
        place["next"] = index + 1
        entry = pltpu.make_async_remote_copy(
            src_ref=src, dst_ref=dst, send_sem=sems.at[0, index], recv_sem=sems.at[1, index],
            device_id=device, device_id_type=pl.DeviceIdType.MESH,
        )
        sends.append(entry)
        return entry

    row_copies = []
    for i in range(rows // ROW_BLOCK):
        at = pl.ds(i * ROW_BLOCK, ROW_BLOCK)
        row_copies.append(copy(rows_ref.at[0, at], rows_ref.at[1, at], (me, 1 - core)))
    ada_copy = copy(ada_ref.at[core], ada_ref.at[core], (me, 1 - core))
    spot = 4 * core + 2 * y + x
    plane_copies = []
    for other in range(1, 8):
        yy, xx = lax.rem(y + other // 2, 2), lax.rem(x + other, 2)
        cc = lax.rem(core + other // 4, 2)
        plane_copies.append((4 * z + 2 * yy + xx, cc))
    beyond = [(4 * lax.rem(z + hop, outer) + 2 * y + x, core) for hop in range(1, outer)]

    barrier = pltpu.get_barrier_semaphore()
    for device in plane_copies + beyond:
        pl.semaphore_signal(barrier, inc=1, device_id=device, device_id_type=pl.DeviceIdType.MESH)
    pl.semaphore_wait(barrier, len(plane_copies) + len(beyond))
    plane_copies = [copy(plane.at[spot], plane.at[spot], device) for device in plane_copies]
    column_copies = [copy(column.at[z], column.at[z], device) for device in beyond]

    turned[...] = h_ref[...].T
    grad_refs = (dq_ref, dk_ref, dv_ref)
    for c in range(3):
        grad = dot(turned[...], grad_refs[c][...])
        far3[c] = grad[:, own:].reshape(shards).astype(BF)
        swaps[c].start()
        mine[c] = grad[:, :own].reshape(shards)
    for load in loads:
        load.wait()
    for c in range(3):
        swaps[c].wait_recv()
        sum3[c] = (mine[c] + sum3[c].astype(F32)).astype(BF)
        scatters[c].start()

    dwa_vm[...] = jnp.zeros_like(dwa_vm)
    dp_vm[...] = jnp.zeros_like(dp_vm)
    gain = p_ref[0:1, :]

    def spread_of(at):
        scale = dot(silu_low(c_vm[at, :]), wa_ref[width : 2 * width, :], NT) + p_ref[3:4, :]
        return 1.0 + scale

    def first_pass(i, _):
        at = pl.ds(pl.multiple_of(i * ROW_BLOCK, ROW_BLOCK), ROW_BLOCK)
        dh = jnp.zeros((ROW_BLOCK, width), F32)
        for first, w_ref in ((0, near_ref), (own, far_ref)):
            cols = slice(first, first + own)
            for c, grad_ref in enumerate(grad_refs):
                dh = dh + dot(grad_ref[at, cols], w_ref[:, c * own : (c + 1) * own], NT)
        dh_vm[at, :] = dh
        normal, _ = normalize(x_vm[at, :].astype(F32))
        dn = dh * normal
        summed = cond_rows(silu_low(c_vm[at, :]))
        dwa_vm[:, :width] += dot(summed, dh.astype(BF))
        dwa_vm[:, width:] += dot(summed, (dn * gain).astype(BF))
        dp_vm[0:1, :] += jnp.sum(dn * spread_of(at), axis=0, keepdims=True)
        return 0

    lax.fori_loop(0, rows // ROW_BLOCK, first_pass, 0)

    dwt[0 : 2 * width, :] = dwa_vm[:conds, :].T
    dwt[2 * width :, :] = dwa_two_ref[:conds, :].T
    dp_vm[1:2, :] = dp_two_ref[0:1, :]
    for block in range(2):
        dp_vm[2 + block : 3 + block, :] = dwa_vm[
            conds : conds + 1, block * width : (block + 1) * width
        ]
    for block in range(4):
        dp_vm[4 + block : 5 + block, :] = dwa_two_ref[
            conds : conds + 1, block * width : (block + 1) * width
        ]
    lane = lax.broadcasted_iota(jnp.int32, (16, conds), 1)

    def place_ada(side, store):
        for shard in range(count):
            spot = (shard // 4, (shard // 2) % 2, shard % 2)
            base = pl.multiple_of(2 * half_cols * shard + half_cols * side, 16)
            store(0, spot, slice(None), dwt[pl.ds(base, cut), :].astype(BF))
            rest = half_cols - cut
            store(1, spot, slice(0, rest), dwt[pl.ds(base + cut, rest), :].astype(BF))
            gone = dp_vm[...] if shard == 0 else pltpu.roll(dp_vm[...], width - shard * part, 1)
            gone = jnp.where(lane < part, gone[:, :conds], 0.0)
            store(1, spot, slice(rest, cut), gone.astype(BF))

    def store_far(index, spot, at, value):
        far2[(index, *spot, at)] = value

    def add_near(index, spot, at, value):
        total = sum2[(index, *spot, at)].astype(F32) + value.astype(F32)
        sum2[(index, *spot, at)] = total.astype(BF)

    place_ada(1 - core, store_far)
    for entry in ada_swaps:
        entry.start()
    scatters[0].phase_two()
    scatters[1].phase_two()
    for entry in ada_swaps:
        entry.wait_recv()
    place_ada(core, add_near)
    for entry in adas:
        entry.start()
    scatters[2].phase_two()

    def events(i):
        if i == 0:
            scatters[0].phase_hops()
            scatters[1].phase_hops()
        if i == 1:
            scatters[2].phase_hops()
        if i == 2:
            for entry in adas:
                entry.phase_two()
        if i == 3:
            for entry in adas:
                entry.phase_hops()

    def second_pass(i, _):
        at = pl.ds(pl.multiple_of(i * ROW_BLOCK, ROW_BLOCK), ROW_BLOCK)
        normal, rstd = normalize(x_vm[at, :].astype(F32))
        grad = dh_vm[at, :] * gain * spread_of(at)
        rows_ref[0, at, :] = dx_ref[at, :] + norm_backward(grad, normal, rstd)
        for step in range(rows // ROW_BLOCK):

            @pl.when(i == step)
            def _():
                row_copies[step].start()
                if step < 4:
                    events(step)

        return 0

    lax.fori_loop(0, rows // ROW_BLOCK, second_pass, 0)

    squares = jnp.sum((mid_ref[...] / token_total) ** 2)
    for c in range(3):
        total = scatters[c].finish()
        qkv_ref[:, c * own : (c + 1) * own] = total
        squares = squares + jnp.sum((total / token_total) ** 2)
    first, second = adas[0].finish(), adas[1].finish()
    rest = half_cols - cut
    ada_ref[core, 0:cut, :] = first
    ada_ref[core, cut:, :] = second[:rest]
    norm_ref[...] = second[rest : rest + 8]
    ada_copy.start()
    squares = squares + jnp.sum((first / token_total) ** 2)
    squares = squares + jnp.sum((second[:rest] / token_total) ** 2)
    squares = squares + 0.5 * jnp.sum((second[rest:] / token_total) ** 2)
    plane[spot] = jnp.full((8, LANES), squares, F32)
    for entry in plane_copies:
        entry.start()
    for entry in plane_copies:
        entry.wait_recv()
    column[z] = jnp.sum(plane[...], axis=0)
    for entry in column_copies:
        entry.start()
    for entry in column_copies:
        entry.wait_recv()
    square_ref[...] = jnp.sum(column[...], axis=0)
    ada_copy.wait_recv()
    for entry in row_copies:
        entry.wait_recv()
    for entry in swaps + ada_swaps + sends:
        entry.wait_send()
    for entry in scatters + adas:
        entry.drain()


def closing(count, tokens, cond, h_one, grads, dx, wa, norms, near, far, dwa_two, dp_two,
            middle_sum, token_total):
    rows, width = dx.shape
    conds = cond.shape[1]
    part = width // count
    outer = count // 4
    half_cols = wa.shape[0] // count // 2
    cut = (half_cols + 16) // 2
    vm = pl.BlockSpec(memory_space=pltpu.VMEM)
    hbm = pl.BlockSpec(memory_space=pl.ANY)
    copies = 5 + 5 * (2 + outer - 1) + rows // ROW_BLOCK + 1 + 7 + outer - 1
    return pl.pallas_call(
        functools.partial(closing_kernel, count=count, token_total=token_total),
        in_specs=[hbm, hbm] + [vm] * 12,
        out_specs=[vm] * 5,
        out_shape=[
            shape_of((2, rows, width), F32),
            shape_of((part, 3 * width // 2), F32),
            shape_of((2, half_cols, conds), F32),
            shape_of((8, conds), F32),
            shape_of((8, LANES), F32),
        ],
        scratch_shapes=[
            pltpu.VMEM((rows, width), BF),
            pltpu.VMEM((rows, conds), BF),
            pltpu.VMEM((width, rows), BF),
            pltpu.VMEM((3, outer, 2, 2, part, width // 2), F32),
            pltpu.VMEM((rows, width), F32),
            pltpu.VMEM((conds + 16, 2 * width), F32),
            pltpu.VMEM((16, width), F32),
            pltpu.VMEM((wa.shape[0], conds), F32),
            pltpu.VMEM((8, 8, LANES), F32),
            pltpu.VMEM((outer, 8, LANES), F32),
        ]
        + scatter_buffers(outer, 3, part, width // 2)
        + scatter_buffers(outer, 2, cut, conds)
        + [pltpu.SemaphoreType.DMA((2,)), pltpu.SemaphoreType.DMA((2, copies))],
        compiler_params=pltpu.CompilerParams(
            vmem_limit_bytes=VMEM_LIMIT, collective_id=2, has_side_effects=True
        ),
        name="closing",
    )(tokens, cond, h_one, *grads, dx, wa, norms, near, far, dwa_two, dp_two, middle_sum)


def factors(count):
    return (count // 4, 2, 2)


def swap_mp(value):
    return lax.ppermute(value, "mp", [(0, 1), (1, 0)])


def swap_dp(value, distance):
    count = lax.axis_size("dp")
    return lax.ppermute(value, "dp", [(i, i ^ distance) for i in range(count)])


def turn_dp(value, distance):
    count = lax.axis_size("dp")
    return lax.ppermute(value, "dp", [(i, (i + distance) % count) for i in range(count)])


def pick(value, index, axis):
    return lax.dynamic_index_in_dim(value, index, axis, keepdims=False)


def scatter_sum(parts, order):
    count = lax.axis_size("dp")
    outer, mid, inner = factors(count)
    me = lax.axis_index("dp")
    place = {4: me // 4, 2: (me // 2) % 2, 1: me % 2}

    def widen(part):
        return part.reshape((outer, mid, inner) + part.shape[1:]).astype(F32)

    total = widen(parts[0])
    for part in parts[1:]:
        total = total + widen(part)
    for distance in order:
        axis = 1 if (distance == 2 or total.ndim == 4) else 2
        gone = pick(total, 1 - place[distance], axis).astype(BF)
        total = pick(total, place[distance], axis) + swap_dp(gone, distance).astype(F32)
    arrived = [
        turn_dp(pick(total, (place[4] + hop) % outer, 0).astype(BF), 4 * hop)
        for hop in range(1, outer)
    ]
    total = pick(total, place[4], 0)
    for piece in arrived:
        total = total + piece.astype(F32)
    return total


def scatter_halves(near, far_sum):
    count = lax.axis_size("dp")
    width, columns = near.shape
    cut = columns // 2 // LANES * LANES
    shards = lambda value: value.reshape(count, width // count, value.shape[1])
    first = scatter_sum([shards(near[:, :cut]), shards(far_sum[:, :cut])], (2, 1))
    second = scatter_sum([shards(near[:, cut:]), shards(far_sum[:, cut:])], (1, 2))
    return jnp.concatenate([first, second], axis=1)


def sum_everywhere(value):
    value = value + swap_mp(value)
    distance = 1
    while distance < lax.axis_size("dp"):
        value = value + swap_dp(value, distance)
        distance *= 2
    return value


def in_order(half, near, far):
    first = jnp.where(half == 0, near, far)
    second = jnp.where(half == 0, far, near)
    return jnp.concatenate([first, second], axis=0)


def per_device(
    tokens, cond, segments, out_grad, step,
    ada_weight, ada_first, ada_second,
    norm_params, norm_first, norm_second,
    qkv_weight, qkv_first, qkv_second,
    out_weight, out_first, out_second,
    up_weight, up_first, up_second,
    down_weight, down_first, down_second,
):
    count = lax.axis_size("dp")
    width = tokens.shape[1]
    rows = tokens.shape[0] // 2
    conds = cond.shape[1]
    part = width // count
    half = lax.axis_index("mp")
    half_ref = half.reshape(1).astype(jnp.int32)
    token_total = float(tokens.shape[0] * count)

    ada_shard = ada_weight.T.astype(BF).reshape(2, -1, cond.shape[1])
    small_shard = jnp.concatenate(
        [
            qkv_weight.astype(BF).transpose(1, 0, 2).reshape(part, -1),
            jnp.pad(norm_params.astype(BF).T, ((0, 0), (0, LANES - 8))),
        ],
        axis=1,
    )
    wide_shard = jnp.concatenate(
        [up_weight.astype(BF), down_weight.astype(BF).T, out_weight.astype(BF).T], axis=1
    )
    segment = pick(segments, half, 0)
    features = document_features(segment)
    tables = rope_tables(rows)
    fused = part % 16 == 0 and ada_shard.shape[1] % 16 == 0
    if fused:
        (h_one, queries, keys, values, mixed, lse, near, far, wa, norms, wide_near,
         wide_far) = opening(
            count, tokens, cond, small_shard, pick(ada_shard, half, 0)[None], wide_shard, tables,
            features,
        )
        wa = wa.reshape(-1, conds)
    else:
        wa = lax.all_gather(ada_shard.reshape(-1, conds), "dp", axis=0, tiled=True)
        near = lax.all_gather(small_shard, "dp", axis=0, tiled=True)
        far = swap_mp(near)
        norms = near[:, -LANES:].T[:8].astype(F32)
        wide_near = lax.all_gather(wide_shard, "dp", axis=0, tiled=True)
        wide_far = swap_mp(wide_near)
        h_one, queries, keys, values = first_stage(
            half_ref, tokens, cond, wa, norms, near, far, tables
        )
        mixed, lse = attend(queries, keys, values, segment, features)
    result, dx, upstream, z, gy, h_two, du, ga, dwa_two, dp_two = middle_stage(
        half_ref, tokens, out_grad, cond, mixed, wa, norms, wide_near, wide_far
    )
    result_far = swap_mp(result)

    block = width // 2
    if fused:
        *grads, middle_sum = spread(
            count, h_two, gy, ga, du, z, mixed, queries, keys, values, upstream, lse, features,
            tables,
        )
    else:
        steps = du.shape[1] // 2 // block

        def middle_grads(which, name):
            return weight_grads(
                [gy, h_two, ga], [du, z, mixed],
                [(steps, 1, 0, which * steps), (steps, 0, 1, which * steps), (1, 2, 2, which)],
                block, name,
            )

        middle_far = swap_mp(middle_grads(1, "middle_grads_far"))
        middle_near = middle_grads(0, "middle_grads_near")
        middle_sum = scatter_halves(middle_near, middle_far)
        grads = attend_back(
            queries, keys, values, upstream, mixed, lse, segment, features, tables
        )

    if fused:
        input_rows, first_sum, ada_halves, norm_sum, squares = closing(
            count, tokens, cond, h_one, grads, dx, wa, norms, near, far, dwa_two, dp_two,
            middle_sum, token_total,
        )
        input_grad, input_far = input_rows[0], input_rows[1]
        norm_sum = norm_sum[:, :part]
        ada_rows = ada_halves.reshape(-1, conds)
        total_sq = squares[0, 0]
    else:
        def first_grads(which, name):
            return weight_grads(
                [h_one], list(grads), [(1, 0, index, which) for index in range(3)], block, name
            )

        first_far = swap_mp(first_grads(1, "first_grads_far"))
        first_near = first_grads(0, "first_grads_near")
        first_sum = scatter_halves(first_near, first_far)

        input_grad, dwa_one, dp_one = last_stage(
            half_ref, tokens, cond, dx, grads, wa, norms, near, far
        )
        input_far = swap_mp(input_grad)

        dwa = jnp.concatenate([dwa_one, dwa_two], axis=1)
        ada_cols = dwa.shape[1] // count
        dwa_rows = dwa[:conds].T.astype(BF).reshape(count, 2, ada_cols // 2, conds)
        norm_rows = jnp.concatenate(
            [dp_one[0:1], dp_two[0:1], dwa[conds].reshape(6, width)], axis=0
        ).astype(BF)
        norm_rows = norm_rows.reshape(8, count, part).transpose(1, 0, 2)
        norm_rows = jnp.pad(norm_rows, ((0, 0), (0, 0), (0, conds - part)))
        ada_near = jnp.concatenate([pick(dwa_rows, half, 1), norm_rows], axis=1)
        ada_far = swap_mp(jnp.concatenate([pick(dwa_rows, 1 - half, 1), norm_rows], axis=1))
        ada_sum = scatter_sum([ada_near, ada_far], (2, 1))
        ada_half, norm_sum = ada_sum[: ada_cols // 2], ada_sum[ada_cols // 2 :, :part]
        ada_rows = in_order(half, ada_half, swap_mp(ada_half))

    wide_cols = du.shape[1] // 2
    up_mean = middle_sum[:, :wide_cols] / token_total
    down_mean = middle_sum[:, wide_cols : 2 * wide_cols] / token_total
    out_mean = middle_sum[:, 2 * wide_cols :] / token_total
    qkv_mean = first_sum / token_total
    ada_mean = ada_rows / token_total
    norm_mean = norm_sum / token_total
    if not fused:
        local_sq = (
            jnp.sum(qkv_mean * qkv_mean)
            + jnp.sum(out_mean * out_mean)
            + jnp.sum(up_mean * up_mean)
            + jnp.sum(down_mean * down_mean)
            + 0.5 * (jnp.sum(ada_mean * ada_mean) + jnp.sum(norm_mean * norm_mean))
        )
        total_sq = sum_everywhere(jnp.full((8, LANES), local_sq, F32))[0, 0]
    grad_norm = jnp.sqrt(total_sq)
    clip_factor = jnp.minimum(1.0, clip_limit / (grad_norm + 1e-06))
    step_count = step[0].astype(F32)
    fix_one = 1.0 - jnp.exp(step_count * math.log(0.9))
    fix_two = 1.0 - jnp.exp(step_count * math.log(0.999))

    ada_grad = ada_mean.T
    qkv_grad = qkv_mean.reshape(part, 3, -1).transpose(1, 0, 2)
    state = (
        (ada_weight, ada_first, ada_second, ada_grad),
        (norm_params, norm_first, norm_second, norm_mean),
        (qkv_weight, qkv_first, qkv_second, qkv_grad),
        (out_weight, out_first, out_second, out_mean.T),
        (up_weight, up_first, up_second, up_mean),
        (down_weight, down_first, down_second, down_mean.T),
    )
    outputs = [
        in_order(half, result, result_far),
        in_order(half, input_grad, input_far),
        grad_norm.reshape(1),
    ]
    for index, entry in enumerate(state):
        outputs += adam_update(
            *entry, clip_factor, fix_one, fix_two, step_rates[index], decay_rates[index]
        )
    return tuple(outputs)


def solution(mesh):
    column = (P(None, "dp"),) * 3
    weights = (
        column
        + column
        + (P(None, "dp", "mp"),) * 3
        + (P("mp", "dp"),) * 3
        + (P("dp", "mp"),) * 3
        + (P("mp", "dp"),) * 3
    )
    row = P("dp", None)
    return jax.shard_map(
        per_device,
        mesh=mesh,
        in_specs=(row, row, row, row, P()) + weights,
        out_specs=(row, row, P()) + weights,
        check_vma=False,
    )
```

```python
import functools
import math

import jax
import jax.numpy as jnp
import numpy as np
from jax import lax
from jax.experimental import pallas as pl
from jax.experimental.pallas import tpu as pltpu
from jax.sharding import PartitionSpec as P

HEAD_DIM = 64
LANES = 128
MASKED = -1e30
ROW_BLOCK = 256
VMEM_LIMIT = 64_000_000
clip_limit = 1.0
step_rates = (0.075, 0.75, 0.075, 0.25, 0.075, 0.075)
decay_rates = (0.01, 0.0, 0.01, 0.01, 0.01, 0.01)

F32 = jnp.float32
BF = jnp.bfloat16
NN = (((1,), (0,)), ((), ()))
NT = (((1,), (1,)), ((), ()))


def dot(left, right, dims=NN):
    return lax.dot_general(left, right, dims, preferred_element_type=F32)


def shape_of(shape, dtype):
    return jax.ShapeDtypeStruct(shape, dtype)


def resident(shape, index):
    return pl.BlockSpec(shape, lambda *_: index, pipeline_mode=pl.Buffered(1))


def params():
    return pltpu.CompilerParams(vmem_limit_bytes=VMEM_LIMIT)


def adam_update(weight, first, second, grad, clip_factor, fix_one, fix_two, rate, decay):
    clipped = grad * clip_factor
    first_new = 0.9 * first + 0.1 * clipped
    second_new = 0.999 * second + 0.001 * clipped * clipped
    update = first_new / fix_one / (jnp.sqrt(second_new / fix_two) + 1e-08) + decay * weight
    return (weight - rate * update, first_new, second_new)


def rope_tables(length):
    half = HEAD_DIM // 2
    inverse = jnp.exp(jnp.arange(half, dtype=F32) * (-2.0 * math.log(10000.0) / HEAD_DIM))
    angles = jnp.arange(length, dtype=F32)[:, None] * inverse[None, :]
    cosines, sines = jnp.cos(angles), jnp.sin(angles)
    return (
        jnp.concatenate([cosines] * 4, axis=1),
        jnp.concatenate([-sines, sines, -sines, sines], axis=1),
    )


def rope_constants(length):
    half = HEAD_DIM // 2
    inverse = np.exp(np.arange(half, dtype=np.float32) * np.float32(-2.0 * math.log(10000.0) / HEAD_DIM))
    angles = np.arange(length, dtype=np.float32)[:, None] * inverse[None, :].astype(np.float32)
    return jnp.asarray(np.concatenate([np.cos(angles), np.sin(angles)], axis=1), F32)


def swap_halves(values):
    width = values.shape[1]
    lane = lax.broadcasted_iota(jnp.int32, values.shape, 1)
    ahead = pltpu.roll(values, width - HEAD_DIM // 2, 1)
    behind = pltpu.roll(values, HEAD_DIM // 2, 1)
    return jnp.where(lane % HEAD_DIM < HEAD_DIM // 2, ahead, behind)


def silu_low(cond):
    value = cond.astype(F32)
    return (value / (1.0 + jnp.exp(-value))).astype(BF)


def normalize(rows):
    centre = rows - jnp.mean(rows, axis=-1, keepdims=True)
    scale = lax.rsqrt(jnp.mean(centre * centre, axis=-1, keepdims=True) + 1e-05)
    return centre * scale, scale


def norm_backward(grad, normal, scale):
    return scale * (
        grad
        - jnp.mean(grad, axis=-1, keepdims=True)
        - normal * jnp.mean(grad * normal, axis=-1, keepdims=True)
    )


def cond_rows(cond):
    return jnp.concatenate([cond.T, jnp.ones((16, cond.shape[0]), BF)], axis=0)


def first_kernel(half, x_ref, c_ref, wa_ref, p_ref, wqa_ref, wqb_ref, cos_ref, sin_ref,
                 h_ref, q_ref, k_ref, v_ref):
    width = x_ref.shape[1]
    own = width // 2
    cond = silu_low(c_ref[...])
    mod = dot(cond, wa_ref[0 : 2 * width, :], NT)
    shift = mod[:, :width] + p_ref[2:3, :]
    scale = mod[:, width:] + p_ref[3:4, :]
    normal, _ = normalize(x_ref[...].astype(F32))
    h = (normal * p_ref[0:1, :] * (1.0 + scale) + shift).astype(BF)
    h_ref[...] = h
    cos = jnp.concatenate([cos_ref[...]] * (own // LANES), axis=1)
    sin = jnp.concatenate([sin_ref[...]] * (own // LANES), axis=1)
    for start, w_ref in ((0, wqa_ref), (own, wqb_ref)):
        cols = slice(start, start + own)
        query = dot(h, w_ref[:, 0:own])
        query = query * cos + swap_halves(query) * sin
        q_ref[:, cols] = (query * HEAD_DIM**-0.5).astype(BF)
        key = dot(h, w_ref[:, own : 2 * own])
        k_ref[:, cols] = (key * cos + swap_halves(key) * sin).astype(BF)
        v_ref[:, cols] = dot(h, w_ref[:, 2 * own :]).astype(BF)


def first_stage(half, tokens, cond, wa, norms, near, far, tables):
    width = tokens.shape[1]
    rows = tables[0].shape[0]
    blocks = rows // ROW_BLOCK
    mine = lambda i, half: (half[0] * blocks + i, 0)
    plain = lambda i, half: (i, 0)
    row = pl.BlockSpec((ROW_BLOCK, width), plain)
    return pl.pallas_call(
        first_kernel,
        grid_spec=pltpu.PrefetchScalarGridSpec(
            num_scalar_prefetch=1,
            grid=(blocks,),
            in_specs=[
                pl.BlockSpec((ROW_BLOCK, width), mine),
                pl.BlockSpec((ROW_BLOCK, cond.shape[1]), mine),
                resident(wa.shape, (0, 0)),
                resident(norms.shape, (0, 0)),
                resident((width, 3 * width // 2), (0, 0)),
                resident((width, 3 * width // 2), (0, 0)),
                pl.BlockSpec((ROW_BLOCK, LANES), plain),
                pl.BlockSpec((ROW_BLOCK, LANES), plain),
            ],
            out_specs=[row] * 4,
        ),
        out_shape=[shape_of((rows, width), BF)] * 4,
        compiler_params=params(),
        name="first_stage",
    )(half, tokens, cond, wa, norms, near, far, *tables)


def split_heads(pair, other):
    low = lax.broadcasted_iota(jnp.int32, pair.shape, 1) < HEAD_DIM
    return jnp.where(low, pair, other), jnp.where(low, other, pair)


def attend_kernel(lo_ref, hi_ref, q_ref, k_ref, v_ref, fq_ref, fk_ref, o_ref, lse_ref,
                  qz, kz, vt, *, bq, bk):
    length = q_ref.shape[0]
    qz[0], qz[1] = split_heads(q_ref[...], fq_ref[...])
    kz[0], kz[1] = split_heads(k_ref[...], fk_ref[...])
    vt[...] = v_ref[...].T

    def query_block(i, _):
        off = pl.multiple_of(i * bq, bq)
        queries = [qz[h, pl.ds(off, bq), :] for h in range(2)]

        def key_block(j, carry):
            koff = pl.multiple_of(j * bk, bk)
            scores = [dot(kz[h, pl.ds(koff, bk), :], queries[h], NT) for h in range(2)]
            out = []
            for h in range(2):
                top, total, mixed = carry[3 * h : 3 * h + 3]
                new_top = jnp.maximum(top, jnp.max(scores[h], axis=0, keepdims=True))
                weights = jnp.exp(scores[h] - new_top)
                fade = jnp.exp(top - new_top)
                total = total * fade + jnp.sum(weights, axis=0, keepdims=True)
                values = vt[HEAD_DIM * h : HEAD_DIM * (h + 1), pl.ds(koff, bk)]
                mixed = mixed * fade + dot(values, weights.astype(BF))
                out += [new_top, total, mixed]
            return tuple(out)

        start = (
            jnp.full((1, bq), -3e38, F32),
            jnp.zeros((1, bq), F32),
            jnp.zeros((HEAD_DIM, bq), F32),
        )
        done = lax.fori_loop(lo_ref[i], hi_ref[i], key_block, start * 2)
        mixed = jnp.concatenate([done[2] / done[1], done[5] / done[4]], axis=0)
        o_ref[pl.ds(off, bq), :] = mixed.T.astype(BF)
        lse_ref[0, 0:1, pl.ds(off, bq)] = done[0] + jnp.log(done[1])
        lse_ref[0, 1:2, pl.ds(off, bq)] = done[3] + jnp.log(done[4])
        return 0

    lax.fori_loop(0, length // bq, query_block, 0)


def block_ranges(segment, block, other):
    first, last = segment[::block], segment[block - 1 :: block]
    low = jnp.sum(segment[None, :] < first[:, None], axis=1)
    high = jnp.sum(segment[None, :] <= last[:, None], axis=1)
    return (low // other).astype(jnp.int32), ((high + other - 1) // other).astype(jnp.int32)


def document_features(segment):
    lane = lax.broadcasted_iota(jnp.int32, (segment.shape[0], LANES), 1) % HEAD_DIM
    same = lane == segment[:, None]
    query = jnp.where(same, 1.0, 0.0).astype(BF)
    key = jnp.where((lane < 4) & ~same, MASKED, 0.0).astype(BF)
    return query, key


def attend(queries, keys, values, segment, features, bq=1024, bk=512):
    length, width = queries.shape
    bq, bk = min(bq, length), min(bk, length)
    pairs = width // LANES
    low, high = block_ranges(segment, bq, bk)
    pair = pl.BlockSpec((length, LANES), lambda p, *_: (0, p))
    fixed = pl.BlockSpec((length, LANES), lambda p, *_: (0, 0))
    scratch = pltpu.VMEM((2, length, LANES), BF)
    return pl.pallas_call(
        functools.partial(attend_kernel, bq=bq, bk=bk),
        grid_spec=pltpu.PrefetchScalarGridSpec(
            num_scalar_prefetch=2,
            grid=(pairs,),
            in_specs=[pair, pair, pair, fixed, fixed],
            out_specs=[pair, pl.BlockSpec((1, 2, length), lambda p, *_: (p, 0, 0))],
            scratch_shapes=[scratch, scratch, pltpu.VMEM((LANES, length), BF)],
        ),
        out_shape=[shape_of((length, width), BF), shape_of((pairs, 2, length), F32)],
        compiler_params=params(),
        name="attend",
    )(low, high, queries, keys, values, *features)


def attend_back_kernel(lo_ref, hi_ref, q_ref, k_ref, v_ref, do_ref, o_ref, lse_ref, fq_ref,
                       fk_ref, cos_ref, sin_ref, dq_ref, dk_ref, dv_ref,
                       qz, kz, qm, dm, vm, kt, delta, dqt, *, bq, bk):
    length = q_ref.shape[0]
    zero = jnp.zeros((length, LANES), BF)
    qz[0], qz[1] = split_heads(q_ref[...], fq_ref[...])
    kz[0], kz[1] = split_heads(k_ref[...], fk_ref[...])
    qm[0], qm[1] = split_heads(q_ref[...], zero)
    dm[0], dm[1] = split_heads(do_ref[...], zero)
    vm[0], vm[1] = split_heads(v_ref[...], zero)
    kt[...] = k_ref[...].T
    product = (do_ref[...].astype(F32) * o_ref[...].astype(F32)).T
    delta[0:1, :] = jnp.sum(product[:HEAD_DIM], axis=0, keepdims=True)
    delta[1:2, :] = jnp.sum(product[HEAD_DIM:], axis=0, keepdims=True)
    dqt[...] = jnp.zeros_like(dqt)

    def unrotate(grad, off, rows):
        cos, sin = cos_ref[pl.ds(off, rows), :], sin_ref[pl.ds(off, rows), :]
        return (grad * cos - swap_halves(grad) * sin).astype(BF)

    def key_block(j, _):
        koff = pl.multiple_of(j * bk, bk)
        keys = [kz[h, pl.ds(koff, bk), :] for h in range(2)]
        values = [vm[h, pl.ds(koff, bk), :] for h in range(2)]

        def query_block(i, carry):
            dk, dv = carry
            off = pl.multiple_of(i * bq, bq)
            scores = [dot(keys[h], qz[h, pl.ds(off, bq), :], NT) for h in range(2)]
            grads = [dot(values[h], dm[h, pl.ds(off, bq), :], NT) for h in range(2)]
            for h in range(2):
                weights = jnp.exp(scores[h] - lse_ref[0, h : h + 1, pl.ds(off, bq)])
                dv = dv + dot(weights.astype(BF), dm[h, pl.ds(off, bq), :])
                ds = (weights * (grads[h] - delta[h : h + 1, pl.ds(off, bq)])).astype(BF)
                dk = dk + dot(ds, qm[h, pl.ds(off, bq), :])
                head = slice(HEAD_DIM * h, HEAD_DIM * (h + 1))
                dqt[head, pl.ds(off, bq)] += dot(kt[head, pl.ds(koff, bk)], ds)
            return dk, dv

        zeros = jnp.zeros((bk, LANES), F32)
        dk, dv = lax.fori_loop(lo_ref[j], hi_ref[j], query_block, (zeros, zeros))
        dk_ref[pl.ds(koff, bk), :] = unrotate(dk, koff, bk)
        dv_ref[pl.ds(koff, bk), :] = dv.astype(BF)
        return 0

    lax.fori_loop(0, length // bk, key_block, 0)
    dq_ref[...] = unrotate(dqt[...].T * HEAD_DIM**-0.5, 0, length)


def attend_back(queries, keys, values, upstream, mixed, lse, segment, features, tables,
                bq=512, bk=256):
    length, width = queries.shape
    bq, bk = min(bq, length), min(bk, length)
    pairs = width // LANES
    low, high = block_ranges(segment, bk, bq)
    pair = pl.BlockSpec((length, LANES), lambda p, *_: (0, p))
    fixed = pl.BlockSpec((length, LANES), lambda p, *_: (0, 0))
    scratch = pltpu.VMEM((2, length, LANES), BF)
    return pl.pallas_call(
        functools.partial(attend_back_kernel, bq=bq, bk=bk),
        grid_spec=pltpu.PrefetchScalarGridSpec(
            num_scalar_prefetch=2,
            grid=(pairs,),
            in_specs=[pair] * 5
            + [pl.BlockSpec((1, 2, length), lambda p, *_: (p, 0, 0))]
            + [fixed] * 4,
            out_specs=[pair] * 3,
            scratch_shapes=[scratch] * 5
            + [
                pltpu.VMEM((LANES, length), BF),
                pltpu.VMEM((8, length), F32),
                pltpu.VMEM((LANES, length), F32),
            ],
        ),
        out_shape=[shape_of((length, width), BF)] * 3,
        compiler_params=params(),
        name="attend_back",
    )(low, high, queries, keys, values, upstream, mixed, lse, *features, *tables)


def middle_kernel(half, x_ref, g_ref, c_ref, o_ref, wa_ref, p_ref, woa_ref, wob_ref, w1a_ref,
                  w1b_ref, w2a_ref, w2b_ref,
                  res_ref, dx_ref, do_ref, z_ref, gy_ref, h_ref, du_ref, ga_ref, dwa_ref,
                  dp_ref, slope, *, chunk):
    width = x_ref.shape[1]
    own = width // 2
    hidden = w1a_ref.shape[1]
    cond = silu_low(c_ref[...])

    def modulation(block):
        rows = wa_ref[block * width : (block + 1) * width, :]
        return dot(cond, rows, NT) + p_ref[block + 2 : block + 3, :]

    gate_one, shift, scale, gate_two = (modulation(block) for block in (2, 3, 4, 5))
    branch = dot(o_ref[:, :own], woa_ref[...], NT) + dot(o_ref[:, own:], wob_ref[...], NT)
    middle = x_ref[...].astype(F32) + gate_one * branch
    normal, rstd = normalize(middle)
    gain = p_ref[1:2, :]
    spread = 1.0 + scale
    h = (normal * gain * spread + shift).astype(BF)
    h_ref[...] = h

    out = jnp.zeros_like(middle)
    for start, up_ref, down_ref in ((0, w1a_ref, w2a_ref), (hidden, w1b_ref, w2b_ref)):
        for at in range(0, hidden, chunk):
            u = dot(h, up_ref[:, at : at + chunk])
            square = u * u
            flat = jnp.tanh(math.sqrt(2.0 / math.pi) * u * (1.0 + 0.044715 * square))
            half_up = 0.5 * (1.0 + flat)
            z = (u * half_up).astype(BF)
            z_ref[:, start + at : start + at + chunk] = z
            slope[:, start + at : start + at + chunk] = half_up + 0.5 * u * (
                1.0 - flat * flat
            ) * (math.sqrt(2.0 / math.pi) * (1.0 + 3.0 * 0.044715 * square))
            out = out + dot(z, down_ref[:, at : at + chunk], NT)

    g = g_ref[...].astype(F32)
    res_ref[...] = (middle + gate_two * out).astype(BF)
    gy = (gate_two * g).astype(BF)
    gy_ref[...] = gy
    dgate_two = (g * out).astype(BF)

    dh = jnp.zeros_like(middle)
    for start, up_ref, down_ref in ((0, w1a_ref, w2a_ref), (hidden, w1b_ref, w2b_ref)):
        for at in range(0, hidden, chunk):
            dz = dot(gy, down_ref[:, at : at + chunk])
            du = (dz * slope[:, start + at : start + at + chunk]).astype(BF)
            du_ref[:, start + at : start + at + chunk] = du
            dh = dh + dot(du, up_ref[:, at : at + chunk], NT)

    dn = dh * normal
    dx = g + norm_backward(dh * gain * spread, normal, rstd)
    dx_ref[...] = dx
    ga = (gate_one * dx).astype(BF)
    ga_ref[...] = ga
    do_ref[:, :own] = dot(ga, woa_ref[...]).astype(BF)
    do_ref[:, own:] = dot(ga, wob_ref[...]).astype(BF)

    @pl.when(pl.program_id(0) == 0)
    def _():
        dwa_ref[...] = jnp.zeros_like(dwa_ref)
        dp_ref[...] = jnp.zeros_like(dp_ref)

    rows = cond_rows(cond)
    grads = ((dx * branch).astype(BF), dh.astype(BF), (dn * gain).astype(BF), dgate_two)
    for block, grad in enumerate(grads):
        dwa_ref[:, block * width : (block + 1) * width] += dot(rows, grad)
    dp_ref[0:1, :] += jnp.sum(dn * spread, axis=0, keepdims=True)


def middle_stage(half, tokens, out_grad, cond, mixed, wa, norms, up_near, up_far, down_near,
                 down_far):
    width = tokens.shape[1]
    rows = mixed.shape[0]
    hidden = up_near.shape[1]
    blocks = rows // ROW_BLOCK
    mine = lambda i, half: (half[0] * blocks + i, 0)
    plain = lambda i, half: (i, 0)
    row = pl.BlockSpec((ROW_BLOCK, width), plain)
    wide = pl.BlockSpec((ROW_BLOCK, 2 * hidden), plain)
    narrow = shape_of((rows, width), BF)
    broad = shape_of((rows, 2 * hidden), BF)
    total = (cond.shape[1] + 16, 4 * width)
    return pl.pallas_call(
        functools.partial(middle_kernel, chunk=768),
        grid_spec=pltpu.PrefetchScalarGridSpec(
            num_scalar_prefetch=1,
            grid=(blocks,),
            in_specs=[
                pl.BlockSpec((ROW_BLOCK, width), mine),
                pl.BlockSpec((ROW_BLOCK, width), mine),
                pl.BlockSpec((ROW_BLOCK, cond.shape[1]), mine),
                row,
                resident(wa.shape, (0, 0)),
                resident(norms.shape, (0, 0)),
                resident((width, width // 2), (0, 2 * hidden // width)),
                resident((width, width // 2), (0, 2 * hidden // width)),
                resident((width, hidden), (0, 0)),
                resident((width, hidden), (0, 0)),
                resident((width, hidden), (0, 0)),
                resident((width, hidden), (0, 0)),
            ],
            out_specs=[row, row, row, wide, row, row, wide, row,
                       pl.BlockSpec(total, lambda i, half: (0, 0)),
                       pl.BlockSpec((8, width), lambda i, half: (0, 0))],
            scratch_shapes=[pltpu.VMEM((ROW_BLOCK, 2 * hidden), F32)],
        ),
        out_shape=[narrow, shape_of((rows, width), F32), narrow, broad, narrow, narrow, broad,
                   narrow, shape_of(total, F32), shape_of((8, width), F32)],
        compiler_params=params(),
        name="middle_stage",
    )(half, tokens, out_grad, cond, mixed, wa, norms, down_near, down_far, up_near, up_far,
      down_near, down_far)


def last_kernel(half, x_ref, c_ref, dx_ref, dq_ref, dk_ref, dv_ref, wa_ref, p_ref, wqa_ref,
                wqb_ref, out_ref, dwa_ref, dp_ref):
    width = x_ref.shape[1]
    own = width // 2
    cond = silu_low(c_ref[...])
    scale = dot(cond, wa_ref[width : 2 * width, :], NT) + p_ref[3:4, :]
    dh = jnp.zeros(x_ref.shape, F32)
    for start, w_ref in ((0, wqa_ref), (own, wqb_ref)):
        cols = slice(start, start + own)
        for index, grad_ref in enumerate((dq_ref, dk_ref, dv_ref)):
            dh = dh + dot(grad_ref[:, cols], w_ref[:, index * own : (index + 1) * own], NT)
    normal, rstd = normalize(x_ref[...].astype(F32))
    gain = p_ref[0:1, :]
    spread = 1.0 + scale
    dn = dh * normal
    out_ref[...] = dx_ref[...] + norm_backward(dh * gain * spread, normal, rstd)

    @pl.when(pl.program_id(0) == 0)
    def _():
        dwa_ref[...] = jnp.zeros_like(dwa_ref)
        dp_ref[...] = jnp.zeros_like(dp_ref)

    rows = cond_rows(cond)
    dwa_ref[:, :width] += dot(rows, dh.astype(BF))
    dwa_ref[:, width:] += dot(rows, (dn * gain).astype(BF))
    dp_ref[0:1, :] += jnp.sum(dn * spread, axis=0, keepdims=True)


def last_stage(half, tokens, cond, dx, grads, wa, norms, near, far):
    width = tokens.shape[1]
    rows = dx.shape[0]
    blocks = rows // ROW_BLOCK
    mine = lambda i, half: (half[0] * blocks + i, 0)
    row = pl.BlockSpec((ROW_BLOCK, width), lambda i, half: (i, 0))
    total = (cond.shape[1] + 16, 2 * width)
    return pl.pallas_call(
        last_kernel,
        grid_spec=pltpu.PrefetchScalarGridSpec(
            num_scalar_prefetch=1,
            grid=(blocks,),
            in_specs=[
                pl.BlockSpec((ROW_BLOCK, width), mine),
                pl.BlockSpec((ROW_BLOCK, cond.shape[1]), mine),
                row, row, row, row,
                resident(wa.shape, (0, 0)),
                resident(norms.shape, (0, 0)),
                resident((width, 3 * width // 2), (0, 0)),
                resident((width, 3 * width // 2), (0, 0)),
            ],
            out_specs=[row, pl.BlockSpec(total, lambda i, half: (0, 0)),
                       pl.BlockSpec((8, width), lambda i, half: (0, 0))],
        ),
        out_shape=[shape_of((rows, width), F32), shape_of(total, F32), shape_of((8, width), F32)],
        compiler_params=params(),
        name="last_stage",
    )(half, tokens, cond, dx, *grads, wa, norms, near, far)


def weight_grad_kernel(*refs, plan):
    lefts, rights = plan["lefts"], plan["rights"]
    left_refs, right_refs = refs[:lefts], refs[lefts : lefts + rights]
    out_ref, turned = refs[lefts + rights :]
    step = pl.program_id(0)
    for begin, end, left, right in plan["spans"]:

        @pl.when(step == begin)
        def _():
            turned[...] = left_refs[left][...].T

        @pl.when((step >= begin) & (step < end))
        def _():
            out_ref[...] = dot(turned[...], right_refs[right][...]).astype(BF)


def weight_grads(lefts, rights, spans, block, name):
    rows, width = lefts[0].shape
    begin, plan, maps = 0, [], []
    for steps, left, right, first in spans:
        plan.append((begin, begin + steps, left, right))
        maps.append((begin, steps, first))
        begin += steps

    def column_map(begin, steps, first):
        return lambda i: (0, first + jnp.clip(i - begin, 0, steps - 1))

    return pl.pallas_call(
        functools.partial(
            weight_grad_kernel,
            plan={"lefts": len(lefts), "rights": len(rights), "spans": plan},
        ),
        grid=(begin,),
        in_specs=[resident((rows, width), (0, 0))] * len(lefts)
        + [pl.BlockSpec((rows, block), column_map(*entry)) for entry in maps],
        out_specs=pl.BlockSpec((width, block), lambda i: (0, i)),
        out_shape=shape_of((width, begin * block), BF),
        scratch_shapes=[pltpu.VMEM((width, rows), BF)],
        compiler_params=params(),
        name=name,
    )(*lefts, *rights)


class Gather:
    def __init__(self, shard, near, far, cut, sems, place):
        outer, x, y, z, core = (place[name] for name in ("outer", "x", "y", "z", "core"))
        columns = near.shape[-1]
        flat = len(near.shape) == 2
        rows = near.shape[0] // (4 * outer)

        def slots(ref, first, number, cols):
            if flat:
                at = pl.multiple_of(first * rows, 16)
                return ref.at[pl.ds(at, number * rows), cols]
            return ref.at[pl.ds(first, number), core, :, cols]

        self.count = 0

        def copy(src, dst, device):
            index = self.count
            self.count += 1
            return pltpu.make_async_remote_copy(
                src_ref=src,
                dst_ref=dst,
                send_sem=sems.at[0, index],
                recv_sem=sems.at[1, index],
                device_id=device,
                device_id_type=pl.DeviceIdType.MESH,
            )

        here = 2 * y + x
        across_x = (4 * z + 2 * y + 1 - x, core)
        across_y = (4 * z + 2 * (1 - y) + x, core)
        other_core = (4 * z + here, 1 - core)
        whole = slice(None)
        self.outer = outer
        own = slots(near, 4 * z + here, 1, whole)
        self.local = (shard, own)
        self.hops = [
            [copy(shard, own, (4 * lax.rem(z + hop, outer) + here, core))]
            for hop in range(1, outer)
        ]
        self.one, self.two, self.swap = [], [], []
        for step in range(outer):
            base = 4 * lax.rem(z + outer - step, outer)
            one, two = [], []
            for odd, cols in enumerate((slice(0, cut), slice(cut, columns))):
                if odd and cut == columns:
                    continue
                mine = slots(near, base + here, 1, cols)
                src = mine
                if step == 0:
                    src = shard.at[:, cols] if flat else shard.at[:, :, cols]
                one.append(copy(src, mine, across_y if odd else across_x))
                if odd:
                    both = [slots(near, base + 2 * yy + x, 1, cols) for yy in range(2)]
                else:
                    both = [slots(near, base + 2 * y, 2, cols)]
                two += [copy(spot, spot, across_x if odd else across_y) for spot in both]
            self.one.append(one)
            self.two.append(two)
            target = far if flat else near
            self.swap.append(
                [copy(slots(near, base, 4, whole), slots(target, base, 4, whole), other_core)]
            )

    @staticmethod
    def semaphores(outer):
        return pltpu.SemaphoreType.DMA((2, 7 * outer))

    @staticmethod
    def begin(copies):
        for entry in copies:
            entry.start()

    @staticmethod
    def arrive(copies):
        for entry in copies:
            entry.wait_recv()

    def start_hops(self):
        for entry in self.hops:
            self.begin(entry)

    def phase_one(self, step):
        if step:
            self.arrive(self.hops[step - 1])
        self.begin(self.one[step])

    def phase_two(self, step):
        self.arrive(self.one[step])
        self.begin(self.two[step])

    def phase_swap(self, step):
        self.arrive(self.two[step])
        self.begin(self.swap[step])

    def finish(self, step):
        self.arrive(self.swap[step])

    def drain(self):
        for copies in self.hops + self.one + self.two + self.swap:
            for entry in copies:
                entry.wait_send()


def my_place(count):
    me, core = lax.axis_index("dp"), lax.axis_index("mp")
    return {"outer": count // 4, "z": me // 4, "y": lax.rem(me // 2, 2), "x": lax.rem(me, 2),
            "core": core, "me": me}


def meet(place):
    z, y, x, core, outer = (place[name] for name in ("z", "y", "x", "core", "outer"))
    here = 2 * y + x
    others = [(4 * lax.rem(z + hop, outer) + here, core) for hop in range(1, outer)]
    others += [(4 * z + 2 * y + 1 - x, core), (4 * z + 2 * (1 - y) + x, core),
               (4 * z + here, 1 - core)]
    barrier = pltpu.get_barrier_semaphore()
    for other in others:
        pl.semaphore_signal(barrier, inc=1, device_id=other, device_id_type=pl.DeviceIdType.MESH)
    pl.semaphore_wait(barrier, len(others))


def opening_kernel(tok_ref, cond_ref, seg_ref, rope_ref, ada_ref, norm_ref, qkv_ref, out_ref,
                   up_ref, down_ref,
                   h_out, q_out, k_out, v_out, o_out, near_out, far_out, wa_out, cos_out, sin_out,
                   fq_out, fk_out, up_near, up_far, down_near, down_far, lse_ref, table_ref,
                   h_ref, q_ref, k_ref, v_ref, o_ref, near_ref, far_ref, wa_ref, cos_ref, sin_ref,
                   fq_ref, fk_ref,
                   ada_vm, small_vm, up_vm, down_vm, x_vm, c_vm, qz, kz, vt, local, saved,
                   ada_sems, small_sems, up_sems, down_sems, *, count, cuts, bk):
    place = my_place(count)
    outer, core = place["outer"], place["core"]
    rows, width = x_vm.shape
    own = width // 2
    hidden = up_ref.shape[1]
    part = width // count
    small = Gather(small_vm, near_ref, far_ref, cuts[0], small_sems, place)
    ada = Gather(ada_vm.at[pl.ds(core, 1)], wa_ref, None, ada_vm.shape[2], ada_sems, place)
    ups = Gather(up_vm, up_near, up_far, cuts[1], up_sems, place)
    downs = Gather(down_vm, down_near, down_far, cuts[2], down_sems, place)

    start = pl.multiple_of(core * rows, rows)
    loads = [
        pltpu.make_async_copy(tok_ref.at[pl.ds(start, rows)], x_vm, local.at[0]),
        pltpu.make_async_copy(cond_ref.at[pl.ds(start, rows)], c_vm, local.at[1]),
    ]
    stores = [
        pltpu.make_async_copy(*entry.local, local.at[2 + index])
        for index, entry in enumerate((ada, small, ups, downs))
    ]
    saves = {
        name: pltpu.make_async_copy(src, dst, saved.at[index])
        for index, (name, src, dst) in enumerate((
            ("h", h_ref, h_out), ("q", q_ref, q_out), ("k", k_ref, k_out), ("v", v_ref, v_out),
            ("near", near_ref, near_out), ("far", far_ref, far_out), ("wa", wa_ref, wa_out),
            ("cos", cos_ref, cos_out), ("sin", sin_ref, sin_out), ("fq", fq_ref, fq_out),
            ("fk", fk_ref, fk_out),
        ))
    }
    for load in loads:
        load.start()
    ada_vm[...] = ada_ref[...].astype(BF).reshape(ada_vm.shape)
    for c in range(3):
        small_vm[:, c * own : (c + 1) * own] = qkv_ref[c].astype(BF)
    spare = jnp.zeros((LANES - 8, part), F32)
    small_vm[:, 3 * own :] = jnp.concatenate([norm_ref[...], spare], axis=0).T.astype(BF)
    meet(place)
    first = (ada, small)

    def each(method, *args):
        for entry in first:
            getattr(entry, method)(*args)

    each("start_hops")
    each("phase_one", 0)
    stores[0].start()
    stores[1].start()
    up_vm[...] = up_ref[...].astype(BF)
    down_vm[:, :hidden] = down_ref[...].astype(BF)
    down_vm[:, hidden:] = out_ref[...].astype(BF)
    stores[2].start()
    stores[3].start()
    stores[0].wait()
    stores[1].wait()
    each("phase_two", 0)
    each("phase_one", 1)
    cosines, sines = rope_ref[:, : HEAD_DIM // 2], rope_ref[:, HEAD_DIM // 2 :]
    cos_ref[...] = jnp.concatenate([cosines] * 4, axis=1)
    sin_ref[...] = jnp.concatenate([-sines, sines, -sines, sines], axis=1)
    each("phase_one", 2)
    each("phase_two", 1)
    documents = seg_ref[pl.ds(core, 1), :].astype(F32)
    documents = jnp.broadcast_to(documents, (LANES, rows)).T
    lane = (lax.broadcasted_iota(jnp.int32, (rows, LANES), 1) % HEAD_DIM).astype(F32)
    same = documents == lane
    fq_ref[...] = jnp.where(same, 1.0, 0.0).astype(BF)
    fk_ref[...] = jnp.where(same, 0.0, jnp.where(lane < 4.0, MASKED, 0.0)).astype(BF)
    each("phase_one", 3)
    ups.start_hops()
    downs.start_hops()
    each("phase_two", 2)
    each("phase_two", 3)
    ups.phase_one(0)
    downs.phase_one(0)
    stores[2].wait()
    stores[3].wait()
    for load in loads:
        load.wait()
    for name in ("cos", "sin", "fq", "fk"):
        saves[name].start()
    for step in range(2):
        each("phase_swap", step)
    ups.phase_two(0)
    ups.phase_one(1)
    downs.phase_two(0)
    for step in range(2, outer):
        each("phase_swap", step)
    for step in range(outer):
        each("finish", step)
    for name in ("near", "far", "wa"):
        saves[name].start()

    table_ref[...] = near_ref[:, 3 * own :].astype(F32).T[0:8, :]
    wa = wa_ref[...].reshape(6 * width, c_vm.shape[1])

    def wide_events(tick):
        if tick == 0:
            ups.phase_two(1)
            ups.phase_one(2)
        if tick == 3:
            ups.phase_one(3)
            downs.phase_one(1)
            ups.phase_two(2)
        if tick == 5:
            ups.phase_two(3)
            downs.phase_two(1)
            downs.phase_one(2)
            downs.phase_one(3)
            ups.phase_swap(0)
            downs.phase_swap(0)
        if tick == 7:
            downs.phase_two(2)
            downs.phase_two(3)
            ups.phase_swap(1)
            ups.phase_swap(2)
        if tick == 8:
            ups.phase_swap(3)
            downs.phase_swap(1)

    def row_block(i, _):
        at = pl.ds(pl.multiple_of(i * ROW_BLOCK, ROW_BLOCK), ROW_BLOCK)
        cond = silu_low(c_vm[at, :])
        shift = dot(cond, wa[:width], NT) + table_ref[2:3, :]
        scale = dot(cond, wa[width : 2 * width], NT) + table_ref[3:4, :]
        normal, _ = normalize(x_vm[at, :].astype(F32))
        h = (normal * table_ref[0:1, :] * (1.0 + scale) + shift).astype(BF)
        h_ref[at, :] = h
        cos = jnp.concatenate([cos_ref[at, :]] * (own // LANES), axis=1)
        sin = jnp.concatenate([sin_ref[at, :]] * (own // LANES), axis=1)
        for first, w_ref in ((0, near_ref), (own, far_ref)):
            cols = slice(first, first + own)
            query = dot(h, w_ref[:, 0:own])
            query = query * cos + swap_halves(query) * sin
            q_ref[at, cols] = (query * HEAD_DIM**-0.5).astype(BF)
            key = dot(h, w_ref[:, own : 2 * own])
            k_ref[at, cols] = (key * cos + swap_halves(key) * sin).astype(BF)
            v_ref[at, cols] = dot(h, w_ref[:, 2 * own : 3 * own]).astype(BF)
        for tick in range(4):

            @pl.when(i == tick)
            def _():
                wide_events(tick)

        return 0

    lax.fori_loop(0, rows // ROW_BLOCK, row_block, 0)
    for name in ("h", "q", "k", "v"):
        saves[name].start()

    def keep(p):
        lanes = pl.ds(pl.multiple_of(p * LANES, LANES), LANES)
        return pltpu.make_async_copy(o_ref.at[:, lanes], o_out.at[:, lanes], saved.at[len(saves)])

    def head_pair(p, _):
        lanes = pl.ds(pl.multiple_of(p * LANES, LANES), LANES)
        qz[0], qz[1] = split_heads(q_ref[:, lanes], fq_ref[...])
        kz[0], kz[1] = split_heads(k_ref[:, lanes], fk_ref[...])
        vt[...] = v_ref[:, lanes].T
        state = [None, None]
        for j in range(rows // bk):
            block = slice(j * bk, (j + 1) * bk)
            scores = [dot(kz[h, block, :], qz[h], NT) for h in range(2)]
            for h in range(2):
                values = vt[HEAD_DIM * h : HEAD_DIM * (h + 1), block]
                top = jnp.max(scores[h], axis=0, keepdims=True)
                if j:
                    top = jnp.maximum(state[h][0], top)
                weights = jnp.exp(scores[h] - top)
                total = jnp.sum(weights, axis=0, keepdims=True)
                result = dot(values, weights.astype(BF))
                if j:
                    fade = jnp.exp(state[h][0] - top)
                    total = state[h][1] * fade + total
                    result = state[h][2] * fade + result
                state[h] = (top, total, result)
        done = jnp.concatenate([entry[2] / entry[1] for entry in state], axis=0)
        o_ref[:, lanes] = done.T.astype(BF)
        for h in range(2):
            lse_ref[p, h : h + 1, :] = state[h][0] + jnp.log(state[h][1])

        @pl.when(p > 0)
        def _():
            keep(p - 1).wait()

        keep(p).start()
        for tick in range(4, 10):

            @pl.when(p == tick - 4)
            def _():
                wide_events(tick)

        return 0

    lax.fori_loop(0, width // LANES, head_pair, 0)
    downs.phase_swap(2)
    downs.phase_swap(3)
    keep(width // LANES - 1).wait()
    for save in saves.values():
        save.wait()
    for step in range(outer):
        ups.finish(step)
        downs.finish(step)
    for entry in (ada, small, ups, downs):
        entry.drain()


def opening(count, tokens, cond, segments, rope, weights):
    ada, norms, qkv, out, up, down = weights
    rows, width = tokens.shape[0] // 2, tokens.shape[1]
    conds, part, hidden = cond.shape[1], width // count, up.shape[1]
    vm = pl.BlockSpec(memory_space=pltpu.VMEM)
    hbm = pl.BlockSpec(memory_space=pl.ANY)
    small = shape_of((width, 3 * width // 2 + LANES), BF)
    act = shape_of((rows, width), BF)
    table = shape_of((rows, LANES), F32)
    feature = shape_of((rows, LANES), BF)
    first = shape_of((width, hidden), BF)
    second = shape_of((width, hidden + width // 2), BF)
    pairs = width // LANES
    pair = pltpu.VMEM((2, rows, LANES), BF)
    half_cols = ada.shape[0] // 2
    kept = [act] * 5 + [small, small, shape_of((count, 2, half_cols, conds), BF), table, table,
                        feature, feature]
    cuts = (512, hidden // 2, second.shape[1] // 2 // LANES * LANES)
    return pl.pallas_call(
        functools.partial(opening_kernel, count=count, cuts=cuts, bk=512),
        in_specs=[hbm, hbm] + [vm] * 8,
        out_specs=[hbm] * (len(kept) + 4) + [vm, vm],
        out_shape=kept + [first, first, second, second]
        + [shape_of((pairs, 2, rows), F32), shape_of((8, width), F32)],
        scratch_shapes=[pltpu.VMEM(entry.shape, entry.dtype) for entry in kept]
        + [
            pltpu.VMEM((2, half_cols, conds), BF),
            pltpu.VMEM((part, small.shape[1]), BF),
            pltpu.VMEM((part, hidden), BF),
            pltpu.VMEM((part, second.shape[1]), BF),
            pltpu.VMEM((rows, width), BF), pltpu.VMEM((rows, conds), BF),
            pair, pair, pltpu.VMEM((LANES, rows), BF),
            pltpu.SemaphoreType.DMA((6,)),
            pltpu.SemaphoreType.DMA((len(kept),)),
        ] + [Gather.semaphores(count // 4)] * 4,
        compiler_params=pltpu.CompilerParams(
            vmem_limit_bytes=VMEM_LIMIT, collective_id=0, has_side_effects=True
        ),
        name="opening",
    )(tokens, cond, segments, rope, ada, norms, qkv, out, up, down)


class Scatter:
    def __init__(self, place, first, total, one, two, hops, sems):
        z, y, x, core, outer = (place[name] for name in ("z", "y", "x", "core", "outer"))

        def copy(src, dst, device):
            index = place["next"]
            place["next"] = index + 1
            return pltpu.make_async_remote_copy(
                src_ref=src,
                dst_ref=dst,
                send_sem=sems.at[0, index],
                recv_sem=sems.at[1, index],
                device_id=device,
                device_id_type=pl.DeviceIdType.MESH,
            )

        across_x = (4 * z + 2 * y + 1 - x, core)
        across_y = (4 * z + 2 * (1 - y) + x, core)
        self.one, self.two, self.hops, self.z, self.outer = one, two, hops, z, outer
        if first == "y":
            self.keep_one, self.keep_two = total.at[:, y], one.at[:, x]
            self.copy_one = copy(total.at[:, 1 - y], one, across_y)
            self.copy_two = copy(one.at[:, 1 - x], two, across_x)
        else:
            self.keep_one, self.keep_two = total.at[:, :, x], one.at[:, y]
            self.copy_one = copy(total.at[:, :, 1 - x], one, across_x)
            self.copy_two = copy(one.at[:, 1 - y], two, across_y)
        self.copy_hops = [
            copy(two.at[lax.rem(z + hop, outer)], hops.at[hop - 1],
                 (4 * lax.rem(z + hop, outer) + 2 * y + x, core))
            for hop in range(1, outer)
        ]

    @classmethod
    def halves(cls, place, buffers, sems, order="yx"):
        columns = buffers[0].shape[-1]
        cut = columns // 2 // LANES * LANES
        out = []
        for first, cols in zip(order, (slice(0, cut), slice(cut, columns))):
            views = [ref.at[(slice(None),) * (len(ref.shape) - 1) + (cols,)] for ref in buffers]
            out.append(cls(place, first, *views, sems))
        return out

    def start(self):
        self.copy_one.start()

    def phase_two(self):
        self.copy_one.wait_recv()
        self.one[...] = (self.one[...].astype(F32) + self.keep_one[...].astype(F32)).astype(BF)
        self.copy_two.start()

    def phase_hops(self):
        self.copy_two.wait_recv()
        self.two[...] = (self.two[...].astype(F32) + self.keep_two[...].astype(F32)).astype(BF)
        for entry in self.copy_hops:
            entry.start()

    def finish(self):
        total = self.two[self.z].astype(F32)
        for hop, entry in enumerate(self.copy_hops):
            entry.wait_recv()
            total = total + self.hops[hop].astype(F32)
        return total

    def drain(self):
        for entry in [self.copy_one, self.copy_two] + self.copy_hops:
            entry.wait_send()


def across_cores(place, src, dst, sems):
    index = place["next"]
    place["next"] = index + 1
    return pltpu.make_async_remote_copy(
        src_ref=src,
        dst_ref=dst,
        send_sem=sems.at[0, index],
        recv_sem=sems.at[1, index],
        device_id=(place["me"], 1 - place["core"]),
        device_id_type=pl.DeviceIdType.MESH,
    )


def scatter_buffers(outer, blocks, rows, columns):
    lead = () if blocks is None else (blocks,)
    return [
        pltpu.VMEM(lead + (outer, 2, 2, rows, columns), BF),
        pltpu.VMEM(lead + (outer, 2, 2, rows, columns), BF),
        pltpu.VMEM(lead + (outer, 2, rows, columns), BF),
        pltpu.VMEM(lead + (outer, rows, columns), BF),
        pltpu.VMEM(lead + (outer - 1, rows, columns), BF),
    ]


def spread_kernel(h_ref, gy_ref, ga_ref, du_ref, z_ref, o_ref, q_ref, k_ref, v_ref, do_ref,
                  lse_ref, fq_ref, fk_ref, cos_ref, sin_ref,
                  dq_ref, dk_ref, dv_ref, sum_ref,
                  h_turn, gy_turn, ga_turn, right, far6, sum6, one6, two6, hop6,
                  far1, sum1, one1, two1, hop1, qz, kz, qm, dm, vm, kt, delta, dqt,
                  load_sems, sems, *, count, bk):
    place = my_place(count)
    place["next"] = 0
    outer = place["outer"]
    rows, width = o_ref.shape
    own = width // 2
    each, block = right.shape[0], right.shape[2]
    span = 2 * each * block
    shards = far6.shape[1:]
    tail = far1.shape

    swaps = [across_cores(place, far6.at[j], sum6.at[j], sems) for j in range(2 * each)]
    swaps.append(across_cores(place, far1, sum1, sems))
    scatters = []
    for j in range(2 * each + 1):
        if j < 2 * each:
            buffers = [ref.at[j] for ref in (sum6, one6, two6, hop6)]
        else:
            buffers = [sum1, one1, two1, hop1]
        scatters.append(Scatter.halves(place, buffers, sems))

    def start(j):
        for entry in scatters[j]:
            entry.start()

    def phase_two(j):
        for entry in scatters[j]:
            entry.phase_two()

    def phase_hops(j):
        for entry in scatters[j]:
            entry.phase_hops()

    def finish(j):
        at = j * block
        for entry in scatters[j]:
            columns = entry.hops.shape[-1]
            sum_ref[:, at : at + columns] = entry.finish()
            at += columns

    lefts, sources = (h_turn, gy_turn), (du_ref, z_ref)
    groups = [(side, index) for index in range(2) for side in (1, 0)]

    def load(group, b):
        side, index = groups[group]
        at = pl.multiple_of(side * (span // 2) + b * block, block)
        return pltpu.make_async_copy(
            sources[index].at[:, pl.ds(at, block)], right.at[b], load_sems.at[b]
        )

    for b in range(each):
        load(0, b).start()
    meet(place)
    h_turn[...] = h_ref[...].T
    gy_turn[...] = gy_ref[...].T
    ga_turn[...] = ga_ref[...].T

    for group, (side, index) in enumerate(groups):

        def grad_block(b, _):
            load(group, b).wait()
            grad = dot(lefts[index][...], right[b])
            if group + 1 < len(groups):
                load(group + 1, b).start()
            j = index * each + b
            if side:
                far6[j] = grad.reshape(shards).astype(BF)
            for b_static in range(each):
                at = index * each + b_static

                @pl.when(b == b_static)
                def _():
                    if side:
                        swaps[at].start()
                    else:
                        swaps[at].wait_recv()

            if not side:
                sum6[j] = (grad.reshape(shards) + sum6[j].astype(F32)).astype(BF)
                if index == 0:
                    for b_static in range(2):

                        @pl.when(b == b_static)
                        def _():
                            start(b_static)

            return 0

        lax.fori_loop(0, each, grad_block, 0)
        if index == 1 and side:
            grad = dot(ga_turn[...], o_ref[:, own:])
            far1[...] = grad.reshape(tail).astype(BF)
            swaps[-1].start()
            phase_two(0)
            start(2)
    grad = dot(ga_turn[...], o_ref[:, :own])
    swaps[-1].wait_recv()
    sum1[...] = (grad.reshape(tail) + sum1[...].astype(F32)).astype(BF)
    phase_two(1)
    start(3)

    def events(p):
        if p < 3:
            start(p + 4)
        if p < 5:
            phase_two(p + 2)
            phase_hops(p)
        if 0 < p < 5:
            finish(p - 1)
        if p == 5:
            phase_hops(5)
            phase_hops(6)
            for j in (4, 5, 6):
                finish(j)

    zero = jnp.zeros((rows, LANES), BF)

    def unrotate(grad, at):
        return (grad * cos_ref[at, :] - swap_halves(grad) * sin_ref[at, :]).astype(BF)

    def head_pair(p, _):
        lanes = pl.ds(pl.multiple_of(p * LANES, LANES), LANES)
        qz[0], qz[1] = split_heads(q_ref[:, lanes], fq_ref[...])
        kz[0], kz[1] = split_heads(k_ref[:, lanes], fk_ref[...])
        qm[0], qm[1] = split_heads(q_ref[:, lanes], zero)
        dm[0], dm[1] = split_heads(do_ref[:, lanes], zero)
        vm[0], vm[1] = split_heads(v_ref[:, lanes], zero)
        kt[...] = k_ref[:, lanes].T
        product = (do_ref[:, lanes].astype(F32) * o_ref[:, lanes].astype(F32)).T
        delta[0:1, :] = jnp.sum(product[:HEAD_DIM], axis=0, keepdims=True)
        delta[1:2, :] = jnp.sum(product[HEAD_DIM:], axis=0, keepdims=True)
        dqt[...] = jnp.zeros_like(dqt)

        for first in range(0, rows, bk):
            at = slice(first, first + bk)
            reach = slice(
                max(0, (first - rows // 2 + 1) // LANES * LANES),
                min(rows, -(-(first + bk + rows // 2 - 1) // LANES) * LANES),
            )
            dk = jnp.zeros((bk, LANES), F32)
            dv = jnp.zeros((bk, LANES), F32)
            scores = [dot(kz[h, at, :], qz[h, reach, :], NT) for h in range(2)]
            grads = [dot(vm[h, at, :], dm[h, reach, :], NT) for h in range(2)]
            for h in range(2):
                weights = jnp.exp(scores[h] - lse_ref[p, h : h + 1, reach])
                dv = dv + dot(weights.astype(BF), dm[h, reach, :])
                ds = (weights * (grads[h] - delta[h : h + 1, reach])).astype(BF)
                dk = dk + dot(ds, qm[h, reach, :])
                head = slice(HEAD_DIM * h, HEAD_DIM * (h + 1))
                dqt[head, reach] += dot(kt[head, at], ds)
            dk_ref[at, lanes] = unrotate(dk, at)
            dv_ref[at, lanes] = dv.astype(BF)

        dq_ref[:, lanes] = unrotate(dqt[...].T * HEAD_DIM**-0.5, pl.ds(0, rows))
        for step in range(6):

            @pl.when(p == step)
            def _():
                events(step)

        return 0

    lax.fori_loop(0, width // LANES, head_pair, 0)
    for entry in swaps:
        entry.wait_send()
    for pair in scatters:
        for entry in pair:
            entry.drain()


def spread(count, h_two, gy, ga, du, z, mixed, queries, keys, values, upstream, lse, features,
           tables):
    rows, width = mixed.shape
    part = width // count
    outer = count // 4
    hidden = du.shape[1] // 2
    each = 3
    block = hidden // each
    vm = pl.BlockSpec(memory_space=pltpu.VMEM)
    hbm = pl.BlockSpec(memory_space=pl.ANY)
    act = shape_of((rows, width), BF)
    turn = pltpu.VMEM((width, rows), BF)
    pair = pltpu.VMEM((2, rows, LANES), BF)
    copies = 7 + 14 * (2 + outer - 1)
    return pl.pallas_call(
        functools.partial(spread_kernel, count=count, bk=256),
        in_specs=[vm, vm, vm, hbm, hbm] + [vm] * 10,
        out_specs=[vm] * 4,
        out_shape=[act, act, act, shape_of((part, 2 * hidden + width // 2), F32)],
        scratch_shapes=[turn, turn, turn, pltpu.VMEM((each, rows, block), BF)]
        + scatter_buffers(outer, 2 * each, part, block)
        + scatter_buffers(outer, None, part, width // 2)
        + [pair] * 5
        + [
            pltpu.VMEM((LANES, rows), BF),
            pltpu.VMEM((8, rows), F32),
            pltpu.VMEM((LANES, rows), F32),
            pltpu.SemaphoreType.DMA((each,)),
            pltpu.SemaphoreType.DMA((2, copies)),
        ],
        compiler_params=pltpu.CompilerParams(
            vmem_limit_bytes=VMEM_LIMIT, collective_id=1, has_side_effects=True
        ),
        name="spread",
    )(h_two, gy, ga, du, z, mixed, queries, keys, values, upstream, lse, *features, *tables)


def closing_kernel(tok_ref, cond_ref, h_in, dq_in, dk_in, dv_in, near_in, far_in, wa_in,
                   dwa_two_in, dx_in, mid_ref, p_ref, dp_two_ref,
                   rows_ref, qkv_ref, ada_ref, norm_ref, square_ref,
                   h_ref, dq_ref, dk_ref, dv_ref, x_vm, c_vm, near_ref, far_ref, wa_ref,
                   dwa_two_ref, dx_ref,
                   turned, mine, dh_vm, dwa_vm, dp_vm, dwt, plane, column,
                   far3, sum3, one3, two3, hop3, far2, sum2, one2, two2, hop2,
                   local, sems, *, count, token_total):
    place = my_place(count)
    place["next"] = 0
    z, y, x, core, outer, me = (place[name] for name in ("z", "y", "x", "core", "outer", "me"))
    rows, width = x_vm.shape
    own = width // 2
    part = width // count
    conds = c_vm.shape[1]
    half_cols = ada_ref.shape[1]
    cut = sum2.shape[4]
    shards = far3.shape[1:]

    start = pl.multiple_of(core * rows, rows)
    columns = near_ref.shape[1]
    pieces = (
        (h_in, h_ref), (dq_in, dq_ref), (dk_in, dk_ref), (dv_in, dv_ref),
        (tok_ref.at[pl.ds(start, rows)], x_vm), (cond_ref.at[pl.ds(start, rows)], c_vm),
        (near_in.at[:, pl.ds(0, columns)], near_ref), (far_in.at[:, pl.ds(0, columns)], far_ref),
        (wa_in.at[pl.ds(width, width)], wa_ref), (dwa_two_in, dwa_two_ref), (dx_in, dx_ref),
    )
    loads = [
        pltpu.make_async_copy(src, dst, local.at[index])
        for index, (src, dst) in enumerate(pieces)
    ]
    for load in loads:
        load.start()

    swaps = [across_cores(place, far3.at[c], sum3.at[c], sems) for c in range(3)]
    scatters = [
        Scatter.halves(place, [ref.at[c] for ref in (sum3, one3, two3, hop3)], sems,
                       "xy" if c % 2 else "yx")
        for c in range(3)
    ]
    ada_swaps = [across_cores(place, far2.at[c], sum2.at[c], sems) for c in range(2)]
    adas = [
        Scatter(place, "xy"[c], sum2.at[c], one2.at[c], two2.at[c], hop2.at[c], sems)
        for c in range(2)
    ]
    sends = []

    def copy(src, dst, device):
        index = place["next"]
        place["next"] = index + 1
        entry = pltpu.make_async_remote_copy(
            src_ref=src, dst_ref=dst, send_sem=sems.at[0, index], recv_sem=sems.at[1, index],
            device_id=device, device_id_type=pl.DeviceIdType.MESH,
        )
        sends.append(entry)
        return entry

    row_copies = []
    for i in range(rows // ROW_BLOCK):
        at = pl.ds(i * ROW_BLOCK, ROW_BLOCK)
        row_copies.append(copy(dh_vm.at[at], rows_ref.at[1, at], (me, 1 - core)))
    ada_copy = copy(ada_ref.at[core], ada_ref.at[core], (me, 1 - core))
    spot = 4 * core + 2 * y + x
    plane_copies = []
    for other in range(1, 8):
        yy, xx = lax.rem(y + other // 2, 2), lax.rem(x + other, 2)
        cc = lax.rem(core + other // 4, 2)
        plane_copies.append((4 * z + 2 * yy + xx, cc))
    beyond = [(4 * lax.rem(z + hop, outer) + 2 * y + x, core) for hop in range(1, outer)]

    barrier = pltpu.get_barrier_semaphore()
    for device in plane_copies + beyond:
        pl.semaphore_signal(barrier, inc=1, device_id=device, device_id_type=pl.DeviceIdType.MESH)
    pl.semaphore_wait(barrier, len(plane_copies) + len(beyond))
    plane_copies = [copy(plane.at[spot], plane.at[spot], device) for device in plane_copies]
    column_copies = [copy(column.at[z], column.at[z], device) for device in beyond]

    def all_of(c, method):
        for entry in scatters[c]:
            getattr(entry, method)()

    grad_refs = (dq_ref, dk_ref, dv_ref)
    loads[0].wait()
    turned[...] = h_ref[...].T
    for c in range(3):
        loads[1 + c].wait()
        grad = dot(turned[...], grad_refs[c][...])
        far3[c] = grad[:, own:].reshape(shards).astype(BF)
        swaps[c].start()
        mine[c] = grad[:, :own].reshape(shards)
        if c:
            swaps[c - 1].wait_recv()
            sum3[c - 1] = (mine[c - 1] + sum3[c - 1].astype(F32)).astype(BF)
            all_of(c - 1, "start")
    for load in loads[4:9]:
        load.wait()

    dwa_vm[...] = jnp.zeros_like(dwa_vm)
    dp_vm[...] = jnp.zeros_like(dp_vm)
    gain = p_ref[0:1, :]

    def spread_of(at):
        scale = dot(silu_low(c_vm[at, :]), wa_ref[...], NT) + p_ref[3:4, :]
        return 1.0 + scale

    def first_pass(i, _):
        at = pl.ds(pl.multiple_of(i * ROW_BLOCK, ROW_BLOCK), ROW_BLOCK)
        dh = jnp.zeros((ROW_BLOCK, width), F32)
        for first, w_ref in ((0, near_ref), (own, far_ref)):
            cols = slice(first, first + own)
            for c, grad_ref in enumerate(grad_refs):
                dh = dh + dot(grad_ref[at, cols], w_ref[:, c * own : (c + 1) * own], NT)
        dh_vm[at, :] = dh
        normal, _ = normalize(x_vm[at, :].astype(F32))
        dn = dh * normal
        summed = cond_rows(silu_low(c_vm[at, :]))
        dwa_vm[:, :width] += dot(summed, dh.astype(BF))
        dwa_vm[:, width:] += dot(summed, (dn * gain).astype(BF))
        dp_vm[0:1, :] += jnp.sum(dn * spread_of(at), axis=0, keepdims=True)

        @pl.when(i == 0)
        def _():
            swaps[2].wait_recv()
            sum3[2] = (mine[2] + sum3[2].astype(F32)).astype(BF)
            all_of(2, "start")

        @pl.when(i == 2)
        def _():
            all_of(0, "phase_two")

        @pl.when(i == 3)
        def _():
            all_of(1, "phase_two")

        return 0

    lax.fori_loop(0, rows // ROW_BLOCK, first_pass, 0)
    loads[9].wait()

    dwt[0 : 2 * width, :] = dwa_vm[:conds, :].T
    dwt[2 * width :, :] = dwa_two_ref[:conds, :].T
    dp_vm[1:2, :] = dp_two_ref[0:1, :]
    for block in range(2):
        dp_vm[2 + block : 3 + block, :] = dwa_vm[
            conds : conds + 1, block * width : (block + 1) * width
        ]
    for block in range(4):
        dp_vm[4 + block : 5 + block, :] = dwa_two_ref[
            conds : conds + 1, block * width : (block + 1) * width
        ]
    lane = lax.broadcasted_iota(jnp.int32, (16, conds), 1)

    def place_ada(side, store):
        for shard in range(count):
            spot = (shard // 4, (shard // 2) % 2, shard % 2)
            base = pl.multiple_of(2 * half_cols * shard + half_cols * side, 16)
            store(0, spot, slice(None), dwt[pl.ds(base, cut), :].astype(BF))
            rest = half_cols - cut
            store(1, spot, slice(0, rest), dwt[pl.ds(base + cut, rest), :].astype(BF))
            gone = dp_vm[...] if shard == 0 else pltpu.roll(dp_vm[...], width - shard * part, 1)
            gone = jnp.where(lane < part, gone[:, :conds], 0.0)
            store(1, spot, slice(rest, cut), gone.astype(BF))

    def store_far(index, spot, at, value):
        far2[(index, *spot, at)] = value

    def add_near(index, spot, at, value):
        total = sum2[(index, *spot, at)].astype(F32) + value.astype(F32)
        sum2[(index, *spot, at)] = total.astype(BF)

    place_ada(1 - core, store_far)
    for entry in ada_swaps:
        entry.start()
    all_of(0, "phase_hops")
    all_of(2, "phase_two")
    for entry in ada_swaps:
        entry.wait_recv()
    place_ada(core, add_near)
    for entry in adas:
        entry.start()
    all_of(1, "phase_hops")
    loads[10].wait()

    def events(i):
        if i == 1:
            all_of(2, "phase_hops")
        if i == 2:
            for entry in adas:
                entry.phase_two()
        if i == 3:
            for entry in adas:
                entry.phase_hops()

    def keep(i):
        at = pl.ds(pl.multiple_of(i * ROW_BLOCK, ROW_BLOCK), ROW_BLOCK)
        return pltpu.make_async_copy(dh_vm.at[at], rows_ref.at[0, at], local.at[i])

    def second_pass(i, _):
        at = pl.ds(pl.multiple_of(i * ROW_BLOCK, ROW_BLOCK), ROW_BLOCK)
        normal, rstd = normalize(x_vm[at, :].astype(F32))
        grad = dh_vm[at, :] * gain * spread_of(at)
        dh_vm[at, :] = dx_ref[at, :] + norm_backward(grad, normal, rstd)
        keep(i).start()
        for step in range(rows // ROW_BLOCK):

            @pl.when(i == step)
            def _():
                row_copies[step].start()
                if step < 4:
                    events(step)

        return 0

    lax.fori_loop(0, rows // ROW_BLOCK, second_pass, 0)

    squares = jnp.sum((mid_ref[...] / token_total) ** 2)
    for c in range(3):
        at = c * own
        for entry in scatters[c]:
            total = entry.finish()
            qkv_ref[:, at : at + total.shape[1]] = total
            squares = squares + jnp.sum((total / token_total) ** 2)
            at += total.shape[1]
    first, second = adas[0].finish(), adas[1].finish()
    rest = half_cols - cut
    ada_ref[core, 0:cut, :] = first
    ada_ref[core, cut:, :] = second[:rest]
    norm_ref[...] = second[rest : rest + 8]
    ada_copy.start()
    squares = squares + jnp.sum((first / token_total) ** 2)
    squares = squares + jnp.sum((second[:rest] / token_total) ** 2)
    squares = squares + 0.5 * jnp.sum((second[rest:] / token_total) ** 2)
    plane[spot] = jnp.full((8, LANES), squares, F32)
    for entry in plane_copies:
        entry.start()
    for entry in plane_copies:
        entry.wait_recv()
    column[z] = jnp.sum(plane[...], axis=0)
    for entry in column_copies:
        entry.start()
    for entry in column_copies:
        entry.wait_recv()
    square_ref[...] = jnp.sum(column[...], axis=0)
    ada_copy.wait_recv()
    for i, entry in enumerate(row_copies):
        keep(i).wait()
        entry.wait_recv()
    for entry in swaps + ada_swaps + sends:
        entry.wait_send()
    for entry in [part for pair in scatters for part in pair] + adas:
        entry.drain()


def closing(count, tokens, cond, h_one, grads, dx, wa, norms, near, far, dwa_two, dp_two,
            middle_sum, token_total):
    rows, width = dx.shape
    conds = cond.shape[1]
    part = width // count
    outer = count // 4
    half_cols = wa.shape[0] // count // 2
    cut = (half_cols + 16) // 2
    vm = pl.BlockSpec(memory_space=pltpu.VMEM)
    hbm = pl.BlockSpec(memory_space=pl.ANY)
    copies = 5 + 8 * (2 + outer - 1) + rows // ROW_BLOCK + 1 + 7 + outer - 1
    act = pltpu.VMEM((rows, width), BF)
    half_weights = pltpu.VMEM((width, 3 * width // 2), BF)
    return pl.pallas_call(
        functools.partial(closing_kernel, count=count, token_total=token_total),
        in_specs=[hbm] * 11 + [vm] * 3,
        out_specs=[hbm] + [vm] * 4,
        out_shape=[
            shape_of((2, rows, width), F32),
            shape_of((part, 3 * width // 2), F32),
            shape_of((2, half_cols, conds), F32),
            shape_of((8, conds), F32),
            shape_of((8, LANES), F32),
        ],
        scratch_shapes=[
            act, act, act, act, act,
            pltpu.VMEM((rows, conds), BF),
            half_weights, half_weights,
            pltpu.VMEM((width, conds), BF),
            pltpu.VMEM(dwa_two.shape, F32),
            pltpu.VMEM((rows, width), F32),
            pltpu.VMEM((width, rows), BF),
            pltpu.VMEM((3, outer, 2, 2, part, width // 2), F32),
            pltpu.VMEM((rows, width), F32),
            pltpu.VMEM((conds + 16, 2 * width), F32),
            pltpu.VMEM((16, width), F32),
            pltpu.VMEM((wa.shape[0], conds), F32),
            pltpu.VMEM((8, 8, LANES), F32),
            pltpu.VMEM((outer, 8, LANES), F32),
        ]
        + scatter_buffers(outer, 3, part, width // 2)
        + scatter_buffers(outer, 2, cut, conds)
        + [pltpu.SemaphoreType.DMA((11,)), pltpu.SemaphoreType.DMA((2, copies))],
        compiler_params=pltpu.CompilerParams(
            vmem_limit_bytes=VMEM_LIMIT, collective_id=2, has_side_effects=True
        ),
        name="closing",
    )(tokens, cond, h_one, *grads, near, far, wa, dwa_two, dx, middle_sum, norms, dp_two)


def update_kernel(half, step, ina_ref, inb_ref, resa_ref, resb_ref, mid_ref, qkv_ref, ada_ref,
                  norm_ref, square_ref, *refs, token_total):
    state, (grad_out, res_out, norm_out), new = refs[:18], refs[18:21], refs[21:]
    i = pl.program_id(0)
    here = (i // (pl.num_programs(0) // 2)) == half[0]

    @pl.when(here)
    def _():
        grad_out[...] = ina_ref[0]
        res_out[...] = resa_ref[...]

    @pl.when(jnp.logical_not(here))
    def _():
        grad_out[...] = inb_ref[0]
        res_out[...] = resb_ref[...]

    @pl.when(i == 0)
    def _():
        grad_norm = jnp.sqrt(square_ref[0:1, :])
        norm_out[...] = grad_norm
        clip_factor = jnp.minimum(1.0, clip_limit / (grad_norm + 1e-06))[:, 0:1] / token_total
        steps = jnp.full((1, LANES), step[0], jnp.int32).astype(F32)
        fix_one = (1.0 - jnp.exp(steps * math.log(0.9)))[:, 0:1]
        fix_two = (1.0 - jnp.exp(steps * math.log(0.999)))[:, 0:1]
        hidden, own = state[12].shape[1], state[9].shape[1]
        half_rows = ada_ref.shape[1]

        def update(index, at, grad):
            entry = [ref[at] for ref in state[3 * index : 3 * index + 3]]
            values = adam_update(*entry, grad, clip_factor, fix_one, fix_two,
                                 step_rates[index], decay_rates[index])
            for ref, value in zip(new[3 * index : 3 * index + 3], values):
                ref[at] = value

        for core in range(2):
            update(0, slice(core * half_rows, (core + 1) * half_rows), ada_ref[core])
        update(1, slice(None), norm_ref[:, : state[3].shape[1]])
        for c in range(3):
            update(2, c, qkv_ref[:, c * own : (c + 1) * own])
        update(3, slice(None), mid_ref[:, 2 * hidden :])
        update(4, slice(None), mid_ref[:, :hidden])
        update(5, slice(None), mid_ref[:, hidden : 2 * hidden])


def update_stage(half, step, input_rows, result, result_far, sums, state, token_total):
    rows, width = result.shape
    blocks = rows // ROW_BLOCK
    held = list(sums) + list(state)

    def side(match, lead):
        def index(i, half, step):
            same = (i // blocks == half[0]) == match
            at = jnp.where(same, i % blocks, jnp.where(i < blocks, 0, blocks - 1))
            return lead + (at, 0)

        return index

    block = (ROW_BLOCK, width)
    whole = lambda entry: resident(entry.shape, (0,) * entry.ndim)
    out = pl.BlockSpec(block, lambda i, half, step: (i, 0))
    fixed = lambda entry: pl.BlockSpec(entry.shape, lambda *_, n=entry.ndim: (0,) * n)
    return pl.pallas_call(
        functools.partial(update_kernel, token_total=token_total),
        grid_spec=pltpu.PrefetchScalarGridSpec(
            num_scalar_prefetch=2,
            grid=(2 * blocks,),
            in_specs=[
                pl.BlockSpec((1,) + block, side(True, (0,))),
                pl.BlockSpec((1,) + block, side(False, (1,))),
                pl.BlockSpec(block, side(True, ())),
                pl.BlockSpec(block, side(False, ())),
            ] + [whole(entry) for entry in held],
            out_specs=[out, out, pl.BlockSpec((1, LANES), lambda *_: (0, 0))]
            + [fixed(entry) for entry in state],
        ),
        out_shape=[shape_of((2 * rows, width), F32), shape_of((2 * rows, width), BF),
                   shape_of((1, LANES), F32)]
        + [shape_of(entry.shape, F32) for entry in state],
        compiler_params=params(),
        name="update_stage",
    )(half, step, input_rows, input_rows, result, result_far, *held)


def factors(count):
    return (count // 4, 2, 2)


def swap_mp(value):
    return lax.ppermute(value, "mp", [(0, 1), (1, 0)])


def swap_dp(value, distance):
    count = lax.axis_size("dp")
    return lax.ppermute(value, "dp", [(i, i ^ distance) for i in range(count)])


def turn_dp(value, distance):
    count = lax.axis_size("dp")
    return lax.ppermute(value, "dp", [(i, (i + distance) % count) for i in range(count)])


def pick(value, index, axis):
    return lax.dynamic_index_in_dim(value, index, axis, keepdims=False)


def scatter_sum(parts, order):
    count = lax.axis_size("dp")
    outer, mid, inner = factors(count)
    me = lax.axis_index("dp")
    place = {4: me // 4, 2: (me // 2) % 2, 1: me % 2}

    def widen(part):
        return part.reshape((outer, mid, inner) + part.shape[1:]).astype(F32)

    total = widen(parts[0])
    for part in parts[1:]:
        total = total + widen(part)
    for distance in order:
        axis = 1 if (distance == 2 or total.ndim == 4) else 2
        gone = pick(total, 1 - place[distance], axis).astype(BF)
        total = pick(total, place[distance], axis) + swap_dp(gone, distance).astype(F32)
    arrived = [
        turn_dp(pick(total, (place[4] + hop) % outer, 0).astype(BF), 4 * hop)
        for hop in range(1, outer)
    ]
    total = pick(total, place[4], 0)
    for piece in arrived:
        total = total + piece.astype(F32)
    return total


def scatter_halves(near, far_sum):
    count = lax.axis_size("dp")
    width, columns = near.shape
    cut = columns // 2 // LANES * LANES
    shards = lambda value: value.reshape(count, width // count, value.shape[1])
    first = scatter_sum([shards(near[:, :cut]), shards(far_sum[:, :cut])], (2, 1))
    second = scatter_sum([shards(near[:, cut:]), shards(far_sum[:, cut:])], (1, 2))
    return jnp.concatenate([first, second], axis=1)


def sum_everywhere(value):
    value = value + swap_mp(value)
    distance = 1
    while distance < lax.axis_size("dp"):
        value = value + swap_dp(value, distance)
        distance *= 2
    return value


def in_order(half, near, far):
    first = jnp.where(half == 0, near, far)
    second = jnp.where(half == 0, far, near)
    return jnp.concatenate([first, second], axis=0)


def per_device(
    tokens, cond, segments, out_grad, step,
    ada_weight, ada_first, ada_second,
    norm_params, norm_first, norm_second,
    qkv_weight, qkv_first, qkv_second,
    out_weight, out_first, out_second,
    up_weight, up_first, up_second,
    down_weight, down_first, down_second,
):
    count = lax.axis_size("dp")
    width = tokens.shape[1]
    rows = tokens.shape[0] // 2
    conds = cond.shape[1]
    part = width // count
    half = lax.axis_index("mp")
    half_ref = half.reshape(1).astype(jnp.int32)
    token_total = float(tokens.shape[0] * count)

    fused = count == 16 and part % 16 == 0 and ada_weight.shape[1] % 32 == 0
    if fused:
        (h_one, queries, keys, values, mixed, near, far, wa, cosines, sines, query_lanes,
         key_lanes, up_near, up_far, down_near, down_far, lse, norms) = opening(
            count, tokens, cond, segments, rope_constants(rows),
            (ada_weight.T, norm_params, qkv_weight, out_weight.T, up_weight, down_weight.T),
        )
        wa = wa.reshape(-1, conds)
        features, tables = (query_lanes, key_lanes), (cosines, sines)
    else:
        ada_shard = ada_weight.T.astype(BF)
        small_shard = jnp.concatenate(
            [
                qkv_weight.astype(BF).transpose(1, 0, 2).reshape(part, -1),
                jnp.pad(norm_params.astype(BF).T, ((0, 0), (0, LANES - 8))),
            ],
            axis=1,
        )
        down_shard = jnp.concatenate([down_weight.astype(BF).T, out_weight.astype(BF).T], axis=1)
        segment = pick(segments, half, 0)
        features = document_features(segment)
        tables = rope_tables(rows)
        wa = lax.all_gather(ada_shard, "dp", axis=0, tiled=True)
        near = lax.all_gather(small_shard, "dp", axis=0, tiled=True)
        far = swap_mp(near)
        norms = near[:, -LANES:].T[:8].astype(F32)
        up_near = lax.all_gather(up_weight.astype(BF), "dp", axis=0, tiled=True)
        down_near = lax.all_gather(down_shard, "dp", axis=0, tiled=True)
        up_far, down_far = swap_mp(up_near), swap_mp(down_near)
        h_one, queries, keys, values = first_stage(
            half_ref, tokens, cond, wa, norms, near, far, tables
        )
        mixed, lse = attend(queries, keys, values, segment, features)
    result, dx, upstream, z, gy, h_two, du, ga, dwa_two, dp_two = middle_stage(
        half_ref, tokens, out_grad, cond, mixed, wa, norms, up_near, up_far, down_near, down_far
    )
    result_far = swap_mp(result)

    block = width // 2
    if fused:
        *grads, middle_sum = spread(
            count, h_two, gy, ga, du, z, mixed, queries, keys, values, upstream, lse, features,
            tables,
        )
    else:
        steps = du.shape[1] // 2 // block

        def middle_grads(which, name):
            return weight_grads(
                [gy, h_two, ga], [du, z, mixed],
                [(steps, 1, 0, which * steps), (steps, 0, 1, which * steps), (1, 2, 2, which)],
                block, name,
            )

        middle_far = swap_mp(middle_grads(1, "middle_grads_far"))
        middle_near = middle_grads(0, "middle_grads_near")
        middle_sum = scatter_halves(middle_near, middle_far)
        grads = attend_back(
            queries, keys, values, upstream, mixed, lse, segment, features, tables
        )

    if fused:
        input_rows, first_sum, ada_halves, norm_sum, squares = closing(
            count, tokens, cond, h_one, grads, dx, wa, norms, near, far, dwa_two, dp_two,
            middle_sum, token_total,
        )
        turn = lambda group: tuple(entry.T for entry in group)
        ada_state = (ada_weight, ada_first, ada_second)
        out_state = (out_weight, out_first, out_second)
        down_state = (down_weight, down_first, down_second)
        state = (
            *turn(ada_state), norm_params, norm_first, norm_second,
            qkv_weight, qkv_first, qkv_second, *turn(out_state), up_weight, up_first, up_second,
            *turn(down_state),
        )
        input_grad, result, grad_norm, *new = update_stage(
            half_ref, step, input_rows, result, result_far,
            (middle_sum, first_sum, ada_halves, norm_sum, squares), state, token_total,
        )
        return (
            result, input_grad, grad_norm[0, :1],
            *turn(new[:3]), *new[3:9], *turn(new[9:12]), *new[12:15], *turn(new[15:]),
        )

    def first_grads(which, name):
        return weight_grads(
            [h_one], list(grads), [(1, 0, index, which) for index in range(3)], block, name
        )

    first_far = swap_mp(first_grads(1, "first_grads_far"))
    first_near = first_grads(0, "first_grads_near")
    first_sum = scatter_halves(first_near, first_far)

    input_grad, dwa_one, dp_one = last_stage(
        half_ref, tokens, cond, dx, grads, wa, norms, near, far
    )
    input_far = swap_mp(input_grad)

    dwa = jnp.concatenate([dwa_one, dwa_two], axis=1)
    ada_cols = dwa.shape[1] // count
    dwa_rows = dwa[:conds].T.astype(BF).reshape(count, 2, ada_cols // 2, conds)
    norm_rows = jnp.concatenate(
        [dp_one[0:1], dp_two[0:1], dwa[conds].reshape(6, width)], axis=0
    ).astype(BF)
    norm_rows = norm_rows.reshape(8, count, part).transpose(1, 0, 2)
    norm_rows = jnp.pad(norm_rows, ((0, 0), (0, 0), (0, conds - part)))
    ada_near = jnp.concatenate([pick(dwa_rows, half, 1), norm_rows], axis=1)
    ada_far = swap_mp(jnp.concatenate([pick(dwa_rows, 1 - half, 1), norm_rows], axis=1))
    ada_sum = scatter_sum([ada_near, ada_far], (2, 1))
    ada_half, norm_sum = ada_sum[: ada_cols // 2], ada_sum[ada_cols // 2 :, :part]
    ada_rows = in_order(half, ada_half, swap_mp(ada_half))

    wide_cols = du.shape[1] // 2
    up_mean = middle_sum[:, :wide_cols] / token_total
    down_mean = middle_sum[:, wide_cols : 2 * wide_cols] / token_total
    out_mean = middle_sum[:, 2 * wide_cols :] / token_total
    qkv_mean = first_sum / token_total
    ada_mean = ada_rows / token_total
    norm_mean = norm_sum / token_total
    local_sq = (
        jnp.sum(qkv_mean * qkv_mean)
        + jnp.sum(out_mean * out_mean)
        + jnp.sum(up_mean * up_mean)
        + jnp.sum(down_mean * down_mean)
        + 0.5 * (jnp.sum(ada_mean * ada_mean) + jnp.sum(norm_mean * norm_mean))
    )
    grad_norm = jnp.sqrt(sum_everywhere(jnp.full((8, LANES), local_sq, F32))[0, 0])
    clip_factor = jnp.minimum(1.0, clip_limit / (grad_norm + 1e-06))
    step_count = step[0].astype(F32)
    fix_one = 1.0 - jnp.exp(step_count * math.log(0.9))
    fix_two = 1.0 - jnp.exp(step_count * math.log(0.999))

    ada_grad = ada_mean.T
    qkv_grad = qkv_mean.reshape(part, 3, -1).transpose(1, 0, 2)
    state = (
        (ada_weight, ada_first, ada_second, ada_grad),
        (norm_params, norm_first, norm_second, norm_mean),
        (qkv_weight, qkv_first, qkv_second, qkv_grad),
        (out_weight, out_first, out_second, out_mean.T),
        (up_weight, up_first, up_second, up_mean),
        (down_weight, down_first, down_second, down_mean.T),
    )
    outputs = [
        in_order(half, result, result_far),
        in_order(half, input_grad, input_far),
        grad_norm.reshape(1),
    ]
    for index, entry in enumerate(state):
        outputs += adam_update(
            *entry, clip_factor, fix_one, fix_two, step_rates[index], decay_rates[index]
        )
    return tuple(outputs)


def solution(mesh):
    column = (P(None, "dp"),) * 3
    weights = (
        column
        + column
        + (P(None, "dp", "mp"),) * 3
        + (P("mp", "dp"),) * 3
        + (P("dp", "mp"),) * 3
        + (P("mp", "dp"),) * 3
    )
    row = P("dp", None)
    return jax.shard_map(
        per_device,
        mesh=mesh,
        in_specs=(row, row, row, row, P()) + weights,
        out_specs=(row, row, P()) + weights,
        check_vma=False,
    )
```

```python
import functools
import math

import jax
import jax.numpy as jnp
import numpy as np
from jax import lax
from jax.experimental import pallas as pl
from jax.experimental.pallas import tpu as pltpu
from jax.sharding import PartitionSpec as P

HEAD_DIM = 64
LANES = 128
MASKED = -1e30
ROW_BLOCK = 256
VMEM_LIMIT = 64_000_000
clip_limit = 1.0
step_rates = (0.075, 0.75, 0.075, 0.25, 0.075, 0.075)
decay_rates = (0.01, 0.0, 0.01, 0.01, 0.01, 0.01)

F32 = jnp.float32
BF = jnp.bfloat16
NN = (((1,), (0,)), ((), ()))
NT = (((1,), (1,)), ((), ()))


def dot(left, right, dims=NN):
    return lax.dot_general(left, right, dims, preferred_element_type=F32)


def shape_of(shape, dtype):
    return jax.ShapeDtypeStruct(shape, dtype)


def resident(shape, index):
    return pl.BlockSpec(shape, lambda *_: index, pipeline_mode=pl.Buffered(1))


def params():
    return pltpu.CompilerParams(vmem_limit_bytes=VMEM_LIMIT)


def adam_update(weight, first, second, grad, clip_factor, fix_one, fix_two, rate, decay):
    clipped = grad * clip_factor
    first_new = 0.9 * first + 0.1 * clipped
    second_new = 0.999 * second + 0.001 * clipped * clipped
    update = first_new / fix_one / (jnp.sqrt(second_new / fix_two) + 1e-08) + decay * weight
    return (weight - rate * update, first_new, second_new)


def rope_tables(length):
    half = HEAD_DIM // 2
    inverse = jnp.exp(jnp.arange(half, dtype=F32) * (-2.0 * math.log(10000.0) / HEAD_DIM))
    angles = jnp.arange(length, dtype=F32)[:, None] * inverse[None, :]
    cosines, sines = jnp.cos(angles), jnp.sin(angles)
    return (
        jnp.concatenate([cosines] * 4, axis=1),
        jnp.concatenate([-sines, sines, -sines, sines], axis=1),
    )


def rope_constants(length, fine=32):
    half = HEAD_DIM // 2
    inverse = np.exp(np.arange(half) * (-2.0 * math.log(10000.0) / HEAD_DIM))
    sign = np.repeat([-1.0, 1.0, -1.0, 1.0], half)
    tables = []
    for positions in (np.arange(0, length, fine), np.arange(fine)):
        angles = np.tile(positions[:, None] * inverse[None, :], (1, 4))
        tables += [np.cos(angles), np.sin(angles) * sign]
    return [jnp.asarray(table, F32) for table in tables]


def swap_halves(values):
    width = values.shape[1]
    lane = lax.broadcasted_iota(jnp.int32, values.shape, 1)
    ahead = pltpu.roll(values, width - HEAD_DIM // 2, 1)
    behind = pltpu.roll(values, HEAD_DIM // 2, 1)
    return jnp.where(lane % HEAD_DIM < HEAD_DIM // 2, ahead, behind)


def silu_low(cond):
    value = cond.astype(F32)
    return (value / (1.0 + jnp.exp(-value))).astype(BF)


def normalize(rows):
    centre = rows - jnp.mean(rows, axis=-1, keepdims=True)
    scale = lax.rsqrt(jnp.mean(centre * centre, axis=-1, keepdims=True) + 1e-05)
    return centre * scale, scale


def norm_backward(grad, normal, scale):
    return scale * (
        grad
        - jnp.mean(grad, axis=-1, keepdims=True)
        - normal * jnp.mean(grad * normal, axis=-1, keepdims=True)
    )


def cond_rows(cond):
    return jnp.concatenate([cond.T, jnp.ones((16, cond.shape[0]), BF)], axis=0)


def first_kernel(half, x_ref, c_ref, wa_ref, p_ref, wqa_ref, wqb_ref, cos_ref, sin_ref,
                 h_ref, q_ref, k_ref, v_ref):
    width = x_ref.shape[1]
    own = width // 2
    cond = silu_low(c_ref[...])
    mod = dot(cond, wa_ref[0 : 2 * width, :], NT)
    shift = mod[:, :width] + p_ref[2:3, :]
    scale = mod[:, width:] + p_ref[3:4, :]
    normal, _ = normalize(x_ref[...].astype(F32))
    h = (normal * p_ref[0:1, :] * (1.0 + scale) + shift).astype(BF)
    h_ref[...] = h
    cos = jnp.concatenate([cos_ref[...]] * (own // LANES), axis=1)
    sin = jnp.concatenate([sin_ref[...]] * (own // LANES), axis=1)
    for start, w_ref in ((0, wqa_ref), (own, wqb_ref)):
        cols = slice(start, start + own)
        query = dot(h, w_ref[:, 0:own])
        query = query * cos + swap_halves(query) * sin
        q_ref[:, cols] = (query * HEAD_DIM**-0.5).astype(BF)
        key = dot(h, w_ref[:, own : 2 * own])
        k_ref[:, cols] = (key * cos + swap_halves(key) * sin).astype(BF)
        v_ref[:, cols] = dot(h, w_ref[:, 2 * own :]).astype(BF)


def first_stage(half, tokens, cond, wa, norms, near, far, tables):
    width = tokens.shape[1]
    rows = tables[0].shape[0]
    blocks = rows // ROW_BLOCK
    mine = lambda i, half: (half[0] * blocks + i, 0)
    plain = lambda i, half: (i, 0)
    row = pl.BlockSpec((ROW_BLOCK, width), plain)
    return pl.pallas_call(
        first_kernel,
        grid_spec=pltpu.PrefetchScalarGridSpec(
            num_scalar_prefetch=1,
            grid=(blocks,),
            in_specs=[
                pl.BlockSpec((ROW_BLOCK, width), mine),
                pl.BlockSpec((ROW_BLOCK, cond.shape[1]), mine),
                resident(wa.shape, (0, 0)),
                resident(norms.shape, (0, 0)),
                resident((width, 3 * width // 2), (0, 0)),
                resident((width, 3 * width // 2), (0, 0)),
                pl.BlockSpec((ROW_BLOCK, LANES), plain),
                pl.BlockSpec((ROW_BLOCK, LANES), plain),
            ],
            out_specs=[row] * 4,
        ),
        out_shape=[shape_of((rows, width), BF)] * 4,
        compiler_params=params(),
        name="first_stage",
    )(half, tokens, cond, wa, norms, near, far, *tables)


def split_heads(pair, other):
    low = lax.broadcasted_iota(jnp.int32, pair.shape, 1) < HEAD_DIM
    return jnp.where(low, pair, other), jnp.where(low, other, pair)


def attend_kernel(lo_ref, hi_ref, q_ref, k_ref, v_ref, fq_ref, fk_ref, o_ref, lse_ref,
                  qz, kz, vt, *, bq, bk):
    length = q_ref.shape[0]
    qz[0], qz[1] = split_heads(q_ref[...], fq_ref[...])
    kz[0], kz[1] = split_heads(k_ref[...], fk_ref[...])
    vt[...] = v_ref[...].T

    def query_block(i, _):
        off = pl.multiple_of(i * bq, bq)
        queries = [qz[h, pl.ds(off, bq), :] for h in range(2)]

        def key_block(j, carry):
            koff = pl.multiple_of(j * bk, bk)
            scores = [dot(kz[h, pl.ds(koff, bk), :], queries[h], NT) for h in range(2)]
            out = []
            for h in range(2):
                top, total, mixed = carry[3 * h : 3 * h + 3]
                new_top = jnp.maximum(top, jnp.max(scores[h], axis=0, keepdims=True))
                weights = jnp.exp(scores[h] - new_top)
                fade = jnp.exp(top - new_top)
                total = total * fade + jnp.sum(weights, axis=0, keepdims=True)
                values = vt[HEAD_DIM * h : HEAD_DIM * (h + 1), pl.ds(koff, bk)]
                mixed = mixed * fade + dot(values, weights.astype(BF))
                out += [new_top, total, mixed]
            return tuple(out)

        start = (
            jnp.full((1, bq), -3e38, F32),
            jnp.zeros((1, bq), F32),
            jnp.zeros((HEAD_DIM, bq), F32),
        )
        done = lax.fori_loop(lo_ref[i], hi_ref[i], key_block, start * 2)
        mixed = jnp.concatenate([done[2] / done[1], done[5] / done[4]], axis=0)
        o_ref[pl.ds(off, bq), :] = mixed.T.astype(BF)
        lse_ref[0, 0:1, pl.ds(off, bq)] = done[0] + jnp.log(done[1])
        lse_ref[0, 1:2, pl.ds(off, bq)] = done[3] + jnp.log(done[4])
        return 0

    lax.fori_loop(0, length // bq, query_block, 0)


def block_ranges(segment, block, other):
    first, last = segment[::block], segment[block - 1 :: block]
    low = jnp.sum(segment[None, :] < first[:, None], axis=1)
    high = jnp.sum(segment[None, :] <= last[:, None], axis=1)
    return (low // other).astype(jnp.int32), ((high + other - 1) // other).astype(jnp.int32)


def document_features(segment):
    lane = lax.broadcasted_iota(jnp.int32, (segment.shape[0], LANES), 1) % HEAD_DIM
    same = lane == segment[:, None]
    query = jnp.where(same, 1.0, 0.0).astype(BF)
    key = jnp.where((lane < 4) & ~same, MASKED, 0.0).astype(BF)
    return query, key


def attend(queries, keys, values, segment, features, bq=1024, bk=512):
    length, width = queries.shape
    bq, bk = min(bq, length), min(bk, length)
    pairs = width // LANES
    low, high = block_ranges(segment, bq, bk)
    pair = pl.BlockSpec((length, LANES), lambda p, *_: (0, p))
    fixed = pl.BlockSpec((length, LANES), lambda p, *_: (0, 0))
    scratch = pltpu.VMEM((2, length, LANES), BF)
    return pl.pallas_call(
        functools.partial(attend_kernel, bq=bq, bk=bk),
        grid_spec=pltpu.PrefetchScalarGridSpec(
            num_scalar_prefetch=2,
            grid=(pairs,),
            in_specs=[pair, pair, pair, fixed, fixed],
            out_specs=[pair, pl.BlockSpec((1, 2, length), lambda p, *_: (p, 0, 0))],
            scratch_shapes=[scratch, scratch, pltpu.VMEM((LANES, length), BF)],
        ),
        out_shape=[shape_of((length, width), BF), shape_of((pairs, 2, length), F32)],
        compiler_params=params(),
        name="attend",
    )(low, high, queries, keys, values, *features)


def attend_back_kernel(lo_ref, hi_ref, q_ref, k_ref, v_ref, do_ref, o_ref, lse_ref, fq_ref,
                       fk_ref, cos_ref, sin_ref, dq_ref, dk_ref, dv_ref,
                       qz, kz, qm, dm, vm, kt, delta, dqt, *, bq, bk):
    length = q_ref.shape[0]
    zero = jnp.zeros((length, LANES), BF)
    qz[0], qz[1] = split_heads(q_ref[...], fq_ref[...])
    kz[0], kz[1] = split_heads(k_ref[...], fk_ref[...])
    qm[0], qm[1] = split_heads(q_ref[...], zero)
    dm[0], dm[1] = split_heads(do_ref[...], zero)
    vm[0], vm[1] = split_heads(v_ref[...], zero)
    kt[...] = k_ref[...].T
    product = (do_ref[...].astype(F32) * o_ref[...].astype(F32)).T
    delta[0:1, :] = jnp.sum(product[:HEAD_DIM], axis=0, keepdims=True)
    delta[1:2, :] = jnp.sum(product[HEAD_DIM:], axis=0, keepdims=True)
    dqt[...] = jnp.zeros_like(dqt)

    def unrotate(grad, off, rows):
        cos, sin = cos_ref[pl.ds(off, rows), :], sin_ref[pl.ds(off, rows), :]
        return (grad * cos - swap_halves(grad) * sin).astype(BF)

    def key_block(j, _):
        koff = pl.multiple_of(j * bk, bk)
        keys = [kz[h, pl.ds(koff, bk), :] for h in range(2)]
        values = [vm[h, pl.ds(koff, bk), :] for h in range(2)]

        def query_block(i, carry):
            dk, dv = carry
            off = pl.multiple_of(i * bq, bq)
            scores = [dot(keys[h], qz[h, pl.ds(off, bq), :], NT) for h in range(2)]
            grads = [dot(values[h], dm[h, pl.ds(off, bq), :], NT) for h in range(2)]
            for h in range(2):
                weights = jnp.exp(scores[h] - lse_ref[0, h : h + 1, pl.ds(off, bq)])
                dv = dv + dot(weights.astype(BF), dm[h, pl.ds(off, bq), :])
                ds = (weights * (grads[h] - delta[h : h + 1, pl.ds(off, bq)])).astype(BF)
                dk = dk + dot(ds, qm[h, pl.ds(off, bq), :])
                head = slice(HEAD_DIM * h, HEAD_DIM * (h + 1))
                dqt[head, pl.ds(off, bq)] += dot(kt[head, pl.ds(koff, bk)], ds)
            return dk, dv

        zeros = jnp.zeros((bk, LANES), F32)
        dk, dv = lax.fori_loop(lo_ref[j], hi_ref[j], query_block, (zeros, zeros))
        dk_ref[pl.ds(koff, bk), :] = unrotate(dk, koff, bk)
        dv_ref[pl.ds(koff, bk), :] = dv.astype(BF)
        return 0

    lax.fori_loop(0, length // bk, key_block, 0)
    dq_ref[...] = unrotate(dqt[...].T * HEAD_DIM**-0.5, 0, length)


def attend_back(queries, keys, values, upstream, mixed, lse, segment, features, tables,
                bq=512, bk=256):
    length, width = queries.shape
    bq, bk = min(bq, length), min(bk, length)
    pairs = width // LANES
    low, high = block_ranges(segment, bk, bq)
    pair = pl.BlockSpec((length, LANES), lambda p, *_: (0, p))
    fixed = pl.BlockSpec((length, LANES), lambda p, *_: (0, 0))
    scratch = pltpu.VMEM((2, length, LANES), BF)
    return pl.pallas_call(
        functools.partial(attend_back_kernel, bq=bq, bk=bk),
        grid_spec=pltpu.PrefetchScalarGridSpec(
            num_scalar_prefetch=2,
            grid=(pairs,),
            in_specs=[pair] * 5
            + [pl.BlockSpec((1, 2, length), lambda p, *_: (p, 0, 0))]
            + [fixed] * 4,
            out_specs=[pair] * 3,
            scratch_shapes=[scratch] * 5
            + [
                pltpu.VMEM((LANES, length), BF),
                pltpu.VMEM((8, length), F32),
                pltpu.VMEM((LANES, length), F32),
            ],
        ),
        out_shape=[shape_of((length, width), BF)] * 3,
        compiler_params=params(),
        name="attend_back",
    )(low, high, queries, keys, values, upstream, mixed, lse, *features, *tables)


def middle_kernel(half, x_ref, g_ref, c_ref, o_ref, wa_ref, p_ref, woa_ref, wob_ref, w1a_in,
                  w1b_in, w2a_in, w2b_in,
                  res_ref, dx_ref, do_ref, z_ref, gy_ref, h_ref, du_ref, ga_ref, dwa_ref,
                  dp_ref, slope, w1a_ref, w1b_ref, w2a_ref, w2b_ref, sems, *, chunk):
    width = x_ref.shape[1]
    own = width // 2
    hidden = w1a_ref.shape[1]
    loads = [
        pltpu.make_async_copy(src.at[:, pl.ds(0, hidden)], dst, sems.at[index])
        for index, (src, dst) in enumerate(
            ((w1a_in, w1a_ref), (w2a_in, w2a_ref), (w1b_in, w1b_ref), (w2b_in, w2b_ref))
        )
    ]

    @pl.when(pl.program_id(0) == 0)
    def _():
        for load in loads:
            load.start()

    cond = silu_low(c_ref[...])

    def modulation(block):
        rows = wa_ref[block * width : (block + 1) * width, :]
        return dot(cond, rows, NT) + p_ref[block + 2 : block + 3, :]

    gate_one, shift, scale, gate_two = (modulation(block) for block in (2, 3, 4, 5))
    branch = dot(o_ref[:, :own], woa_ref[...], NT) + dot(o_ref[:, own:], wob_ref[...], NT)
    middle = x_ref[...].astype(F32) + gate_one * branch
    normal, rstd = normalize(middle)
    gain = p_ref[1:2, :]
    spread = 1.0 + scale
    h = (normal * gain * spread + shift).astype(BF)
    h_ref[...] = h

    @pl.when(pl.program_id(0) == 0)
    def _():
        for load in loads:
            load.wait()

    out = jnp.zeros_like(middle)
    for start, up_ref, down_ref in ((0, w1a_ref, w2a_ref), (hidden, w1b_ref, w2b_ref)):
        for at in range(0, hidden, chunk):
            u = dot(h, up_ref[:, at : at + chunk])
            square = u * u
            flat = jnp.tanh(math.sqrt(2.0 / math.pi) * u * (1.0 + 0.044715 * square))
            half_up = 0.5 * (1.0 + flat)
            z = (u * half_up).astype(BF)
            z_ref[:, start + at : start + at + chunk] = z
            slope[:, start + at : start + at + chunk] = half_up + 0.5 * u * (
                1.0 - flat * flat
            ) * (math.sqrt(2.0 / math.pi) * (1.0 + 3.0 * 0.044715 * square))
            out = out + dot(z, down_ref[:, at : at + chunk], NT)

    g = g_ref[...].astype(F32)
    res_ref[...] = (middle + gate_two * out).astype(BF)
    gy = (gate_two * g).astype(BF)
    gy_ref[...] = gy
    dgate_two = (g * out).astype(BF)

    dh = jnp.zeros_like(middle)
    for start, up_ref, down_ref in ((0, w1a_ref, w2a_ref), (hidden, w1b_ref, w2b_ref)):
        for at in range(0, hidden, chunk):
            dz = dot(gy, down_ref[:, at : at + chunk])
            du = (dz * slope[:, start + at : start + at + chunk]).astype(BF)
            du_ref[:, start + at : start + at + chunk] = du
            dh = dh + dot(du, up_ref[:, at : at + chunk], NT)

    dn = dh * normal
    dx = g + norm_backward(dh * gain * spread, normal, rstd)
    dx_ref[...] = dx
    ga = (gate_one * dx).astype(BF)
    ga_ref[...] = ga
    do_ref[:, :own] = dot(ga, woa_ref[...]).astype(BF)
    do_ref[:, own:] = dot(ga, wob_ref[...]).astype(BF)

    @pl.when(pl.program_id(0) == 0)
    def _():
        dwa_ref[...] = jnp.zeros_like(dwa_ref)
        dp_ref[...] = jnp.zeros_like(dp_ref)

    rows = cond_rows(cond)
    grads = ((dx * branch).astype(BF), dh.astype(BF), (dn * gain).astype(BF), dgate_two)
    for block, grad in enumerate(grads):
        dwa_ref[:, block * width : (block + 1) * width] += dot(rows, grad)
    dp_ref[0:1, :] += jnp.sum(dn * spread, axis=0, keepdims=True)


def middle_stage(half, tokens, out_grad, cond, mixed, wa, norms, up_near, up_far, down_near,
                 down_far):
    width = tokens.shape[1]
    rows = mixed.shape[0]
    hidden = up_near.shape[1]
    blocks = rows // ROW_BLOCK
    mine = lambda i, half: (half[0] * blocks + i, 0)
    plain = lambda i, half: (i, 0)
    row = pl.BlockSpec((ROW_BLOCK, width), plain)
    wide = pl.BlockSpec((ROW_BLOCK, 2 * hidden), plain)
    narrow = shape_of((rows, width), BF)
    broad = shape_of((rows, 2 * hidden), BF)
    total = (cond.shape[1] + 16, 4 * width)
    return pl.pallas_call(
        functools.partial(middle_kernel, chunk=768),
        grid_spec=pltpu.PrefetchScalarGridSpec(
            num_scalar_prefetch=1,
            grid=(blocks,),
            in_specs=[
                pl.BlockSpec((ROW_BLOCK, width), mine),
                pl.BlockSpec((ROW_BLOCK, width), mine),
                pl.BlockSpec((ROW_BLOCK, cond.shape[1]), mine),
                row,
                resident(wa.shape, (0, 0)),
                resident(norms.shape, (0, 0)),
                resident((width, width // 2), (0, 2 * hidden // width)),
                resident((width, width // 2), (0, 2 * hidden // width)),
                *[pl.BlockSpec(memory_space=pl.ANY)] * 4,
            ],
            out_specs=[row, row, row, wide, row, row, wide, row,
                       pl.BlockSpec(total, lambda i, half: (0, 0)),
                       pl.BlockSpec((8, width), lambda i, half: (0, 0))],
            scratch_shapes=[pltpu.VMEM((ROW_BLOCK, 2 * hidden), F32)]
            + [pltpu.VMEM((width, hidden), BF)] * 4
            + [pltpu.SemaphoreType.DMA((4,))],
        ),
        out_shape=[narrow, shape_of((rows, width), F32), narrow, broad, narrow, narrow, broad,
                   narrow, shape_of(total, F32), shape_of((8, width), F32)],
        compiler_params=params(),
        name="middle_stage",
    )(half, tokens, out_grad, cond, mixed, wa, norms, down_near, down_far, up_near, up_far,
      down_near, down_far)


def last_kernel(half, x_ref, c_ref, dx_ref, dq_ref, dk_ref, dv_ref, wa_ref, p_ref, wqa_ref,
                wqb_ref, out_ref, dwa_ref, dp_ref):
    width = x_ref.shape[1]
    own = width // 2
    cond = silu_low(c_ref[...])
    scale = dot(cond, wa_ref[width : 2 * width, :], NT) + p_ref[3:4, :]
    dh = jnp.zeros(x_ref.shape, F32)
    for start, w_ref in ((0, wqa_ref), (own, wqb_ref)):
        cols = slice(start, start + own)
        for index, grad_ref in enumerate((dq_ref, dk_ref, dv_ref)):
            dh = dh + dot(grad_ref[:, cols], w_ref[:, index * own : (index + 1) * own], NT)
    normal, rstd = normalize(x_ref[...].astype(F32))
    gain = p_ref[0:1, :]
    spread = 1.0 + scale
    dn = dh * normal
    out_ref[...] = dx_ref[...] + norm_backward(dh * gain * spread, normal, rstd)

    @pl.when(pl.program_id(0) == 0)
    def _():
        dwa_ref[...] = jnp.zeros_like(dwa_ref)
        dp_ref[...] = jnp.zeros_like(dp_ref)

    rows = cond_rows(cond)
    dwa_ref[:, :width] += dot(rows, dh.astype(BF))
    dwa_ref[:, width:] += dot(rows, (dn * gain).astype(BF))
    dp_ref[0:1, :] += jnp.sum(dn * spread, axis=0, keepdims=True)


def last_stage(half, tokens, cond, dx, grads, wa, norms, near, far):
    width = tokens.shape[1]
    rows = dx.shape[0]
    blocks = rows // ROW_BLOCK
    mine = lambda i, half: (half[0] * blocks + i, 0)
    row = pl.BlockSpec((ROW_BLOCK, width), lambda i, half: (i, 0))
    total = (cond.shape[1] + 16, 2 * width)
    return pl.pallas_call(
        last_kernel,
        grid_spec=pltpu.PrefetchScalarGridSpec(
            num_scalar_prefetch=1,
            grid=(blocks,),
            in_specs=[
                pl.BlockSpec((ROW_BLOCK, width), mine),
                pl.BlockSpec((ROW_BLOCK, cond.shape[1]), mine),
                row, row, row, row,
                resident(wa.shape, (0, 0)),
                resident(norms.shape, (0, 0)),
                resident((width, 3 * width // 2), (0, 0)),
                resident((width, 3 * width // 2), (0, 0)),
            ],
            out_specs=[row, pl.BlockSpec(total, lambda i, half: (0, 0)),
                       pl.BlockSpec((8, width), lambda i, half: (0, 0))],
        ),
        out_shape=[shape_of((rows, width), F32), shape_of(total, F32), shape_of((8, width), F32)],
        compiler_params=params(),
        name="last_stage",
    )(half, tokens, cond, dx, *grads, wa, norms, near, far)


def weight_grad_kernel(*refs, plan):
    lefts, rights = plan["lefts"], plan["rights"]
    left_refs, right_refs = refs[:lefts], refs[lefts : lefts + rights]
    out_ref, turned = refs[lefts + rights :]
    step = pl.program_id(0)
    for begin, end, left, right in plan["spans"]:

        @pl.when(step == begin)
        def _():
            turned[...] = left_refs[left][...].T

        @pl.when((step >= begin) & (step < end))
        def _():
            out_ref[...] = dot(turned[...], right_refs[right][...]).astype(BF)


def weight_grads(lefts, rights, spans, block, name):
    rows, width = lefts[0].shape
    begin, plan, maps = 0, [], []
    for steps, left, right, first in spans:
        plan.append((begin, begin + steps, left, right))
        maps.append((begin, steps, first))
        begin += steps

    def column_map(begin, steps, first):
        return lambda i: (0, first + jnp.clip(i - begin, 0, steps - 1))

    return pl.pallas_call(
        functools.partial(
            weight_grad_kernel,
            plan={"lefts": len(lefts), "rights": len(rights), "spans": plan},
        ),
        grid=(begin,),
        in_specs=[resident((rows, width), (0, 0))] * len(lefts)
        + [pl.BlockSpec((rows, block), column_map(*entry)) for entry in maps],
        out_specs=pl.BlockSpec((width, block), lambda i: (0, i)),
        out_shape=shape_of((width, begin * block), BF),
        scratch_shapes=[pltpu.VMEM((width, rows), BF)],
        compiler_params=params(),
        name=name,
    )(*lefts, *rights)


class Gather:
    def __init__(self, shard, near, far, cut, sems, place, inner_first=False):
        outer, x, y, z, core = (place[name] for name in ("outer", "x", "y", "z", "core"))
        columns = near.shape[-1]
        flat = len(near.shape) == 2
        rows = near.shape[0] // (4 * outer)

        def slots(ref, first, number, cols):
            if flat:
                at = pl.multiple_of(first * rows, 16)
                return ref.at[pl.ds(at, number * rows), cols]
            return ref.at[pl.ds(first, number), core, :, cols]

        self.count = 0

        def copy(src, dst, device):
            index = self.count
            self.count += 1
            return pltpu.make_async_remote_copy(
                src_ref=src,
                dst_ref=dst,
                send_sem=sems.at[0, index],
                recv_sem=sems.at[1, index],
                device_id=device,
                device_id_type=pl.DeviceIdType.MESH,
            )

        here = 2 * y + x
        across_x = (4 * z + 2 * y + 1 - x, core)
        across_y = (4 * z + 2 * (1 - y) + x, core)
        other_core = (4 * z + here, 1 - core)
        whole = slice(None)
        self.outer = outer
        own = slots(near, 4 * z + here, 1, whole)
        self.local = (shard, own)
        self.inner_first = inner_first
        beyond = [(4 * lax.rem(z + hop, outer) + here, core) for hop in range(1, outer)]
        self.hops = [[copy(shard, own, device)] for device in beyond if not inner_first]
        self.one, self.two, self.swap = [], [], []
        for step in range(outer):
            base = 4 * lax.rem(z + outer - step, outer)
            one, two = [], []
            for odd, cols in enumerate((slice(0, cut), slice(cut, columns))):
                if odd and cut == columns:
                    continue
                mine = slots(near, base + here, 1, cols)
                src = mine
                if step == 0:
                    src = shard.at[:, cols] if flat else shard.at[:, :, cols]
                if step == 0 or not inner_first:
                    one.append(copy(src, mine, across_y if odd else across_x))
                if odd:
                    both = [slots(near, base + 2 * yy + x, 1, cols) for yy in range(2)]
                else:
                    both = [slots(near, base + 2 * y, 2, cols)]
                two += [copy(spot, spot, across_x if odd else across_y) for spot in both]
            self.one.append(one)
            self.two.append(two)
            if step == 0 and inner_first:
                spots = [slots(near, base + 2 * y, 2, slice(0, cut))]
                spots += [slots(near, base + 2 * yy + x, 1, slice(cut, columns)) for yy in range(2)]
                self.hops = [[copy(spot, spot, device) for spot in spots] for device in beyond]
            target = far if flat else near
            self.swap.append(
                [copy(slots(near, base, 4, whole), slots(target, base, 4, whole), other_core)]
            )

    @staticmethod
    def semaphores(outer):
        return pltpu.SemaphoreType.DMA((2, 8 * outer))

    @staticmethod
    def begin(copies):
        for entry in copies:
            entry.start()

    @staticmethod
    def arrive(copies):
        for entry in copies:
            entry.wait_recv()

    def start_hops(self):
        if self.inner_first:
            self.arrive(self.one[0])
        for entry in self.hops:
            self.begin(entry)

    def phase_one(self, step):
        if step:
            self.arrive(self.hops[step - 1])
        self.begin(self.one[step])

    def phase_two(self, step):
        if self.inner_first:
            if step:
                self.arrive(self.hops[step - 1])
        else:
            self.arrive(self.one[step])
        self.begin(self.two[step])

    def phase_swap(self, step):
        self.arrive(self.two[step])
        self.begin(self.swap[step])

    def finish(self, step):
        self.arrive(self.swap[step])

    def drain(self):
        for copies in self.hops + self.one + self.two + self.swap:
            for entry in copies:
                entry.wait_send()


def my_place(count):
    me, core = lax.axis_index("dp"), lax.axis_index("mp")
    return {"outer": count // 4, "z": me // 4, "y": lax.rem(me // 2, 2), "x": lax.rem(me, 2),
            "core": core, "me": me}


def greet(devices):
    barrier = pltpu.get_barrier_semaphore()
    for device in devices:
        pl.semaphore_signal(barrier, inc=1, device_id=device, device_id_type=pl.DeviceIdType.MESH)


def meet(devices):
    pl.semaphore_wait(pltpu.get_barrier_semaphore(), len(devices))


def partners(place):
    z, y, x, core, outer = (place[name] for name in ("z", "y", "x", "core", "outer"))
    here = 2 * y + x
    others = [(4 * lax.rem(z + hop, outer) + here, core) for hop in range(1, outer)]
    return others + [(4 * z + 2 * y + 1 - x, core), (4 * z + 2 * (1 - y) + x, core),
                     (4 * z + here, 1 - core)]


def opening_kernel(tok_ref, cond_ref, seg_ref, cosa_ref, sina_ref, cosb_ref, sinb_ref, ada_ref, norm_ref, qkv_ref, out_ref,
                   up_ref, down_ref,
                   h_out, q_out, k_out, v_out, o_out, near_out, far_out, wa_out, cos_out, sin_out,
                   fq_out, fk_out, up_near, up_far, down_near, down_far, lse_ref, table_ref,
                   h_ref, q_ref, k_ref, v_ref, o_ref, near_ref, far_ref, wa_ref, cos_ref, sin_ref,
                   fq_ref, fk_ref,
                   ada_vm, small_vm, up_vm, down_vm, x_vm, c_vm, qz, kz, vt, local, saved,
                   ada_sems, small_sems, up_sems, down_sems, *, count, cuts, bk):
    place = my_place(count)
    others = partners(place)
    greet(others)
    outer, core = place["outer"], place["core"]
    rows, width = x_vm.shape
    own = width // 2
    hidden = up_ref.shape[1]
    part = width // count
    small = Gather(small_vm, near_ref, far_ref, cuts[0], small_sems, place)
    ada = Gather(ada_vm.at[pl.ds(core, 1)], wa_ref, None, ada_vm.shape[2], ada_sems, place)
    ups = Gather(up_vm, up_near, up_far, cuts[1], up_sems, place)
    downs = Gather(down_vm, down_near, down_far, cuts[2], down_sems, place, inner_first=True)

    start = pl.multiple_of(core * rows, rows)
    loads = [
        pltpu.make_async_copy(tok_ref.at[pl.ds(start, rows)], x_vm, local.at[0]),
        pltpu.make_async_copy(cond_ref.at[pl.ds(start, rows)], c_vm, local.at[1]),
    ]
    stores = [
        pltpu.make_async_copy(*entry.local, local.at[2 + index])
        for index, entry in enumerate((ada, small, ups, downs))
    ]
    saves = {
        name: pltpu.make_async_copy(src, dst, saved.at[index])
        for index, (name, src, dst) in enumerate((
            ("h", h_ref, h_out), ("q", q_ref, q_out), ("k", k_ref, k_out), ("v", v_ref, v_out),
            ("near", near_ref, near_out), ("far", far_ref, far_out), ("wa", wa_ref, wa_out),
            ("cos", cos_ref, cos_out), ("sin", sin_ref, sin_out), ("fq", fq_ref, fq_out),
            ("fk", fk_ref, fk_out),
        ))
    }
    for load in loads:
        load.start()
    ada_vm[...] = ada_ref[...].astype(BF).reshape(ada_vm.shape)
    for c in range(3):
        small_vm[:, c * own : (c + 1) * own] = qkv_ref[c].astype(BF)
    spare = jnp.zeros((LANES - 8, part), F32)
    small_vm[:, 3 * own :] = jnp.concatenate([norm_ref[...], spare], axis=0).T.astype(BF)
    up_vm[...] = up_ref[...].astype(BF)
    down_vm[:, :hidden] = down_ref[...].astype(BF)
    down_vm[:, hidden:] = out_ref[...].astype(BF)
    meet(others)
    first = (ada, small)

    def each(method, *args):
        for entry in first:
            getattr(entry, method)(*args)

    each("start_hops")
    each("phase_one", 0)
    stores[0].start()
    stores[1].start()
    stores[2].start()
    stores[3].start()
    stores[0].wait()
    stores[1].wait()
    each("phase_two", 0)
    downs.phase_one(0)
    each("phase_one", 1)
    fine = cosb_ref.shape[0]
    for step in range(cosa_ref.shape[0]):
        at, row = slice(step * fine, (step + 1) * fine), slice(step, step + 1)
        cos_ref[at, :] = cosa_ref[row, :] * cosb_ref[...] - sina_ref[row, :] * sinb_ref[...]
        sin_ref[at, :] = sina_ref[row, :] * cosb_ref[...] + cosa_ref[row, :] * sinb_ref[...]
    each("phase_one", 2)
    each("phase_two", 1)
    documents = seg_ref[pl.ds(core, 1), :].astype(F32)
    documents = jnp.broadcast_to(documents, (LANES, rows)).T
    lane = (lax.broadcasted_iota(jnp.int32, (rows, LANES), 1) % HEAD_DIM).astype(F32)
    same = documents == lane
    fq_ref[...] = jnp.where(same, 1.0, 0.0).astype(BF)
    fk_ref[...] = jnp.where(same, 0.0, jnp.where(lane < 4.0, MASKED, 0.0)).astype(BF)
    each("phase_one", 3)
    ups.start_hops()
    each("phase_two", 2)
    stores[2].wait()
    stores[3].wait()
    downs.start_hops()
    each("phase_two", 3)
    ups.phase_one(0)
    for load in loads:
        load.wait()
    for name in ("cos", "sin", "fq", "fk"):
        saves[name].start()
    for step in range(2):
        each("phase_swap", step)
    ups.phase_two(0)
    ups.phase_one(1)
    downs.phase_two(0)
    for step in range(2, outer):
        each("phase_swap", step)
    for step in range(outer):
        each("finish", step)
    for name in ("near", "far", "wa"):
        saves[name].start()

    table_ref[...] = near_ref[:, 3 * own :].astype(F32).T[0:8, :]
    wa = wa_ref[...].reshape(6 * width, c_vm.shape[1])

    def wide_events(tick):
        if tick == 0:
            ups.phase_two(1)
            ups.phase_one(2)
        if tick == 2:
            ups.phase_one(3)
            ups.phase_two(2)
        if tick == 4:
            ups.phase_two(3)
            downs.phase_two(1)
            ups.phase_swap(0)
        if tick == 6:
            downs.phase_two(2)
            downs.phase_swap(0)
            ups.phase_swap(1)
        if tick == 7:
            ups.phase_swap(2)
            downs.phase_swap(1)
        if tick == 8:
            ups.phase_swap(3)

    def row_block(i, _):
        at = pl.ds(pl.multiple_of(i * ROW_BLOCK, ROW_BLOCK), ROW_BLOCK)
        cond = silu_low(c_vm[at, :])
        shift = dot(cond, wa[:width], NT) + table_ref[2:3, :]
        scale = dot(cond, wa[width : 2 * width], NT) + table_ref[3:4, :]
        normal, _ = normalize(x_vm[at, :].astype(F32))
        h = (normal * table_ref[0:1, :] * (1.0 + scale) + shift).astype(BF)
        h_ref[at, :] = h
        cos = jnp.concatenate([cos_ref[at, :]] * (own // LANES), axis=1)
        sin = jnp.concatenate([sin_ref[at, :]] * (own // LANES), axis=1)
        for first, w_ref in ((0, near_ref), (own, far_ref)):
            cols = slice(first, first + own)
            query = dot(h, w_ref[:, 0:own])
            query = query * cos + swap_halves(query) * sin
            q_ref[at, cols] = (query * HEAD_DIM**-0.5).astype(BF)
            key = dot(h, w_ref[:, own : 2 * own])
            k_ref[at, cols] = (key * cos + swap_halves(key) * sin).astype(BF)
            v_ref[at, cols] = dot(h, w_ref[:, 2 * own : 3 * own]).astype(BF)
        for tick in range(4):

            @pl.when(i == tick)
            def _():
                wide_events(tick)

        return 0

    lax.fori_loop(0, rows // ROW_BLOCK, row_block, 0)
    for name in ("h", "q", "k", "v"):
        saves[name].start()

    def keep(p):
        lanes = pl.ds(pl.multiple_of(p * LANES, LANES), LANES)
        return pltpu.make_async_copy(o_ref.at[:, lanes], o_out.at[:, lanes], saved.at[len(saves)])

    def head_pair(p, _):
        lanes = pl.ds(pl.multiple_of(p * LANES, LANES), LANES)
        qz[0], qz[1] = split_heads(q_ref[:, lanes], fq_ref[...])
        kz[0], kz[1] = split_heads(k_ref[:, lanes], fk_ref[...])
        vt[...] = v_ref[:, lanes].T
        state = [None, None]
        for j in range(rows // bk):
            block = slice(j * bk, (j + 1) * bk)
            scores = [dot(kz[h, block, :], qz[h], NT) for h in range(2)]
            for h in range(2):
                values = vt[HEAD_DIM * h : HEAD_DIM * (h + 1), block]
                top = jnp.max(scores[h], axis=0, keepdims=True)
                if j:
                    top = jnp.maximum(state[h][0], top)
                weights = jnp.exp(scores[h] - top)
                total = jnp.sum(weights, axis=0, keepdims=True)
                result = dot(values, weights.astype(BF))
                if j:
                    fade = jnp.exp(state[h][0] - top)
                    total = state[h][1] * fade + total
                    result = state[h][2] * fade + result
                state[h] = (top, total, result)
        done = jnp.concatenate([entry[2] / entry[1] for entry in state], axis=0)
        o_ref[:, lanes] = done.T.astype(BF)
        for h in range(2):
            lse_ref[p, h : h + 1, :] = state[h][0] + jnp.log(state[h][1])

        @pl.when(p > 0)
        def _():
            keep(p - 1).wait()

        keep(p).start()
        for tick in range(4, 10):

            @pl.when(p == tick - 4)
            def _():
                wide_events(tick)

        return 0

    lax.fori_loop(0, width // LANES, head_pair, 0)
    downs.phase_two(3)
    downs.phase_swap(2)
    downs.phase_swap(3)
    keep(width // LANES - 1).wait()
    for save in saves.values():
        save.wait()
    for step in range(outer):
        ups.finish(step)
        downs.finish(step)
    for entry in (ada, small, ups, downs):
        entry.drain()


def opening(count, tokens, cond, segments, rope, weights):
    ada, norms, qkv, out, up, down = weights
    rows, width = tokens.shape[0] // 2, tokens.shape[1]
    conds, part, hidden = cond.shape[1], width // count, up.shape[1]
    vm = pl.BlockSpec(memory_space=pltpu.VMEM)
    hbm = pl.BlockSpec(memory_space=pl.ANY)
    small = shape_of((width, 3 * width // 2 + LANES), BF)
    act = shape_of((rows, width), BF)
    table = shape_of((rows, LANES), F32)
    feature = shape_of((rows, LANES), BF)
    first = shape_of((width, hidden), BF)
    second = shape_of((width, hidden + width // 2), BF)
    pairs = width // LANES
    pair = pltpu.VMEM((2, rows, LANES), BF)
    half_cols = ada.shape[0] // 2
    kept = [act] * 5 + [small, small, shape_of((count, 2, half_cols, conds), BF), table, table,
                        feature, feature]
    cuts = (512, hidden // 2, second.shape[1] // 2 // LANES * LANES)
    return pl.pallas_call(
        functools.partial(opening_kernel, count=count, cuts=cuts, bk=512),
        in_specs=[hbm, hbm] + [vm] * 11,
        out_specs=[hbm] * (len(kept) + 4) + [vm, vm],
        out_shape=kept + [first, first, second, second]
        + [shape_of((pairs, 2, rows), F32), shape_of((8, width), F32)],
        scratch_shapes=[pltpu.VMEM(entry.shape, entry.dtype) for entry in kept]
        + [
            pltpu.VMEM((2, half_cols, conds), BF),
            pltpu.VMEM((part, small.shape[1]), BF),
            pltpu.VMEM((part, hidden), BF),
            pltpu.VMEM((part, second.shape[1]), BF),
            pltpu.VMEM((rows, width), BF), pltpu.VMEM((rows, conds), BF),
            pair, pair, pltpu.VMEM((LANES, rows), BF),
            pltpu.SemaphoreType.DMA((6,)),
            pltpu.SemaphoreType.DMA((len(kept),)),
        ] + [Gather.semaphores(count // 4)] * 4,
        compiler_params=pltpu.CompilerParams(
            vmem_limit_bytes=VMEM_LIMIT, collective_id=0, has_side_effects=True
        ),
        name="opening",
    )(tokens, cond, segments, *rope, ada, norms, qkv, out, up, down)


class Scatter:
    def __init__(self, place, first, total, one, two, hops, sems):
        z, y, x, core, outer = (place[name] for name in ("z", "y", "x", "core", "outer"))

        def copy(src, dst, device):
            index = place["next"]
            place["next"] = index + 1
            return pltpu.make_async_remote_copy(
                src_ref=src,
                dst_ref=dst,
                send_sem=sems.at[0, index],
                recv_sem=sems.at[1, index],
                device_id=device,
                device_id_type=pl.DeviceIdType.MESH,
            )

        across_x = (4 * z + 2 * y + 1 - x, core)
        across_y = (4 * z + 2 * (1 - y) + x, core)
        self.one, self.two, self.hops, self.z, self.outer = one, two, hops, z, outer
        if first == "y":
            self.keep_one, self.keep_two = total.at[:, y], one.at[:, x]
            self.copy_one = copy(total.at[:, 1 - y], one, across_y)
            self.copy_two = copy(one.at[:, 1 - x], two, across_x)
        else:
            self.keep_one, self.keep_two = total.at[:, :, x], one.at[:, y]
            self.copy_one = copy(total.at[:, :, 1 - x], one, across_x)
            self.copy_two = copy(one.at[:, 1 - y], two, across_y)
        self.copy_hops = [
            copy(two.at[lax.rem(z + hop, outer)], hops.at[hop - 1],
                 (4 * lax.rem(z + hop, outer) + 2 * y + x, core))
            for hop in range(1, outer)
        ]

    @classmethod
    def halves(cls, place, buffers, sems, order="yx"):
        columns = buffers[0].shape[-1]
        cut = columns // 2 // LANES * LANES
        out = []
        for first, cols in zip(order, (slice(0, cut), slice(cut, columns))):
            views = [ref.at[(slice(None),) * (len(ref.shape) - 1) + (cols,)] for ref in buffers]
            out.append(cls(place, first, *views, sems))
        return out

    def start(self):
        self.copy_one.start()

    def phase_two(self):
        self.copy_one.wait_recv()
        self.one[...] = self.one[...] + self.keep_one[...]
        self.copy_two.start()

    def phase_hops(self):
        self.copy_two.wait_recv()
        self.two[...] = self.two[...] + self.keep_two[...]
        for entry in self.copy_hops:
            entry.start()

    def finish(self):
        total = self.two[self.z].astype(F32)
        for hop, entry in enumerate(self.copy_hops):
            entry.wait_recv()
            total = total + self.hops[hop].astype(F32)
        return total

    def drain(self):
        for entry in [self.copy_one, self.copy_two] + self.copy_hops:
            entry.wait_send()


def across_cores(place, src, dst, sems):
    index = place["next"]
    place["next"] = index + 1
    return pltpu.make_async_remote_copy(
        src_ref=src,
        dst_ref=dst,
        send_sem=sems.at[0, index],
        recv_sem=sems.at[1, index],
        device_id=(place["me"], 1 - place["core"]),
        device_id_type=pl.DeviceIdType.MESH,
    )


def scatter_buffers(outer, blocks, rows, columns):
    lead = () if blocks is None else (blocks,)
    return [
        pltpu.VMEM(lead + (outer, 2, 2, rows, columns), BF),
        pltpu.VMEM(lead + (outer, 2, 2, rows, columns), BF),
        pltpu.VMEM(lead + (outer, 2, rows, columns), BF),
        pltpu.VMEM(lead + (outer, rows, columns), BF),
        pltpu.VMEM(lead + (outer - 1, rows, columns), BF),
    ]


def spread_kernel(h_in, gy_in, ga_in, du_ref, z_ref, o_in, q_in, k_in, v_in, do_in, lse_in,
                  fq_in, fk_in, cos_in, sin_in,
                  dq_out, dk_out, dv_out, last_ref, sum_ref,
                  h_ref, gy_ref, ga_ref, o_ref, q_ref, k_ref, v_ref, do_ref, lse_ref,
                  fq_ref, fk_ref, cos_ref, sin_ref, dq_ref, dk_ref, dv_ref,
                  h_turn, gy_turn, ga_turn, right, far6, sum6, one6, two6, hop6, far1,
                  qz, kz, qm, dm, vm, kt, delta, dqt,
                  load_sems, input_sems, keep_sems, sems, *, count, bk):
    place = my_place(count)
    others = partners(place)
    greet(others)
    place["next"] = 0
    outer = place["outer"]
    rows, width = o_ref.shape
    pieces = (
        (h_in, h_ref), (gy_in, gy_ref), (ga_in, ga_ref), (o_in, o_ref), (q_in, q_ref),
        (k_in, k_ref), (v_in, v_ref), (do_in, do_ref), (lse_in, lse_ref), (fq_in, fq_ref),
        (fk_in, fk_ref), (cos_in, cos_ref), (sin_in, sin_ref),
    )
    inputs = [
        pltpu.make_async_copy(src, dst, input_sems.at[index])
        for index, (src, dst) in enumerate(pieces)
    ]
    own = width // 2
    each, block = right.shape[0], right.shape[2]
    span = 2 * each * block
    shards = far6.shape[1:]
    tail = far1.shape

    swaps = [across_cores(place, far6.at[j], sum6.at[j], sems) for j in range(2 * each)]
    swaps.append(across_cores(place, far1, last_ref, sems))
    scatters = [
        Scatter.halves(place, [ref.at[j] for ref in (sum6, one6, two6, hop6)], sems)
        for j in range(2 * each)
    ]

    def start(j):
        for entry in scatters[j]:
            entry.start()

    def phase_two(j):
        for entry in scatters[j]:
            entry.phase_two()

    def phase_hops(j):
        for entry in scatters[j]:
            entry.phase_hops()

    def finish(j):
        at = j * block
        for entry in scatters[j]:
            columns = entry.hops.shape[-1]
            sum_ref[:, at : at + columns] = entry.finish()
            at += columns

    lefts, sources = (h_turn, gy_turn), (du_ref, z_ref)
    groups = [(side, index) for index in range(2) for side in (1, 0)]

    def load(group, b):
        side, index = groups[group]
        at = pl.multiple_of(side * (span // 2) + b * block, block)
        return pltpu.make_async_copy(
            sources[index].at[:, pl.ds(at, block)], right.at[b], load_sems.at[b]
        )

    inputs[0].start()
    load(0, 0).start()
    for item in inputs[1:4]:
        item.start()
    for b in range(1, each):
        load(0, b).start()
    for item in inputs[4:]:
        item.start()
    inputs[0].wait()
    h_turn[...] = h_ref[...].T
    meet(others)

    for group, (side, index) in enumerate(groups):

        def grad_block(b, _):
            load(group, b).wait()
            grad = dot(lefts[index][...], right[b])
            if group + 1 < len(groups):
                load(group + 1, b).start()
            j = index * each + b
            if side:
                far6[j] = grad.reshape(shards).astype(BF)
            for b_static in range(each):
                at = index * each + b_static

                @pl.when(b == b_static)
                def _():
                    if side:
                        swaps[at].start()
                    else:
                        swaps[at].wait_recv()

            if not side:
                sum6[j] = (grad.reshape(shards) + sum6[j].astype(F32)).astype(BF)
                if index == 0:
                    for b_static in range(2):

                        @pl.when(b == b_static)
                        def _():
                            start(b_static)

            return 0

        if index == 1 and side:
            inputs[1].wait()
            gy_turn[...] = gy_ref[...].T
        lax.fori_loop(0, each, grad_block, 0)
        if index == 1 and side:
            inputs[2].wait()
            inputs[3].wait()
            ga_turn[...] = ga_ref[...].T
            grad = dot(ga_turn[...], o_ref[:, own:])
            far1[...] = grad.reshape(tail).astype(BF)
            swaps[-1].start()
            phase_two(0)
            start(2)
    grad = dot(ga_turn[...], o_ref[:, :own])
    swaps[-1].wait_recv()
    last_ref[...] = (grad.reshape(tail) + last_ref[...].astype(F32)).astype(BF)
    phase_two(1)
    start(3)
    for item in inputs[4:]:
        item.wait()

    def events(p):
        if p < 4:
            phase_two(p + 2)
        if p < 2:
            start(p + 4)
        if p < 5:
            phase_hops(p)
        if p == 4:
            phase_hops(5)
        if 1 < p:
            finish(p - 2)
        if p == 5:
            finish(4)
            finish(5)

    def keep(p):
        lanes = pl.ds(pl.multiple_of(p * LANES, LANES), LANES)
        return [
            pltpu.make_async_copy(src.at[:, lanes], dst.at[:, lanes], keep_sems.at[index])
            for index, (src, dst) in enumerate(
                ((dq_ref, dq_out), (dk_ref, dk_out), (dv_ref, dv_out))
            )
        ]

    zero = jnp.zeros((rows, LANES), BF)

    def unrotate(grad, at):
        return (grad * cos_ref[at, :] - swap_halves(grad) * sin_ref[at, :]).astype(BF)

    def head_pair(p, _):
        lanes = pl.ds(pl.multiple_of(p * LANES, LANES), LANES)
        qz[0], qz[1] = split_heads(q_ref[:, lanes], fq_ref[...])
        kz[0], kz[1] = split_heads(k_ref[:, lanes], fk_ref[...])
        qm[0], qm[1] = split_heads(q_ref[:, lanes], zero)
        dm[0], dm[1] = split_heads(do_ref[:, lanes], zero)
        vm[0], vm[1] = split_heads(v_ref[:, lanes], zero)
        kt[...] = k_ref[:, lanes].T
        product = (do_ref[:, lanes].astype(F32) * o_ref[:, lanes].astype(F32)).T
        delta[0:1, :] = jnp.sum(product[:HEAD_DIM], axis=0, keepdims=True)
        delta[1:2, :] = jnp.sum(product[HEAD_DIM:], axis=0, keepdims=True)
        dqt[...] = jnp.zeros_like(dqt)

        def key_block(j, reach):
            at = pl.ds(pl.multiple_of(j * bk, bk), bk)
            dk = jnp.zeros((bk, LANES), F32)
            dv = jnp.zeros((bk, LANES), F32)
            scores = [dot(kz[h, at, :], qz[h, reach, :], NT) for h in range(2)]
            grads = [dot(vm[h, at, :], dm[h, reach, :], NT) for h in range(2)]
            for h in range(2):
                weights = jnp.exp(scores[h] - lse_ref[p, h : h + 1, reach])
                dv = dv + dot(weights.astype(BF), dm[h, reach, :])
                ds = (weights * (grads[h] - delta[h : h + 1, reach])).astype(BF)
                dk = dk + dot(ds, qm[h, reach, :])
                head = slice(HEAD_DIM * h, HEAD_DIM * (h + 1))
                dqt[head, reach] += dot(kt[head, at], ds)
            dk_ref[at, lanes] = unrotate(dk, at)
            dv_ref[at, lanes] = dv.astype(BF)

        reaches = {}
        for first in range(0, rows, bk):
            low = max(0, (first - rows // 2 + 1) // LANES * LANES)
            high = min(rows, -(-(first + bk + rows // 2 - 1) // LANES) * LANES)
            reaches.setdefault((low, high), []).append(first // bk)
        for (low, high), blocks in reaches.items():

            def one_block(j, _):
                key_block(j, slice(low, high))
                return 0

            if len(blocks) == 1:
                key_block(blocks[0], slice(low, high))
            else:
                lax.fori_loop(blocks[0], blocks[-1] + 1, one_block, 0)

        dq_ref[:, lanes] = unrotate(dqt[...].T * HEAD_DIM**-0.5, pl.ds(0, rows))

        @pl.when(p > 0)
        def _():
            for entry in keep(p - 1):
                entry.wait()

        for entry in keep(p):
            entry.start()
        for step in range(6):

            @pl.when(p == step)
            def _():
                events(step)

        return 0

    lax.fori_loop(0, width // LANES, head_pair, 0)
    for entry in keep(width // LANES - 1):
        entry.wait()
    for entry in swaps:
        entry.wait_send()
    for pair in scatters:
        for entry in pair:
            entry.drain()


def spread(count, h_two, gy, ga, du, z, mixed, queries, keys, values, upstream, lse, features,
           tables):
    rows, width = mixed.shape
    part = width // count
    outer = count // 4
    hidden = du.shape[1] // 2
    each = 3
    block = hidden // each
    vm = pl.BlockSpec(memory_space=pltpu.VMEM)
    hbm = pl.BlockSpec(memory_space=pl.ANY)
    act = shape_of((rows, width), BF)
    last = shape_of((outer, 2, 2, part, width // 2), BF)
    turn = pltpu.VMEM((width, rows), BF)
    pair = pltpu.VMEM((2, rows, LANES), BF)
    copies = 7 + 12 * (2 + outer - 1)
    held = [h_two, gy, ga, mixed, queries, keys, values, upstream, lse, *features, *tables]
    return pl.pallas_call(
        functools.partial(spread_kernel, count=count, bk=256),
        in_specs=[hbm] * (len(held) + 2),
        out_specs=[hbm] * 3 + [vm] * 2,
        out_shape=[act, act, act, last, shape_of((part, 2 * hidden), F32)],
        scratch_shapes=[pltpu.VMEM(entry.shape, entry.dtype) for entry in held + [act] * 3]
        + [turn, turn, turn, pltpu.VMEM((each, rows, block), BF)]
        + scatter_buffers(outer, 2 * each, part, block)
        + [pltpu.VMEM(last.shape, BF)]
        + [pair] * 5
        + [
            pltpu.VMEM((LANES, rows), BF),
            pltpu.VMEM((8, rows), F32),
            pltpu.VMEM((LANES, rows), F32),
            pltpu.SemaphoreType.DMA((each,)),
            pltpu.SemaphoreType.DMA((len(held),)),
            pltpu.SemaphoreType.DMA((3,)),
            pltpu.SemaphoreType.DMA((2, copies)),
        ],
        compiler_params=pltpu.CompilerParams(
            vmem_limit_bytes=VMEM_LIMIT, collective_id=1, has_side_effects=True
        ),
        name="spread",
    )(h_two, gy, ga, du, z, mixed, queries, keys, values, upstream, lse, *features, *tables)


def closing_kernel(tok_ref, cond_ref, h_in, dq_in, dk_in, dv_in, near_in, far_in, wa_in,
                   dwa_two_in, dx_in, last_in, mid_ref, p_ref, dp_two_ref,
                   rows_ref, qkv_ref, out_ref, ada_ref, norm_ref, square_ref,
                   h_ref, grads, x_vm, c_vm, near_ref, far_ref, wa_ref, dwa_two_ref, dx_ref,
                   turned, mine, dh_vm, dwa_vm, dp_vm, dwt, plane, column,
                   far3, sum3, one3, two3, hop3, sum2, one2, two2, hop2,
                   sum1, one1, two1, hop1, local, sems, *, count, token_total):
    place = my_place(count)
    place["next"] = 0
    z, y, x, core, outer, me = (place[name] for name in ("z", "y", "x", "core", "outer", "me"))
    rows, width = x_vm.shape
    own = width // 2
    part = width // count
    conds = c_vm.shape[1]
    half_cols = ada_ref.shape[1]
    shards = far3.shape[1:]

    start = pl.multiple_of(core * rows, rows)
    columns = near_ref.shape[1]
    pieces = (
        (h_in, h_ref), (dq_in, grads.at[0]), (dk_in, grads.at[1]), (dv_in, grads.at[2]),
        (tok_ref.at[pl.ds(start, rows)], x_vm), (cond_ref.at[pl.ds(start, rows)], c_vm),
        (near_in.at[:, pl.ds(0, columns)], near_ref), (far_in.at[:, pl.ds(0, columns)], far_ref),
        (wa_in.at[pl.ds(width, width)], wa_ref), (dwa_two_in, dwa_two_ref), (dx_in, dx_ref),
        (last_in, sum1),
    )
    loads = [
        pltpu.make_async_copy(src, dst, local.at[index])
        for index, (src, dst) in enumerate(pieces)
    ]
    loads[11].start()
    for load in loads[:11]:
        load.start()

    swaps = [across_cores(place, far3.at[c], sum3.at[c], sems) for c in range(3)]
    scatters = [
        Scatter.halves(place, [ref.at[c] for ref in (sum3, one3, two3, hop3)], sems,
                       "xy" if c % 2 else "yx")
        for c in range(3)
    ]
    scatters.append(Scatter.halves(place, [sum1, one1, two1, hop1], sems, "xy"))
    dwt_rows = dwt.shape[4]
    ada_swap = across_cores(place, dwt.at[:, :, :, 1 - core], sum2, sems)
    cut = dwt_rows // 2
    adas = []
    for first, at in (("x", slice(0, cut)), ("y", slice(cut, dwt_rows))):
        views = [ref.at[(slice(None),) * (len(ref.shape) - 2) + (at,)]
                 for ref in (sum2, one2, two2, hop2)]
        adas.append(Scatter(place, first, *views, sems))
    sends = []

    def copy(src, dst, device):
        index = place["next"]
        place["next"] = index + 1
        entry = pltpu.make_async_remote_copy(
            src_ref=src, dst_ref=dst, send_sem=sems.at[0, index], recv_sem=sems.at[1, index],
            device_id=device, device_id_type=pl.DeviceIdType.MESH,
        )
        sends.append(entry)
        return entry

    row_copies = []
    for i in range(rows // ROW_BLOCK):
        at = pl.ds(i * ROW_BLOCK, ROW_BLOCK)
        row_copies.append(copy(dh_vm.at[at], rows_ref.at[1, at], (me, 1 - core)))
    ada_copy = copy(ada_ref.at[core], ada_ref.at[core], (me, 1 - core))
    spot = 4 * core + 2 * y + x
    plane_copies = []
    for other in range(1, 8):
        yy, xx = lax.rem(y + other // 2, 2), lax.rem(x + other, 2)
        cc = lax.rem(core + other // 4, 2)
        plane_copies.append((4 * z + 2 * yy + xx, cc))
    beyond = [(4 * lax.rem(z + hop, outer) + 2 * y + x, core) for hop in range(1, outer)]

    others = plane_copies + beyond
    greet(others)
    plane_copies = [copy(plane.at[spot], plane.at[spot], device) for device in plane_copies]
    column_copies = [copy(column.at[z], column.at[z], device) for device in beyond]

    def all_of(c, method):
        for entry in scatters[c]:
            getattr(entry, method)()

    loads[0].wait()
    turned[...] = h_ref[...].T
    meet(others)
    loads[11].wait()
    all_of(3, "start")

    def add_near_grad(c):
        swaps[c].wait_recv()
        sum3[c] = (mine[c] + sum3[c].astype(F32)).astype(BF)
        all_of(c, "start")

    for c in range(3):
        loads[1 + c].wait()
        grad = dot(turned[...], grads[c])
        far3[c] = grad[:, own:].reshape(shards).astype(BF)
        swaps[c].start()
        mine[c] = grad[:, :own].reshape(shards)
        if c:
            add_near_grad(c - 1)
    for load in loads[4:10]:
        load.wait()

    def place_rows(start, values):
        at = 0
        while at < values.shape[0]:
            block, low = divmod(start + at, half_cols)
            high = min(half_cols, low + values.shape[0] - at)
            shard, side = divmod(block, 2)
            dwt[shard // 4, (shard // 2) % 2, shard % 2, side, low:high, :] = values[
                at : at + high - low
            ]
            at += high - low

    place_rows(2 * width, dwa_two_ref[:conds, :].T.astype(BF))
    dwa_vm[...] = jnp.zeros_like(dwa_vm)
    dp_vm[...] = jnp.zeros_like(dp_vm)
    dp_vm[1:2, :] = dp_two_ref[0:1, :]
    for block in range(4):
        dp_vm[4 + block : 5 + block, :] = dwa_two_ref[
            conds : conds + 1, block * width : (block + 1) * width
        ]
    gain = p_ref[0:1, :]

    def spread_of(at):
        scale = dot(silu_low(c_vm[at, :]), wa_ref[...], NT) + p_ref[3:4, :]
        return 1.0 + scale

    def first_pass(i, _):
        at = pl.ds(pl.multiple_of(i * ROW_BLOCK, ROW_BLOCK), ROW_BLOCK)
        dh = jnp.zeros((ROW_BLOCK, width), F32)
        for first, w_ref in ((0, near_ref), (own, far_ref)):
            cols = slice(first, first + own)
            for c in range(3):
                dh = dh + dot(grads[c, at, cols], w_ref[:, c * own : (c + 1) * own], NT)
        dh_vm[at, :] = dh
        normal, _ = normalize(x_vm[at, :].astype(F32))
        dn = dh * normal
        summed = cond_rows(silu_low(c_vm[at, :]))
        dwa_vm[:, :width] += dot(summed, dh.astype(BF))
        dwa_vm[:, width:] += dot(summed, (dn * gain).astype(BF))
        dp_vm[0:1, :] += jnp.sum(dn * spread_of(at), axis=0, keepdims=True)

        @pl.when(i == 0)
        def _():
            add_near_grad(2)
            all_of(3, "phase_two")

        @pl.when(i == 2)
        def _():
            all_of(0, "phase_two")
            all_of(3, "phase_hops")

        @pl.when(i == 3)
        def _():
            all_of(1, "phase_two")

        return 0

    lax.fori_loop(0, rows // ROW_BLOCK, first_pass, 0)

    place_rows(0, dwa_vm[:conds, :].T.astype(BF))
    for block in range(2):
        dp_vm[2 + block : 3 + block, :] = dwa_vm[
            conds : conds + 1, block * width : (block + 1) * width
        ]
    lane = lax.broadcasted_iota(jnp.int32, (16, conds), 1)
    for shard in range(count):
        gone = dp_vm[...] if shard == 0 else pltpu.roll(dp_vm[...], width - shard * part, 1)
        gone = jnp.where(lane < part, gone[:, :conds], 0.0).astype(BF)
        for side in range(2):
            dwt[shard // 4, (shard // 2) % 2, shard % 2, side, half_cols:, :] = gone
    ada_swap.start()
    all_of(0, "phase_hops")
    all_of(2, "phase_two")
    ada_swap.wait_recv()
    sum2[...] = sum2[...] + dwt[:, :, :, core]
    for entry in adas:
        entry.start()
    all_of(1, "phase_hops")
    loads[10].wait()

    def events(i):
        if i == 1:
            all_of(2, "phase_hops")
        if i == 2:
            for entry in adas:
                entry.phase_two()
        if i == 3:
            for entry in adas:
                entry.phase_hops()

    def keep(i):
        at = pl.ds(pl.multiple_of(i * ROW_BLOCK, ROW_BLOCK), ROW_BLOCK)
        return pltpu.make_async_copy(dh_vm.at[at], rows_ref.at[0, at], local.at[i])

    def second_pass(i, _):
        at = pl.ds(pl.multiple_of(i * ROW_BLOCK, ROW_BLOCK), ROW_BLOCK)
        normal, rstd = normalize(x_vm[at, :].astype(F32))
        grad = dh_vm[at, :] * gain * spread_of(at)
        dh_vm[at, :] = dx_ref[at, :] + norm_backward(grad, normal, rstd)
        keep(i).start()
        for step in range(rows // ROW_BLOCK):

            @pl.when(i == step)
            def _():
                row_copies[step].start()
                if step < 4:
                    events(step)

        return 0

    lax.fori_loop(0, rows // ROW_BLOCK, second_pass, 0)

    squares = jnp.sum((mid_ref[...] / token_total) ** 2)
    for c in range(4):
        target, at = (qkv_ref, c * own) if c < 3 else (out_ref, 0)
        for entry in scatters[c]:
            total = entry.finish()
            target[:, at : at + total.shape[1]] = total
            squares = squares + jnp.sum((total / token_total) ** 2)
            at += total.shape[1]
    first, second = adas[0].finish(), adas[1].finish()
    rest = half_cols - cut
    ada_ref[core, 0:cut, :] = first
    ada_ref[core, cut:, :] = second[:rest]
    norm_ref[...] = second[rest : rest + 8]
    ada_copy.start()
    squares = squares + jnp.sum((first / token_total) ** 2)
    squares = squares + jnp.sum((second[:rest] / token_total) ** 2)
    squares = squares + 0.5 * jnp.sum((second[rest:] / token_total) ** 2)
    plane[spot] = jnp.full((8, LANES), squares, F32)
    for entry in plane_copies:
        entry.start()
    for entry in plane_copies:
        entry.wait_recv()
    column[z] = jnp.sum(plane[...], axis=0)
    for entry in column_copies:
        entry.start()
    for entry in column_copies:
        entry.wait_recv()
    square_ref[...] = jnp.sum(column[...], axis=0)
    ada_copy.wait_recv()
    for i, entry in enumerate(row_copies):
        keep(i).wait()
        entry.wait_recv()
    for entry in swaps + [ada_swap] + sends:
        entry.wait_send()
    for entry in [part for pair in scatters for part in pair] + adas:
        entry.drain()


def closing(count, tokens, cond, h_one, grads, dx, wa, norms, near, far, dwa_two, dp_two,
            last, middle_sum, token_total):
    rows, width = dx.shape
    conds = cond.shape[1]
    part = width // count
    outer = count // 4
    half_cols = wa.shape[0] // count // 2
    vm = pl.BlockSpec(memory_space=pltpu.VMEM)
    hbm = pl.BlockSpec(memory_space=pl.ANY)
    copies = 5 + 10 * (2 + outer - 1) + rows // ROW_BLOCK + 1 + 7 + outer - 1
    act = pltpu.VMEM((rows, width), BF)
    half_weights = pltpu.VMEM((width, 3 * width // 2), BF)
    return pl.pallas_call(
        functools.partial(closing_kernel, count=count, token_total=token_total),
        in_specs=[hbm] * 12 + [vm] * 3,
        out_specs=[hbm] + [vm] * 5,
        out_shape=[
            shape_of((2, rows, width), F32),
            shape_of((part, 3 * width // 2), F32),
            shape_of((part, width // 2), F32),
            shape_of((2, half_cols, conds), F32),
            shape_of((8, conds), F32),
            shape_of((8, LANES), F32),
        ],
        scratch_shapes=[
            act, pltpu.VMEM((3, rows, width), BF), act,
            pltpu.VMEM((rows, conds), BF),
            half_weights, half_weights,
            pltpu.VMEM((width, conds), BF),
            pltpu.VMEM(dwa_two.shape, F32),
            pltpu.VMEM((rows, width), F32),
            pltpu.VMEM((width, rows), BF),
            pltpu.VMEM((3, outer, 2, 2, part, width // 2), F32),
            pltpu.VMEM((rows, width), F32),
            pltpu.VMEM((conds + 16, 2 * width), F32),
            pltpu.VMEM((16, width), F32),
            pltpu.VMEM((outer, 2, 2, 2, half_cols + 16, conds), BF),
            pltpu.VMEM((8, 8, LANES), F32),
            pltpu.VMEM((outer, 8, LANES), F32),
        ]
        + scatter_buffers(outer, 3, part, width // 2)
        + scatter_buffers(outer, None, half_cols + 16, conds)[1:]
        + scatter_buffers(outer, None, part, width // 2)[1:]
        + [pltpu.SemaphoreType.DMA((12,)), pltpu.SemaphoreType.DMA((2, copies))],
        compiler_params=pltpu.CompilerParams(
            vmem_limit_bytes=VMEM_LIMIT, collective_id=2, has_side_effects=True
        ),
        name="closing",
    )(tokens, cond, h_one, *grads, near, far, wa, dwa_two, dx, last, middle_sum, norms, dp_two)


def update_kernel(half, step, ina_ref, inb_ref, resa_ref, resb_ref, up_ref, down_ref, qkv_ref,
                  out_ref, ada_ref, norm_ref, square_ref, *refs, token_total):
    state, (grad_out, res_out, norm_out), new = refs[:18], refs[18:21], refs[21:]
    i, steps = pl.program_id(0), pl.num_programs(0)
    here = (i // (steps // 2)) == half[0]

    @pl.when(here)
    def _():
        grad_out[...] = ina_ref[0]
        res_out[...] = resa_ref[...]

    @pl.when(jnp.logical_not(here))
    def _():
        grad_out[...] = inb_ref[0]
        res_out[...] = resb_ref[...]

    grad_norm = jnp.sqrt(square_ref[0:1, :])
    norm_out[...] = grad_norm
    clip_factor = jnp.minimum(1.0, clip_limit / (grad_norm + 1e-06))[:, 0:1] / token_total
    count = jnp.full((1, LANES), step[0], jnp.int32).astype(F32)
    fix_one = (1.0 - jnp.exp(count * math.log(0.9)))[:, 0:1]
    fix_two = (1.0 - jnp.exp(count * math.log(0.999)))[:, 0:1]

    def update(index, grad):
        entry = [ref[...] for ref in state[3 * index : 3 * index + 3]]
        values = adam_update(*entry, grad, clip_factor, fix_one, fix_two, step_rates[index],
                             decay_rates[index])
        for ref, value in zip(new[3 * index : 3 * index + 3], values):
            ref[...] = value

    update(0, ada_ref[...])
    update(4, up_ref[...])
    update(5, down_ref[...])

    @pl.when(i < 3)
    def _():
        update(2, qkv_ref[...][None])

    @pl.when(i == 3)
    def _():
        update(1, norm_ref[:, : state[3].shape[1]])
        update(3, out_ref[...])


def update_stage(half, step, input_rows, result, result_far, sums, state, token_total):
    rows, width = result.shape
    middle_sum, qkv_sum, out_sum, ada_sum, norm_sum, squares = sums
    ada_sum = ada_sum.reshape(-1, ada_sum.shape[-1])
    steps = 4
    blocks = steps // 2
    size = rows // blocks
    hidden = middle_sum.shape[1] // 2

    def side(match, lead):
        def index(i, half, step):
            same = (i // blocks == half[0]) == match
            at = jnp.where(same, i % blocks, jnp.where(i < blocks, 0, blocks - 1))
            return lead + (at, 0)

        return index

    block = (size, width)
    out = pl.BlockSpec(block, lambda i, half, step: (i, 0))
    fixed = lambda entry: pl.BlockSpec(entry.shape, lambda *_, n=entry.ndim: (0,) * n)
    slab = pl.BlockSpec((state[12].shape[0], hidden // steps), lambda i, *_: (0, i))
    next_slab = pl.BlockSpec((state[12].shape[0], hidden // steps), lambda i, *_: (0, steps + i))
    third = (state[6].shape[1], state[6].shape[2])
    qkv_spec = pl.BlockSpec((1,) + third, lambda i, *_: (jnp.minimum(i, 2), 0, 0))
    ada_spec = pl.BlockSpec((ada_sum.shape[0] // steps, ada_sum.shape[1]), lambda i, *_: (i, 0))
    specs = (
        [ada_spec] * 3 + [fixed(state[3])] * 3 + [qkv_spec] * 3 + [fixed(state[9])] * 3
        + [slab] * 6
    )
    return pl.pallas_call(
        functools.partial(update_kernel, token_total=token_total),
        grid_spec=pltpu.PrefetchScalarGridSpec(
            num_scalar_prefetch=2,
            grid=(steps,),
            in_specs=[
                pl.BlockSpec((1,) + block, side(True, (0,))),
                pl.BlockSpec((1,) + block, side(False, (1,))),
                pl.BlockSpec(block, side(True, ())),
                pl.BlockSpec(block, side(False, ())),
                slab, next_slab,
                pl.BlockSpec(third, lambda i, *_: (0, jnp.minimum(i, 2))),
                fixed(out_sum), ada_spec, fixed(norm_sum), fixed(squares),
            ] + specs,
            out_specs=[out, out, pl.BlockSpec((1, LANES), lambda *_: (0, 0))] + specs,
        ),
        out_shape=[shape_of((2 * rows, width), F32), shape_of((2 * rows, width), BF),
                   shape_of((1, LANES), F32)]
        + [shape_of(entry.shape, F32) for entry in state],
        compiler_params=params(),
        name="update_stage",
    )(half, step, input_rows, input_rows, result, result_far, middle_sum, middle_sum, qkv_sum,
      out_sum, ada_sum, norm_sum, squares, *state)


def factors(count):
    return (count // 4, 2, 2)


def swap_mp(value):
    return lax.ppermute(value, "mp", [(0, 1), (1, 0)])


def swap_dp(value, distance):
    count = lax.axis_size("dp")
    return lax.ppermute(value, "dp", [(i, i ^ distance) for i in range(count)])


def turn_dp(value, distance):
    count = lax.axis_size("dp")
    return lax.ppermute(value, "dp", [(i, (i + distance) % count) for i in range(count)])


def pick(value, index, axis):
    return lax.dynamic_index_in_dim(value, index, axis, keepdims=False)


def scatter_sum(parts, order):
    count = lax.axis_size("dp")
    outer, mid, inner = factors(count)
    me = lax.axis_index("dp")
    place = {4: me // 4, 2: (me // 2) % 2, 1: me % 2}

    def widen(part):
        return part.reshape((outer, mid, inner) + part.shape[1:]).astype(F32)

    total = widen(parts[0])
    for part in parts[1:]:
        total = total + widen(part)
    for distance in order:
        axis = 1 if (distance == 2 or total.ndim == 4) else 2
        gone = pick(total, 1 - place[distance], axis).astype(BF)
        total = pick(total, place[distance], axis) + swap_dp(gone, distance).astype(F32)
    arrived = [
        turn_dp(pick(total, (place[4] + hop) % outer, 0).astype(BF), 4 * hop)
        for hop in range(1, outer)
    ]
    total = pick(total, place[4], 0)
    for piece in arrived:
        total = total + piece.astype(F32)
    return total


def scatter_halves(near, far_sum):
    count = lax.axis_size("dp")
    width, columns = near.shape
    cut = columns // 2 // LANES * LANES
    shards = lambda value: value.reshape(count, width // count, value.shape[1])
    first = scatter_sum([shards(near[:, :cut]), shards(far_sum[:, :cut])], (2, 1))
    second = scatter_sum([shards(near[:, cut:]), shards(far_sum[:, cut:])], (1, 2))
    return jnp.concatenate([first, second], axis=1)


def sum_everywhere(value):
    value = value + swap_mp(value)
    distance = 1
    while distance < lax.axis_size("dp"):
        value = value + swap_dp(value, distance)
        distance *= 2
    return value


def in_order(half, near, far):
    first = jnp.where(half == 0, near, far)
    second = jnp.where(half == 0, far, near)
    return jnp.concatenate([first, second], axis=0)


def per_device(
    tokens, cond, segments, out_grad, step,
    ada_weight, ada_first, ada_second,
    norm_params, norm_first, norm_second,
    qkv_weight, qkv_first, qkv_second,
    out_weight, out_first, out_second,
    up_weight, up_first, up_second,
    down_weight, down_first, down_second,
):
    count = lax.axis_size("dp")
    width = tokens.shape[1]
    rows = tokens.shape[0] // 2
    conds = cond.shape[1]
    part = width // count
    half = lax.axis_index("mp")
    half_ref = half.reshape(1).astype(jnp.int32)
    token_total = float(tokens.shape[0] * count)

    fused = count == 16 and part % 16 == 0 and ada_weight.shape[1] % 32 == 0
    if fused:
        (h_one, queries, keys, values, mixed, near, far, wa, cosines, sines, query_lanes,
         key_lanes, up_near, up_far, down_near, down_far, lse, norms) = opening(
            count, tokens, cond, segments, rope_constants(rows),
            (ada_weight.T, norm_params, qkv_weight, out_weight.T, up_weight, down_weight.T),
        )
        wa = wa.reshape(-1, conds)
        features, tables = (query_lanes, key_lanes), (cosines, sines)
    else:
        ada_shard = ada_weight.T.astype(BF)
        small_shard = jnp.concatenate(
            [
                qkv_weight.astype(BF).transpose(1, 0, 2).reshape(part, -1),
                jnp.pad(norm_params.astype(BF).T, ((0, 0), (0, LANES - 8))),
            ],
            axis=1,
        )
        down_shard = jnp.concatenate([down_weight.astype(BF).T, out_weight.astype(BF).T], axis=1)
        segment = pick(segments, half, 0)
        features = document_features(segment)
        tables = rope_tables(rows)
        wa = lax.all_gather(ada_shard, "dp", axis=0, tiled=True)
        near = lax.all_gather(small_shard, "dp", axis=0, tiled=True)
        far = swap_mp(near)
        norms = near[:, -LANES:].T[:8].astype(F32)
        up_near = lax.all_gather(up_weight.astype(BF), "dp", axis=0, tiled=True)
        down_near = lax.all_gather(down_shard, "dp", axis=0, tiled=True)
        up_far, down_far = swap_mp(up_near), swap_mp(down_near)
        h_one, queries, keys, values = first_stage(
            half_ref, tokens, cond, wa, norms, near, far, tables
        )
        mixed, lse = attend(queries, keys, values, segment, features)
    result, dx, upstream, z, gy, h_two, du, ga, dwa_two, dp_two = middle_stage(
        half_ref, tokens, out_grad, cond, mixed, wa, norms, up_near, up_far, down_near, down_far
    )
    result_far = swap_mp(result)

    block = width // 2
    if fused:
        *grads, last, middle_sum = spread(
            count, h_two, gy, ga, du, z, mixed, queries, keys, values, upstream, lse, features,
            tables,
        )
    else:
        steps = du.shape[1] // 2 // block

        def middle_grads(which, name):
            return weight_grads(
                [gy, h_two, ga], [du, z, mixed],
                [(steps, 1, 0, which * steps), (steps, 0, 1, which * steps), (1, 2, 2, which)],
                block, name,
            )

        middle_far = swap_mp(middle_grads(1, "middle_grads_far"))
        middle_near = middle_grads(0, "middle_grads_near")
        middle_sum = scatter_halves(middle_near, middle_far)
        grads = attend_back(
            queries, keys, values, upstream, mixed, lse, segment, features, tables
        )

    if fused:
        input_rows, first_sum, out_sum, ada_halves, norm_sum, squares = closing(
            count, tokens, cond, h_one, grads, dx, wa, norms, near, far, dwa_two, dp_two,
            last, middle_sum, token_total,
        )
        turn = lambda group: tuple(entry.T for entry in group)
        ada_state = (ada_weight, ada_first, ada_second)
        out_state = (out_weight, out_first, out_second)
        down_state = (down_weight, down_first, down_second)
        state = (
            *turn(ada_state), norm_params, norm_first, norm_second,
            qkv_weight, qkv_first, qkv_second, *turn(out_state), up_weight, up_first, up_second,
            *turn(down_state),
        )
        input_grad, result, grad_norm, *new = update_stage(
            half_ref, step, input_rows, result, result_far,
            (middle_sum, first_sum, out_sum, ada_halves, norm_sum, squares), state, token_total,
        )
        return (
            result, input_grad, grad_norm[0, :1],
            *turn(new[:3]), *new[3:9], *turn(new[9:12]), *new[12:15], *turn(new[15:]),
        )

    def first_grads(which, name):
        return weight_grads(
            [h_one], list(grads), [(1, 0, index, which) for index in range(3)], block, name
        )

    first_far = swap_mp(first_grads(1, "first_grads_far"))
    first_near = first_grads(0, "first_grads_near")
    first_sum = scatter_halves(first_near, first_far)

    input_grad, dwa_one, dp_one = last_stage(
        half_ref, tokens, cond, dx, grads, wa, norms, near, far
    )
    input_far = swap_mp(input_grad)

    dwa = jnp.concatenate([dwa_one, dwa_two], axis=1)
    ada_cols = dwa.shape[1] // count
    dwa_rows = dwa[:conds].T.astype(BF).reshape(count, 2, ada_cols // 2, conds)
    norm_rows = jnp.concatenate(
        [dp_one[0:1], dp_two[0:1], dwa[conds].reshape(6, width)], axis=0
    ).astype(BF)
    norm_rows = norm_rows.reshape(8, count, part).transpose(1, 0, 2)
    norm_rows = jnp.pad(norm_rows, ((0, 0), (0, 0), (0, conds - part)))
    ada_near = jnp.concatenate([pick(dwa_rows, half, 1), norm_rows], axis=1)
    ada_far = swap_mp(jnp.concatenate([pick(dwa_rows, 1 - half, 1), norm_rows], axis=1))
    ada_sum = scatter_sum([ada_near, ada_far], (2, 1))
    ada_half, norm_sum = ada_sum[: ada_cols // 2], ada_sum[ada_cols // 2 :, :part]
    ada_rows = in_order(half, ada_half, swap_mp(ada_half))

    wide_cols = du.shape[1] // 2
    up_mean = middle_sum[:, :wide_cols] / token_total
    down_mean = middle_sum[:, wide_cols : 2 * wide_cols] / token_total
    out_mean = middle_sum[:, 2 * wide_cols :] / token_total
    qkv_mean = first_sum / token_total
    ada_mean = ada_rows / token_total
    norm_mean = norm_sum / token_total
    local_sq = (
        jnp.sum(qkv_mean * qkv_mean)
        + jnp.sum(out_mean * out_mean)
        + jnp.sum(up_mean * up_mean)
        + jnp.sum(down_mean * down_mean)
        + 0.5 * (jnp.sum(ada_mean * ada_mean) + jnp.sum(norm_mean * norm_mean))
    )
    grad_norm = jnp.sqrt(sum_everywhere(jnp.full((8, LANES), local_sq, F32))[0, 0])
    clip_factor = jnp.minimum(1.0, clip_limit / (grad_norm + 1e-06))
    step_count = step[0].astype(F32)
    fix_one = 1.0 - jnp.exp(step_count * math.log(0.9))
    fix_two = 1.0 - jnp.exp(step_count * math.log(0.999))

    ada_grad = ada_mean.T
    qkv_grad = qkv_mean.reshape(part, 3, -1).transpose(1, 0, 2)
    state = (
        (ada_weight, ada_first, ada_second, ada_grad),
        (norm_params, norm_first, norm_second, norm_mean),
        (qkv_weight, qkv_first, qkv_second, qkv_grad),
        (out_weight, out_first, out_second, out_mean.T),
        (up_weight, up_first, up_second, up_mean),
        (down_weight, down_first, down_second, down_mean.T),
    )
    outputs = [
        in_order(half, result, result_far),
        in_order(half, input_grad, input_far),
        grad_norm.reshape(1),
    ]
    for index, entry in enumerate(state):
        outputs += adam_update(
            *entry, clip_factor, fix_one, fix_two, step_rates[index], decay_rates[index]
        )
    return tuple(outputs)


def solution(mesh):
    column = (P(None, "dp"),) * 3
    weights = (
        column
        + column
        + (P(None, "dp", "mp"),) * 3
        + (P("mp", "dp"),) * 3
        + (P("dp", "mp"),) * 3
        + (P("mp", "dp"),) * 3
    )
    row = P("dp", None)
    return jax.shard_map(
        per_device,
        mesh=mesh,
        in_specs=(row, row, row, row, P()) + weights,
        out_specs=(row, row, P()) + weights,
        check_vma=False,
    )
```

```python
import functools
import math

import jax
import jax.numpy as jnp
import numpy as np
from jax import lax
from jax.experimental import pallas as pl
from jax.experimental.pallas import tpu as pltpu
from jax.sharding import PartitionSpec as P

HEAD_DIM = 64
LANES = 128
MASKED = -1e30
ROW_BLOCK = 256
VMEM_LIMIT = 64_000_000
clip_limit = 1.0
step_rates = (0.075, 0.75, 0.075, 0.25, 0.075, 0.075)
decay_rates = (0.01, 0.0, 0.01, 0.01, 0.01, 0.01)

F32 = jnp.float32
BF = jnp.bfloat16
NN = (((1,), (0,)), ((), ()))
NT = (((1,), (1,)), ((), ()))


def dot(left, right, dims=NN):
    return lax.dot_general(left, right, dims, preferred_element_type=F32)


def shape_of(shape, dtype):
    return jax.ShapeDtypeStruct(shape, dtype)


def resident(shape, index):
    return pl.BlockSpec(shape, lambda *_: index, pipeline_mode=pl.Buffered(1))


def params():
    return pltpu.CompilerParams(vmem_limit_bytes=VMEM_LIMIT)


def adam_update(weight, first, second, grad, clip_factor, fix_one, fix_two, rate, decay):
    clipped = grad * clip_factor
    first_new = 0.9 * first + 0.1 * clipped
    second_new = 0.999 * second + 0.001 * clipped * clipped
    update = first_new / fix_one / (jnp.sqrt(second_new / fix_two) + 1e-08) + decay * weight
    return (weight - rate * update, first_new, second_new)


def rope_tables(length):
    half = HEAD_DIM // 2
    inverse = jnp.exp(jnp.arange(half, dtype=F32) * (-2.0 * math.log(10000.0) / HEAD_DIM))
    angles = jnp.arange(length, dtype=F32)[:, None] * inverse[None, :]
    cosines, sines = jnp.cos(angles), jnp.sin(angles)
    return (
        jnp.concatenate([cosines] * 4, axis=1),
        jnp.concatenate([-sines, sines, -sines, sines], axis=1),
    )


def rope_constants(length, fine=32):
    half = HEAD_DIM // 2
    inverse = np.exp(np.arange(half) * (-2.0 * math.log(10000.0) / HEAD_DIM))
    sign = np.repeat([-1.0, 1.0, -1.0, 1.0], half)
    tables = []
    for positions in (np.arange(0, length, fine), np.arange(fine)):
        angles = np.tile(positions[:, None] * inverse[None, :], (1, 4))
        tables += [np.cos(angles), np.sin(angles) * sign]
    return [jnp.asarray(table, F32) for table in tables]


def swap_halves(values):
    width = values.shape[1]
    lane = lax.broadcasted_iota(jnp.int32, values.shape, 1)
    ahead = pltpu.roll(values, width - HEAD_DIM // 2, 1)
    behind = pltpu.roll(values, HEAD_DIM // 2, 1)
    return jnp.where(lane % HEAD_DIM < HEAD_DIM // 2, ahead, behind)


def silu_low(cond):
    value = cond.astype(F32)
    return (value / (1.0 + jnp.exp(-value))).astype(BF)


def normalize(rows):
    centre = rows - jnp.mean(rows, axis=-1, keepdims=True)
    scale = lax.rsqrt(jnp.mean(centre * centre, axis=-1, keepdims=True) + 1e-05)
    return centre * scale, scale


def norm_backward(grad, normal, scale):
    return scale * (
        grad
        - jnp.mean(grad, axis=-1, keepdims=True)
        - normal * jnp.mean(grad * normal, axis=-1, keepdims=True)
    )


def cond_rows(cond):
    return jnp.concatenate([cond.T, jnp.ones((16, cond.shape[0]), BF)], axis=0)


def first_kernel(half, x_ref, c_ref, wa_ref, p_ref, wqa_ref, wqb_ref, cos_ref, sin_ref,
                 h_ref, q_ref, k_ref, v_ref):
    width = x_ref.shape[1]
    own = width // 2
    cond = silu_low(c_ref[...])
    mod = dot(cond, wa_ref[0 : 2 * width, :], NT)
    shift = mod[:, :width] + p_ref[2:3, :]
    scale = mod[:, width:] + p_ref[3:4, :]
    normal, _ = normalize(x_ref[...].astype(F32))
    h = (normal * p_ref[0:1, :] * (1.0 + scale) + shift).astype(BF)
    h_ref[...] = h
    cos = jnp.concatenate([cos_ref[...]] * (own // LANES), axis=1)
    sin = jnp.concatenate([sin_ref[...]] * (own // LANES), axis=1)
    for start, w_ref in ((0, wqa_ref), (own, wqb_ref)):
        cols = slice(start, start + own)
        query = dot(h, w_ref[:, 0:own])
        query = query * cos + swap_halves(query) * sin
        q_ref[:, cols] = (query * HEAD_DIM**-0.5).astype(BF)
        key = dot(h, w_ref[:, own : 2 * own])
        k_ref[:, cols] = (key * cos + swap_halves(key) * sin).astype(BF)
        v_ref[:, cols] = dot(h, w_ref[:, 2 * own :]).astype(BF)


def first_stage(half, tokens, cond, wa, norms, near, far, tables):
    width = tokens.shape[1]
    rows = tables[0].shape[0]
    blocks = rows // ROW_BLOCK
    mine = lambda i, half: (half[0] * blocks + i, 0)
    plain = lambda i, half: (i, 0)
    row = pl.BlockSpec((ROW_BLOCK, width), plain)
    return pl.pallas_call(
        first_kernel,
        grid_spec=pltpu.PrefetchScalarGridSpec(
            num_scalar_prefetch=1,
            grid=(blocks,),
            in_specs=[
                pl.BlockSpec((ROW_BLOCK, width), mine),
                pl.BlockSpec((ROW_BLOCK, cond.shape[1]), mine),
                resident(wa.shape, (0, 0)),
                resident(norms.shape, (0, 0)),
                resident((width, 3 * width // 2), (0, 0)),
                resident((width, 3 * width // 2), (0, 0)),
                pl.BlockSpec((ROW_BLOCK, LANES), plain),
                pl.BlockSpec((ROW_BLOCK, LANES), plain),
            ],
            out_specs=[row] * 4,
        ),
        out_shape=[shape_of((rows, width), BF)] * 4,
        compiler_params=params(),
        name="first_stage",
    )(half, tokens, cond, wa, norms, near, far, *tables)


def split_heads(pair, other):
    low = lax.broadcasted_iota(jnp.int32, pair.shape, 1) < HEAD_DIM
    return jnp.where(low, pair, other), jnp.where(low, other, pair)


def attend_kernel(lo_ref, hi_ref, q_ref, k_ref, v_ref, fq_ref, fk_ref, o_ref, lse_ref,
                  qz, kz, vt, *, bq, bk):
    length = q_ref.shape[0]
    qz[0], qz[1] = split_heads(q_ref[...], fq_ref[...])
    kz[0], kz[1] = split_heads(k_ref[...], fk_ref[...])
    vt[...] = v_ref[...].T

    def query_block(i, _):
        off = pl.multiple_of(i * bq, bq)
        queries = [qz[h, pl.ds(off, bq), :] for h in range(2)]

        def key_block(j, carry):
            koff = pl.multiple_of(j * bk, bk)
            scores = [dot(kz[h, pl.ds(koff, bk), :], queries[h], NT) for h in range(2)]
            out = []
            for h in range(2):
                top, total, mixed = carry[3 * h : 3 * h + 3]
                new_top = jnp.maximum(top, jnp.max(scores[h], axis=0, keepdims=True))
                weights = jnp.exp(scores[h] - new_top)
                fade = jnp.exp(top - new_top)
                total = total * fade + jnp.sum(weights, axis=0, keepdims=True)
                values = vt[HEAD_DIM * h : HEAD_DIM * (h + 1), pl.ds(koff, bk)]
                mixed = mixed * fade + dot(values, weights.astype(BF))
                out += [new_top, total, mixed]
            return tuple(out)

        start = (
            jnp.full((1, bq), -3e38, F32),
            jnp.zeros((1, bq), F32),
            jnp.zeros((HEAD_DIM, bq), F32),
        )
        done = lax.fori_loop(lo_ref[i], hi_ref[i], key_block, start * 2)
        mixed = jnp.concatenate([done[2] / done[1], done[5] / done[4]], axis=0)
        o_ref[pl.ds(off, bq), :] = mixed.T.astype(BF)
        lse_ref[0, 0:1, pl.ds(off, bq)] = done[0] + jnp.log(done[1])
        lse_ref[0, 1:2, pl.ds(off, bq)] = done[3] + jnp.log(done[4])
        return 0

    lax.fori_loop(0, length // bq, query_block, 0)


def block_ranges(segment, block, other):
    first, last = segment[::block], segment[block - 1 :: block]
    low = jnp.sum(segment[None, :] < first[:, None], axis=1)
    high = jnp.sum(segment[None, :] <= last[:, None], axis=1)
    return (low // other).astype(jnp.int32), ((high + other - 1) // other).astype(jnp.int32)


def document_features(segment):
    lane = lax.broadcasted_iota(jnp.int32, (segment.shape[0], LANES), 1) % HEAD_DIM
    same = lane == segment[:, None]
    query = jnp.where(same, 1.0, 0.0).astype(BF)
    key = jnp.where((lane < 4) & ~same, MASKED, 0.0).astype(BF)
    return query, key


def attend(queries, keys, values, segment, features, bq=1024, bk=512):
    length, width = queries.shape
    bq, bk = min(bq, length), min(bk, length)
    pairs = width // LANES
    low, high = block_ranges(segment, bq, bk)
    pair = pl.BlockSpec((length, LANES), lambda p, *_: (0, p))
    fixed = pl.BlockSpec((length, LANES), lambda p, *_: (0, 0))
    scratch = pltpu.VMEM((2, length, LANES), BF)
    return pl.pallas_call(
        functools.partial(attend_kernel, bq=bq, bk=bk),
        grid_spec=pltpu.PrefetchScalarGridSpec(
            num_scalar_prefetch=2,
            grid=(pairs,),
            in_specs=[pair, pair, pair, fixed, fixed],
            out_specs=[pair, pl.BlockSpec((1, 2, length), lambda p, *_: (p, 0, 0))],
            scratch_shapes=[scratch, scratch, pltpu.VMEM((LANES, length), BF)],
        ),
        out_shape=[shape_of((length, width), BF), shape_of((pairs, 2, length), F32)],
        compiler_params=params(),
        name="attend",
    )(low, high, queries, keys, values, *features)


def attend_back_kernel(lo_ref, hi_ref, q_ref, k_ref, v_ref, do_ref, o_ref, lse_ref, fq_ref,
                       fk_ref, cos_ref, sin_ref, dq_ref, dk_ref, dv_ref,
                       qz, kz, qm, dm, vm, kt, delta, dqt, *, bq, bk):
    length = q_ref.shape[0]
    zero = jnp.zeros((length, LANES), BF)
    qz[0], qz[1] = split_heads(q_ref[...], fq_ref[...])
    kz[0], kz[1] = split_heads(k_ref[...], fk_ref[...])
    qm[0], qm[1] = split_heads(q_ref[...], zero)
    dm[0], dm[1] = split_heads(do_ref[...], zero)
    vm[0], vm[1] = split_heads(v_ref[...], zero)
    kt[...] = k_ref[...].T
    product = (do_ref[...].astype(F32) * o_ref[...].astype(F32)).T
    delta[0:1, :] = jnp.sum(product[:HEAD_DIM], axis=0, keepdims=True)
    delta[1:2, :] = jnp.sum(product[HEAD_DIM:], axis=0, keepdims=True)
    dqt[...] = jnp.zeros_like(dqt)

    def unrotate(grad, off, rows):
        cos, sin = cos_ref[pl.ds(off, rows), :], sin_ref[pl.ds(off, rows), :]
        return (grad * cos - swap_halves(grad) * sin).astype(BF)

    def key_block(j, _):
        koff = pl.multiple_of(j * bk, bk)
        keys = [kz[h, pl.ds(koff, bk), :] for h in range(2)]
        values = [vm[h, pl.ds(koff, bk), :] for h in range(2)]

        def query_block(i, carry):
            dk, dv = carry
            off = pl.multiple_of(i * bq, bq)
            scores = [dot(keys[h], qz[h, pl.ds(off, bq), :], NT) for h in range(2)]
            grads = [dot(values[h], dm[h, pl.ds(off, bq), :], NT) for h in range(2)]
            for h in range(2):
                weights = jnp.exp(scores[h] - lse_ref[0, h : h + 1, pl.ds(off, bq)])
                dv = dv + dot(weights.astype(BF), dm[h, pl.ds(off, bq), :])
                ds = (weights * (grads[h] - delta[h : h + 1, pl.ds(off, bq)])).astype(BF)
                dk = dk + dot(ds, qm[h, pl.ds(off, bq), :])
                head = slice(HEAD_DIM * h, HEAD_DIM * (h + 1))
                dqt[head, pl.ds(off, bq)] += dot(kt[head, pl.ds(koff, bk)], ds)
            return dk, dv

        zeros = jnp.zeros((bk, LANES), F32)
        dk, dv = lax.fori_loop(lo_ref[j], hi_ref[j], query_block, (zeros, zeros))
        dk_ref[pl.ds(koff, bk), :] = unrotate(dk, koff, bk)
        dv_ref[pl.ds(koff, bk), :] = dv.astype(BF)
        return 0

    lax.fori_loop(0, length // bk, key_block, 0)
    dq_ref[...] = unrotate(dqt[...].T * HEAD_DIM**-0.5, 0, length)


def attend_back(queries, keys, values, upstream, mixed, lse, segment, features, tables,
                bq=512, bk=256):
    length, width = queries.shape
    bq, bk = min(bq, length), min(bk, length)
    pairs = width // LANES
    low, high = block_ranges(segment, bk, bq)
    pair = pl.BlockSpec((length, LANES), lambda p, *_: (0, p))
    fixed = pl.BlockSpec((length, LANES), lambda p, *_: (0, 0))
    scratch = pltpu.VMEM((2, length, LANES), BF)
    return pl.pallas_call(
        functools.partial(attend_back_kernel, bq=bq, bk=bk),
        grid_spec=pltpu.PrefetchScalarGridSpec(
            num_scalar_prefetch=2,
            grid=(pairs,),
            in_specs=[pair] * 5
            + [pl.BlockSpec((1, 2, length), lambda p, *_: (p, 0, 0))]
            + [fixed] * 4,
            out_specs=[pair] * 3,
            scratch_shapes=[scratch] * 5
            + [
                pltpu.VMEM((LANES, length), BF),
                pltpu.VMEM((8, length), F32),
                pltpu.VMEM((LANES, length), F32),
            ],
        ),
        out_shape=[shape_of((length, width), BF)] * 3,
        compiler_params=params(),
        name="attend_back",
    )(low, high, queries, keys, values, upstream, mixed, lse, *features, *tables)


def middle_kernel(half, x_ref, g_ref, c_ref, o_ref, wa_ref, p_ref, woa_ref, wob_ref, w1a_in,
                  w1b_in, w2a_in, w2b_in,
                  res_ref, dx_ref, do_ref, z_ref, gy_ref, h_ref, du_ref, ga_ref, dwa_ref,
                  dp_ref, slope, w1a_ref, w1b_ref, w2a_ref, w2b_ref, sems, *, chunk):
    width = x_ref.shape[1]
    own = width // 2
    hidden = w1a_ref.shape[1]
    loads = [
        pltpu.make_async_copy(src.at[:, pl.ds(0, hidden)], dst, sems.at[index])
        for index, (src, dst) in enumerate(
            ((w1a_in, w1a_ref), (w2a_in, w2a_ref), (w1b_in, w1b_ref), (w2b_in, w2b_ref))
        )
    ]

    @pl.when(pl.program_id(0) == 0)
    def _():
        for load in loads:
            load.start()

    cond = silu_low(c_ref[...])

    def modulation(block):
        rows = wa_ref[block * width : (block + 1) * width, :]
        return dot(cond, rows, NT) + p_ref[block + 2 : block + 3, :]

    gate_one, shift, scale, gate_two = (modulation(block) for block in (2, 3, 4, 5))
    branch = dot(o_ref[:, :own], woa_ref[...], NT) + dot(o_ref[:, own:], wob_ref[...], NT)
    middle = x_ref[...].astype(F32) + gate_one * branch
    normal, rstd = normalize(middle)
    gain = p_ref[1:2, :]
    spread = 1.0 + scale
    h = (normal * gain * spread + shift).astype(BF)
    h_ref[...] = h.T

    @pl.when(pl.program_id(0) == 0)
    def _():
        for load in loads:
            load.wait()

    root = math.sqrt(2.0 / math.pi)
    out = jnp.zeros_like(middle)
    for start, up_ref, down_ref in ((0, w1a_ref, w2a_ref), (hidden, w1b_ref, w2b_ref)):
        for at in range(0, hidden, chunk):
            u = dot(h, up_ref[:, at : at + chunk])
            square = u * u
            flat = jnp.tanh(u * (0.044715 * root * square + root))
            half_up = 0.5 * flat + 0.5
            z = (u * half_up).astype(BF)
            z_ref[:, start + at : start + at + chunk] = z
            bend = u * (6.0 * 0.044715 * root * square + 2.0 * root)
            slope[:, start + at : start + at + chunk] = (
                half_up * (bend * (1.0 - half_up) + 1.0)
            ).astype(slope.dtype)
            out = out + dot(z, down_ref[:, at : at + chunk], NT)

    g = g_ref[...].astype(F32)
    res_ref[...] = (middle + gate_two * out).astype(BF)
    gy = (gate_two * g).astype(BF)
    gy_ref[...] = gy.T
    dgate_two = (g * out).astype(BF)

    dh = jnp.zeros_like(middle)
    for start, up_ref, down_ref in ((0, w1a_ref, w2a_ref), (hidden, w1b_ref, w2b_ref)):
        for at in range(0, hidden, chunk):
            dz = dot(gy, down_ref[:, at : at + chunk])
            du = (dz * slope[:, start + at : start + at + chunk]).astype(BF)
            du_ref[:, start + at : start + at + chunk] = du
            dh = dh + dot(du, up_ref[:, at : at + chunk], NT)

    dn = dh * normal
    dx = g + norm_backward(dh * gain * spread, normal, rstd)
    dx_ref[...] = dx
    ga = (gate_one * dx).astype(BF)
    ga_ref[...] = ga.T
    do_ref[:, :own] = dot(ga, woa_ref[...]).astype(BF)
    do_ref[:, own:] = dot(ga, wob_ref[...]).astype(BF)

    @pl.when(pl.program_id(0) == 0)
    def _():
        dwa_ref[...] = jnp.zeros_like(dwa_ref)
        dp_ref[...] = jnp.zeros_like(dp_ref)

    rows = cond_rows(cond)
    grads = ((dx * branch).astype(BF), dh.astype(BF), (dn * gain).astype(BF), dgate_two)
    for block, grad in enumerate(grads):
        dwa_ref[:, block * width : (block + 1) * width] += dot(rows, grad)
    dp_ref[0:1, :] += jnp.sum(dn * spread, axis=0, keepdims=True)


def middle_stage(half, tokens, out_grad, cond, mixed, wa, norms, up_near, up_far, down_near,
                 down_far):
    width = tokens.shape[1]
    rows = mixed.shape[0]
    hidden = up_near.shape[1]
    blocks = rows // ROW_BLOCK
    mine = lambda i, half: (half[0] * blocks + i, 0)
    plain = lambda i, half: (i, 0)
    row = pl.BlockSpec((ROW_BLOCK, width), plain)
    wide = pl.BlockSpec((ROW_BLOCK, 2 * hidden), plain)
    narrow = shape_of((rows, width), BF)
    turned = pl.BlockSpec((width, ROW_BLOCK), lambda i, half: (0, i))
    tall = shape_of((width, rows), BF)
    broad = shape_of((rows, 2 * hidden), BF)
    total = (cond.shape[1] + 16, 4 * width)
    return pl.pallas_call(
        functools.partial(middle_kernel, chunk=768),
        grid_spec=pltpu.PrefetchScalarGridSpec(
            num_scalar_prefetch=1,
            grid=(blocks,),
            in_specs=[
                pl.BlockSpec((ROW_BLOCK, width), mine),
                pl.BlockSpec((ROW_BLOCK, width), mine),
                pl.BlockSpec((ROW_BLOCK, cond.shape[1]), mine),
                row,
                resident(wa.shape, (0, 0)),
                resident(norms.shape, (0, 0)),
                resident((width, width // 2), (0, 2 * hidden // width)),
                resident((width, width // 2), (0, 2 * hidden // width)),
                *[pl.BlockSpec(memory_space=pl.ANY)] * 4,
            ],
            out_specs=[row, row, row, wide, turned, turned, wide, turned,
                       pl.BlockSpec(total, lambda i, half: (0, 0)),
                       pl.BlockSpec((8, width), lambda i, half: (0, 0))],
            scratch_shapes=[pltpu.VMEM((ROW_BLOCK, 2 * hidden), F32)]
            + [pltpu.VMEM((width, hidden), BF)] * 4
            + [pltpu.SemaphoreType.DMA((4,))],
        ),
        out_shape=[narrow, shape_of((rows, width), F32), narrow, broad, tall, tall, broad,
                   tall, shape_of(total, F32), shape_of((8, width), F32)],
        compiler_params=params(),
        name="middle_stage",
    )(half, tokens, out_grad, cond, mixed, wa, norms, down_near, down_far, up_near, up_far,
      down_near, down_far)


def last_kernel(half, x_ref, c_ref, dx_ref, dq_ref, dk_ref, dv_ref, wa_ref, p_ref, wqa_ref,
                wqb_ref, out_ref, dwa_ref, dp_ref):
    width = x_ref.shape[1]
    own = width // 2
    cond = silu_low(c_ref[...])
    scale = dot(cond, wa_ref[width : 2 * width, :], NT) + p_ref[3:4, :]
    dh = jnp.zeros(x_ref.shape, F32)
    for start, w_ref in ((0, wqa_ref), (own, wqb_ref)):
        cols = slice(start, start + own)
        for index, grad_ref in enumerate((dq_ref, dk_ref, dv_ref)):
            dh = dh + dot(grad_ref[:, cols], w_ref[:, index * own : (index + 1) * own], NT)
    normal, rstd = normalize(x_ref[...].astype(F32))
    gain = p_ref[0:1, :]
    spread = 1.0 + scale
    dn = dh * normal
    out_ref[...] = dx_ref[...] + norm_backward(dh * gain * spread, normal, rstd)

    @pl.when(pl.program_id(0) == 0)
    def _():
        dwa_ref[...] = jnp.zeros_like(dwa_ref)
        dp_ref[...] = jnp.zeros_like(dp_ref)

    rows = cond_rows(cond)
    dwa_ref[:, :width] += dot(rows, dh.astype(BF))
    dwa_ref[:, width:] += dot(rows, (dn * gain).astype(BF))
    dp_ref[0:1, :] += jnp.sum(dn * spread, axis=0, keepdims=True)


def last_stage(half, tokens, cond, dx, grads, wa, norms, near, far):
    width = tokens.shape[1]
    rows = dx.shape[0]
    blocks = rows // ROW_BLOCK
    mine = lambda i, half: (half[0] * blocks + i, 0)
    row = pl.BlockSpec((ROW_BLOCK, width), lambda i, half: (i, 0))
    total = (cond.shape[1] + 16, 2 * width)
    return pl.pallas_call(
        last_kernel,
        grid_spec=pltpu.PrefetchScalarGridSpec(
            num_scalar_prefetch=1,
            grid=(blocks,),
            in_specs=[
                pl.BlockSpec((ROW_BLOCK, width), mine),
                pl.BlockSpec((ROW_BLOCK, cond.shape[1]), mine),
                row, row, row, row,
                resident(wa.shape, (0, 0)),
                resident(norms.shape, (0, 0)),
                resident((width, 3 * width // 2), (0, 0)),
                resident((width, 3 * width // 2), (0, 0)),
            ],
            out_specs=[row, pl.BlockSpec(total, lambda i, half: (0, 0)),
                       pl.BlockSpec((8, width), lambda i, half: (0, 0))],
        ),
        out_shape=[shape_of((rows, width), F32), shape_of(total, F32), shape_of((8, width), F32)],
        compiler_params=params(),
        name="last_stage",
    )(half, tokens, cond, dx, *grads, wa, norms, near, far)


def weight_grad_kernel(*refs, plan):
    lefts, rights = plan["lefts"], plan["rights"]
    left_refs, right_refs = refs[:lefts], refs[lefts : lefts + rights]
    out_ref, turned = refs[lefts + rights :]
    step = pl.program_id(0)
    for begin, end, left, right in plan["spans"]:

        @pl.when(step == begin)
        def _():
            turned[...] = left_refs[left][...].T

        @pl.when((step >= begin) & (step < end))
        def _():
            out_ref[...] = dot(turned[...], right_refs[right][...]).astype(BF)


def weight_grads(lefts, rights, spans, block, name):
    rows, width = lefts[0].shape
    begin, plan, maps = 0, [], []
    for steps, left, right, first in spans:
        plan.append((begin, begin + steps, left, right))
        maps.append((begin, steps, first))
        begin += steps

    def column_map(begin, steps, first):
        return lambda i: (0, first + jnp.clip(i - begin, 0, steps - 1))

    return pl.pallas_call(
        functools.partial(
            weight_grad_kernel,
            plan={"lefts": len(lefts), "rights": len(rights), "spans": plan},
        ),
        grid=(begin,),
        in_specs=[resident((rows, width), (0, 0))] * len(lefts)
        + [pl.BlockSpec((rows, block), column_map(*entry)) for entry in maps],
        out_specs=pl.BlockSpec((width, block), lambda i: (0, i)),
        out_shape=shape_of((width, begin * block), BF),
        scratch_shapes=[pltpu.VMEM((width, rows), BF)],
        compiler_params=params(),
        name=name,
    )(*lefts, *rights)


class Gather:
    def __init__(self, shard, near, far, cut, sems, place, inner_first=False):
        outer, x, y, z, core = (place[name] for name in ("outer", "x", "y", "z", "core"))
        columns = near.shape[-1]
        flat = len(near.shape) == 2
        rows = near.shape[0] // (4 * outer)

        def slots(ref, first, number, cols):
            if flat:
                at = pl.multiple_of(first * rows, 16)
                return ref.at[pl.ds(at, number * rows), cols]
            return ref.at[pl.ds(first, number), core, :, cols]

        self.count = 0

        def copy(src, dst, device):
            index = self.count
            self.count += 1
            return pltpu.make_async_remote_copy(
                src_ref=src,
                dst_ref=dst,
                send_sem=sems.at[0, index],
                recv_sem=sems.at[1, index],
                device_id=device,
                device_id_type=pl.DeviceIdType.MESH,
            )

        here = 2 * y + x
        across_x = (4 * z + 2 * y + 1 - x, core)
        across_y = (4 * z + 2 * (1 - y) + x, core)
        other_core = (4 * z + here, 1 - core)
        whole = slice(None)
        self.outer = outer
        own = slots(near, 4 * z + here, 1, whole)
        self.local = (shard, own)
        self.inner_first = inner_first
        beyond = [(4 * lax.rem(z + hop, outer) + here, core) for hop in range(1, outer)]
        self.hops = [[copy(shard, own, device)] for device in beyond if not inner_first]
        self.one, self.two, self.swap = [], [], []
        for step in range(outer):
            base = 4 * lax.rem(z + outer - step, outer)
            one, two = [], []
            for odd, cols in enumerate((slice(0, cut), slice(cut, columns))):
                if odd and cut == columns:
                    continue
                mine = slots(near, base + here, 1, cols)
                src = mine
                if step == 0:
                    src = shard.at[:, cols] if flat else shard.at[:, :, cols]
                if step == 0 or not inner_first:
                    one.append(copy(src, mine, across_y if odd else across_x))
                if odd:
                    both = [slots(near, base + 2 * yy + x, 1, cols) for yy in range(2)]
                else:
                    both = [slots(near, base + 2 * y, 2, cols)]
                two += [copy(spot, spot, across_x if odd else across_y) for spot in both]
            self.one.append(one)
            self.two.append(two)
            if step == 0 and inner_first:
                spots = [slots(near, base + 2 * y, 2, slice(0, cut))]
                spots += [slots(near, base + 2 * yy + x, 1, slice(cut, columns)) for yy in range(2)]
                self.hops = [[copy(spot, spot, device) for spot in spots] for device in beyond]
            target = far if flat else near
            self.swap.append(
                [copy(slots(near, base, 4, whole), slots(target, base, 4, whole), other_core)]
            )

    @staticmethod
    def semaphores(outer):
        return pltpu.SemaphoreType.DMA((2, 8 * outer))

    @staticmethod
    def begin(copies):
        for entry in copies:
            entry.start()

    @staticmethod
    def arrive(copies):
        for entry in copies:
            entry.wait_recv()

    def start_hops(self):
        if self.inner_first:
            self.arrive(self.one[0])
        for entry in self.hops:
            self.begin(entry)

    def phase_one(self, step):
        if step:
            self.arrive(self.hops[step - 1])
        self.begin(self.one[step])

    def phase_two(self, step):
        if self.inner_first:
            if step:
                self.arrive(self.hops[step - 1])
        else:
            self.arrive(self.one[step])
        self.begin(self.two[step])

    def phase_swap(self, step):
        self.arrive(self.two[step])
        self.begin(self.swap[step])

    def finish(self, step):
        self.arrive(self.swap[step])

    def drain(self):
        for copies in self.hops + self.one + self.two + self.swap:
            for entry in copies:
                entry.wait_send()


def my_place(count):
    me, core = lax.axis_index("dp"), lax.axis_index("mp")
    return {"outer": count // 4, "z": me // 4, "y": lax.rem(me // 2, 2), "x": lax.rem(me, 2),
            "core": core, "me": me}


def greet(devices):
    barrier = pltpu.get_barrier_semaphore()
    for device in devices:
        pl.semaphore_signal(barrier, inc=1, device_id=device, device_id_type=pl.DeviceIdType.MESH)


def meet(devices):
    pl.semaphore_wait(pltpu.get_barrier_semaphore(), len(devices))


def partners(place):
    z, y, x, core, outer = (place[name] for name in ("z", "y", "x", "core", "outer"))
    here = 2 * y + x
    others = [(4 * lax.rem(z + hop, outer) + here, core) for hop in range(1, outer)]
    return others + [(4 * z + 2 * y + 1 - x, core), (4 * z + 2 * (1 - y) + x, core),
                     (4 * z + here, 1 - core)]


def opening_kernel(tok_ref, cond_ref, seg_ref, cosa_ref, sina_ref, cosb_ref, sinb_ref, ada_ref, norm_ref, qkv_ref, out_ref,
                   up_ref, down_ref,
                   h_out, q_out, k_out, v_out, o_out, near_out, far_out, wa_out, cos_out, sin_out,
                   fq_out, fk_out, up_near, up_far, down_near, down_far, lse_ref, table_ref,
                   h_ref, q_ref, k_ref, v_ref, o_ref, near_ref, far_ref, wa_ref, cos_ref, sin_ref,
                   fq_ref, fk_ref,
                   ada_vm, small_vm, up_vm, down_vm, x_vm, c_vm, qz, kz, vt, local, saved,
                   ada_sems, small_sems, up_sems, down_sems, *, count, cuts, bk):
    place = my_place(count)
    others = partners(place)
    greet(others)
    outer, core = place["outer"], place["core"]
    rows, width = x_vm.shape
    own = width // 2
    hidden = up_ref.shape[1]
    part = width // count
    small = Gather(small_vm, near_ref, far_ref, cuts[0], small_sems, place)
    ada = Gather(ada_vm.at[pl.ds(core, 1)], wa_ref, None, ada_vm.shape[2], ada_sems, place)
    ups = Gather(up_vm, up_near, up_far, cuts[1], up_sems, place)
    downs = Gather(down_vm, down_near, down_far, cuts[2], down_sems, place, inner_first=True)

    start = pl.multiple_of(core * rows, rows)
    loads = [
        pltpu.make_async_copy(tok_ref.at[pl.ds(start, rows)], x_vm, local.at[0]),
        pltpu.make_async_copy(cond_ref.at[pl.ds(start, rows)], c_vm, local.at[1]),
    ]
    stores = [
        pltpu.make_async_copy(*entry.local, local.at[2 + index])
        for index, entry in enumerate((ada, small, ups, downs))
    ]
    saves = {
        name: pltpu.make_async_copy(src, dst, saved.at[index])
        for index, (name, src, dst) in enumerate((
            ("h", h_ref, h_out), ("q", q_ref, q_out), ("k", k_ref, k_out), ("v", v_ref, v_out),
            ("near", near_ref, near_out), ("far", far_ref, far_out), ("wa", wa_ref, wa_out),
            ("cos", cos_ref, cos_out), ("sin", sin_ref, sin_out), ("fq", fq_ref, fq_out),
            ("fk", fk_ref, fk_out),
        ))
    }
    for load in loads:
        load.start()
    ada_vm[...] = ada_ref[...].astype(BF).reshape(ada_vm.shape)
    for c in range(3):
        small_vm[:, c * own : (c + 1) * own] = qkv_ref[c].astype(BF)
    spare = jnp.zeros((LANES - 8, part), F32)
    small_vm[:, 3 * own :] = jnp.concatenate([norm_ref[...], spare], axis=0).T.astype(BF)
    up_vm[...] = up_ref[...].astype(BF)
    down_vm[:, :hidden] = down_ref[...].astype(BF)
    down_vm[:, hidden:] = out_ref[...].astype(BF)
    meet(others)
    first = (ada, small)

    def each(method, *args):
        for entry in first:
            getattr(entry, method)(*args)

    each("start_hops")
    each("phase_one", 0)
    stores[0].start()
    stores[1].start()
    stores[2].start()
    stores[3].start()
    stores[0].wait()
    stores[1].wait()
    each("phase_two", 0)
    downs.phase_one(0)
    each("phase_one", 1)
    fine = cosb_ref.shape[0]

    def rope_rows(step, _):
        at, row = pl.ds(pl.multiple_of(step * fine, fine), fine), pl.ds(step, 1)
        cos_ref[at, :] = cosa_ref[row, :] * cosb_ref[...] - sina_ref[row, :] * sinb_ref[...]
        sin_ref[at, :] = sina_ref[row, :] * cosb_ref[...] + cosa_ref[row, :] * sinb_ref[...]
        return 0

    lax.fori_loop(0, cosa_ref.shape[0], rope_rows, 0)
    each("phase_one", 2)
    each("phase_two", 1)
    documents = seg_ref[pl.ds(core, 1), :].astype(F32)
    documents = jnp.broadcast_to(documents, (LANES, rows)).T
    lane = (lax.broadcasted_iota(jnp.int32, (rows, LANES), 1) % HEAD_DIM).astype(F32)
    same = documents == lane
    fq_ref[...] = jnp.where(same, 1.0, 0.0).astype(BF)
    fk_ref[...] = jnp.where(same, 0.0, jnp.where(lane < 4.0, MASKED, 0.0)).astype(BF)
    each("phase_one", 3)
    ups.start_hops()
    each("phase_two", 2)
    stores[2].wait()
    stores[3].wait()
    downs.start_hops()
    each("phase_two", 3)
    ups.phase_one(0)
    for load in loads:
        load.wait()
    for name in ("cos", "sin", "fq", "fk"):
        saves[name].start()
    for step in range(2):
        each("phase_swap", step)
    ups.phase_two(0)
    ups.phase_one(1)
    downs.phase_two(0)
    for step in range(2, outer):
        each("phase_swap", step)
    for step in range(outer):
        each("finish", step)
    for name in ("near", "far", "wa"):
        saves[name].start()

    table_ref[...] = near_ref[:, 3 * own :].astype(F32).T[0:8, :]
    wa = wa_ref[...].reshape(6 * width, c_vm.shape[1])

    def wide_events(tick):
        if tick == 0:
            ups.phase_two(1)
            ups.phase_one(2)
        if tick == 1:
            ups.phase_one(3)
            ups.phase_two(2)
        if tick == 3:
            ups.phase_two(3)
        if tick == 4:
            downs.phase_two(1)
            ups.phase_swap(0)
        if tick == 5:
            ups.phase_swap(1)
            downs.phase_swap(0)
        if tick == 6:
            downs.phase_two(2)
            ups.phase_swap(2)
        if tick == 7:
            ups.phase_swap(3)
        if tick == 8:
            downs.phase_two(3)
            downs.phase_swap(1)
        if tick == 9:
            downs.phase_swap(2)

    def row_block(i, _):
        at = pl.ds(pl.multiple_of(i * ROW_BLOCK, ROW_BLOCK), ROW_BLOCK)
        cond = silu_low(c_vm[at, :])
        shift = dot(cond, wa[:width], NT) + table_ref[2:3, :]
        scale = dot(cond, wa[width : 2 * width], NT) + table_ref[3:4, :]
        normal, _ = normalize(x_vm[at, :].astype(F32))
        h = (normal * table_ref[0:1, :] * (1.0 + scale) + shift).astype(BF)
        h_ref[:, at] = h.T
        cos = jnp.concatenate([cos_ref[at, :]] * (own // LANES), axis=1)
        sin = jnp.concatenate([sin_ref[at, :]] * (own // LANES), axis=1)
        for first, w_ref in ((0, near_ref), (own, far_ref)):
            cols = slice(first, first + own)
            query = dot(h, w_ref[:, 0:own])
            query = query * cos + swap_halves(query) * sin
            q_ref[at, cols] = (query * HEAD_DIM**-0.5).astype(BF)
            key = dot(h, w_ref[:, own : 2 * own])
            k_ref[at, cols] = (key * cos + swap_halves(key) * sin).astype(BF)
            v_ref[at, cols] = dot(h, w_ref[:, 2 * own : 3 * own]).astype(BF)
        for tick in range(4):

            @pl.when(i == tick)
            def _():
                wide_events(tick)

        return 0

    lax.fori_loop(0, rows // ROW_BLOCK, row_block, 0)
    for name in ("h", "q", "k", "v"):
        saves[name].start()

    def keep(p):
        lanes = pl.ds(pl.multiple_of(p * LANES, LANES), LANES)
        return pltpu.make_async_copy(o_ref.at[:, lanes], o_out.at[:, lanes], saved.at[len(saves)])

    def head_pair(p, _):
        lanes = pl.ds(pl.multiple_of(p * LANES, LANES), LANES)
        qz[0], qz[1] = split_heads(q_ref[:, lanes], fq_ref[...])
        kz[0], kz[1] = split_heads(k_ref[:, lanes], fk_ref[...])
        vt[...] = v_ref[:, lanes].T
        state = [None, None]
        for j in range(rows // bk):
            block = slice(j * bk, (j + 1) * bk)
            scores = [dot(kz[h, block, :], qz[h], NT) for h in range(2)]
            for h in range(2):
                values = vt[HEAD_DIM * h : HEAD_DIM * (h + 1), block]
                top = jnp.max(scores[h], axis=0, keepdims=True)
                if j:
                    top = jnp.maximum(state[h][0], top)
                weights = jnp.exp(scores[h] - top)
                total = jnp.sum(weights, axis=0, keepdims=True)
                result = dot(values, weights.astype(BF))
                if j:
                    fade = jnp.exp(state[h][0] - top)
                    total = state[h][1] * fade + total
                    result = state[h][2] * fade + result
                state[h] = (top, total, result)
        done = jnp.concatenate([entry[2] / entry[1] for entry in state], axis=0)
        o_ref[:, lanes] = done.T.astype(BF)
        for h in range(2):
            lse_ref[p, h : h + 1, :] = state[h][0] + jnp.log(state[h][1])

        @pl.when(p > 0)
        def _():
            keep(p - 1).wait()

        keep(p).start()
        for tick in range(4, 10):

            @pl.when(p == tick - 4)
            def _():
                wide_events(tick)

        return 0

    lax.fori_loop(0, width // LANES, head_pair, 0)
    downs.phase_swap(3)
    keep(width // LANES - 1).wait()
    for save in saves.values():
        save.wait()
    for step in range(outer):
        ups.finish(step)
        downs.finish(step)
    for entry in (ada, small, ups, downs):
        entry.drain()


def opening(count, tokens, cond, segments, rope, weights):
    ada, norms, qkv, out, up, down = weights
    rows, width = tokens.shape[0] // 2, tokens.shape[1]
    conds, part, hidden = cond.shape[1], width // count, up.shape[1]
    vm = pl.BlockSpec(memory_space=pltpu.VMEM)
    hbm = pl.BlockSpec(memory_space=pl.ANY)
    small = shape_of((width, 3 * width // 2 + LANES), BF)
    act = shape_of((rows, width), BF)
    table = shape_of((rows, LANES), F32)
    feature = shape_of((rows, LANES), BF)
    first = shape_of((width, hidden), BF)
    second = shape_of((width, hidden + width // 2), BF)
    pairs = width // LANES
    pair = pltpu.VMEM((2, rows, LANES), BF)
    half_cols = ada.shape[0] // 2
    kept = [shape_of((width, rows), BF)] + [act] * 4 + [small, small, shape_of((count, 2, half_cols, conds), BF), table, table,
                        feature, feature]
    cuts = (512, hidden // 2, second.shape[1] // 2 // LANES * LANES)
    return pl.pallas_call(
        functools.partial(opening_kernel, count=count, cuts=cuts, bk=512),
        in_specs=[hbm, hbm] + [vm] * 11,
        out_specs=[hbm] * (len(kept) + 4) + [vm, vm],
        out_shape=kept + [first, first, second, second]
        + [shape_of((pairs, 2, rows), F32), shape_of((8, width), F32)],
        scratch_shapes=[pltpu.VMEM(entry.shape, entry.dtype) for entry in kept]
        + [
            pltpu.VMEM((2, half_cols, conds), BF),
            pltpu.VMEM((part, small.shape[1]), BF),
            pltpu.VMEM((part, hidden), BF),
            pltpu.VMEM((part, second.shape[1]), BF),
            pltpu.VMEM((rows, width), BF), pltpu.VMEM((rows, conds), BF),
            pair, pair, pltpu.VMEM((LANES, rows), BF),
            pltpu.SemaphoreType.DMA((6,)),
            pltpu.SemaphoreType.DMA((len(kept),)),
        ] + [Gather.semaphores(count // 4)] * 4,
        compiler_params=pltpu.CompilerParams(
            vmem_limit_bytes=VMEM_LIMIT, collective_id=0, has_side_effects=True
        ),
        name="opening",
    )(tokens, cond, segments, *rope, ada, norms, qkv, out, up, down)


class Scatter:
    def __init__(self, place, first, total, one, two, hops, sems):
        z, y, x, core, outer = (place[name] for name in ("z", "y", "x", "core", "outer"))

        def copy(src, dst, device):
            index = place["next"]
            place["next"] = index + 1
            return pltpu.make_async_remote_copy(
                src_ref=src,
                dst_ref=dst,
                send_sem=sems.at[0, index],
                recv_sem=sems.at[1, index],
                device_id=device,
                device_id_type=pl.DeviceIdType.MESH,
            )

        across_x = (4 * z + 2 * y + 1 - x, core)
        across_y = (4 * z + 2 * (1 - y) + x, core)
        self.one, self.two, self.hops, self.z, self.outer = one, two, hops, z, outer
        if first == "y":
            self.keep_one, self.keep_two = total.at[:, y], one.at[:, x]
            self.copy_one = copy(total.at[:, 1 - y], one, across_y)
            self.copy_two = copy(one.at[:, 1 - x], two, across_x)
        else:
            self.keep_one, self.keep_two = total.at[:, :, x], one.at[:, y]
            self.copy_one = copy(total.at[:, :, 1 - x], one, across_x)
            self.copy_two = copy(one.at[:, 1 - y], two, across_y)
        self.copy_hops = [
            copy(two.at[lax.rem(z + hop, outer)], hops.at[hop - 1],
                 (4 * lax.rem(z + hop, outer) + 2 * y + x, core))
            for hop in range(1, outer)
        ]

    @classmethod
    def halves(cls, place, buffers, sems, order="yx"):
        columns = buffers[0].shape[-1]
        cut = columns // 2 // LANES * LANES
        out = []
        for first, cols in zip(order, (slice(0, cut), slice(cut, columns))):
            views = [ref.at[(slice(None),) * (len(ref.shape) - 1) + (cols,)] for ref in buffers]
            out.append(cls(place, first, *views, sems))
        return out

    def start(self):
        self.copy_one.start()

    def phase_two(self):
        self.copy_one.wait_recv()
        self.one[...] = self.one[...] + self.keep_one[...]
        self.copy_two.start()

    def phase_hops(self):
        self.copy_two.wait_recv()
        self.two[...] = self.two[...] + self.keep_two[...]
        for entry in self.copy_hops:
            entry.start()

    def finish(self):
        total = self.two[self.z].astype(F32)
        for hop, entry in enumerate(self.copy_hops):
            entry.wait_recv()
            total = total + self.hops[hop].astype(F32)
        return total

    def drain(self):
        for entry in [self.copy_one, self.copy_two] + self.copy_hops:
            entry.wait_send()


def across_cores(place, src, dst, sems):
    index = place["next"]
    place["next"] = index + 1
    return pltpu.make_async_remote_copy(
        src_ref=src,
        dst_ref=dst,
        send_sem=sems.at[0, index],
        recv_sem=sems.at[1, index],
        device_id=(place["me"], 1 - place["core"]),
        device_id_type=pl.DeviceIdType.MESH,
    )


def scatter_buffers(outer, blocks, rows, columns):
    lead = () if blocks is None else (blocks,)
    return [
        pltpu.VMEM(lead + (outer, 2, 2, rows, columns), BF),
        pltpu.VMEM(lead + (outer, 2, 2, rows, columns), BF),
        pltpu.VMEM(lead + (outer, 2, rows, columns), BF),
        pltpu.VMEM(lead + (outer, rows, columns), BF),
        pltpu.VMEM(lead + (outer - 1, rows, columns), BF),
    ]


def spread_kernel(h_in, gy_in, ga_in, du_ref, z_ref, o_in, q_in, k_in, v_in, do_in, lse_in,
                  fq_in, fk_in, cos_in, sin_in,
                  dq_out, dk_out, dv_out, last_ref, sum_ref,
                  h_ref, gy_ref, ga_ref, o_ref, q_ref, k_ref, v_ref, do_ref, lse_ref,
                  fq_ref, fk_ref, cos_ref, sin_ref, dq_ref, dk_ref, dv_ref,
                  right, far6, sum6, one6, two6, hop6, far1,
                  qz, kz, qm, dm, vm, kt, delta, dqt,
                  load_sems, input_sems, keep_sems, sems, *, count, bk):
    place = my_place(count)
    others = partners(place)
    greet(others)
    place["next"] = 0
    outer = place["outer"]
    rows, width = o_ref.shape
    pieces = (
        (h_in, h_ref), (gy_in, gy_ref), (ga_in, ga_ref), (o_in, o_ref), (q_in, q_ref),
        (k_in, k_ref), (v_in, v_ref), (do_in, do_ref), (lse_in, lse_ref), (fq_in, fq_ref),
        (fk_in, fk_ref), (cos_in, cos_ref), (sin_in, sin_ref),
    )
    inputs = [
        pltpu.make_async_copy(src, dst, input_sems.at[index])
        for index, (src, dst) in enumerate(pieces)
    ]
    own = width // 2
    each, block = right.shape[0], right.shape[2]
    span = 2 * each * block
    shards = far6.shape[1:]
    tail = far1.shape

    swaps = [across_cores(place, far6.at[j], sum6.at[j], sems) for j in range(2 * each)]
    swaps.append(across_cores(place, far1, last_ref, sems))
    scatters = [
        Scatter.halves(place, [ref.at[j] for ref in (sum6, one6, two6, hop6)], sems)
        for j in range(2 * each)
    ]

    def start(j):
        for entry in scatters[j]:
            entry.start()

    def phase_two(j):
        for entry in scatters[j]:
            entry.phase_two()

    def phase_hops(j):
        for entry in scatters[j]:
            entry.phase_hops()

    def finish(j):
        at = j * block
        for entry in scatters[j]:
            columns = entry.hops.shape[-1]
            sum_ref[:, at : at + columns] = entry.finish()
            at += columns

    lefts, sources = (h_ref, gy_ref), (du_ref, z_ref)

    def load(index, turn):
        b = lax.rem(turn, each)
        at = pl.multiple_of((1 - turn // each) * (span // 2) + b * block, block)
        return pltpu.make_async_copy(
            sources[index].at[:, pl.ds(at, block)], right.at[b], load_sems.at[b]
        )

    inputs[0].start()
    load(0, 0).start()
    for item in inputs[1:4]:
        item.start()
    for b in range(1, each):
        load(0, b).start()
    for item in inputs[4:]:
        item.start()
    inputs[0].wait()
    meet(others)

    for index in range(2):

        def grad_block(turn, _):
            b = lax.rem(turn, each)
            load(index, turn).wait()
            grad = dot(lefts[index][...], right[b])

            @pl.when(turn < each)
            def _():
                load(index, turn + each).start()
                far6[index * each + b] = grad.reshape(shards).astype(BF)

            for step in range(each):

                @pl.when(turn == step)
                def _():
                    swaps[index * each + step].start()

                @pl.when(turn == each + step)
                def _():
                    if index == 0:
                        load(1, step).start()
                    at = index * each + step
                    swaps[at].wait_recv()
                    sum6[at] = (grad.reshape(shards) + sum6[at].astype(F32)).astype(BF)
                    if at < 2:
                        start(at)

            return 0

        if index:
            inputs[1].wait()
        lax.fori_loop(0, 2 * each, grad_block, 0)
        if index == 0:
            start(2)
    inputs[2].wait()
    inputs[3].wait()
    phase_two(0)
    start(3)
    far1[...] = dot(ga_ref[...], o_ref[:, own:]).reshape(tail).astype(BF)
    swaps[-1].start()
    phase_two(1)
    grad = dot(ga_ref[...], o_ref[:, :own])
    swaps[-1].wait_recv()
    last_ref[...] = (grad.reshape(tail) + last_ref[...].astype(F32)).astype(BF)
    for item in inputs[4:]:
        item.wait()

    def events(p):
        if p < 4:
            phase_two(p + 2)
        if p < 2:
            start(p + 4)
        if p < 4:
            phase_hops(p)
        if p == 4:
            phase_hops(5)
        if 1 < p:
            finish(p - 2)
        if p == 5:
            finish(4)
            finish(5)

    def keep(p):
        lanes = pl.ds(pl.multiple_of(p * LANES, LANES), LANES)
        return [
            pltpu.make_async_copy(src.at[:, lanes], dst.at[:, lanes], keep_sems.at[index])
            for index, (src, dst) in enumerate(
                ((dq_ref, dq_out), (dk_ref, dk_out), (dv_ref, dv_out))
            )
        ]

    zero = jnp.zeros((rows, LANES), BF)

    def unrotate(grad, at):
        return (grad * cos_ref[at, :] - swap_halves(grad) * sin_ref[at, :]).astype(BF)

    def head_pair(p, _):
        lanes = pl.ds(pl.multiple_of(p * LANES, LANES), LANES)
        qz[0], qz[1] = split_heads(q_ref[:, lanes], fq_ref[...])
        kz[0], kz[1] = split_heads(k_ref[:, lanes], fk_ref[...])
        qm[0], qm[1] = split_heads(q_ref[:, lanes], zero)
        dm[0], dm[1] = split_heads(do_ref[:, lanes], zero)
        vm[0], vm[1] = split_heads(v_ref[:, lanes], zero)
        kt[...] = k_ref[:, lanes].T
        product = (do_ref[:, lanes].astype(F32) * o_ref[:, lanes].astype(F32)).T
        delta[0:1, :] = jnp.sum(product[:HEAD_DIM], axis=0, keepdims=True)
        delta[1:2, :] = jnp.sum(product[HEAD_DIM:], axis=0, keepdims=True)
        dqt[...] = jnp.zeros_like(dqt)

        def key_block(first, reach):
            at = slice(first, first + bk)
            dk = jnp.zeros((bk, LANES), F32)
            dv = jnp.zeros((bk, LANES), F32)
            scores = [dot(kz[h, at, :], qz[h, reach, :], NT) for h in range(2)]
            grads = [dot(vm[h, at, :], dm[h, reach, :], NT) for h in range(2)]
            for h in range(2):
                weights = jnp.exp(scores[h] - lse_ref[p, h : h + 1, reach])
                dv = dv + dot(weights.astype(BF), dm[h, reach, :])
                ds = (weights * (grads[h] - delta[h : h + 1, reach])).astype(BF)
                dk = dk + dot(ds, qm[h, reach, :])
                head = slice(HEAD_DIM * h, HEAD_DIM * (h + 1))
                dqt[head, reach] += dot(kt[head, at], ds)
            dk_ref[at, lanes] = unrotate(dk, at)
            dv_ref[at, lanes] = dv.astype(BF)

        for first in range(0, rows, bk):
            low = max(0, (first - rows // 2 + 1) // LANES * LANES)
            high = min(rows, -(-(first + bk + rows // 2 - 1) // LANES) * LANES)
            key_block(first, slice(low, high))
            if first + bk == rows // 2:

                @pl.when(p == 4)
                def _():
                    phase_hops(4)

        dq_ref[:, lanes] = unrotate(dqt[...].T * HEAD_DIM**-0.5, pl.ds(0, rows))

        @pl.when(p > 0)
        def _():
            for entry in keep(p - 1):
                entry.wait()

        for entry in keep(p):
            entry.start()
        for step in range(6):

            @pl.when(p == step)
            def _():
                events(step)

        return 0

    lax.fori_loop(0, width // LANES, head_pair, 0)
    for entry in keep(width // LANES - 1):
        entry.wait()
    for entry in swaps:
        entry.wait_send()
    for pair in scatters:
        for entry in pair:
            entry.drain()


def spread(count, h_two, gy, ga, du, z, mixed, queries, keys, values, upstream, lse, features,
           tables):
    rows, width = mixed.shape
    part = width // count
    outer = count // 4
    hidden = du.shape[1] // 2
    each = 3
    block = hidden // each
    vm = pl.BlockSpec(memory_space=pltpu.VMEM)
    hbm = pl.BlockSpec(memory_space=pl.ANY)
    act = shape_of((rows, width), BF)
    last = shape_of((outer, 2, 2, part, width // 2), BF)
    pair = pltpu.VMEM((2, rows, LANES), BF)
    copies = 7 + 12 * (2 + outer - 1)
    held = [h_two, gy, ga, mixed, queries, keys, values, upstream, lse, *features, *tables]
    return pl.pallas_call(
        functools.partial(spread_kernel, count=count, bk=256),
        in_specs=[hbm] * (len(held) + 2),
        out_specs=[hbm] * 3 + [vm] * 2,
        out_shape=[act, act, act, last, shape_of((part, 2 * hidden), F32)],
        scratch_shapes=[pltpu.VMEM(entry.shape, entry.dtype) for entry in held + [act] * 3]
        + [pltpu.VMEM((each, rows, block), BF)]
        + scatter_buffers(outer, 2 * each, part, block)
        + [pltpu.VMEM(last.shape, BF)]
        + [pair] * 5
        + [
            pltpu.VMEM((LANES, rows), BF),
            pltpu.VMEM((8, rows), F32),
            pltpu.VMEM((LANES, rows), F32),
            pltpu.SemaphoreType.DMA((each,)),
            pltpu.SemaphoreType.DMA((len(held),)),
            pltpu.SemaphoreType.DMA((3,)),
            pltpu.SemaphoreType.DMA((2, copies)),
        ],
        compiler_params=pltpu.CompilerParams(
            vmem_limit_bytes=VMEM_LIMIT, collective_id=1, has_side_effects=True
        ),
        name="spread",
    )(h_two, gy, ga, du, z, mixed, queries, keys, values, upstream, lse, *features, *tables)


def closing_kernel(tok_ref, cond_ref, h_in, dq_in, dk_in, dv_in, near_in, far_in, wa_in,
                   dwa_two_in, dx_in, last_in, mid_ref, p_ref, dp_two_ref,
                   rows_ref, qkv_ref, out_ref, ada_ref, norm_ref, square_ref,
                   h_ref, grads, x_vm, c_vm, near_ref, far_ref, wa_ref, dwa_two_ref, dx_ref,
                   mine, dh_vm, dwa_vm, dp_vm, dwt, plane, column,
                   far3, sum3, one3, two3, hop3, sum2, one2, two2, hop2,
                   sum1, one1, two1, hop1, local, sems, *, count, token_total):
    place = my_place(count)
    place["next"] = 0
    z, y, x, core, outer, me = (place[name] for name in ("z", "y", "x", "core", "outer", "me"))
    rows, width = x_vm.shape
    own = width // 2
    part = width // count
    conds = c_vm.shape[1]
    half_cols = ada_ref.shape[1]
    shards = far3.shape[1:]

    start = pl.multiple_of(core * rows, rows)
    columns = near_ref.shape[1]
    pieces = (
        (h_in, h_ref), (dq_in, grads.at[0]), (dk_in, grads.at[1]), (dv_in, grads.at[2]),
        (tok_ref.at[pl.ds(start, rows)], x_vm), (cond_ref.at[pl.ds(start, rows)], c_vm),
        (near_in.at[:, pl.ds(0, columns)], near_ref), (far_in.at[:, pl.ds(0, columns)], far_ref),
        (wa_in.at[pl.ds(width, width)], wa_ref), (dwa_two_in, dwa_two_ref), (dx_in, dx_ref),
        (last_in, sum1),
    )
    loads = [
        pltpu.make_async_copy(src, dst, local.at[index])
        for index, (src, dst) in enumerate(pieces)
    ]
    loads[9].start()
    loads[11].start()
    for load in loads[:9] + loads[10:11]:
        load.start()

    swaps = [across_cores(place, far3.at[c], sum3.at[c], sems) for c in range(3)]
    scatters = [
        Scatter.halves(place, [ref.at[c] for ref in (sum3, one3, two3, hop3)], sems,
                       "xy" if c % 2 else "yx")
        for c in range(3)
    ]
    scatters.append(Scatter.halves(place, [sum1, one1, two1, hop1], sems, "xy"))
    dwt_rows = dwt.shape[4]
    ada_swap = across_cores(place, dwt.at[:, :, :, 1 - core], sum2, sems)
    cut = dwt_rows // 2
    adas = []
    for first, at in (("x", slice(0, cut)), ("y", slice(cut, dwt_rows))):
        views = [ref.at[(slice(None),) * (len(ref.shape) - 2) + (at,)]
                 for ref in (sum2, one2, two2, hop2)]
        adas.append(Scatter(place, first, *views, sems))
    sends = []

    def copy(src, dst, device):
        index = place["next"]
        place["next"] = index + 1
        entry = pltpu.make_async_remote_copy(
            src_ref=src, dst_ref=dst, send_sem=sems.at[0, index], recv_sem=sems.at[1, index],
            device_id=device, device_id_type=pl.DeviceIdType.MESH,
        )
        sends.append(entry)
        return entry

    row_copies = []
    for i in range(rows // ROW_BLOCK):
        at = pl.ds(i * ROW_BLOCK, ROW_BLOCK)
        row_copies.append(copy(dh_vm.at[at], rows_ref.at[1, at], (me, 1 - core)))
    ada_copy = copy(ada_ref.at[core], ada_ref.at[core], (me, 1 - core))
    spot = 4 * core + 2 * y + x
    plane_copies = []
    for other in range(1, 8):
        yy, xx = lax.rem(y + other // 2, 2), lax.rem(x + other, 2)
        cc = lax.rem(core + other // 4, 2)
        plane_copies.append((4 * z + 2 * yy + xx, cc))
    beyond = [(4 * lax.rem(z + hop, outer) + 2 * y + x, core) for hop in range(1, outer)]

    others = plane_copies + beyond
    greet(others)
    plane_copies = [copy(plane.at[spot], plane.at[spot], device) for device in plane_copies]
    column_copies = [copy(column.at[z], column.at[z], device) for device in beyond]

    def all_of(c, method):
        for entry in scatters[c]:
            getattr(entry, method)()

    def project(c):
        if c < 2:
            loads[1 + c].wait()
        grad = dot(h_ref[...], grads[c])
        far3[c] = grad[:, own:].reshape(shards).astype(BF)
        swaps[c].start()
        mine[c] = grad[:, :own].reshape(shards)

    def add_near_grad(c):
        swaps[c].wait_recv()
        sum3[c] = (mine[c] + sum3[c].astype(F32)).astype(BF)
        all_of(c, "start")

    def place_rows(start, values):
        at = 0
        while at < values.shape[0]:
            block, low = divmod(start + at, half_cols)
            high = min(half_cols, low + values.shape[0] - at)
            shard, side = divmod(block, 2)
            dwt[shard // 4, (shard // 2) % 2, shard % 2, side, low:high, :] = values[
                at : at + high - low
            ]
            at += high - low

    loads[9].wait()
    place_rows(2 * width, dwa_two_ref[:conds, :].T.astype(BF))
    dwa_vm[...] = jnp.zeros_like(dwa_vm)
    dp_vm[...] = jnp.zeros_like(dp_vm)
    dp_vm[1:2, :] = dp_two_ref[0:1, :]
    for block in range(4):
        dp_vm[4 + block : 5 + block, :] = dwa_two_ref[
            conds : conds + 1, block * width : (block + 1) * width
        ]
    loads[0].wait()
    meet(others)
    loads[11].wait()
    all_of(3, "start")
    project(0)
    project(1)
    add_near_grad(0)
    loads[3].wait()
    for load in loads[4:9]:
        load.wait()

    gain = p_ref[0:1, :]

    def spread_of(at):
        scale = dot(silu_low(c_vm[at, :]), wa_ref[...], NT) + p_ref[3:4, :]
        return 1.0 + scale

    def first_pass(i, _):
        at = pl.ds(pl.multiple_of(i * ROW_BLOCK, ROW_BLOCK), ROW_BLOCK)
        dh = jnp.zeros((ROW_BLOCK, width), F32)
        for first, w_ref in ((0, near_ref), (own, far_ref)):
            cols = slice(first, first + own)
            for c in range(3):
                dh = dh + dot(grads[c, at, cols], w_ref[:, c * own : (c + 1) * own], NT)
        dh_vm[at, :] = dh
        normal, _ = normalize(x_vm[at, :].astype(F32))
        dn = dh * normal
        summed = cond_rows(silu_low(c_vm[at, :]))
        dwa_vm[:, :width] += dot(summed, dh.astype(BF))
        dwa_vm[:, width:] += dot(summed, (dn * gain).astype(BF))
        dp_vm[0:1, :] += jnp.sum(dn * spread_of(at), axis=0, keepdims=True)

        @pl.when(i == 0)
        def _():
            add_near_grad(1)
            all_of(3, "phase_two")

        @pl.when(i == 2)
        def _():
            all_of(0, "phase_two")
            all_of(3, "phase_hops")

        return 0

    lax.fori_loop(0, rows // ROW_BLOCK, first_pass, 0)

    place_rows(0, dwa_vm[:conds, :].T.astype(BF))
    for block in range(2):
        dp_vm[2 + block : 3 + block, :] = dwa_vm[
            conds : conds + 1, block * width : (block + 1) * width
        ]
    lane = lax.broadcasted_iota(jnp.int32, (16, conds), 1)
    for shard in range(count):
        gone = dp_vm[...] if shard == 0 else pltpu.roll(dp_vm[...], width - shard * part, 1)
        gone = jnp.where(lane < part, gone[:, :conds], 0.0).astype(BF)
        for side in range(2):
            dwt[shard // 4, (shard // 2) % 2, shard % 2, side, half_cols:, :] = gone
    ada_swap.start()
    all_of(1, "phase_two")
    project(2)
    ada_swap.wait_recv()
    sum2[...] = sum2[...] + dwt[:, :, :, core]
    for entry in adas:
        entry.start()
    add_near_grad(2)
    all_of(0, "phase_hops")
    loads[10].wait()

    def events(i):
        if i == 1:
            all_of(1, "phase_hops")
        if i == 2:
            for entry in adas:
                entry.phase_two()
        if i == 3:
            all_of(2, "phase_two")

    def keep(i):
        at = pl.ds(pl.multiple_of(i * ROW_BLOCK, ROW_BLOCK), ROW_BLOCK)
        return pltpu.make_async_copy(dh_vm.at[at], rows_ref.at[0, at], local.at[i])

    def second_pass(i, _):
        at = pl.ds(pl.multiple_of(i * ROW_BLOCK, ROW_BLOCK), ROW_BLOCK)
        normal, rstd = normalize(x_vm[at, :].astype(F32))
        grad = dh_vm[at, :] * gain * spread_of(at)
        dh_vm[at, :] = dx_ref[at, :] + norm_backward(grad, normal, rstd)
        keep(i).start()
        for step in range(rows // ROW_BLOCK):

            @pl.when(i == step)
            def _():
                row_copies[step].start()
                if step < 4:
                    events(step)

        return 0

    lax.fori_loop(0, rows // ROW_BLOCK, second_pass, 0)

    for entry in adas:
        entry.phase_hops()
    squares = jnp.sum((mid_ref[...] / token_total) ** 2)
    all_of(2, "phase_hops")
    for c in range(4):
        target, at = (qkv_ref, c * own) if c < 3 else (out_ref, 0)
        for entry in scatters[c]:
            total = entry.finish()
            target[:, at : at + total.shape[1]] = total
            squares = squares + jnp.sum((total / token_total) ** 2)
            at += total.shape[1]
    first, second = adas[0].finish(), adas[1].finish()
    rest = half_cols - cut
    ada_ref[core, 0:cut, :] = first
    ada_ref[core, cut:, :] = second[:rest]
    norm_ref[...] = second[rest : rest + 8]
    ada_copy.start()
    squares = squares + jnp.sum((first / token_total) ** 2)
    squares = squares + jnp.sum((second[:rest] / token_total) ** 2)
    squares = squares + 0.5 * jnp.sum((second[rest:] / token_total) ** 2)
    plane[spot] = jnp.full((8, LANES), squares, F32)
    for entry in plane_copies:
        entry.start()
    for entry in plane_copies:
        entry.wait_recv()
    column[z] = jnp.sum(plane[...], axis=0)
    for entry in column_copies:
        entry.start()
    for entry in column_copies:
        entry.wait_recv()
    square_ref[...] = jnp.sum(column[...], axis=0)
    ada_copy.wait_recv()
    for i, entry in enumerate(row_copies):
        keep(i).wait()
        entry.wait_recv()
    for entry in swaps + [ada_swap] + sends:
        entry.wait_send()
    for entry in [part for pair in scatters for part in pair] + adas:
        entry.drain()


def closing(count, tokens, cond, h_one, grads, dx, wa, norms, near, far, dwa_two, dp_two,
            last, middle_sum, token_total):
    rows, width = dx.shape
    conds = cond.shape[1]
    part = width // count
    outer = count // 4
    half_cols = wa.shape[0] // count // 2
    vm = pl.BlockSpec(memory_space=pltpu.VMEM)
    hbm = pl.BlockSpec(memory_space=pl.ANY)
    copies = 5 + 10 * (2 + outer - 1) + rows // ROW_BLOCK + 1 + 7 + outer - 1
    act = pltpu.VMEM((rows, width), BF)
    half_weights = pltpu.VMEM((width, 3 * width // 2), BF)
    return pl.pallas_call(
        functools.partial(closing_kernel, count=count, token_total=token_total),
        in_specs=[hbm] * 12 + [vm] * 3,
        out_specs=[hbm] + [vm] * 5,
        out_shape=[
            shape_of((2, rows, width), F32),
            shape_of((part, 3 * width // 2), F32),
            shape_of((part, width // 2), F32),
            shape_of((2, half_cols, conds), F32),
            shape_of((8, conds), F32),
            shape_of((8, LANES), F32),
        ],
        scratch_shapes=[
            pltpu.VMEM((width, rows), BF), pltpu.VMEM((3, rows, width), BF), act,
            pltpu.VMEM((rows, conds), BF),
            half_weights, half_weights,
            pltpu.VMEM((width, conds), BF),
            pltpu.VMEM(dwa_two.shape, F32),
            pltpu.VMEM((rows, width), F32),
            pltpu.VMEM((3, outer, 2, 2, part, width // 2), F32),
            pltpu.VMEM((rows, width), F32),
            pltpu.VMEM((conds + 16, 2 * width), F32),
            pltpu.VMEM((16, width), F32),
            pltpu.VMEM((outer, 2, 2, 2, half_cols + 16, conds), BF),
            pltpu.VMEM((8, 8, LANES), F32),
            pltpu.VMEM((outer, 8, LANES), F32),
        ]
        + scatter_buffers(outer, 3, part, width // 2)
        + scatter_buffers(outer, None, half_cols + 16, conds)[1:]
        + scatter_buffers(outer, None, part, width // 2)[1:]
        + [pltpu.SemaphoreType.DMA((12,)), pltpu.SemaphoreType.DMA((2, copies))],
        compiler_params=pltpu.CompilerParams(
            vmem_limit_bytes=VMEM_LIMIT, collective_id=2, has_side_effects=True
        ),
        name="closing",
    )(tokens, cond, h_one, *grads, near, far, wa, dwa_two, dx, last, middle_sum, norms, dp_two)


def update_kernel(half, step, ina_ref, inb_ref, resa_ref, resb_ref, up_ref, down_ref, qkv_ref,
                  out_ref, ada_ref, norm_ref, square_ref, *refs, token_total):
    state, (grad_out, res_out, norm_out), new = refs[:18], refs[18:21], refs[21:]
    i, steps = pl.program_id(0), pl.num_programs(0)
    here = (i // (steps // 2)) == half[0]

    @pl.when(here)
    def _():
        grad_out[...] = ina_ref[0]
        res_out[...] = resa_ref[...]

    @pl.when(jnp.logical_not(here))
    def _():
        grad_out[...] = inb_ref[0]
        res_out[...] = resb_ref[...]

    grad_norm = jnp.sqrt(square_ref[0:1, :])
    norm_out[...] = grad_norm
    clip_factor = jnp.minimum(1.0, clip_limit / (grad_norm + 1e-06))[:, 0:1] / token_total
    count = jnp.full((1, LANES), step[0], jnp.int32).astype(F32)
    fix_one = (1.0 - jnp.exp(count * math.log(0.9)))[:, 0:1]
    fix_two = (1.0 - jnp.exp(count * math.log(0.999)))[:, 0:1]

    def update(index, grad):
        entry = [ref[...] for ref in state[3 * index : 3 * index + 3]]
        values = adam_update(*entry, grad, clip_factor, fix_one, fix_two, step_rates[index],
                             decay_rates[index])
        for ref, value in zip(new[3 * index : 3 * index + 3], values):
            ref[...] = value

    update(0, ada_ref[...])
    update(4, up_ref[...])
    update(5, down_ref[...])

    @pl.when(i < 3)
    def _():
        update(2, qkv_ref[...][None])

    @pl.when(i == 3)
    def _():
        update(1, norm_ref[:, : state[3].shape[1]])
        update(3, out_ref[...])


def update_stage(half, step, input_rows, result, result_far, sums, state, token_total):
    rows, width = result.shape
    middle_sum, qkv_sum, out_sum, ada_sum, norm_sum, squares = sums
    ada_sum = ada_sum.reshape(-1, ada_sum.shape[-1])
    steps = 4
    blocks = steps // 2
    size = rows // blocks
    hidden = middle_sum.shape[1] // 2

    def side(match, lead):
        def index(i, half, step):
            same = (i // blocks == half[0]) == match
            at = jnp.where(same, i % blocks, jnp.where(i < blocks, 0, blocks - 1))
            return lead + (at, 0)

        return index

    block = (size, width)
    out = pl.BlockSpec(block, lambda i, half, step: (i, 0))
    fixed = lambda entry: pl.BlockSpec(entry.shape, lambda *_, n=entry.ndim: (0,) * n)
    slab = pl.BlockSpec((state[12].shape[0], hidden // steps), lambda i, *_: (0, i))
    next_slab = pl.BlockSpec((state[12].shape[0], hidden // steps), lambda i, *_: (0, steps + i))
    third = (state[6].shape[1], state[6].shape[2])
    qkv_spec = pl.BlockSpec((1,) + third, lambda i, *_: (jnp.minimum(i, 2), 0, 0))
    ada_spec = pl.BlockSpec((ada_sum.shape[0] // steps, ada_sum.shape[1]), lambda i, *_: (i, 0))
    specs = (
        [ada_spec] * 3 + [fixed(state[3])] * 3 + [qkv_spec] * 3 + [fixed(state[9])] * 3
        + [slab] * 6
    )
    return pl.pallas_call(
        functools.partial(update_kernel, token_total=token_total),
        grid_spec=pltpu.PrefetchScalarGridSpec(
            num_scalar_prefetch=2,
            grid=(steps,),
            in_specs=[
                pl.BlockSpec((1,) + block, side(True, (0,))),
                pl.BlockSpec((1,) + block, side(False, (1,))),
                pl.BlockSpec(block, side(True, ())),
                pl.BlockSpec(block, side(False, ())),
                slab, next_slab,
                pl.BlockSpec(third, lambda i, *_: (0, jnp.minimum(i, 2))),
                fixed(out_sum), ada_spec, fixed(norm_sum), fixed(squares),
            ] + specs,
            out_specs=[out, out, pl.BlockSpec((1, LANES), lambda *_: (0, 0))] + specs,
        ),
        out_shape=[shape_of((2 * rows, width), F32), shape_of((2 * rows, width), BF),
                   shape_of((1, LANES), F32)]
        + [shape_of(entry.shape, F32) for entry in state],
        compiler_params=params(),
        name="update_stage",
    )(half, step, input_rows, input_rows, result, result_far, middle_sum, middle_sum, qkv_sum,
      out_sum, ada_sum, norm_sum, squares, *state)


def factors(count):
    return (count // 4, 2, 2)


def swap_mp(value):
    return lax.ppermute(value, "mp", [(0, 1), (1, 0)])


def swap_dp(value, distance):
    count = lax.axis_size("dp")
    return lax.ppermute(value, "dp", [(i, i ^ distance) for i in range(count)])


def turn_dp(value, distance):
    count = lax.axis_size("dp")
    return lax.ppermute(value, "dp", [(i, (i + distance) % count) for i in range(count)])


def pick(value, index, axis):
    return lax.dynamic_index_in_dim(value, index, axis, keepdims=False)


def scatter_sum(parts, order):
    count = lax.axis_size("dp")
    outer, mid, inner = factors(count)
    me = lax.axis_index("dp")
    place = {4: me // 4, 2: (me // 2) % 2, 1: me % 2}

    def widen(part):
        return part.reshape((outer, mid, inner) + part.shape[1:]).astype(F32)

    total = widen(parts[0])
    for part in parts[1:]:
        total = total + widen(part)
    for distance in order:
        axis = 1 if (distance == 2 or total.ndim == 4) else 2
        gone = pick(total, 1 - place[distance], axis).astype(BF)
        total = pick(total, place[distance], axis) + swap_dp(gone, distance).astype(F32)
    arrived = [
        turn_dp(pick(total, (place[4] + hop) % outer, 0).astype(BF), 4 * hop)
        for hop in range(1, outer)
    ]
    total = pick(total, place[4], 0)
    for piece in arrived:
        total = total + piece.astype(F32)
    return total


def scatter_halves(near, far_sum):
    count = lax.axis_size("dp")
    width, columns = near.shape
    cut = columns // 2 // LANES * LANES
    shards = lambda value: value.reshape(count, width // count, value.shape[1])
    first = scatter_sum([shards(near[:, :cut]), shards(far_sum[:, :cut])], (2, 1))
    second = scatter_sum([shards(near[:, cut:]), shards(far_sum[:, cut:])], (1, 2))
    return jnp.concatenate([first, second], axis=1)


def sum_everywhere(value):
    value = value + swap_mp(value)
    distance = 1
    while distance < lax.axis_size("dp"):
        value = value + swap_dp(value, distance)
        distance *= 2
    return value


def in_order(half, near, far):
    first = jnp.where(half == 0, near, far)
    second = jnp.where(half == 0, far, near)
    return jnp.concatenate([first, second], axis=0)


def per_device(
    tokens, cond, segments, out_grad, step,
    ada_weight, ada_first, ada_second,
    norm_params, norm_first, norm_second,
    qkv_weight, qkv_first, qkv_second,
    out_weight, out_first, out_second,
    up_weight, up_first, up_second,
    down_weight, down_first, down_second,
):
    count = lax.axis_size("dp")
    width = tokens.shape[1]
    rows = tokens.shape[0] // 2
    conds = cond.shape[1]
    part = width // count
    half = lax.axis_index("mp")
    half_ref = half.reshape(1).astype(jnp.int32)
    token_total = float(tokens.shape[0] * count)

    fused = count == 16 and part % 16 == 0 and ada_weight.shape[1] % 32 == 0
    if fused:
        (h_one, queries, keys, values, mixed, near, far, wa, cosines, sines, query_lanes,
         key_lanes, up_near, up_far, down_near, down_far, lse, norms) = opening(
            count, tokens, cond, segments, rope_constants(rows),
            (ada_weight.T, norm_params, qkv_weight, out_weight.T, up_weight, down_weight.T),
        )
        wa = wa.reshape(-1, conds)
        features, tables = (query_lanes, key_lanes), (cosines, sines)
    else:
        ada_shard = ada_weight.T.astype(BF)
        small_shard = jnp.concatenate(
            [
                qkv_weight.astype(BF).transpose(1, 0, 2).reshape(part, -1),
                jnp.pad(norm_params.astype(BF).T, ((0, 0), (0, LANES - 8))),
            ],
            axis=1,
        )
        down_shard = jnp.concatenate([down_weight.astype(BF).T, out_weight.astype(BF).T], axis=1)
        segment = pick(segments, half, 0)
        features = document_features(segment)
        tables = rope_tables(rows)
        wa = lax.all_gather(ada_shard, "dp", axis=0, tiled=True)
        near = lax.all_gather(small_shard, "dp", axis=0, tiled=True)
        far = swap_mp(near)
        norms = near[:, -LANES:].T[:8].astype(F32)
        up_near = lax.all_gather(up_weight.astype(BF), "dp", axis=0, tiled=True)
        down_near = lax.all_gather(down_shard, "dp", axis=0, tiled=True)
        up_far, down_far = swap_mp(up_near), swap_mp(down_near)
        h_one, queries, keys, values = first_stage(
            half_ref, tokens, cond, wa, norms, near, far, tables
        )
        mixed, lse = attend(queries, keys, values, segment, features)
    result, dx, upstream, z, gy, h_two, du, ga, dwa_two, dp_two = middle_stage(
        half_ref, tokens, out_grad, cond, mixed, wa, norms, up_near, up_far, down_near, down_far
    )
    result_far = swap_mp(result)

    block = width // 2
    if fused:
        *grads, last, middle_sum = spread(
            count, h_two, gy, ga, du, z, mixed, queries, keys, values, upstream, lse, features,
            tables,
        )
    else:
        steps = du.shape[1] // 2 // block

        def middle_grads(which, name):
            return weight_grads(
                [gy.T, h_two.T, ga.T], [du, z, mixed],
                [(steps, 1, 0, which * steps), (steps, 0, 1, which * steps), (1, 2, 2, which)],
                block, name,
            )

        middle_far = swap_mp(middle_grads(1, "middle_grads_far"))
        middle_near = middle_grads(0, "middle_grads_near")
        middle_sum = scatter_halves(middle_near, middle_far)
        grads = attend_back(
            queries, keys, values, upstream, mixed, lse, segment, features, tables
        )

    if fused:
        input_rows, first_sum, out_sum, ada_halves, norm_sum, squares = closing(
            count, tokens, cond, h_one, grads, dx, wa, norms, near, far, dwa_two, dp_two,
            last, middle_sum, token_total,
        )
        turn = lambda group: tuple(entry.T for entry in group)
        ada_state = (ada_weight, ada_first, ada_second)
        out_state = (out_weight, out_first, out_second)
        down_state = (down_weight, down_first, down_second)
        state = (
            *turn(ada_state), norm_params, norm_first, norm_second,
            qkv_weight, qkv_first, qkv_second, *turn(out_state), up_weight, up_first, up_second,
            *turn(down_state),
        )
        input_grad, result, grad_norm, *new = update_stage(
            half_ref, step, input_rows, result, result_far,
            (middle_sum, first_sum, out_sum, ada_halves, norm_sum, squares), state, token_total,
        )
        return (
            result, input_grad, grad_norm[0, :1],
            *turn(new[:3]), *new[3:9], *turn(new[9:12]), *new[12:15], *turn(new[15:]),
        )

    def first_grads(which, name):
        return weight_grads(
            [h_one], list(grads), [(1, 0, index, which) for index in range(3)], block, name
        )

    first_far = swap_mp(first_grads(1, "first_grads_far"))
    first_near = first_grads(0, "first_grads_near")
    first_sum = scatter_halves(first_near, first_far)

    input_grad, dwa_one, dp_one = last_stage(
        half_ref, tokens, cond, dx, grads, wa, norms, near, far
    )
    input_far = swap_mp(input_grad)

    dwa = jnp.concatenate([dwa_one, dwa_two], axis=1)
    ada_cols = dwa.shape[1] // count
    dwa_rows = dwa[:conds].T.astype(BF).reshape(count, 2, ada_cols // 2, conds)
    norm_rows = jnp.concatenate(
        [dp_one[0:1], dp_two[0:1], dwa[conds].reshape(6, width)], axis=0
    ).astype(BF)
    norm_rows = norm_rows.reshape(8, count, part).transpose(1, 0, 2)
    norm_rows = jnp.pad(norm_rows, ((0, 0), (0, 0), (0, conds - part)))
    ada_near = jnp.concatenate([pick(dwa_rows, half, 1), norm_rows], axis=1)
    ada_far = swap_mp(jnp.concatenate([pick(dwa_rows, 1 - half, 1), norm_rows], axis=1))
    ada_sum = scatter_sum([ada_near, ada_far], (2, 1))
    ada_half, norm_sum = ada_sum[: ada_cols // 2], ada_sum[ada_cols // 2 :, :part]
    ada_rows = in_order(half, ada_half, swap_mp(ada_half))

    wide_cols = du.shape[1] // 2
    up_mean = middle_sum[:, :wide_cols] / token_total
    down_mean = middle_sum[:, wide_cols : 2 * wide_cols] / token_total
    out_mean = middle_sum[:, 2 * wide_cols :] / token_total
    qkv_mean = first_sum / token_total
    ada_mean = ada_rows / token_total
    norm_mean = norm_sum / token_total
    local_sq = (
        jnp.sum(qkv_mean * qkv_mean)
        + jnp.sum(out_mean * out_mean)
        + jnp.sum(up_mean * up_mean)
        + jnp.sum(down_mean * down_mean)
        + 0.5 * (jnp.sum(ada_mean * ada_mean) + jnp.sum(norm_mean * norm_mean))
    )
    grad_norm = jnp.sqrt(sum_everywhere(jnp.full((8, LANES), local_sq, F32))[0, 0])
    clip_factor = jnp.minimum(1.0, clip_limit / (grad_norm + 1e-06))
    step_count = step[0].astype(F32)
    fix_one = 1.0 - jnp.exp(step_count * math.log(0.9))
    fix_two = 1.0 - jnp.exp(step_count * math.log(0.999))

    ada_grad = ada_mean.T
    qkv_grad = qkv_mean.reshape(part, 3, -1).transpose(1, 0, 2)
    state = (
        (ada_weight, ada_first, ada_second, ada_grad),
        (norm_params, norm_first, norm_second, norm_mean),
        (qkv_weight, qkv_first, qkv_second, qkv_grad),
        (out_weight, out_first, out_second, out_mean.T),
        (up_weight, up_first, up_second, up_mean),
        (down_weight, down_first, down_second, down_mean.T),
    )
    outputs = [
        in_order(half, result, result_far),
        in_order(half, input_grad, input_far),
        grad_norm.reshape(1),
    ]
    for index, entry in enumerate(state):
        outputs += adam_update(
            *entry, clip_factor, fix_one, fix_two, step_rates[index], decay_rates[index]
        )
    return tuple(outputs)


def solution(mesh):
    column = (P(None, "dp"),) * 3
    weights = (
        column
        + column
        + (P(None, "dp", "mp"),) * 3
        + (P("mp", "dp"),) * 3
        + (P("dp", "mp"),) * 3
        + (P("mp", "dp"),) * 3
    )
    row = P("dp", None)
    return jax.shard_map(
        per_device,
        mesh=mesh,
        in_specs=(row, row, row, row, P()) + weights,
        out_specs=(row, row, P()) + weights,
        check_vma=False,
    )
```

```python
import functools
import math

import jax
import jax.numpy as jnp
import numpy as np
from jax import lax
from jax.experimental import pallas as pl
from jax.experimental.pallas import tpu as pltpu
from jax.sharding import PartitionSpec as P

HEAD_DIM = 64
LANES = 128
MASKED = -1e30
ROW_BLOCK = 256
VMEM_LIMIT = 64_000_000
clip_limit = 1.0
step_rates = (0.075, 0.75, 0.075, 0.25, 0.075, 0.075)
decay_rates = (0.01, 0.0, 0.01, 0.01, 0.01, 0.01)

F32 = jnp.float32
BF = jnp.bfloat16
NN = (((1,), (0,)), ((), ()))
NT = (((1,), (1,)), ((), ()))


def dot(left, right, dims=NN):
    return lax.dot_general(left, right, dims, preferred_element_type=F32)


def shape_of(shape, dtype):
    return jax.ShapeDtypeStruct(shape, dtype)


def resident(shape, index):
    return pl.BlockSpec(shape, lambda *_: index, pipeline_mode=pl.Buffered(1))


def params():
    return pltpu.CompilerParams(vmem_limit_bytes=VMEM_LIMIT)


def adam_update(weight, first, second, grad, clip_factor, fix_one, fix_two, rate, decay):
    clipped = grad * clip_factor
    first_new = 0.9 * first + 0.1 * clipped
    second_new = 0.999 * second + 0.001 * clipped * clipped
    update = first_new / fix_one / (jnp.sqrt(second_new / fix_two) + 1e-08) + decay * weight
    return (weight - rate * update, first_new, second_new)


def rope_tables(length):
    half = HEAD_DIM // 2
    inverse = jnp.exp(jnp.arange(half, dtype=F32) * (-2.0 * math.log(10000.0) / HEAD_DIM))
    angles = jnp.arange(length, dtype=F32)[:, None] * inverse[None, :]
    cosines, sines = jnp.cos(angles), jnp.sin(angles)
    return (
        jnp.concatenate([cosines] * 4, axis=1),
        jnp.concatenate([-sines, sines, -sines, sines], axis=1),
    )


def rope_constants(length, fine=32):
    half = HEAD_DIM // 2
    inverse = np.exp(np.arange(half) * (-2.0 * math.log(10000.0) / HEAD_DIM))
    sign = np.repeat([-1.0, 1.0, -1.0, 1.0], half)
    tables = []
    for positions in (np.arange(0, length, fine), np.arange(fine)):
        angles = np.tile(positions[:, None] * inverse[None, :], (1, 4))
        tables += [np.cos(angles), np.sin(angles) * sign]
    return [jnp.asarray(table, F32) for table in tables]


def swap_halves(values):
    width = values.shape[1]
    lane = lax.broadcasted_iota(jnp.int32, values.shape, 1)
    ahead = pltpu.roll(values, width - HEAD_DIM // 2, 1)
    behind = pltpu.roll(values, HEAD_DIM // 2, 1)
    return jnp.where(lane % HEAD_DIM < HEAD_DIM // 2, ahead, behind)


def silu_low(cond):
    value = cond.astype(F32)
    return (value / (1.0 + jnp.exp(-value))).astype(BF)


def normalize(rows):
    centre = rows - jnp.mean(rows, axis=-1, keepdims=True)
    scale = lax.rsqrt(jnp.mean(centre * centre, axis=-1, keepdims=True) + 1e-05)
    return centre * scale, scale


def norm_backward(grad, normal, scale):
    return scale * (
        grad
        - jnp.mean(grad, axis=-1, keepdims=True)
        - normal * jnp.mean(grad * normal, axis=-1, keepdims=True)
    )


def cond_rows(cond):
    return jnp.concatenate([cond.T, jnp.ones((16, cond.shape[0]), BF)], axis=0)


def first_kernel(half, x_ref, c_ref, wa_ref, p_ref, wqa_ref, wqb_ref, cos_ref, sin_ref,
                 h_ref, q_ref, k_ref, v_ref):
    width = x_ref.shape[1]
    own = width // 2
    cond = silu_low(c_ref[...])
    mod = dot(cond, wa_ref[0 : 2 * width, :], NT)
    shift = mod[:, :width] + p_ref[2:3, :]
    scale = mod[:, width:] + p_ref[3:4, :]
    normal, _ = normalize(x_ref[...].astype(F32))
    h = (normal * p_ref[0:1, :] * (1.0 + scale) + shift).astype(BF)
    h_ref[...] = h
    cos = jnp.concatenate([cos_ref[...]] * (own // LANES), axis=1)
    sin = jnp.concatenate([sin_ref[...]] * (own // LANES), axis=1)
    for start, w_ref in ((0, wqa_ref), (own, wqb_ref)):
        cols = slice(start, start + own)
        query = dot(h, w_ref[:, 0:own])
        query = query * cos + swap_halves(query) * sin
        q_ref[:, cols] = (query * HEAD_DIM**-0.5).astype(BF)
        key = dot(h, w_ref[:, own : 2 * own])
        k_ref[:, cols] = (key * cos + swap_halves(key) * sin).astype(BF)
        v_ref[:, cols] = dot(h, w_ref[:, 2 * own :]).astype(BF)


def first_stage(half, tokens, cond, wa, norms, near, far, tables):
    width = tokens.shape[1]
    rows = tables[0].shape[0]
    blocks = rows // ROW_BLOCK
    mine = lambda i, half: (half[0] * blocks + i, 0)
    plain = lambda i, half: (i, 0)
    row = pl.BlockSpec((ROW_BLOCK, width), plain)
    return pl.pallas_call(
        first_kernel,
        grid_spec=pltpu.PrefetchScalarGridSpec(
            num_scalar_prefetch=1,
            grid=(blocks,),
            in_specs=[
                pl.BlockSpec((ROW_BLOCK, width), mine),
                pl.BlockSpec((ROW_BLOCK, cond.shape[1]), mine),
                resident(wa.shape, (0, 0)),
                resident(norms.shape, (0, 0)),
                resident((width, 3 * width // 2), (0, 0)),
                resident((width, 3 * width // 2), (0, 0)),
                pl.BlockSpec((ROW_BLOCK, LANES), plain),
                pl.BlockSpec((ROW_BLOCK, LANES), plain),
            ],
            out_specs=[row] * 4,
        ),
        out_shape=[shape_of((rows, width), BF)] * 4,
        compiler_params=params(),
        name="first_stage",
    )(half, tokens, cond, wa, norms, near, far, *tables)


def split_heads(pair, other):
    low = lax.broadcasted_iota(jnp.int32, pair.shape, 1) < HEAD_DIM
    return jnp.where(low, pair, other), jnp.where(low, other, pair)


def attend_kernel(lo_ref, hi_ref, q_ref, k_ref, v_ref, fq_ref, fk_ref, o_ref, lse_ref,
                  qz, kz, vt, *, bq, bk):
    length = q_ref.shape[0]
    qz[0], qz[1] = split_heads(q_ref[...], fq_ref[...])
    kz[0], kz[1] = split_heads(k_ref[...], fk_ref[...])
    vt[...] = v_ref[...].T

    def query_block(i, _):
        off = pl.multiple_of(i * bq, bq)
        queries = [qz[h, pl.ds(off, bq), :] for h in range(2)]

        def key_block(j, carry):
            koff = pl.multiple_of(j * bk, bk)
            scores = [dot(kz[h, pl.ds(koff, bk), :], queries[h], NT) for h in range(2)]
            out = []
            for h in range(2):
                top, total, mixed = carry[3 * h : 3 * h + 3]
                new_top = jnp.maximum(top, jnp.max(scores[h], axis=0, keepdims=True))
                weights = jnp.exp(scores[h] - new_top)
                fade = jnp.exp(top - new_top)
                total = total * fade + jnp.sum(weights, axis=0, keepdims=True)
                values = vt[HEAD_DIM * h : HEAD_DIM * (h + 1), pl.ds(koff, bk)]
                mixed = mixed * fade + dot(values, weights.astype(BF))
                out += [new_top, total, mixed]
            return tuple(out)

        start = (
            jnp.full((1, bq), -3e38, F32),
            jnp.zeros((1, bq), F32),
            jnp.zeros((HEAD_DIM, bq), F32),
        )
        done = lax.fori_loop(lo_ref[i], hi_ref[i], key_block, start * 2)
        mixed = jnp.concatenate([done[2] / done[1], done[5] / done[4]], axis=0)
        o_ref[pl.ds(off, bq), :] = mixed.T.astype(BF)
        lse_ref[0, 0:1, pl.ds(off, bq)] = done[0] + jnp.log(done[1])
        lse_ref[0, 1:2, pl.ds(off, bq)] = done[3] + jnp.log(done[4])
        return 0

    lax.fori_loop(0, length // bq, query_block, 0)


def block_ranges(segment, block, other):
    first, last = segment[::block], segment[block - 1 :: block]
    low = jnp.sum(segment[None, :] < first[:, None], axis=1)
    high = jnp.sum(segment[None, :] <= last[:, None], axis=1)
    return (low // other).astype(jnp.int32), ((high + other - 1) // other).astype(jnp.int32)


def document_features(segment):
    lane = lax.broadcasted_iota(jnp.int32, (segment.shape[0], LANES), 1) % HEAD_DIM
    same = lane == segment[:, None]
    query = jnp.where(same, 1.0, 0.0).astype(BF)
    key = jnp.where((lane < 4) & ~same, MASKED, 0.0).astype(BF)
    return query, key


def attend(queries, keys, values, segment, features, bq=1024, bk=512):
    length, width = queries.shape
    bq, bk = min(bq, length), min(bk, length)
    pairs = width // LANES
    low, high = block_ranges(segment, bq, bk)
    pair = pl.BlockSpec((length, LANES), lambda p, *_: (0, p))
    fixed = pl.BlockSpec((length, LANES), lambda p, *_: (0, 0))
    scratch = pltpu.VMEM((2, length, LANES), BF)
    return pl.pallas_call(
        functools.partial(attend_kernel, bq=bq, bk=bk),
        grid_spec=pltpu.PrefetchScalarGridSpec(
            num_scalar_prefetch=2,
            grid=(pairs,),
            in_specs=[pair, pair, pair, fixed, fixed],
            out_specs=[pair, pl.BlockSpec((1, 2, length), lambda p, *_: (p, 0, 0))],
            scratch_shapes=[scratch, scratch, pltpu.VMEM((LANES, length), BF)],
        ),
        out_shape=[shape_of((length, width), BF), shape_of((pairs, 2, length), F32)],
        compiler_params=params(),
        name="attend",
    )(low, high, queries, keys, values, *features)


def attend_back_kernel(lo_ref, hi_ref, q_ref, k_ref, v_ref, do_ref, o_ref, lse_ref, fq_ref,
                       fk_ref, cos_ref, sin_ref, dq_ref, dk_ref, dv_ref,
                       qz, kz, qm, dm, vm, kt, delta, dqt, *, bq, bk):
    length = q_ref.shape[0]
    zero = jnp.zeros((length, LANES), BF)
    qz[0], qz[1] = split_heads(q_ref[...], fq_ref[...])
    kz[0], kz[1] = split_heads(k_ref[...], fk_ref[...])
    qm[0], qm[1] = split_heads(q_ref[...], zero)
    dm[0], dm[1] = split_heads(do_ref[...], zero)
    vm[0], vm[1] = split_heads(v_ref[...], zero)
    kt[...] = k_ref[...].T
    product = (do_ref[...].astype(F32) * o_ref[...].astype(F32)).T
    delta[0:1, :] = jnp.sum(product[:HEAD_DIM], axis=0, keepdims=True)
    delta[1:2, :] = jnp.sum(product[HEAD_DIM:], axis=0, keepdims=True)
    dqt[...] = jnp.zeros_like(dqt)

    def unrotate(grad, off, rows):
        cos, sin = cos_ref[pl.ds(off, rows), :], sin_ref[pl.ds(off, rows), :]
        return (grad * cos - swap_halves(grad) * sin).astype(BF)

    def key_block(j, _):
        koff = pl.multiple_of(j * bk, bk)
        keys = [kz[h, pl.ds(koff, bk), :] for h in range(2)]
        values = [vm[h, pl.ds(koff, bk), :] for h in range(2)]

        def query_block(i, carry):
            dk, dv = carry
            off = pl.multiple_of(i * bq, bq)
            scores = [dot(keys[h], qz[h, pl.ds(off, bq), :], NT) for h in range(2)]
            grads = [dot(values[h], dm[h, pl.ds(off, bq), :], NT) for h in range(2)]
            for h in range(2):
                weights = jnp.exp(scores[h] - lse_ref[0, h : h + 1, pl.ds(off, bq)])
                dv = dv + dot(weights.astype(BF), dm[h, pl.ds(off, bq), :])
                ds = (weights * (grads[h] - delta[h : h + 1, pl.ds(off, bq)])).astype(BF)
                dk = dk + dot(ds, qm[h, pl.ds(off, bq), :])
                head = slice(HEAD_DIM * h, HEAD_DIM * (h + 1))
                dqt[head, pl.ds(off, bq)] += dot(kt[head, pl.ds(koff, bk)], ds)
            return dk, dv

        zeros = jnp.zeros((bk, LANES), F32)
        dk, dv = lax.fori_loop(lo_ref[j], hi_ref[j], query_block, (zeros, zeros))
        dk_ref[pl.ds(koff, bk), :] = unrotate(dk, koff, bk)
        dv_ref[pl.ds(koff, bk), :] = dv.astype(BF)
        return 0

    lax.fori_loop(0, length // bk, key_block, 0)
    dq_ref[...] = unrotate(dqt[...].T * HEAD_DIM**-0.5, 0, length)


def attend_back(queries, keys, values, upstream, mixed, lse, segment, features, tables,
                bq=512, bk=256):
    length, width = queries.shape
    bq, bk = min(bq, length), min(bk, length)
    pairs = width // LANES
    low, high = block_ranges(segment, bk, bq)
    pair = pl.BlockSpec((length, LANES), lambda p, *_: (0, p))
    fixed = pl.BlockSpec((length, LANES), lambda p, *_: (0, 0))
    scratch = pltpu.VMEM((2, length, LANES), BF)
    return pl.pallas_call(
        functools.partial(attend_back_kernel, bq=bq, bk=bk),
        grid_spec=pltpu.PrefetchScalarGridSpec(
            num_scalar_prefetch=2,
            grid=(pairs,),
            in_specs=[pair] * 5
            + [pl.BlockSpec((1, 2, length), lambda p, *_: (p, 0, 0))]
            + [fixed] * 4,
            out_specs=[pair] * 3,
            scratch_shapes=[scratch] * 5
            + [
                pltpu.VMEM((LANES, length), BF),
                pltpu.VMEM((8, length), F32),
                pltpu.VMEM((LANES, length), F32),
            ],
        ),
        out_shape=[shape_of((length, width), BF)] * 3,
        compiler_params=params(),
        name="attend_back",
    )(low, high, queries, keys, values, upstream, mixed, lse, *features, *tables)


def middle_kernel(half, x_ref, g_ref, c_ref, o_ref, wa_ref, p_ref, woa_ref, wob_ref, w1a_in,
                  w1b_in, w2a_in, w2b_in,
                  res_ref, dx_ref, do_ref, z_ref, gy_ref, h_ref, du_ref, ga_ref, dwa_ref,
                  dp_ref, slope, w1a_ref, w1b_ref, w2a_ref, w2b_ref, sems, *, chunk):
    width = x_ref.shape[1]
    own = width // 2
    hidden = w1a_ref.shape[1]
    loads = [
        pltpu.make_async_copy(src.at[:, pl.ds(0, hidden)], dst, sems.at[index])
        for index, (src, dst) in enumerate(
            ((w1a_in, w1a_ref), (w2a_in, w2a_ref), (w1b_in, w1b_ref), (w2b_in, w2b_ref))
        )
    ]

    @pl.when(pl.program_id(0) == 0)
    def _():
        for load in loads:
            load.start()

    cond = silu_low(c_ref[...])

    def modulation(block):
        rows = wa_ref[block * width : (block + 1) * width, :]
        return dot(cond, rows, NT) + p_ref[block + 2 : block + 3, :]

    gate_one, shift, scale, gate_two = (modulation(block) for block in (2, 3, 4, 5))
    branch = dot(o_ref[:, :own], woa_ref[...], NT) + dot(o_ref[:, own:], wob_ref[...], NT)
    middle = x_ref[...].astype(F32) + gate_one * branch
    normal, rstd = normalize(middle)
    gain = p_ref[1:2, :]
    spread = 1.0 + scale
    h = (normal * gain * spread + shift).astype(BF)
    h_ref[...] = h.T

    @pl.when(pl.program_id(0) == 0)
    def _():
        for load in loads:
            load.wait()

    root = math.sqrt(2.0 / math.pi)
    out = jnp.zeros_like(middle)
    for start, up_ref, down_ref in ((0, w1a_ref, w2a_ref), (hidden, w1b_ref, w2b_ref)):
        for at in range(0, hidden, chunk):
            u = dot(h, up_ref[:, at : at + chunk])
            square = u * u
            flat = jnp.tanh(u * (0.044715 * root * square + root))
            half_up = 0.5 * flat + 0.5
            z = (u * half_up).astype(BF)
            z_ref[:, start + at : start + at + chunk] = z
            bend = u * (6.0 * 0.044715 * root * square + 2.0 * root)
            slope[:, start + at : start + at + chunk] = (
                half_up * (bend * (1.0 - half_up) + 1.0)
            ).astype(slope.dtype)
            out = out + dot(z, down_ref[:, at : at + chunk], NT)

    g = g_ref[...].astype(F32)
    res_ref[...] = (middle + gate_two * out).astype(BF)
    gy = (gate_two * g).astype(BF)
    gy_ref[...] = gy.T
    dgate_two = (g * out).astype(BF)

    dh = jnp.zeros_like(middle)
    for start, up_ref, down_ref in ((0, w1a_ref, w2a_ref), (hidden, w1b_ref, w2b_ref)):
        for at in range(0, hidden, chunk):
            dz = dot(gy, down_ref[:, at : at + chunk])
            du = (dz * slope[:, start + at : start + at + chunk]).astype(BF)
            du_ref[:, start + at : start + at + chunk] = du
            dh = dh + dot(du, up_ref[:, at : at + chunk], NT)

    dn = dh * normal
    dx = g + norm_backward(dh * gain * spread, normal, rstd)
    dx_ref[...] = dx
    ga = (gate_one * dx).astype(BF)
    ga_ref[...] = ga.T
    do_ref[:, :own] = dot(ga, woa_ref[...]).astype(BF)
    do_ref[:, own:] = dot(ga, wob_ref[...]).astype(BF)

    @pl.when(pl.program_id(0) == 0)
    def _():
        dwa_ref[...] = jnp.zeros_like(dwa_ref)
        dp_ref[...] = jnp.zeros_like(dp_ref)

    rows = cond_rows(cond)
    grads = ((dx * branch).astype(BF), dh.astype(BF), (dn * gain).astype(BF), dgate_two)
    for block, grad in enumerate(grads):
        dwa_ref[:, block * width : (block + 1) * width] += dot(rows, grad)
    dp_ref[0:1, :] += jnp.sum(dn * spread, axis=0, keepdims=True)


def middle_stage(half, tokens, out_grad, cond, mixed, wa, norms, up_near, up_far, down_near,
                 down_far):
    width = tokens.shape[1]
    rows = mixed.shape[0]
    hidden = up_near.shape[1]
    blocks = rows // ROW_BLOCK
    mine = lambda i, half: (half[0] * blocks + i, 0)
    plain = lambda i, half: (i, 0)
    row = pl.BlockSpec((ROW_BLOCK, width), plain)
    wide = pl.BlockSpec((ROW_BLOCK, 2 * hidden), plain)
    narrow = shape_of((rows, width), BF)
    turned = pl.BlockSpec((width, ROW_BLOCK), lambda i, half: (0, i))
    tall = shape_of((width, rows), BF)
    broad = shape_of((rows, 2 * hidden), BF)
    total = (cond.shape[1] + 16, 4 * width)
    return pl.pallas_call(
        functools.partial(middle_kernel, chunk=768),
        grid_spec=pltpu.PrefetchScalarGridSpec(
            num_scalar_prefetch=1,
            grid=(blocks,),
            in_specs=[
                pl.BlockSpec((ROW_BLOCK, width), mine),
                pl.BlockSpec((ROW_BLOCK, width), mine),
                pl.BlockSpec((ROW_BLOCK, cond.shape[1]), mine),
                row,
                resident(wa.shape, (0, 0)),
                resident(norms.shape, (0, 0)),
                resident((width, width // 2), (0, 2 * hidden // width)),
                resident((width, width // 2), (0, 2 * hidden // width)),
                *[pl.BlockSpec(memory_space=pl.ANY)] * 4,
            ],
            out_specs=[row, row, row, wide, turned, turned, wide, turned,
                       pl.BlockSpec(total, lambda i, half: (0, 0)),
                       pl.BlockSpec((8, width), lambda i, half: (0, 0))],
            scratch_shapes=[pltpu.VMEM((ROW_BLOCK, 2 * hidden), F32)]
            + [pltpu.VMEM((width, hidden), BF)] * 4
            + [pltpu.SemaphoreType.DMA((4,))],
        ),
        out_shape=[narrow, shape_of((rows, width), F32), narrow, broad, tall, tall, broad,
                   tall, shape_of(total, F32), shape_of((8, width), F32)],
        compiler_params=params(),
        name="middle_stage",
    )(half, tokens, out_grad, cond, mixed, wa, norms, down_near, down_far, up_near, up_far,
      down_near, down_far)


def last_kernel(half, x_ref, c_ref, dx_ref, dq_ref, dk_ref, dv_ref, wa_ref, p_ref, wqa_ref,
                wqb_ref, out_ref, dwa_ref, dp_ref):
    width = x_ref.shape[1]
    own = width // 2
    cond = silu_low(c_ref[...])
    scale = dot(cond, wa_ref[width : 2 * width, :], NT) + p_ref[3:4, :]
    dh = jnp.zeros(x_ref.shape, F32)
    for start, w_ref in ((0, wqa_ref), (own, wqb_ref)):
        cols = slice(start, start + own)
        for index, grad_ref in enumerate((dq_ref, dk_ref, dv_ref)):
            dh = dh + dot(grad_ref[:, cols], w_ref[:, index * own : (index + 1) * own], NT)
    normal, rstd = normalize(x_ref[...].astype(F32))
    gain = p_ref[0:1, :]
    spread = 1.0 + scale
    dn = dh * normal
    out_ref[...] = dx_ref[...] + norm_backward(dh * gain * spread, normal, rstd)

    @pl.when(pl.program_id(0) == 0)
    def _():
        dwa_ref[...] = jnp.zeros_like(dwa_ref)
        dp_ref[...] = jnp.zeros_like(dp_ref)

    rows = cond_rows(cond)
    dwa_ref[:, :width] += dot(rows, dh.astype(BF))
    dwa_ref[:, width:] += dot(rows, (dn * gain).astype(BF))
    dp_ref[0:1, :] += jnp.sum(dn * spread, axis=0, keepdims=True)


def last_stage(half, tokens, cond, dx, grads, wa, norms, near, far):
    width = tokens.shape[1]
    rows = dx.shape[0]
    blocks = rows // ROW_BLOCK
    mine = lambda i, half: (half[0] * blocks + i, 0)
    row = pl.BlockSpec((ROW_BLOCK, width), lambda i, half: (i, 0))
    total = (cond.shape[1] + 16, 2 * width)
    return pl.pallas_call(
        last_kernel,
        grid_spec=pltpu.PrefetchScalarGridSpec(
            num_scalar_prefetch=1,
            grid=(blocks,),
            in_specs=[
                pl.BlockSpec((ROW_BLOCK, width), mine),
                pl.BlockSpec((ROW_BLOCK, cond.shape[1]), mine),
                row, row, row, row,
                resident(wa.shape, (0, 0)),
                resident(norms.shape, (0, 0)),
                resident((width, 3 * width // 2), (0, 0)),
                resident((width, 3 * width // 2), (0, 0)),
            ],
            out_specs=[row, pl.BlockSpec(total, lambda i, half: (0, 0)),
                       pl.BlockSpec((8, width), lambda i, half: (0, 0))],
        ),
        out_shape=[shape_of((rows, width), F32), shape_of(total, F32), shape_of((8, width), F32)],
        compiler_params=params(),
        name="last_stage",
    )(half, tokens, cond, dx, *grads, wa, norms, near, far)


def weight_grad_kernel(*refs, plan):
    lefts, rights = plan["lefts"], plan["rights"]
    left_refs, right_refs = refs[:lefts], refs[lefts : lefts + rights]
    out_ref, turned = refs[lefts + rights :]
    step = pl.program_id(0)
    for begin, end, left, right in plan["spans"]:

        @pl.when(step == begin)
        def _():
            turned[...] = left_refs[left][...].T

        @pl.when((step >= begin) & (step < end))
        def _():
            out_ref[...] = dot(turned[...], right_refs[right][...]).astype(BF)


def weight_grads(lefts, rights, spans, block, name):
    rows, width = lefts[0].shape
    begin, plan, maps = 0, [], []
    for steps, left, right, first in spans:
        plan.append((begin, begin + steps, left, right))
        maps.append((begin, steps, first))
        begin += steps

    def column_map(begin, steps, first):
        return lambda i: (0, first + jnp.clip(i - begin, 0, steps - 1))

    return pl.pallas_call(
        functools.partial(
            weight_grad_kernel,
            plan={"lefts": len(lefts), "rights": len(rights), "spans": plan},
        ),
        grid=(begin,),
        in_specs=[resident((rows, width), (0, 0))] * len(lefts)
        + [pl.BlockSpec((rows, block), column_map(*entry)) for entry in maps],
        out_specs=pl.BlockSpec((width, block), lambda i: (0, i)),
        out_shape=shape_of((width, begin * block), BF),
        scratch_shapes=[pltpu.VMEM((width, rows), BF)],
        compiler_params=params(),
        name=name,
    )(*lefts, *rights)


class Gather:
    def __init__(self, shard, near, far, cut, sems, place, inner_first=False):
        outer, x, y, z, core = (place[name] for name in ("outer", "x", "y", "z", "core"))
        columns = near.shape[-1]
        flat = len(near.shape) == 2
        rows = near.shape[0] // (4 * outer)

        def slots(ref, first, number, cols):
            if flat:
                at = pl.multiple_of(first * rows, 16)
                return ref.at[pl.ds(at, number * rows), cols]
            return ref.at[pl.ds(first, number), core, :, cols]

        self.count = 0

        def copy(src, dst, device):
            index = self.count
            self.count += 1
            return pltpu.make_async_remote_copy(
                src_ref=src,
                dst_ref=dst,
                send_sem=sems.at[0, index],
                recv_sem=sems.at[1, index],
                device_id=device,
                device_id_type=pl.DeviceIdType.MESH,
            )

        here = 2 * y + x
        across_x = (4 * z + 2 * y + 1 - x, core)
        across_y = (4 * z + 2 * (1 - y) + x, core)
        other_core = (4 * z + here, 1 - core)
        whole = slice(None)
        self.outer = outer
        own = slots(near, 4 * z + here, 1, whole)
        self.local = (shard, own)
        self.inner_first = inner_first
        beyond = [(4 * lax.rem(z + hop, outer) + here, core) for hop in range(1, outer)]
        self.hops = [[copy(shard, own, device)] for device in beyond if not inner_first]
        self.one, self.two, self.swap = [], [], []
        for step in range(outer):
            base = 4 * lax.rem(z + outer - step, outer)
            one, two = [], []
            for odd, cols in enumerate((slice(0, cut), slice(cut, columns))):
                if odd and cut == columns:
                    continue
                mine = slots(near, base + here, 1, cols)
                src = mine
                if step == 0:
                    src = shard.at[:, cols] if flat else shard.at[:, :, cols]
                if step == 0 or not inner_first:
                    one.append(copy(src, mine, across_y if odd else across_x))
                if odd:
                    both = [slots(near, base + 2 * yy + x, 1, cols) for yy in range(2)]
                else:
                    both = [slots(near, base + 2 * y, 2, cols)]
                two += [copy(spot, spot, across_x if odd else across_y) for spot in both]
            self.one.append(one)
            self.two.append(two)
            if step == 0 and inner_first:
                spots = [slots(near, base + 2 * y, 2, slice(0, cut))]
                spots += [slots(near, base + 2 * yy + x, 1, slice(cut, columns)) for yy in range(2)]
                self.hops = [[copy(spot, spot, device) for spot in spots] for device in beyond]
            target = far if flat else near
            self.swap.append(
                [copy(slots(near, base, 4, whole), slots(target, base, 4, whole), other_core)]
            )

    @staticmethod
    def semaphores(outer):
        return pltpu.SemaphoreType.DMA((2, 8 * outer))

    @staticmethod
    def begin(copies):
        for entry in copies:
            entry.start()

    @staticmethod
    def arrive(copies):
        for entry in copies:
            entry.wait_recv()

    def start_hops(self):
        if self.inner_first:
            self.arrive(self.one[0])
        for entry in self.hops:
            self.begin(entry)

    def phase_one(self, step):
        if step:
            self.arrive(self.hops[step - 1])
        self.begin(self.one[step])

    def phase_two(self, step):
        if self.inner_first:
            if step:
                self.arrive(self.hops[step - 1])
        else:
            self.arrive(self.one[step])
        self.begin(self.two[step])

    def phase_swap(self, step):
        self.arrive(self.two[step])
        self.begin(self.swap[step])

    def finish(self, step):
        self.arrive(self.swap[step])

    def drain(self):
        for copies in self.hops + self.one + self.two + self.swap:
            for entry in copies:
                entry.wait_send()


def my_place(count):
    me, core = lax.axis_index("dp"), lax.axis_index("mp")
    return {"outer": count // 4, "z": me // 4, "y": lax.rem(me // 2, 2), "x": lax.rem(me, 2),
            "core": core, "me": me}


def greet(devices):
    barrier = pltpu.get_barrier_semaphore()
    for device in devices:
        pl.semaphore_signal(barrier, inc=1, device_id=device, device_id_type=pl.DeviceIdType.MESH)


def meet(devices):
    pl.semaphore_wait(pltpu.get_barrier_semaphore(), len(devices))


def partners(place):
    z, y, x, core, outer = (place[name] for name in ("z", "y", "x", "core", "outer"))
    here = 2 * y + x
    others = [(4 * lax.rem(z + hop, outer) + here, core) for hop in range(1, outer)]
    return others + [(4 * z + 2 * y + 1 - x, core), (4 * z + 2 * (1 - y) + x, core),
                     (4 * z + here, 1 - core)]


def opening_kernel(tok_ref, cond_ref, seg_ref, cosa_ref, sina_ref, cosb_ref, sinb_ref, ada_ref, norm_ref, qkv_ref, out_ref,
                   up_ref, down_ref,
                   h_out, q_out, k_out, v_out, o_out, near_out, far_out, wa_out, cos_out, sin_out,
                   fq_out, fk_out, up_near, up_far, down_near, down_far, lse_ref, table_ref,
                   h_ref, q_ref, k_ref, v_ref, o_ref, near_ref, far_ref, wa_ref, cos_ref, sin_ref,
                   fq_ref, fk_ref,
                   ada_vm, small_vm, up_vm, down_vm, x_vm, c_vm, qz, kz, vt, local, saved,
                   ada_sems, small_sems, up_sems, down_sems, *, count, cuts, bk):
    place = my_place(count)
    others = partners(place)
    greet(others)
    outer, core = place["outer"], place["core"]
    rows, width = x_vm.shape
    own = width // 2
    hidden = up_ref.shape[1]
    part = width // count
    small = Gather(small_vm, near_ref, far_ref, cuts[0], small_sems, place)
    ada = Gather(ada_vm.at[pl.ds(core, 1)], wa_ref, None, ada_vm.shape[2], ada_sems, place)
    ups = Gather(up_vm, up_near, up_far, cuts[1], up_sems, place)
    downs = Gather(down_vm, down_near, down_far, cuts[2], down_sems, place, inner_first=True)

    start = pl.multiple_of(core * rows, rows)
    loads = [
        pltpu.make_async_copy(tok_ref.at[pl.ds(start, rows)], x_vm, local.at[0]),
        pltpu.make_async_copy(cond_ref.at[pl.ds(start, rows)], c_vm, local.at[1]),
    ]
    stores = [
        pltpu.make_async_copy(*entry.local, local.at[2 + index])
        for index, entry in enumerate((ada, small, ups, downs))
    ]
    saves = {
        name: pltpu.make_async_copy(src, dst, saved.at[index])
        for index, (name, src, dst) in enumerate((
            ("h", h_ref, h_out), ("q", q_ref, q_out), ("k", k_ref, k_out), ("v", v_ref, v_out),
            ("near", near_ref, near_out), ("far", far_ref, far_out), ("wa", wa_ref, wa_out),
            ("cos", cos_ref, cos_out), ("sin", sin_ref, sin_out), ("fq", fq_ref, fq_out),
            ("fk", fk_ref, fk_out),
        ))
    }
    for load in loads:
        load.start()
    ada_vm[...] = ada_ref[...].astype(BF).reshape(ada_vm.shape)
    for c in range(3):
        small_vm[:, c * own : (c + 1) * own] = qkv_ref[c].astype(BF)
    spare = jnp.zeros((LANES - 8, part), F32)
    small_vm[:, 3 * own :] = jnp.concatenate([norm_ref[...], spare], axis=0).T.astype(BF)
    up_vm[...] = up_ref[...].astype(BF)
    down_vm[:, :hidden] = down_ref[...].astype(BF)
    down_vm[:, hidden:] = out_ref[...].astype(BF)
    meet(others)
    first = (ada, small)

    def each(method, *args):
        for entry in first:
            getattr(entry, method)(*args)

    each("start_hops")
    each("phase_one", 0)
    stores[0].start()
    stores[1].start()
    stores[2].start()
    stores[3].start()
    stores[0].wait()
    stores[1].wait()
    each("phase_two", 0)
    downs.phase_one(0)
    each("phase_one", 1)
    fine = cosb_ref.shape[0]

    def rope_rows(step, _):
        at, row = pl.ds(pl.multiple_of(step * fine, fine), fine), pl.ds(step, 1)
        cos_ref[at, :] = cosa_ref[row, :] * cosb_ref[...] - sina_ref[row, :] * sinb_ref[...]
        sin_ref[at, :] = sina_ref[row, :] * cosb_ref[...] + cosa_ref[row, :] * sinb_ref[...]
        return 0

    lax.fori_loop(0, cosa_ref.shape[0], rope_rows, 0)
    each("phase_one", 2)
    each("phase_two", 1)
    documents = seg_ref[pl.ds(core, 1), :].astype(F32)
    documents = jnp.broadcast_to(documents, (LANES, rows)).T
    lane = (lax.broadcasted_iota(jnp.int32, (rows, LANES), 1) % HEAD_DIM).astype(F32)
    same = documents == lane
    fq_ref[...] = jnp.where(same, 1.0, 0.0).astype(BF)
    fk_ref[...] = jnp.where(same, 0.0, jnp.where(lane < 4.0, MASKED, 0.0)).astype(BF)
    each("phase_one", 3)
    ups.start_hops()
    each("phase_two", 2)
    stores[2].wait()
    stores[3].wait()
    downs.start_hops()
    each("phase_two", 3)
    ups.phase_one(0)
    for load in loads:
        load.wait()
    for name in ("cos", "sin", "fq", "fk"):
        saves[name].start()
    for step in range(2):
        each("phase_swap", step)
    ups.phase_two(0)
    ups.phase_one(1)
    downs.phase_two(0)
    for step in range(2, outer):
        each("phase_swap", step)
    for step in range(outer):
        each("finish", step)
    for name in ("near", "far", "wa"):
        saves[name].start()

    table_ref[...] = near_ref[:, 3 * own :].astype(F32).T[0:8, :]
    wa = wa_ref[...].reshape(6 * width, c_vm.shape[1])

    def wide_events(tick):
        if tick == 0:
            ups.phase_two(1)
            ups.phase_one(2)
        if tick == 1:
            ups.phase_one(3)
            ups.phase_two(2)
        if tick == 3:
            ups.phase_two(3)
        if tick == 4:
            downs.phase_two(1)
            ups.phase_swap(0)
        if tick == 5:
            ups.phase_swap(1)
            downs.phase_swap(0)
        if tick == 6:
            downs.phase_two(2)
            ups.phase_swap(2)
        if tick == 7:
            ups.phase_swap(3)
        if tick == 8:
            downs.phase_two(3)
            downs.phase_swap(1)
        if tick == 9:
            downs.phase_swap(2)

    def row_block(i, _):
        at = pl.ds(pl.multiple_of(i * ROW_BLOCK, ROW_BLOCK), ROW_BLOCK)
        cond = silu_low(c_vm[at, :])
        shift = dot(cond, wa[:width], NT) + table_ref[2:3, :]
        scale = dot(cond, wa[width : 2 * width], NT) + table_ref[3:4, :]
        normal, _ = normalize(x_vm[at, :].astype(F32))
        h = (normal * table_ref[0:1, :] * (1.0 + scale) + shift).astype(BF)
        h_ref[:, at] = h.T
        cos = jnp.concatenate([cos_ref[at, :]] * (own // LANES), axis=1)
        sin = jnp.concatenate([sin_ref[at, :]] * (own // LANES), axis=1)
        for first, w_ref in ((0, near_ref), (own, far_ref)):
            cols = slice(first, first + own)
            query = dot(h, w_ref[:, 0:own])
            query = query * cos + swap_halves(query) * sin
            q_ref[at, cols] = (query * HEAD_DIM**-0.5).astype(BF)
            key = dot(h, w_ref[:, own : 2 * own])
            k_ref[at, cols] = (key * cos + swap_halves(key) * sin).astype(BF)
            v_ref[at, cols] = dot(h, w_ref[:, 2 * own : 3 * own]).astype(BF)
        for tick in range(4):

            @pl.when(i == tick)
            def _():
                wide_events(tick)

        return 0

    lax.fori_loop(0, rows // ROW_BLOCK, row_block, 0)
    for name in ("h", "q", "k", "v"):
        saves[name].start()

    def keep(p):
        lanes = pl.ds(pl.multiple_of(p * LANES, LANES), LANES)
        return pltpu.make_async_copy(o_ref.at[:, lanes], o_out.at[:, lanes], saved.at[len(saves)])

    def head_pair(p, _):
        lanes = pl.ds(pl.multiple_of(p * LANES, LANES), LANES)
        qz[0], qz[1] = split_heads(q_ref[:, lanes], fq_ref[...])
        kz[0], kz[1] = split_heads(k_ref[:, lanes], fk_ref[...])
        vt[...] = v_ref[:, lanes].T
        state = [None, None]
        for j in range(rows // bk):
            block = slice(j * bk, (j + 1) * bk)
            scores = [dot(kz[h, block, :], qz[h], NT) for h in range(2)]
            for h in range(2):
                values = vt[HEAD_DIM * h : HEAD_DIM * (h + 1), block]
                top = jnp.max(scores[h], axis=0, keepdims=True)
                if j:
                    top = jnp.maximum(state[h][0], top)
                weights = jnp.exp(scores[h] - top)
                total = jnp.sum(weights, axis=0, keepdims=True)
                result = dot(values, weights.astype(BF))
                if j:
                    fade = jnp.exp(state[h][0] - top)
                    total = state[h][1] * fade + total
                    result = state[h][2] * fade + result
                state[h] = (top, total, result)
        done = jnp.concatenate([entry[2] / entry[1] for entry in state], axis=0)
        o_ref[:, lanes] = done.T.astype(BF)
        for h in range(2):
            lse_ref[p, h : h + 1, :] = state[h][0] + jnp.log(state[h][1])

        @pl.when(p > 0)
        def _():
            keep(p - 1).wait()

        keep(p).start()
        for tick in range(4, 10):

            @pl.when(p == tick - 4)
            def _():
                wide_events(tick)

        return 0

    lax.fori_loop(0, width // LANES, head_pair, 0)
    downs.phase_swap(3)
    keep(width // LANES - 1).wait()
    for save in saves.values():
        save.wait()
    for step in range(outer):
        ups.finish(step)
        downs.finish(step)
    for entry in (ada, small, ups, downs):
        entry.drain()


def opening(count, tokens, cond, segments, rope, weights):
    ada, norms, qkv, out, up, down = weights
    rows, width = tokens.shape[0] // 2, tokens.shape[1]
    conds, part, hidden = cond.shape[1], width // count, up.shape[1]
    vm = pl.BlockSpec(memory_space=pltpu.VMEM)
    hbm = pl.BlockSpec(memory_space=pl.ANY)
    small = shape_of((width, 3 * width // 2 + LANES), BF)
    act = shape_of((rows, width), BF)
    table = shape_of((rows, LANES), F32)
    feature = shape_of((rows, LANES), BF)
    first = shape_of((width, hidden), BF)
    second = shape_of((width, hidden + width // 2), BF)
    pairs = width // LANES
    pair = pltpu.VMEM((2, rows, LANES), BF)
    half_cols = ada.shape[0] // 2
    kept = [shape_of((width, rows), BF)] + [act] * 4 + [small, small, shape_of((count, 2, half_cols, conds), BF), table, table,
                        feature, feature]
    cuts = (512, hidden // 2, second.shape[1] // 2 // LANES * LANES)
    return pl.pallas_call(
        functools.partial(opening_kernel, count=count, cuts=cuts, bk=512),
        in_specs=[hbm, hbm] + [vm] * 11,
        out_specs=[hbm] * (len(kept) + 4) + [vm, vm],
        out_shape=kept + [first, first, second, second]
        + [shape_of((pairs, 2, rows), F32), shape_of((8, width), F32)],
        scratch_shapes=[pltpu.VMEM(entry.shape, entry.dtype) for entry in kept]
        + [
            pltpu.VMEM((2, half_cols, conds), BF),
            pltpu.VMEM((part, small.shape[1]), BF),
            pltpu.VMEM((part, hidden), BF),
            pltpu.VMEM((part, second.shape[1]), BF),
            pltpu.VMEM((rows, width), BF), pltpu.VMEM((rows, conds), BF),
            pair, pair, pltpu.VMEM((LANES, rows), BF),
            pltpu.SemaphoreType.DMA((6,)),
            pltpu.SemaphoreType.DMA((len(kept),)),
        ] + [Gather.semaphores(count // 4)] * 4,
        compiler_params=pltpu.CompilerParams(
            vmem_limit_bytes=VMEM_LIMIT, collective_id=0, has_side_effects=True
        ),
        name="opening",
    )(tokens, cond, segments, *rope, ada, norms, qkv, out, up, down)


class Scatter:
    def __init__(self, place, first, total, one, two, hops, sems):
        z, y, x, core, outer = (place[name] for name in ("z", "y", "x", "core", "outer"))

        def copy(src, dst, device):
            index = place["next"]
            place["next"] = index + 1
            return pltpu.make_async_remote_copy(
                src_ref=src,
                dst_ref=dst,
                send_sem=sems.at[0, index],
                recv_sem=sems.at[1, index],
                device_id=device,
                device_id_type=pl.DeviceIdType.MESH,
            )

        across_x = (4 * z + 2 * y + 1 - x, core)
        across_y = (4 * z + 2 * (1 - y) + x, core)
        self.one, self.two, self.hops, self.z, self.outer = one, two, hops, z, outer
        if first == "y":
            self.keep_one, self.keep_two = total.at[:, y], one.at[:, x]
            self.copy_one = copy(total.at[:, 1 - y], one, across_y)
            self.copy_two = copy(one.at[:, 1 - x], two, across_x)
        else:
            self.keep_one, self.keep_two = total.at[:, :, x], one.at[:, y]
            self.copy_one = copy(total.at[:, :, 1 - x], one, across_x)
            self.copy_two = copy(one.at[:, 1 - y], two, across_y)
        self.copy_hops = [
            copy(two.at[lax.rem(z + hop, outer)], hops.at[hop - 1],
                 (4 * lax.rem(z + hop, outer) + 2 * y + x, core))
            for hop in range(1, outer)
        ]

    @classmethod
    def halves(cls, place, buffers, sems, order="yx"):
        columns = buffers[0].shape[-1]
        cut = columns // 2 // LANES * LANES
        out = []
        for first, cols in zip(order, (slice(0, cut), slice(cut, columns))):
            views = [ref.at[(slice(None),) * (len(ref.shape) - 1) + (cols,)] for ref in buffers]
            out.append(cls(place, first, *views, sems))
        return out

    def start(self):
        self.copy_one.start()

    def phase_two(self):
        self.copy_one.wait_recv()
        self.one[...] = self.one[...] + self.keep_one[...]
        self.copy_two.start()

    def phase_hops(self):
        self.copy_two.wait_recv()
        self.two[...] = self.two[...] + self.keep_two[...]
        for entry in self.copy_hops:
            entry.start()

    def finish(self):
        total = self.two[self.z].astype(F32)
        for hop, entry in enumerate(self.copy_hops):
            entry.wait_recv()
            total = total + self.hops[hop].astype(F32)
        return total

    def drain(self):
        for entry in [self.copy_one, self.copy_two] + self.copy_hops:
            entry.wait_send()


def across_cores(place, src, dst, sems):
    index = place["next"]
    place["next"] = index + 1
    return pltpu.make_async_remote_copy(
        src_ref=src,
        dst_ref=dst,
        send_sem=sems.at[0, index],
        recv_sem=sems.at[1, index],
        device_id=(place["me"], 1 - place["core"]),
        device_id_type=pl.DeviceIdType.MESH,
    )


def scatter_buffers(outer, blocks, rows, columns):
    lead = () if blocks is None else (blocks,)
    return [
        pltpu.VMEM(lead + (outer, 2, 2, rows, columns), BF),
        pltpu.VMEM(lead + (outer, 2, 2, rows, columns), BF),
        pltpu.VMEM(lead + (outer, 2, rows, columns), BF),
        pltpu.VMEM(lead + (outer, rows, columns), BF),
        pltpu.VMEM(lead + (outer - 1, rows, columns), BF),
    ]


def spread_kernel(h_in, gy_in, ga_in, du_ref, z_ref, o_in, q_in, k_in, v_in, do_in, lse_in,
                  fq_in, fk_in, cos_in, sin_in,
                  dq_out, dk_out, dv_out, last_ref, sum_ref,
                  h_ref, gy_ref, ga_ref, o_ref, q_ref, k_ref, v_ref, do_ref, lse_ref,
                  fq_ref, fk_ref, cos_ref, sin_ref, dq_ref, dk_ref, dv_ref,
                  right, far6, sum6, one6, two6, hop6, far1,
                  qz, kz, qm, dm, vm, kt, delta, dqt,
                  load_sems, input_sems, keep_sems, sems, *, count, bk):
    place = my_place(count)
    others = partners(place)
    greet(others)
    place["next"] = 0
    outer = place["outer"]
    rows, width = o_ref.shape
    pieces = (
        (h_in, h_ref), (gy_in, gy_ref), (ga_in, ga_ref), (o_in, o_ref), (q_in, q_ref),
        (k_in, k_ref), (v_in, v_ref), (do_in, do_ref), (lse_in, lse_ref), (fq_in, fq_ref),
        (fk_in, fk_ref), (cos_in, cos_ref), (sin_in, sin_ref),
    )
    inputs = [
        pltpu.make_async_copy(src, dst, input_sems.at[index])
        for index, (src, dst) in enumerate(pieces)
    ]
    own = width // 2
    each, block = right.shape[0], right.shape[2]
    span = 2 * each * block
    shards = far6.shape[1:]
    tail = far1.shape

    swaps = [across_cores(place, far6.at[j], sum6.at[j], sems) for j in range(2 * each)]
    swaps.append(across_cores(place, far1, last_ref, sems))
    scatters = [
        Scatter.halves(place, [ref.at[j] for ref in (sum6, one6, two6, hop6)], sems)
        for j in range(2 * each)
    ]

    def start(j):
        for entry in scatters[j]:
            entry.start()

    def phase_two(j):
        for entry in scatters[j]:
            entry.phase_two()

    def phase_hops(j):
        for entry in scatters[j]:
            entry.phase_hops()

    def finish(j):
        at = j * block
        for entry in scatters[j]:
            columns = entry.hops.shape[-1]
            sum_ref[:, at : at + columns] = entry.finish()
            at += columns

    lefts, sources = (h_ref, gy_ref), (du_ref, z_ref)

    def load(index, turn):
        near, b = of_turn(turn)
        at = pl.multiple_of((1 - near) * (span // 2) + b * block, block)
        slot = lax.rem(turn, each)
        return pltpu.make_async_copy(
            sources[index].at[:, pl.ds(at, block)], right.at[slot], load_sems.at[slot]
        )

    def of_turn(turn):
        return lax.rem((3 * turn + 0) // 4, 2), lax.rem((7 * turn + 0) // 4, 3)

    inputs[0].start()
    load(0, 0).start()
    for item in inputs[1:4]:
        item.start()
    for b in range(1, each):
        load(0, b).start()
    for item in inputs[4:]:
        item.start()
    inputs[0].wait()
    meet(others)

    for index in range(2):

        def grad_block(turn, _):
            near, b = of_turn(turn)
            load(index, turn).wait()
            grad = dot(lefts[index][...], right[lax.rem(turn, each)])

            @pl.when(turn < each)
            def _():
                load(index, turn + each).start()

            if index == 0:

                @pl.when(turn >= each)
                def _():
                    load(1, turn - each).start()

            @pl.when(near == 0)
            def _():
                far6[index * each + b] = grad.reshape(shards).astype(BF)

            for step in range(each):
                at = index * each + step

                @pl.when(turn == (0, 1, 3)[step])
                def _():
                    swaps[at].start()

                @pl.when(turn == (2, 4, 5)[step])
                def _():
                    swaps[at].wait_recv()
                    sum6[at] = (grad.reshape(shards) + sum6[at].astype(F32)).astype(BF)
                    if at < 2:
                        start(at)

            return 0

        if index:
            inputs[1].wait()
        lax.fori_loop(0, 2 * each, grad_block, 0)
        if index == 0:
            start(2)
    inputs[2].wait()
    inputs[3].wait()
    phase_two(0)
    start(3)
    far1[...] = dot(ga_ref[...], o_ref[:, own:]).reshape(tail).astype(BF)
    swaps[-1].start()
    phase_two(1)
    grad = dot(ga_ref[...], o_ref[:, :own])
    swaps[-1].wait_recv()
    last_ref[...] = (grad.reshape(tail) + last_ref[...].astype(F32)).astype(BF)
    for item in inputs[4:]:
        item.wait()

    def events(p):
        if p < 4:
            phase_two(p + 2)
        if p < 2:
            start(p + 4)
        if p < 4:
            phase_hops(p)
        if p == 4:
            phase_hops(5)
        if 1 < p:
            finish(p - 2)
        if p == 5:
            finish(4)
            finish(5)

    def keep(p):
        lanes = pl.ds(pl.multiple_of(p * LANES, LANES), LANES)
        return [
            pltpu.make_async_copy(src.at[:, lanes], dst.at[:, lanes], keep_sems.at[index])
            for index, (src, dst) in enumerate(
                ((dq_ref, dq_out), (dk_ref, dk_out), (dv_ref, dv_out))
            )
        ]

    zero = jnp.zeros((rows, LANES), BF)

    def unrotate(grad, at):
        return (grad * cos_ref[at, :] - swap_halves(grad) * sin_ref[at, :]).astype(BF)

    def head_pair(p, _):
        lanes = pl.ds(pl.multiple_of(p * LANES, LANES), LANES)
        qz[0], qz[1] = split_heads(q_ref[:, lanes], fq_ref[...])
        kz[0], kz[1] = split_heads(k_ref[:, lanes], fk_ref[...])
        qm[0], qm[1] = split_heads(q_ref[:, lanes], zero)
        dm[0], dm[1] = split_heads(do_ref[:, lanes], zero)
        vm[0], vm[1] = split_heads(v_ref[:, lanes], zero)
        kt[...] = k_ref[:, lanes].T
        product = (do_ref[:, lanes].astype(F32) * o_ref[:, lanes].astype(F32)).T
        delta[0:1, :] = jnp.sum(product[:HEAD_DIM], axis=0, keepdims=True)
        delta[1:2, :] = jnp.sum(product[HEAD_DIM:], axis=0, keepdims=True)
        dqt[...] = jnp.zeros_like(dqt)

        def key_block(first, reach):
            at = slice(first, first + bk)
            dk = jnp.zeros((bk, LANES), F32)
            dv = jnp.zeros((bk, LANES), F32)
            scores = [dot(kz[h, at, :], qz[h, reach, :], NT) for h in range(2)]
            grads = [dot(vm[h, at, :], dm[h, reach, :], NT) for h in range(2)]
            for h in range(2):
                weights = jnp.exp(scores[h] - lse_ref[p, h : h + 1, reach])
                dv = dv + dot(weights.astype(BF), dm[h, reach, :])
                ds = (weights * (grads[h] - delta[h : h + 1, reach])).astype(BF)
                dk = dk + dot(ds, qm[h, reach, :])
                head = slice(HEAD_DIM * h, HEAD_DIM * (h + 1))
                dqt[head, reach] += dot(kt[head, at], ds)
            dk_ref[at, lanes] = unrotate(dk, at)
            dv_ref[at, lanes] = dv.astype(BF)

        for first in range(0, rows, bk):
            low = max(0, (first - rows // 2 + 1) // LANES * LANES)
            high = min(rows, -(-(first + bk + rows // 2 - 1) // LANES) * LANES)
            key_block(first, slice(low, high))
            if first + bk == rows // 2:

                @pl.when(p == 4)
                def _():
                    phase_hops(4)

        dq_ref[:, lanes] = unrotate(dqt[...].T * HEAD_DIM**-0.5, pl.ds(0, rows))

        @pl.when(p > 0)
        def _():
            for entry in keep(p - 1):
                entry.wait()

        for entry in keep(p):
            entry.start()
        for step in range(6):

            @pl.when(p == step)
            def _():
                events(step)

        return 0

    lax.fori_loop(0, width // LANES, head_pair, 0)
    for entry in keep(width // LANES - 1):
        entry.wait()
    for entry in swaps:
        entry.wait_send()
    for pair in scatters:
        for entry in pair:
            entry.drain()


def spread(count, h_two, gy, ga, du, z, mixed, queries, keys, values, upstream, lse, features,
           tables):
    rows, width = mixed.shape
    part = width // count
    outer = count // 4
    hidden = du.shape[1] // 2
    each = 3
    block = hidden // each
    vm = pl.BlockSpec(memory_space=pltpu.VMEM)
    hbm = pl.BlockSpec(memory_space=pl.ANY)
    act = shape_of((rows, width), BF)
    last = shape_of((outer, 2, 2, part, width // 2), BF)
    pair = pltpu.VMEM((2, rows, LANES), BF)
    copies = 7 + 12 * (2 + outer - 1)
    held = [h_two, gy, ga, mixed, queries, keys, values, upstream, lse, *features, *tables]
    return pl.pallas_call(
        functools.partial(spread_kernel, count=count, bk=256),
        in_specs=[hbm] * (len(held) + 2),
        out_specs=[hbm] * 3 + [vm] * 2,
        out_shape=[act, act, act, last, shape_of((part, 2 * hidden), F32)],
        scratch_shapes=[pltpu.VMEM(entry.shape, entry.dtype) for entry in held + [act] * 3]
        + [pltpu.VMEM((each, rows, block), BF)]
        + scatter_buffers(outer, 2 * each, part, block)
        + [pltpu.VMEM(last.shape, BF)]
        + [pair] * 5
        + [
            pltpu.VMEM((LANES, rows), BF),
            pltpu.VMEM((8, rows), F32),
            pltpu.VMEM((LANES, rows), F32),
            pltpu.SemaphoreType.DMA((each,)),
            pltpu.SemaphoreType.DMA((len(held),)),
            pltpu.SemaphoreType.DMA((3,)),
            pltpu.SemaphoreType.DMA((2, copies)),
        ],
        compiler_params=pltpu.CompilerParams(
            vmem_limit_bytes=VMEM_LIMIT, collective_id=1, has_side_effects=True
        ),
        name="spread",
    )(h_two, gy, ga, du, z, mixed, queries, keys, values, upstream, lse, *features, *tables)


def closing_kernel(tok_ref, cond_ref, h_in, dq_in, dk_in, dv_in, near_in, far_in, wa_in,
                   dwa_two_in, dx_in, last_in, mid_ref, p_ref, dp_two_ref,
                   rows_ref, qkv_ref, out_ref, ada_ref, norm_ref, square_ref,
                   h_ref, grads, x_vm, c_vm, near_ref, far_ref, wa_ref, dwa_two_ref, dx_ref,
                   mine, dh_vm, dwa_vm, dp_vm, dwt, plane, column,
                   far3, sum3, one3, two3, hop3, sum2, one2, two2, hop2,
                   sum1, one1, two1, hop1, local, sems, *, count, token_total):
    place = my_place(count)
    place["next"] = 0
    z, y, x, core, outer, me = (place[name] for name in ("z", "y", "x", "core", "outer", "me"))
    rows, width = x_vm.shape
    own = width // 2
    part = width // count
    conds = c_vm.shape[1]
    half_cols = ada_ref.shape[1]
    shards = far3.shape[1:]

    start = pl.multiple_of(core * rows, rows)
    columns = near_ref.shape[1]
    pieces = (
        (h_in, h_ref), (dq_in, grads.at[0]), (dk_in, grads.at[1]), (dv_in, grads.at[2]),
        (tok_ref.at[pl.ds(start, rows)], x_vm), (cond_ref.at[pl.ds(start, rows)], c_vm),
        (near_in.at[:, pl.ds(0, columns)], near_ref), (far_in.at[:, pl.ds(0, columns)], far_ref),
        (wa_in.at[pl.ds(width, width)], wa_ref), (dwa_two_in, dwa_two_ref), (dx_in, dx_ref),
        (last_in, sum1),
    )
    loads = [
        pltpu.make_async_copy(src, dst, local.at[index])
        for index, (src, dst) in enumerate(pieces)
    ]
    loads[9].start()
    loads[11].start()
    for load in loads[:9] + loads[10:11]:
        load.start()

    swaps = [across_cores(place, far3.at[c], sum3.at[c], sems) for c in range(3)]
    scatters = [
        Scatter.halves(place, [ref.at[c] for ref in (sum3, one3, two3, hop3)], sems,
                       "xy" if c % 2 else "yx")
        for c in range(3)
    ]
    scatters.append(Scatter.halves(place, [sum1, one1, two1, hop1], sems, "xy"))
    dwt_rows = dwt.shape[4]
    ada_swap = across_cores(place, dwt.at[:, :, :, 1 - core], sum2, sems)
    cut = dwt_rows // 2
    adas = []
    for first, at in (("x", slice(0, cut)), ("y", slice(cut, dwt_rows))):
        views = [ref.at[(slice(None),) * (len(ref.shape) - 2) + (at,)]
                 for ref in (sum2, one2, two2, hop2)]
        adas.append(Scatter(place, first, *views, sems))
    sends = []

    def copy(src, dst, device):
        index = place["next"]
        place["next"] = index + 1
        entry = pltpu.make_async_remote_copy(
            src_ref=src, dst_ref=dst, send_sem=sems.at[0, index], recv_sem=sems.at[1, index],
            device_id=device, device_id_type=pl.DeviceIdType.MESH,
        )
        sends.append(entry)
        return entry

    row_copies = []
    for i in range(rows // ROW_BLOCK):
        at = pl.ds(i * ROW_BLOCK, ROW_BLOCK)
        row_copies.append(copy(dh_vm.at[at], rows_ref.at[1, at], (me, 1 - core)))
    ada_copy = copy(ada_ref.at[core], ada_ref.at[core], (me, 1 - core))
    beyond = [(lax.rem(me + hop, count), core) for hop in range(1, count)]
    others = beyond + [(me, 1 - core)]
    greet(others)
    plane_copies = [copy(plane.at[core], plane.at[core], (me, 1 - core))]
    column_copies = [copy(column.at[me], column.at[me], device) for device in beyond]

    def all_of(c, method):
        for entry in scatters[c]:
            getattr(entry, method)()

    def project(c):
        if c < 2:
            loads[1 + c].wait()
        grad = dot(h_ref[...], grads[c])
        far3[c] = grad[:, own:].reshape(shards).astype(BF)
        swaps[c].start()
        mine[c] = grad[:, :own].reshape(shards)

    def add_near_grad(c):
        swaps[c].wait_recv()
        sum3[c] = (mine[c] + sum3[c].astype(F32)).astype(BF)
        all_of(c, "start")

    def place_rows(start, values):
        at = 0
        while at < values.shape[0]:
            block, low = divmod(start + at, half_cols)
            high = min(half_cols, low + values.shape[0] - at)
            shard, side = divmod(block, 2)
            dwt[shard // 4, (shard // 2) % 2, shard % 2, side, low:high, :] = values[
                at : at + high - low
            ]
            at += high - low

    loads[9].wait()
    place_rows(2 * width, dwa_two_ref[:conds, :].T.astype(BF))
    dwa_vm[...] = jnp.zeros_like(dwa_vm)
    dp_vm[...] = jnp.zeros_like(dp_vm)
    dp_vm[1:2, :] = dp_two_ref[0:1, :]
    for block in range(4):
        dp_vm[4 + block : 5 + block, :] = dwa_two_ref[
            conds : conds + 1, block * width : (block + 1) * width
        ]
    loads[0].wait()
    meet(others)
    loads[11].wait()
    all_of(3, "start")
    project(0)
    project(1)
    add_near_grad(0)
    loads[3].wait()
    for load in loads[4:9]:
        load.wait()

    gain = p_ref[0:1, :]

    def spread_of(at):
        scale = dot(silu_low(c_vm[at, :]), wa_ref[...], NT) + p_ref[3:4, :]
        return 1.0 + scale

    def first_pass(i, _):
        at = pl.ds(pl.multiple_of(i * ROW_BLOCK, ROW_BLOCK), ROW_BLOCK)
        dh = jnp.zeros((ROW_BLOCK, width), F32)
        for first, w_ref in ((0, near_ref), (own, far_ref)):
            cols = slice(first, first + own)
            for c in range(3):
                dh = dh + dot(grads[c, at, cols], w_ref[:, c * own : (c + 1) * own], NT)
        dh_vm[at, :] = dh
        normal, _ = normalize(x_vm[at, :].astype(F32))
        dn = dh * normal
        summed = cond_rows(silu_low(c_vm[at, :]))
        dwa_vm[:, :width] += dot(summed, dh.astype(BF))
        dwa_vm[:, width:] += dot(summed, (dn * gain).astype(BF))
        dp_vm[0:1, :] += jnp.sum(dn * spread_of(at), axis=0, keepdims=True)

        @pl.when(i == 0)
        def _():
            add_near_grad(1)
            all_of(3, "phase_two")

        @pl.when(i == 2)
        def _():
            all_of(0, "phase_two")
            all_of(3, "phase_hops")

        return 0

    lax.fori_loop(0, rows // ROW_BLOCK, first_pass, 0)

    place_rows(0, dwa_vm[:conds, :].T.astype(BF))
    for block in range(2):
        dp_vm[2 + block : 3 + block, :] = dwa_vm[
            conds : conds + 1, block * width : (block + 1) * width
        ]
    lane = lax.broadcasted_iota(jnp.int32, (16, conds), 1)
    for shard in range(count):
        gone = dp_vm[...] if shard == 0 else pltpu.roll(dp_vm[...], width - shard * part, 1)
        gone = jnp.where(lane < part, gone[:, :conds], 0.0).astype(BF)
        for side in range(2):
            dwt[shard // 4, (shard // 2) % 2, shard % 2, side, half_cols:, :] = gone
    ada_swap.start()
    all_of(1, "phase_two")
    project(2)
    ada_swap.wait_recv()
    sum2[...] = sum2[...] + dwt[:, :, :, core]
    for entry in adas:
        entry.start()
    add_near_grad(2)
    all_of(0, "phase_hops")
    loads[10].wait()

    def events(i):
        if i == 1:
            all_of(1, "phase_hops")
        if i == 2:
            for entry in adas:
                entry.phase_two()
        if i == 3:
            all_of(2, "phase_two")

    def keep(i):
        at = pl.ds(pl.multiple_of(i * ROW_BLOCK, ROW_BLOCK), ROW_BLOCK)
        return pltpu.make_async_copy(dh_vm.at[at], rows_ref.at[0, at], local.at[i])

    def second_pass(i, _):
        at = pl.ds(pl.multiple_of(i * ROW_BLOCK, ROW_BLOCK), ROW_BLOCK)
        normal, rstd = normalize(x_vm[at, :].astype(F32))
        grad = dh_vm[at, :] * gain * spread_of(at)
        dh_vm[at, :] = dx_ref[at, :] + norm_backward(grad, normal, rstd)
        keep(i).start()
        for step in range(rows // ROW_BLOCK):

            @pl.when(i == step)
            def _():
                row_copies[step].start()
                if step < 4:
                    events(step)

        return 0

    lax.fori_loop(0, rows // ROW_BLOCK, second_pass, 0)

    for entry in adas:
        entry.phase_hops()
    squares = jnp.sum((mid_ref[...] / token_total) ** 2)
    all_of(2, "phase_hops")
    for c in range(4):
        target, at = (qkv_ref, c * own) if c < 3 else (out_ref, 0)
        for entry in scatters[c]:
            total = entry.finish()
            target[:, at : at + total.shape[1]] = total
            squares = squares + jnp.sum((total / token_total) ** 2)
            at += total.shape[1]
    first, second = adas[0].finish(), adas[1].finish()
    rest = half_cols - cut
    ada_ref[core, 0:cut, :] = first
    ada_ref[core, cut:, :] = second[:rest]
    norm_ref[...] = second[rest : rest + 8]
    ada_copy.start()
    squares = squares + jnp.sum((first / token_total) ** 2)
    squares = squares + jnp.sum((second[:rest] / token_total) ** 2)
    squares = squares + 0.5 * jnp.sum((second[rest:] / token_total) ** 2)
    plane[core] = jnp.full((8, LANES), squares, F32)
    for entry in plane_copies:
        entry.start()
    for entry in plane_copies:
        entry.wait_recv()
    column[me] = plane[0] + plane[1]
    for entry in column_copies:
        entry.start()
    for entry in column_copies:
        entry.wait_recv()
    square_ref[...] = jnp.sum(column[...], axis=0)
    ada_copy.wait_recv()
    for i, entry in enumerate(row_copies):
        keep(i).wait()
        entry.wait_recv()
    for entry in swaps + [ada_swap] + sends:
        entry.wait_send()
    for entry in [part for pair in scatters for part in pair] + adas:
        entry.drain()


def closing(count, tokens, cond, h_one, grads, dx, wa, norms, near, far, dwa_two, dp_two,
            last, middle_sum, token_total):
    rows, width = dx.shape
    conds = cond.shape[1]
    part = width // count
    outer = count // 4
    half_cols = wa.shape[0] // count // 2
    vm = pl.BlockSpec(memory_space=pltpu.VMEM)
    hbm = pl.BlockSpec(memory_space=pl.ANY)
    copies = 5 + 10 * (2 + outer - 1) + rows // ROW_BLOCK + 2 + count - 1
    act = pltpu.VMEM((rows, width), BF)
    half_weights = pltpu.VMEM((width, 3 * width // 2), BF)
    return pl.pallas_call(
        functools.partial(closing_kernel, count=count, token_total=token_total),
        in_specs=[hbm] * 12 + [vm] * 3,
        out_specs=[hbm] + [vm] * 5,
        out_shape=[
            shape_of((2, rows, width), F32),
            shape_of((part, 3 * width // 2), F32),
            shape_of((part, width // 2), F32),
            shape_of((2, half_cols, conds), F32),
            shape_of((8, conds), F32),
            shape_of((8, LANES), F32),
        ],
        scratch_shapes=[
            pltpu.VMEM((width, rows), BF), pltpu.VMEM((3, rows, width), BF), act,
            pltpu.VMEM((rows, conds), BF),
            half_weights, half_weights,
            pltpu.VMEM((width, conds), BF),
            pltpu.VMEM(dwa_two.shape, F32),
            pltpu.VMEM((rows, width), F32),
            pltpu.VMEM((3, outer, 2, 2, part, width // 2), F32),
            pltpu.VMEM((rows, width), F32),
            pltpu.VMEM((conds + 16, 2 * width), F32),
            pltpu.VMEM((16, width), F32),
            pltpu.VMEM((outer, 2, 2, 2, half_cols + 16, conds), BF),
            pltpu.VMEM((2, 8, LANES), F32),
            pltpu.VMEM((count, 8, LANES), F32),
        ]
        + scatter_buffers(outer, 3, part, width // 2)
        + scatter_buffers(outer, None, half_cols + 16, conds)[1:]
        + scatter_buffers(outer, None, part, width // 2)[1:]
        + [pltpu.SemaphoreType.DMA((12,)), pltpu.SemaphoreType.DMA((2, copies))],
        compiler_params=pltpu.CompilerParams(
            vmem_limit_bytes=VMEM_LIMIT, collective_id=2, has_side_effects=True
        ),
        name="closing",
    )(tokens, cond, h_one, *grads, near, far, wa, dwa_two, dx, last, middle_sum, norms, dp_two)


def update_kernel(half, step, ina_ref, inb_ref, resa_ref, resb_ref, up_ref, down_ref, qkv_ref,
                  out_ref, ada_ref, norm_ref, square_ref, *refs, token_total):
    state, (grad_out, res_out, norm_out), new = refs[:18], refs[18:21], refs[21:]
    i, steps = pl.program_id(0), pl.num_programs(0)
    here = (i // (steps // 2)) == half[0]

    @pl.when(here)
    def _():
        grad_out[...] = ina_ref[0]
        res_out[...] = resa_ref[...]

    @pl.when(jnp.logical_not(here))
    def _():
        grad_out[...] = inb_ref[0]
        res_out[...] = resb_ref[...]

    grad_norm = jnp.sqrt(square_ref[0:1, :])
    norm_out[...] = grad_norm
    clip_factor = jnp.minimum(1.0, clip_limit / (grad_norm + 1e-06))[:, 0:1] / token_total
    count = jnp.full((1, LANES), step[0], jnp.int32).astype(F32)
    fix_one = (1.0 - jnp.exp(count * math.log(0.9)))[:, 0:1]
    fix_two = (1.0 - jnp.exp(count * math.log(0.999)))[:, 0:1]

    def update(index, grad):
        entry = [ref[...] for ref in state[3 * index : 3 * index + 3]]
        values = adam_update(*entry, grad, clip_factor, fix_one, fix_two, step_rates[index],
                             decay_rates[index])
        for ref, value in zip(new[3 * index : 3 * index + 3], values):
            ref[...] = value

    update(0, ada_ref[...])
    update(4, up_ref[...])
    update(5, down_ref[...])

    @pl.when(i < 3)
    def _():
        update(2, qkv_ref[...][None])

    @pl.when(i == 3)
    def _():
        update(1, norm_ref[:, : state[3].shape[1]])
        update(3, out_ref[...])


def update_stage(half, step, input_rows, result, result_far, sums, state, token_total):
    rows, width = result.shape
    middle_sum, qkv_sum, out_sum, ada_sum, norm_sum, squares = sums
    ada_sum = ada_sum.reshape(-1, ada_sum.shape[-1])
    steps = 4
    blocks = steps // 2
    size = rows // blocks
    hidden = middle_sum.shape[1] // 2

    def side(match, lead):
        def index(i, half, step):
            same = (i // blocks == half[0]) == match
            at = jnp.where(same, i % blocks, jnp.where(i < blocks, 0, blocks - 1))
            return lead + (at, 0)

        return index

    block = (size, width)
    out = pl.BlockSpec(block, lambda i, half, step: (i, 0))
    fixed = lambda entry: pl.BlockSpec(entry.shape, lambda *_, n=entry.ndim: (0,) * n)
    slab = pl.BlockSpec((state[12].shape[0], hidden // steps), lambda i, *_: (0, i))
    next_slab = pl.BlockSpec((state[12].shape[0], hidden // steps), lambda i, *_: (0, steps + i))
    third = (state[6].shape[1], state[6].shape[2])
    qkv_spec = pl.BlockSpec((1,) + third, lambda i, *_: (jnp.minimum(i, 2), 0, 0))
    ada_spec = pl.BlockSpec((ada_sum.shape[0] // steps, ada_sum.shape[1]), lambda i, *_: (i, 0))
    specs = (
        [ada_spec] * 3 + [fixed(state[3])] * 3 + [qkv_spec] * 3 + [fixed(state[9])] * 3
        + [slab] * 6
    )
    return pl.pallas_call(
        functools.partial(update_kernel, token_total=token_total),
        grid_spec=pltpu.PrefetchScalarGridSpec(
            num_scalar_prefetch=2,
            grid=(steps,),
            in_specs=[
                pl.BlockSpec((1,) + block, side(True, (0,))),
                pl.BlockSpec((1,) + block, side(False, (1,))),
                pl.BlockSpec(block, side(True, ())),
                pl.BlockSpec(block, side(False, ())),
                slab, next_slab,
                pl.BlockSpec(third, lambda i, *_: (0, jnp.minimum(i, 2))),
                fixed(out_sum), ada_spec, fixed(norm_sum), fixed(squares),
            ] + specs,
            out_specs=[out, out, pl.BlockSpec((1, LANES), lambda *_: (0, 0))] + specs,
        ),
        out_shape=[shape_of((2 * rows, width), F32), shape_of((2 * rows, width), BF),
                   shape_of((1, LANES), F32)]
        + [shape_of(entry.shape, F32) for entry in state],
        compiler_params=params(),
        name="update_stage",
    )(half, step, input_rows, input_rows, result, result_far, middle_sum, middle_sum, qkv_sum,
      out_sum, ada_sum, norm_sum, squares, *state)


def factors(count):
    return (count // 4, 2, 2)


def swap_mp(value):
    return lax.ppermute(value, "mp", [(0, 1), (1, 0)])


def swap_dp(value, distance):
    count = lax.axis_size("dp")
    return lax.ppermute(value, "dp", [(i, i ^ distance) for i in range(count)])


def turn_dp(value, distance):
    count = lax.axis_size("dp")
    return lax.ppermute(value, "dp", [(i, (i + distance) % count) for i in range(count)])


def pick(value, index, axis):
    return lax.dynamic_index_in_dim(value, index, axis, keepdims=False)


def scatter_sum(parts, order):
    count = lax.axis_size("dp")
    outer, mid, inner = factors(count)
    me = lax.axis_index("dp")
    place = {4: me // 4, 2: (me // 2) % 2, 1: me % 2}

    def widen(part):
        return part.reshape((outer, mid, inner) + part.shape[1:]).astype(F32)

    total = widen(parts[0])
    for part in parts[1:]:
        total = total + widen(part)
    for distance in order:
        axis = 1 if (distance == 2 or total.ndim == 4) else 2
        gone = pick(total, 1 - place[distance], axis).astype(BF)
        total = pick(total, place[distance], axis) + swap_dp(gone, distance).astype(F32)
    arrived = [
        turn_dp(pick(total, (place[4] + hop) % outer, 0).astype(BF), 4 * hop)
        for hop in range(1, outer)
    ]
    total = pick(total, place[4], 0)
    for piece in arrived:
        total = total + piece.astype(F32)
    return total


def scatter_halves(near, far_sum):
    count = lax.axis_size("dp")
    width, columns = near.shape
    cut = columns // 2 // LANES * LANES
    shards = lambda value: value.reshape(count, width // count, value.shape[1])
    first = scatter_sum([shards(near[:, :cut]), shards(far_sum[:, :cut])], (2, 1))
    second = scatter_sum([shards(near[:, cut:]), shards(far_sum[:, cut:])], (1, 2))
    return jnp.concatenate([first, second], axis=1)


def sum_everywhere(value):
    value = value + swap_mp(value)
    distance = 1
    while distance < lax.axis_size("dp"):
        value = value + swap_dp(value, distance)
        distance *= 2
    return value


def in_order(half, near, far):
    first = jnp.where(half == 0, near, far)
    second = jnp.where(half == 0, far, near)
    return jnp.concatenate([first, second], axis=0)


def per_device(
    tokens, cond, segments, out_grad, step,
    ada_weight, ada_first, ada_second,
    norm_params, norm_first, norm_second,
    qkv_weight, qkv_first, qkv_second,
    out_weight, out_first, out_second,
    up_weight, up_first, up_second,
    down_weight, down_first, down_second,
):
    count = lax.axis_size("dp")
    width = tokens.shape[1]
    rows = tokens.shape[0] // 2
    conds = cond.shape[1]
    part = width // count
    half = lax.axis_index("mp")
    half_ref = half.reshape(1).astype(jnp.int32)
    token_total = float(tokens.shape[0] * count)

    fused = count == 16 and part % 16 == 0 and ada_weight.shape[1] % 32 == 0
    if fused:
        (h_one, queries, keys, values, mixed, near, far, wa, cosines, sines, query_lanes,
         key_lanes, up_near, up_far, down_near, down_far, lse, norms) = opening(
            count, tokens, cond, segments, rope_constants(rows),
            (ada_weight.T, norm_params, qkv_weight, out_weight.T, up_weight, down_weight.T),
        )
        wa = wa.reshape(-1, conds)
        features, tables = (query_lanes, key_lanes), (cosines, sines)
    else:
        ada_shard = ada_weight.T.astype(BF)
        small_shard = jnp.concatenate(
            [
                qkv_weight.astype(BF).transpose(1, 0, 2).reshape(part, -1),
                jnp.pad(norm_params.astype(BF).T, ((0, 0), (0, LANES - 8))),
            ],
            axis=1,
        )
        down_shard = jnp.concatenate([down_weight.astype(BF).T, out_weight.astype(BF).T], axis=1)
        segment = pick(segments, half, 0)
        features = document_features(segment)
        tables = rope_tables(rows)
        wa = lax.all_gather(ada_shard, "dp", axis=0, tiled=True)
        near = lax.all_gather(small_shard, "dp", axis=0, tiled=True)
        far = swap_mp(near)
        norms = near[:, -LANES:].T[:8].astype(F32)
        up_near = lax.all_gather(up_weight.astype(BF), "dp", axis=0, tiled=True)
        down_near = lax.all_gather(down_shard, "dp", axis=0, tiled=True)
        up_far, down_far = swap_mp(up_near), swap_mp(down_near)
        h_one, queries, keys, values = first_stage(
            half_ref, tokens, cond, wa, norms, near, far, tables
        )
        mixed, lse = attend(queries, keys, values, segment, features)
    result, dx, upstream, z, gy, h_two, du, ga, dwa_two, dp_two = middle_stage(
        half_ref, tokens, out_grad, cond, mixed, wa, norms, up_near, up_far, down_near, down_far
    )
    result_far = swap_mp(result)

    block = width // 2
    if fused:
        *grads, last, middle_sum = spread(
            count, h_two, gy, ga, du, z, mixed, queries, keys, values, upstream, lse, features,
            tables,
        )
    else:
        steps = du.shape[1] // 2 // block

        def middle_grads(which, name):
            return weight_grads(
                [gy.T, h_two.T, ga.T], [du, z, mixed],
                [(steps, 1, 0, which * steps), (steps, 0, 1, which * steps), (1, 2, 2, which)],
                block, name,
            )

        middle_far = swap_mp(middle_grads(1, "middle_grads_far"))
        middle_near = middle_grads(0, "middle_grads_near")
        middle_sum = scatter_halves(middle_near, middle_far)
        grads = attend_back(
            queries, keys, values, upstream, mixed, lse, segment, features, tables
        )

    if fused:
        input_rows, first_sum, out_sum, ada_halves, norm_sum, squares = closing(
            count, tokens, cond, h_one, grads, dx, wa, norms, near, far, dwa_two, dp_two,
            last, middle_sum, token_total,
        )
        turn = lambda group: tuple(entry.T for entry in group)
        ada_state = (ada_weight, ada_first, ada_second)
        out_state = (out_weight, out_first, out_second)
        down_state = (down_weight, down_first, down_second)
        state = (
            *turn(ada_state), norm_params, norm_first, norm_second,
            qkv_weight, qkv_first, qkv_second, *turn(out_state), up_weight, up_first, up_second,
            *turn(down_state),
        )
        input_grad, result, grad_norm, *new = update_stage(
            half_ref, step, input_rows, result, result_far,
            (middle_sum, first_sum, out_sum, ada_halves, norm_sum, squares), state, token_total,
        )
        return (
            result, input_grad, grad_norm[0, :1],
            *turn(new[:3]), *new[3:9], *turn(new[9:12]), *new[12:15], *turn(new[15:]),
        )

    def first_grads(which, name):
        return weight_grads(
            [h_one], list(grads), [(1, 0, index, which) for index in range(3)], block, name
        )

    first_far = swap_mp(first_grads(1, "first_grads_far"))
    first_near = first_grads(0, "first_grads_near")
    first_sum = scatter_halves(first_near, first_far)

    input_grad, dwa_one, dp_one = last_stage(
        half_ref, tokens, cond, dx, grads, wa, norms, near, far
    )
    input_far = swap_mp(input_grad)

    dwa = jnp.concatenate([dwa_one, dwa_two], axis=1)
    ada_cols = dwa.shape[1] // count
    dwa_rows = dwa[:conds].T.astype(BF).reshape(count, 2, ada_cols // 2, conds)
    norm_rows = jnp.concatenate(
        [dp_one[0:1], dp_two[0:1], dwa[conds].reshape(6, width)], axis=0
    ).astype(BF)
    norm_rows = norm_rows.reshape(8, count, part).transpose(1, 0, 2)
    norm_rows = jnp.pad(norm_rows, ((0, 0), (0, 0), (0, conds - part)))
    ada_near = jnp.concatenate([pick(dwa_rows, half, 1), norm_rows], axis=1)
    ada_far = swap_mp(jnp.concatenate([pick(dwa_rows, 1 - half, 1), norm_rows], axis=1))
    ada_sum = scatter_sum([ada_near, ada_far], (2, 1))
    ada_half, norm_sum = ada_sum[: ada_cols // 2], ada_sum[ada_cols // 2 :, :part]
    ada_rows = in_order(half, ada_half, swap_mp(ada_half))

    wide_cols = du.shape[1] // 2
    up_mean = middle_sum[:, :wide_cols] / token_total
    down_mean = middle_sum[:, wide_cols : 2 * wide_cols] / token_total
    out_mean = middle_sum[:, 2 * wide_cols :] / token_total
    qkv_mean = first_sum / token_total
    ada_mean = ada_rows / token_total
    norm_mean = norm_sum / token_total
    local_sq = (
        jnp.sum(qkv_mean * qkv_mean)
        + jnp.sum(out_mean * out_mean)
        + jnp.sum(up_mean * up_mean)
        + jnp.sum(down_mean * down_mean)
        + 0.5 * (jnp.sum(ada_mean * ada_mean) + jnp.sum(norm_mean * norm_mean))
    )
    grad_norm = jnp.sqrt(sum_everywhere(jnp.full((8, LANES), local_sq, F32))[0, 0])
    clip_factor = jnp.minimum(1.0, clip_limit / (grad_norm + 1e-06))
    step_count = step[0].astype(F32)
    fix_one = 1.0 - jnp.exp(step_count * math.log(0.9))
    fix_two = 1.0 - jnp.exp(step_count * math.log(0.999))

    ada_grad = ada_mean.T
    qkv_grad = qkv_mean.reshape(part, 3, -1).transpose(1, 0, 2)
    state = (
        (ada_weight, ada_first, ada_second, ada_grad),
        (norm_params, norm_first, norm_second, norm_mean),
        (qkv_weight, qkv_first, qkv_second, qkv_grad),
        (out_weight, out_first, out_second, out_mean.T),
        (up_weight, up_first, up_second, up_mean),
        (down_weight, down_first, down_second, down_mean.T),
    )
    outputs = [
        in_order(half, result, result_far),
        in_order(half, input_grad, input_far),
        grad_norm.reshape(1),
    ]
    for index, entry in enumerate(state):
        outputs += adam_update(
            *entry, clip_factor, fix_one, fix_two, step_rates[index], decay_rates[index]
        )
    return tuple(outputs)


def solution(mesh):
    column = (P(None, "dp"),) * 3
    weights = (
        column
        + column
        + (P(None, "dp", "mp"),) * 3
        + (P("mp", "dp"),) * 3
        + (P("dp", "mp"),) * 3
        + (P("mp", "dp"),) * 3
    )
    row = P("dp", None)
    return jax.shard_map(
        per_device,
        mesh=mesh,
        in_specs=(row, row, row, row, P()) + weights,
        out_specs=(row, row, P()) + weights,
        check_vma=False,
    )
```
